32 devices in a mesh: section: 2 (over y), row: 4 (over z), col: 4 (over x, core).
Axes of the slice: x: 2, y: 2, z: 4, core: 2. Of those that a mesh axis runs over, the one named last changes fastest.
Arguments:
- inputs: bfloat16 [2, 4096, 2048], P(None, ('row', 'col')), may hold values from -6 to 6
- cotangent: bfloat16 [2, 4096, 2048], P(None, ('row', 'col')), may hold values from -6 to 6
- qkv_weight: bfloat16 [2, 2048, 8, 768], P('section', 'row', 'col'), may hold values from -0.125 to 0.125
- qkv_bias: bfloat16 [2, 8, 768], P('section', 'col', 'row'), may hold values from -3 to 3
- out_weight: bfloat16 [2, 2048, 2048], P('section', 'col', 'row'), may hold values from -1 to 1
- fc_in_weight: bfloat16 [2, 2048, 8192], P('section', 'row', 'col'), may hold values from -0.125 to 0.125
- fc_in_bias: bfloat16 [2, 8192], P('section', ('col', 'row')), may hold values from -3 to 3
- fc_out_weight: bfloat16 [2, 8192, 2048], P('section', 'col', 'row'), may hold values from -0.0625 to 0.0625
- norm1_gain: bfloat16 [2, 2048], P('section', ('row', 'col')), may hold values from 0.099609375 to 1.8984375
- norm1_bias: bfloat16 [2, 2048], P('section', ('row', 'col')), may hold values from -2 to 2
- norm2_gain: bfloat16 [2, 2048], P('section', ('row', 'col')), may hold values from 0.099609375 to 1.8984375
- norm2_bias: bfloat16 [2, 2048], P('section', ('row', 'col')), may hold values from -2 to 2
- out_bias: bfloat16 [2, 2048], P('section', ('row', 'col')), may hold values from -3 to 3
- fc_out_bias: bfloat16 [2, 2048], P('section', ('row', 'col')), may hold values from -3 to 3
Outputs:
- layer_outputs: bfloat16 [2, 2, 4096, 2048], P('section', None, ('row', 'col'))
- input_gradients: bfloat16 [2, 2, 4096, 2048], P('section', None, ('row', 'col'))
- qkv_weight_grad: float32 [2, 2048, 8, 768], P('section', 'row', 'col')
- qkv_bias_grad: float32 [2, 8, 768], P('section', 'col', 'row')
- out_weight_grad: float32 [2, 2048, 2048], P('section', 'col', 'row')
- fc_in_weight_grad: float32 [2, 2048, 8192], P('section', 'row', 'col')
- fc_in_bias_grad: float32 [2, 8192], P('section', ('col', 'row'))
- fc_out_weight_grad: float32 [2, 8192, 2048], P('section', 'col', 'row')
- norm1_gain_grad: float32 [2, 2048], P('section', ('row', 'col'))
- norm1_bias_grad: float32 [2, 2048], P('section', ('row', 'col'))
- norm2_gain_grad: float32 [2, 2048], P('section', ('row', 'col'))
- norm2_bias_grad: float32 [2, 2048], P('section', ('row', 'col'))
- out_bias_grad: float32 [2, 2048], P('section', ('row', 'col'))
- fc_out_bias_grad: float32 [2, 2048], P('section', ('row', 'col'))
The draws below stay inside these ranges and needn't reach their ends.
All inputs are finite; a program needn't handle non-finite values.
Results may differ from the reference program's by a relative error of at most 0.015.
Values may be sent and summed in bfloat16 or wider, within the bound.
No kernel may reach another device: no remote copies, remote signals or barrier semaphores. Data moves between devices by JAX's collectives and lax.ppermute only.
A program may use at most 384 MiB of HBM per device.

```python
import jax
import jax.numpy as jnp
from jax import lax

D = 2048
H = 8
HD = 256
ROT = 64
FF = 8192
SEQ_LEN = 1024
MICRO = 2
LAYERS = 2
ROWS = 4096
N_ROW = 4


def steps_of(stream_key, dims, shards, smallest, high):
    def one(dim, parts):
        steps = jax.random.uniform(jax.random.fold_in(jax.random.fold_in(stream_key, 6), dim), (parts,), jnp.float32, smallest / len(shards), high / len(shards))
        return jnp.repeat(jnp.exp(steps), dims[dim] // parts).reshape((-1,) + (1,) * (len(dims) - dim - 1))

    loudness = one(*shards[0])
    for cut in shards[1:]:
        loudness = loudness * one(*cut)
    return loudness


def normal_values(key, extent, spread, reach, pieces=(), held_as=jnp.bfloat16):
    entries = jax.random.normal(key, extent, jnp.float32) * spread
    if len(pieces) > 0:
        entries = steps_of(key, extent, pieces, -0.22, 0.18) * entries
    return jnp.clip(entries, min=-reach, max=reach).astype(held_as)


def setup_inputs(seed: int = 0) -> dict:
    arg_keys = jax.random.split(jax.random.key(seed), 15)
    return {
        "inputs": normal_values(arg_keys[0], (MICRO, ROWS, D), 1.0, 6.0, ((1, 16),)),
        "cotangent": normal_values(arg_keys[1], (MICRO, ROWS, D), 1.0, 6.0, ((1, 16),)),
        "qkv_weight": normal_values(arg_keys[2], (LAYERS, D, H, 3 * HD), D ** -0.5, 0.125, ((0, 2), (1, 4), (2, 4))),
        "qkv_bias": normal_values(arg_keys[3], (LAYERS, H, 3 * HD), 0.5, 3.0, ((0, 2), (1, 4), (2, 4))),
        "out_weight": normal_values(arg_keys[4], (LAYERS, D, D), (max(D // 64, 4)) ** -0.5, 1.0, ((0, 2), (1, 4), (2, 4))),
        "fc_in_weight": normal_values(arg_keys[5], (LAYERS, D, FF), D ** -0.5, 0.125, ((0, 2), (1, 4), (2, 4))),
        "fc_in_bias": normal_values(arg_keys[6], (LAYERS, FF), 0.5, 3.0, ((0, 2), (1, 16))),
        "fc_out_weight": normal_values(arg_keys[7], (LAYERS, FF, D), FF ** -0.5, 0.0625, ((0, 2), (1, 4), (2, 4))),
        "norm1_gain": jnp.clip(1.0 + 0.18 * jax.random.normal(arg_keys[8], (LAYERS, D), jnp.float32), 0.099609375, 1.8984375).astype(jnp.bfloat16),
        "norm1_bias": normal_values(arg_keys[9], (LAYERS, D), 0.3, 2.0, ((0, 2), (1, 16))),
        "norm2_gain": jnp.clip(1.0 + 0.18 * jax.random.normal(arg_keys[10], (LAYERS, D), jnp.float32), 0.099609375, 1.8984375).astype(jnp.bfloat16),
        "norm2_bias": normal_values(arg_keys[11], (LAYERS, D), 0.3, 2.0, ((0, 2), (1, 16))),
        "out_bias": normal_values(arg_keys[12], (LAYERS, D), 0.5, 3.0, ((0, 2), (1, 16))),
        "fc_out_bias": normal_values(arg_keys[13], (LAYERS, D), 0.5, 3.0, ((0, 2), (1, 16))),
    }


@jax.custom_vjp
def low(v):
    return lax.optimization_barrier(v.astype(jnp.bfloat16)).astype(jnp.float32)

@jax.custom_vjp
def low_back(v):
    return v

def low_keep(v):
    return (low(v), None)

def low_pass(kept, grad):
    return (grad,)

def back_keep(v):
    return (v, None)

def back_low(kept, grad):
    return (low(grad),)
low.defvjp(low_keep, low_pass)
low_back.defvjp(back_keep, back_low)

def matmul(first_operand, second_operand):
    return jnp.dot(first_operand, second_operand, precision=lax.Precision.HIGHEST)

def rotary_tables(length):
    positions = jnp.arange(length).astype(jnp.float32)
    inverse = 10000.0 ** (-jnp.arange(0, ROT, 2).astype(jnp.float32) / ROT)
    angles = positions[:, None] * inverse[None, :]
    angles = jnp.concatenate([angles, angles], axis=-1)
    return (jnp.cos(angles), jnp.sin(angles))

def rotate(values, cosines, sines):
    half_rot = ROT // 2
    turned = values[..., :ROT]
    first_half = turned[..., :half_rot]
    second_half = turned[..., half_rot:]
    swapped = jnp.concatenate([-second_half, first_half], axis=-1)
    return jnp.concatenate([turned * cosines + swapped * sines, values[..., ROT:]], axis=-1)

def layer_forward(hidden, weights, cosines, sines):
    qkv_w, qkv_b, out_w, fc_in_w, fc_in_b, fc_out_w, gain_one, bias_one, gain_two, bias_two, out_b, fc_out_b = weights
    centred = hidden - lax.optimization_barrier(jnp.mean(hidden, axis=-1, keepdims=True))
    scaled = centred * lax.rsqrt(lax.optimization_barrier(jnp.mean(centred * centred, axis=-1, keepdims=True)) + 1e-05)
    normed_one = low(scaled * gain_one + bias_one)
    normed_two = low(scaled * gain_two + bias_two)
    projected = matmul(normed_one, qkv_w.reshape(D, 3 * D)) + qkv_b.reshape(3 * D)
    projected = low_back(projected).reshape(N_ROW, SEQ_LEN, H, 3, HD)
    queries = low(rotate(projected[:, :, :, 0], cosines, sines))
    keys_all = low(rotate(projected[:, :, :, 1], cosines, sines))
    values_all = low(projected[:, :, :, 2])
    scores = jnp.einsum('bqhd,bkhd->bhqk', queries, keys_all, precision=lax.Precision.HIGHEST) * HD ** (-0.5)
    scores = low_back(scores)
    causal_mask = lax.broadcasted_iota(jnp.int32, (SEQ_LEN, SEQ_LEN), 0) >= lax.broadcasted_iota(jnp.int32, (SEQ_LEN, SEQ_LEN), 1)
    scores = jnp.where(causal_mask, scores, -1e+30)
    attention_probs = low(jax.nn.softmax(scores, axis=-1))
    attended = jnp.einsum('bhqk,bkhd->bqhd', attention_probs, values_all, precision=lax.Precision.HIGHEST)
    attended = low(low_back(attended)).reshape(N_ROW * SEQ_LEN, D)
    inner_act = low_back(matmul(normed_two, fc_in_w) + fc_in_b)
    activated = low(jax.nn.gelu(inner_act, approximate=False))
    return hidden + matmul(attended, out_w) + out_b + matmul(activated, fc_out_w) + fc_out_b

def reference(inputs, cotangent, qkv_weight, qkv_bias, out_weight, fc_in_weight, fc_in_bias, fc_out_weight, norm1_gain, norm1_bias, norm2_gain, norm2_bias, out_bias, fc_out_bias):
    params = tuple((member.astype(jnp.float32) for member in (qkv_weight, qkv_bias, out_weight, fc_in_weight, fc_in_bias, fc_out_weight, norm1_gain, norm1_bias, norm2_gain, norm2_bias, out_bias, fc_out_bias)))
    cosines, sines = rotary_tables(SEQ_LEN)
    cosines = cosines[:, None, :]
    sines = sines[:, None, :]

    def chain_layers(first_input, weights, boundaries):
        current = first_input
        outputs_list = []
        for layer_index in range(LAYERS):
            if layer_index > 0:
                current = low(low_back(current)) + boundaries[layer_index - 1]
            current = layer_forward(current, tuple((member[layer_index] for member in weights)), cosines, sines)
            outputs_list.append(current)
        return (current, tuple(outputs_list))

    def micro_step(totals, batch_pair):
        first_input, seed_grad = batch_pair
        boundaries = tuple((jnp.zeros((ROWS, D), jnp.float32) for layer_index in range(LAYERS - 1)))
        unused, pullback, layer_values = jax.vjp(chain_layers, first_input.astype(jnp.float32), params, boundaries, has_aux=True)
        grad_input, grad_params, grad_bounds = pullback(seed_grad.astype(jnp.float32))
        totals = tuple((running + addend for running, addend in zip(totals, grad_params)))
        stacked_values = jnp.stack(layer_values).astype(jnp.bfloat16)
        stacked_grads = jnp.stack((grad_input,) + tuple(grad_bounds)).astype(jnp.bfloat16)
        return (totals, (stacked_values, stacked_grads))
    start_totals = tuple((jnp.zeros_like(member) for member in params))
    totals, (layer_values, grad_values) = lax.scan(micro_step, start_totals, (inputs, cotangent))
    layer_outputs = jnp.swapaxes(layer_values, 0, 1)
    input_gradients = jnp.swapaxes(grad_values, 0, 1)
    return (layer_outputs, input_gradients, totals[0], totals[1], totals[2], totals[3], totals[4], totals[5], totals[6], totals[7], totals[8], totals[9], totals[10], totals[11])
```

```python
import jax
import jax.numpy as jnp
from jax import lax
from jax.experimental import pallas as pl
from jax.experimental.pallas import tpu as pltpu
from jax.sharding import PartitionSpec as P

HD = 256
ROT = 64
SEQ_LEN = 1024


def from_behind(value, axis, steps):
    count = lax.axis_size(axis)
    initial, last = (max(0, -steps), min(count, count - steps))
    return lax.ppermute(value, axis, [(source, source + steps) for source in range(initial, last)])


def rotary_tables(length):
    positions = jnp.arange(length).astype(jnp.float32)
    inverse = 10000.0 ** (-jnp.arange(0, ROT, 2).astype(jnp.float32) / ROT)
    angles = positions[:, None] * inverse[None, :]
    angles = jnp.concatenate([angles, angles], axis=-1)
    return (jnp.cos(angles)[:, None, :], jnp.sin(angles)[:, None, :])


def rotate(values, cosines, sines):
    half_rot = ROT // 2
    turned = values[..., :ROT]
    first_half = turned[..., :half_rot]
    second_half = turned[..., half_rot:]
    swapped = jnp.concatenate([-second_half, first_half], axis=-1)
    return jnp.concatenate([turned * cosines + swapped * sines, values[..., ROT:]], axis=-1)


def rotate_back(grads, cosines, sines):

    def turn_values(values):
        return rotate(values, cosines, sines)

    unused, turn_pull = jax.vjp(turn_values, grads)
    return turn_pull(grads)[0]


def gelu_exact(values):
    return jax.nn.gelu(values, approximate=False)


def norm_rows(row_values):
    centred = row_values - jnp.mean(row_values, axis=-1, keepdims=True)
    inverse_std = lax.rsqrt(jnp.mean(centred * centred, axis=-1, keepdims=True) + 1e-05)
    return (centred * inverse_std, inverse_std)


def contract_rows(first_operand, second_operand):
    return lax.dot_general(
        first_operand, second_operand, (((0,), (0,)), ((), ())), preferred_element_type=jnp.float32
    )


def contract_cols(first_operand, second_operand):
    return lax.dot_general(
        first_operand, second_operand, (((1,), (1,)), ((), ())), preferred_element_type=jnp.float32
    )


def causal_block(row_start, block_rows, row_stop):
    query_pos = row_start + lax.broadcasted_iota(jnp.int32, (block_rows, row_stop), 0)
    key_pos = lax.broadcasted_iota(jnp.int32, (block_rows, row_stop), 1)
    return query_pos >= key_pos


def attention_forward(queries, keys_all, values_all):
    length = queries.shape[0]
    block_rows = min(512, length)
    score_scale = HD ** (-0.5)
    outputs_list = []
    sums_list = []
    for block_index in range(length // block_rows):
        row_start = block_index * block_rows
        row_stop = row_start + block_rows
        scores = (
            jnp.einsum(
                "qhd,khd->hqk",
                queries[row_start:row_stop],
                keys_all[:row_stop],
                preferred_element_type=jnp.float32,
            )
            * score_scale
        )
        scores = jnp.where(causal_block(row_start, block_rows, row_stop)[None], scores, -1e30)
        row_peak = jnp.max(scores, axis=-1, keepdims=True)
        exponents = jnp.exp(scores - row_peak)
        row_total = jnp.sum(exponents, axis=-1, keepdims=True)
        attention_probs = (exponents / row_total).astype(jnp.bfloat16)
        outputs_list.append(
            jnp.einsum(
                "hqk,khd->qhd",
                attention_probs,
                values_all[:row_stop],
                preferred_element_type=jnp.float32,
            )
        )
        sums_list.append((row_peak + jnp.log(row_total))[..., 0])
    attended = jnp.concatenate(outputs_list, axis=0).astype(jnp.bfloat16).reshape(length, -1)
    return (attended, jnp.concatenate(sums_list, axis=1))


def attention_backward(queries, keys_all, values_all, log_sums, grad_attended):
    length, heads_here = (queries.shape[0], queries.shape[1])
    block_rows = min(512, length)
    score_scale = HD ** (-0.5)
    grad_out = grad_attended.reshape(length, heads_here, HD)
    grad_queries_list = []
    grad_keys = jnp.zeros(queries.shape, jnp.float32)
    grad_values = jnp.zeros(queries.shape, jnp.float32)
    for block_index in range(length // block_rows):
        row_start = block_index * block_rows
        row_stop = row_start + block_rows
        scores = (
            jnp.einsum(
                "qhd,khd->hqk",
                queries[row_start:row_stop],
                keys_all[:row_stop],
                preferred_element_type=jnp.float32,
            )
            * score_scale
        )
        scores = jnp.where(causal_block(row_start, block_rows, row_stop)[None], scores, -1e30)
        attention_probs = jnp.exp(scores - log_sums[:, row_start:row_stop, None])
        low_probs = attention_probs.astype(jnp.bfloat16)
        grad_probs = jnp.einsum(
            "qhd,khd->hqk",
            grad_out[row_start:row_stop],
            values_all[:row_stop],
            preferred_element_type=jnp.float32,
        )
        centre_term = jnp.sum(attention_probs * grad_probs, axis=-1, keepdims=True)
        grad_scores = (attention_probs * (grad_probs - centre_term)).astype(jnp.bfloat16)
        grad_queries_list.append(
            jnp.einsum(
                "hqk,khd->qhd", grad_scores, keys_all[:row_stop], preferred_element_type=jnp.float32
            )
            * score_scale
        )
        grad_keys = grad_keys.at[:row_stop].add(
            jnp.einsum(
                "hqk,qhd->khd",
                grad_scores,
                queries[row_start:row_stop],
                preferred_element_type=jnp.float32,
            )
            * score_scale
        )
        grad_values = grad_values.at[:row_stop].add(
            jnp.einsum(
                "hqk,qhd->khd",
                low_probs,
                grad_out[row_start:row_stop],
                preferred_element_type=jnp.float32,
            )
        )
    return (jnp.concatenate(grad_queries_list, axis=0), grad_keys, grad_values)


def forward_turn(my_rows, weights, vectors, cosines, sines):
    qkv_w, qkv_b, out_w, fc_in_w, fc_in_b, fc_out_w = weights
    gain_one, bias_one, gain_two, bias_two, out_b, fc_out_b = vectors
    gathered = lax.all_gather(my_rows, "col", axis=0, tiled=True)
    scaled, inverse_std = norm_rows(gathered.astype(jnp.float32))
    normed_one = (scaled * gain_one + bias_one).astype(jnp.bfloat16)
    normed_two = (scaled * gain_two + bias_two).astype(jnp.bfloat16)
    length = gathered.shape[0]
    heads_here = qkv_w.shape[1]
    projected = jnp.dot(
        normed_one, qkv_w.reshape(qkv_w.shape[0], -1), preferred_element_type=jnp.float32
    ) + qkv_b.reshape(-1).astype(jnp.float32)
    projected = projected.reshape(length, heads_here, 3, HD)
    queries = rotate(projected[:, :, 0], cosines, sines).astype(jnp.bfloat16)
    keys_all = rotate(projected[:, :, 1], cosines, sines).astype(jnp.bfloat16)
    values_all = projected[:, :, 2].astype(jnp.bfloat16)
    attended, log_sums = attention_forward(queries, keys_all, values_all)
    inner_act = jnp.dot(normed_two, fc_in_w, preferred_element_type=jnp.float32) + fc_in_b.astype(
        jnp.float32
    )
    activated = gelu_exact(inner_act).astype(jnp.bfloat16)
    summed = lax.psum_scatter(
        jnp.dot(attended, out_w, preferred_element_type=jnp.float32)
        + jnp.dot(activated, fc_out_w, preferred_element_type=jnp.float32),
        "col",
        scatter_dimension=0,
        tiled=True,
    )
    output = (my_rows.astype(jnp.float32) + summed + out_b + fc_out_b).astype(jnp.bfloat16)
    kept_values = (
        gathered,
        normed_one,
        normed_two,
        queries,
        keys_all,
        values_all,
        attended,
        log_sums,
        inner_act,
    )
    return (output, kept_values)


def backward_turn(grad_rows, kept_values, weights, vectors, cosines, sines):
    (
        gathered,
        normed_one,
        normed_two,
        queries,
        keys_all,
        values_all,
        attended,
        log_sums,
        inner_act,
    ) = kept_values
    qkv_w, qkv_b, out_w, fc_in_w, fc_in_b, fc_out_w = weights
    gain_one, bias_one, gain_two, bias_two, out_b, fc_out_b = vectors
    grad_full = lax.all_gather(grad_rows, "col", axis=0, tiled=True)
    length = grad_full.shape[0]
    rows_here = grad_rows.shape[0]
    own_start = lax.axis_index("col") * rows_here
    activated = gelu_exact(inner_act).astype(jnp.bfloat16)
    out_w_grad = contract_rows(attended, grad_full)
    fc_out_w_grad = contract_rows(activated, grad_full)
    grad_attended = contract_cols(grad_full, out_w).astype(jnp.bfloat16)
    grad_activated = contract_cols(grad_full, fc_out_w)
    unused, gelu_pull = jax.vjp(gelu_exact, inner_act)
    grad_inner = gelu_pull(grad_activated)[0].astype(jnp.bfloat16)
    grad_queries, grad_keys, grad_values = attention_backward(
        queries, keys_all, values_all, log_sums, grad_attended
    )
    grad_q_pre = rotate_back(grad_queries, cosines, sines)
    grad_k_pre = rotate_back(grad_keys, cosines, sines)
    grad_projected = (
        jnp.stack([grad_q_pre, grad_k_pre, grad_values], axis=2)
        .astype(jnp.bfloat16)
        .reshape(length, -1)
    )
    qkv_flat = qkv_w.reshape(qkv_w.shape[0], -1)
    qkv_w_grad = contract_rows(normed_one, grad_projected).reshape(qkv_w.shape)
    qkv_b_grad = jnp.sum(grad_projected.astype(jnp.float32), axis=0).reshape(qkv_b.shape)
    fc_in_w_grad = contract_rows(normed_two, grad_inner)
    fc_in_b_grad = jnp.sum(grad_inner.astype(jnp.float32), axis=0)
    width = qkv_w.shape[0]
    scaled_full, inverse_full = norm_rows(gathered.astype(jnp.float32))
    scaled = lax.dynamic_slice_in_dim(scaled_full, own_start, rows_here, 0)
    inverse_std = lax.dynamic_slice_in_dim(inverse_full, own_start, rows_here, 0)
    dy_sum = jnp.sum(grad_rows.astype(jnp.float32), axis=0)
    both_grads = lax.psum_scatter(
        jnp.concatenate(
            [contract_cols(grad_projected, qkv_flat), contract_cols(grad_inner, fc_in_w)], axis=1
        ),
        "col",
        scatter_dimension=0,
        tiled=True,
    )
    grad_one = both_grads[:, :width]
    grad_two = both_grads[:, width:]
    combined = gain_one * grad_one + gain_two * grad_two
    vector_grads = (
        jnp.sum(grad_one * scaled, axis=0),
        jnp.sum(grad_one, axis=0),
        jnp.sum(grad_two * scaled, axis=0),
        jnp.sum(grad_two, axis=0),
        dy_sum,
    )
    grad_norm = inverse_std * (
        combined
        - jnp.mean(combined, axis=-1, keepdims=True)
        - scaled * jnp.mean(combined * scaled, axis=-1, keepdims=True)
    )
    grad_input = (grad_rows.astype(jnp.float32) + grad_norm).astype(jnp.bfloat16)
    matrix_grads = (qkv_w_grad, qkv_b_grad, out_w_grad, fc_in_w_grad, fc_in_b_grad, fc_out_w_grad)
    return (grad_input, matrix_grads, vector_grads)


def add_tuples(running, addend):
    if running is None:
        return addend
    return tuple((first_part + second_part for first_part, second_part in zip(running, addend)))


def relay_local(
    inputs,
    cotangent,
    qkv_weight,
    qkv_bias,
    out_weight,
    fc_in_weight,
    fc_in_bias,
    fc_out_weight,
    norm1_gain,
    norm1_bias,
    norm2_gain,
    norm2_bias,
    out_bias,
    fc_out_bias,
):
    sections = lax.axis_size("section")
    section_index = lax.axis_index("section")
    micro_count = inputs.shape[0]
    tick_count = micro_count + sections - 1
    is_first = section_index == 0
    is_last = section_index == sections - 1
    cosines, sines = rotary_tables(SEQ_LEN)
    vectors = (
        lax.all_gather(norm1_gain[0], ("row", "col"), axis=0, tiled=True),
        lax.all_gather(norm1_bias[0], ("row", "col"), axis=0, tiled=True),
        lax.all_gather(norm2_gain[0], ("row", "col"), axis=0, tiled=True),
        lax.all_gather(norm2_bias[0], ("row", "col"), axis=0, tiled=True),
        lax.all_gather(out_bias[0], ("row", "col"), axis=0, tiled=True),
        lax.all_gather(fc_out_bias[0], ("row", "col"), axis=0, tiled=True),
    )
    vectors = tuple((member.astype(jnp.float32) for member in vectors))
    received = jnp.zeros_like(inputs[0])
    outputs_list = []
    kept_list = []
    for tick_index in range(tick_count):
        weights = (
            lax.all_gather(qkv_weight[0], "row", axis=0, tiled=True),
            lax.all_gather(qkv_bias[0], "row", axis=1, tiled=True),
            lax.all_gather(out_weight[0], "row", axis=1, tiled=True),
            lax.all_gather(fc_in_weight[0], "row", axis=0, tiled=True),
            lax.all_gather(fc_in_bias[0], "row", axis=0, tiled=True),
            lax.all_gather(fc_out_weight[0], "row", axis=1, tiled=True),
        )
        first_rows = inputs[min(tick_index, micro_count - 1)]
        my_rows = jnp.where(is_first, first_rows, received)
        output, kept_values = forward_turn(my_rows, weights, vectors, cosines, sines)
        outputs_list.append(output)
        kept_list.append(kept_values)
        if tick_index + 1 < tick_count:
            received = from_behind(output, "section", 1)
    layer_outputs = lax.dynamic_slice_in_dim(jnp.stack(outputs_list), section_index, micro_count, 0)
    stacked_kept = tuple((jnp.stack(members) for members in zip(*kept_list)))
    received_grad = jnp.zeros_like(inputs[0])
    grads_list = []
    matrix_total = None
    vector_total = None
    for tick_index in range(tick_count):
        weights = (
            lax.all_gather(qkv_weight[0], "row", axis=0, tiled=True),
            lax.all_gather(qkv_bias[0], "row", axis=1, tiled=True),
            lax.all_gather(out_weight[0], "row", axis=1, tiled=True),
            lax.all_gather(fc_in_weight[0], "row", axis=0, tiled=True),
            lax.all_gather(fc_in_bias[0], "row", axis=0, tiled=True),
            lax.all_gather(fc_out_weight[0], "row", axis=1, tiled=True),
        )
        if tick_index < micro_count:
            seed_grad = cotangent[tick_index]
        else:
            seed_grad = jnp.zeros_like(cotangent[0])
        grad_rows = jnp.where(is_last, seed_grad, received_grad)
        forward_index = jnp.clip(tick_index - sections + 1 + 2 * section_index, 0, tick_count - 1)
        kept_values = tuple(
            (
                lax.dynamic_index_in_dim(member, forward_index, 0, keepdims=False)
                for member in stacked_kept
            )
        )
        grad_input, matrix_grads, vector_grads = backward_turn(
            grad_rows, kept_values, weights, vectors, cosines, sines
        )
        grads_list.append(grad_input)
        if tick_index + 1 < tick_count:
            received_grad = from_behind(grad_input, "section", -1)
        matrix_part = (
            lax.psum_scatter(matrix_grads[0], "row", scatter_dimension=0, tiled=True),
            lax.psum_scatter(matrix_grads[1], "row", scatter_dimension=1, tiled=True),
            lax.psum_scatter(matrix_grads[2], "row", scatter_dimension=1, tiled=True),
            lax.psum_scatter(matrix_grads[3], "row", scatter_dimension=0, tiled=True),
            lax.psum_scatter(matrix_grads[4], "row", scatter_dimension=0, tiled=True),
            lax.psum_scatter(matrix_grads[5], "row", scatter_dimension=1, tiled=True),
        )
        vector_part = (
            lax.psum_scatter(vector_grads[0], ("row", "col"), scatter_dimension=0, tiled=True),
            lax.psum_scatter(vector_grads[1], ("row", "col"), scatter_dimension=0, tiled=True),
            lax.psum_scatter(vector_grads[2], ("row", "col"), scatter_dimension=0, tiled=True),
            lax.psum_scatter(vector_grads[3], ("row", "col"), scatter_dimension=0, tiled=True),
            lax.psum_scatter(vector_grads[4], ("row", "col"), scatter_dimension=0, tiled=True),
        )
        matrix_total = add_tuples(matrix_total, tuple(matrix_part))
        vector_total = add_tuples(vector_total, tuple(vector_part))
    input_gradients = lax.dynamic_slice_in_dim(
        jnp.stack(grads_list), sections - 1 - section_index, micro_count, 0
    )
    return (
        layer_outputs[None],
        input_gradients[None],
        matrix_total[0][None],
        matrix_total[1][None],
        matrix_total[2][None],
        matrix_total[3][None],
        matrix_total[4][None],
        matrix_total[5][None],
        vector_total[0][None],
        vector_total[1][None],
        vector_total[2][None],
        vector_total[3][None],
        vector_total[4][None],
        vector_total[4][None],
    )


F32 = jnp.float32
BF16 = jnp.bfloat16
LANES = 128


def swap(value, axis, bit):
    count = lax.axis_size(axis)
    return lax.ppermute(value, axis, [(source, source ^ bit) for source in range(count)])


def sum_over(value, axis):
    bit = 1
    while bit < lax.axis_size(axis):
        value = value + swap(value, axis, bit)
        bit *= 2
    return value


def place(part, axis, index, length):
    shape = list(part.shape)
    shape[axis] = length
    start = index * part.shape[axis]
    return lax.dynamic_update_slice_in_dim(jnp.zeros(shape, part.dtype), part, start, axis)


def take(value, axis, index, size):
    return lax.dynamic_slice_in_dim(value, index * size, size, axis)


def gather_rows(block):
    half = block.shape[0] // 2
    beside = swap(block, "col", 2)
    across = swap(block, "section", 1)
    corner = jnp.concatenate(
        [swap(beside[:half], "section", 1), swap(across[half:], "col", 2)], axis=0
    )
    near = jnp.concatenate([block, beside], axis=0)
    far = jnp.concatenate([across, corner], axis=0)
    return jnp.concatenate([near, swap(near, "col", 1), far, swap(far, "col", 1)], axis=0), across


def scatter_rows(partial):
    rows, width = partial.shape
    block = rows // 8
    half = block // 2
    parts = partial.reshape(2, 2, 2 * block, width)
    sums = []
    for micro in range(2):
        arrived = swap(parts[micro, 1], "col", 1)
        sums.append((parts[micro, 0].astype(F32) + arrived.astype(F32)).astype(BF16))
    near, far = sums
    first = swap(
        jnp.concatenate([far[:half], far[block : block + half]], axis=0), "section", 1
    ).astype(F32)
    second = swap(
        jnp.concatenate([near[block + half :], far[block + half :]], axis=0), "col", 2
    ).astype(F32)
    top_keep = near[:half].astype(F32) + first[:half]
    top_send = (near[block : block + half].astype(F32) + first[half:]).astype(BF16)
    low_keep = near[half:block].astype(F32) + second[:half]
    low_send = (far[half:block].astype(F32) + second[half:]).astype(BF16)
    top = top_keep + swap(top_send, "col", 2).astype(F32)
    low = low_keep + swap(low_send, "section", 1).astype(F32)
    return jnp.concatenate([top, low], axis=0)


def turn(values, cosines, sines):
    lead = values[:, :LANES]
    lane = lax.broadcasted_iota(jnp.int32, lead.shape, 1)
    ahead = pltpu.roll(lead, LANES - ROT // 2, 1)
    behind = pltpu.roll(lead, ROT // 2, 1)
    lead = lead * cosines + jnp.where(lane < ROT // 2, ahead, behind) * sines
    return jnp.concatenate([lead, values[:, LANES:]], axis=1)


def mm(first_operand, second_operand):
    return jnp.dot(first_operand, second_operand, preferred_element_type=F32)


def project_kernel(x_ref, w_ref, e_ref, cos_ref, sin_ref, q_ref, k_ref, v_ref):
    projected = mm(x_ref[...], w_ref[...]) + e_ref[...]
    cosines, sines = cos_ref[...], sin_ref[...]
    q_ref[...] = (turn(projected[:, :HD], cosines, sines) * HD ** (-0.5)).astype(BF16)
    k_ref[...] = turn(projected[:, HD : 2 * HD], cosines, sines).astype(BF16)
    v_ref[...] = projected[:, 2 * HD :].astype(BF16)


def inner_kernel(x_ref, w_ref, e_ref, act_ref, slope_ref):
    inner = mm(x_ref[...], w_ref[...]) + e_ref[...]
    below = 0.5 + 0.5 * lax.erf(inner * 0.7071067811865476)
    act_ref[...] = (inner * below).astype(BF16)
    density = jnp.exp(-0.5 * inner * inner) * 0.3989422804014327
    slope_ref[...] = (below + inner * density).astype(BF16)


def two_kernel(a_ref, b_ref, c_ref, d_ref, out_ref):
    out_ref[...] = (mm(a_ref[...], b_ref[...]) + mm(c_ref[...], d_ref[...])).astype(BF16)


def two_turned_kernel(a_ref, b_ref, c_ref, d_ref, out_ref):
    out_ref[...] = (
        contract_cols(a_ref[...], b_ref[...]) + contract_cols(c_ref[...], d_ref[...])
    ).astype(BF16)


def attend_kernel(q_ref, k_ref, v_ref, row_ref, col_ref, out_ref, log_ref):
    scores = contract_cols(q_ref[...], k_ref[...])
    scores = jnp.where(row_ref[...] >= col_ref[...], scores, -1e30)
    peak = jnp.max(scores, axis=1, keepdims=True)
    exponents = jnp.exp(scores - peak)
    total = jnp.sum(exponents, axis=1, keepdims=True)
    out_ref[...] = mm((exponents / total).astype(BF16), v_ref[...]).astype(BF16)
    log_ref[...] = peak + jnp.log(total)


def attend_back_kernel(
    q_ref, k_ref, v_ref, row_ref, col_ref, log_ref, do_ref, cos_ref, sin_ref, out_ref, dk_ref, dv_ref
):
    step = pl.program_id(1)
    block = q_ref.shape[0]

    @pl.when(step == 0)
    def _():
        dk_ref[...] = jnp.zeros_like(dk_ref)
        dv_ref[...] = jnp.zeros_like(dv_ref)

    queries, keys_all, grads = (q_ref[...], k_ref[...], do_ref[...])
    scores = contract_cols(queries, keys_all)
    scores = jnp.where(row_ref[...] >= col_ref[...], scores, -1e30)
    probs = jnp.exp(scores - log_ref[...])
    grad_probs = contract_cols(grads, v_ref[...])
    centre = jnp.sum(probs * grad_probs, axis=1, keepdims=True)
    grad_scores = (probs * (grad_probs - centre)).astype(BF16)
    rows = pl.ds(pl.multiple_of(step * block, block), block)
    cosines, sines = cos_ref[rows, :], sin_ref[rows, :]
    grad_queries = mm(grad_scores, keys_all) * HD ** (-0.5)
    out_ref[rows, :HD] = turn(grad_queries, cosines, -sines).astype(BF16)
    dk_ref[...] += contract_rows(grad_scores, queries)
    dv_ref[...] += contract_rows(probs.astype(BF16), grads)

    @pl.when(step == pl.num_programs(1) - 1)
    def _():
        out_ref[:, HD : 2 * HD] = turn(dk_ref[...], cos_ref[...], -sin_ref[...]).astype(BF16)
        out_ref[:, 2 * HD :] = dv_ref[...].astype(BF16)


ROW_BLOCK = 256


def by_rows(width, block=ROW_BLOCK):
    return pl.BlockSpec((block, width), lambda i: (i, 0))


def whole(shape):
    return pl.BlockSpec(shape, lambda *unused: (0,) * len(shape))


def cost(flops, *arrays):
    return pl.CostEstimate(
        flops=flops,
        transcendentals=0,
        bytes_accessed=sum(array.size * array.dtype.itemsize for array in arrays),
    )


def project(x, w, e, tables):
    rows, width = x.shape
    per_micro = tables[0].shape[0] // ROW_BLOCK
    table = pl.BlockSpec((ROW_BLOCK, LANES), lambda i: (i % per_micro, 0))
    out = jax.ShapeDtypeStruct((rows, HD), BF16)
    return pl.pallas_call(
        project_kernel,
        grid=(rows // ROW_BLOCK,),
        in_specs=[by_rows(width), whole(w.shape), whole(e.shape), table, table],
        out_specs=[by_rows(HD)] * 3,
        out_shape=[out] * 3,
        cost_estimate=cost(2 * rows * w.size, x, w, out, out, out),
        name="project",
    )(x, w, e, *tables)


def inner_layer(x, w, e):
    rows, width = x.shape
    out = jax.ShapeDtypeStruct((rows, w.shape[1]), BF16)
    return pl.pallas_call(
        inner_kernel,
        grid=(rows // ROW_BLOCK,),
        in_specs=[by_rows(width), whole(w.shape), whole(e.shape)],
        out_specs=[by_rows(w.shape[1])] * 2,
        out_shape=[out] * 2,
        cost_estimate=cost(2 * rows * w.size, x, w, out, out),
        name="inner",
    )(x, w, e)


def two_products(kernel, a, b, c, d, width, name):
    rows = a.shape[0]
    out = jax.ShapeDtypeStruct((rows, width), BF16)
    return pl.pallas_call(
        kernel,
        grid=(rows // ROW_BLOCK,),
        in_specs=[by_rows(a.shape[1]), whole(b.shape), by_rows(c.shape[1]), whole(d.shape)],
        out_specs=by_rows(width),
        out_shape=out,
        cost_estimate=cost(2 * rows * (b.size + d.size), a, b, c, d, out),
        name=name,
    )(a, b, c, d)


def attend(queries, keys_all, values_all, places):
    rows = queries.shape[0]
    length = places.shape[0]
    steps = length // ROW_BLOCK
    row = pl.BlockSpec((ROW_BLOCK, HD), lambda m, i: (m * steps + i, 0))
    every = pl.BlockSpec((length, HD), lambda m, i: (m, 0))
    out = jax.ShapeDtypeStruct((rows, HD), BF16)
    return pl.pallas_call(
        attend_kernel,
        grid=(rows // length, steps),
        in_specs=[
            row,
            every,
            every,
            pl.BlockSpec((ROW_BLOCK, 1), lambda m, i: (i, 0)),
            pl.BlockSpec((1, length), lambda m, i: (0, 0)),
        ],
        out_specs=[row, pl.BlockSpec((ROW_BLOCK, 1), lambda m, i: (m * steps + i, 0))],
        out_shape=[out, jax.ShapeDtypeStruct((rows, 1), F32)],
        cost_estimate=cost(4 * rows * length * HD, queries, keys_all, values_all, out),
        name="attend",
    )(queries, keys_all, values_all, places[:, None], places[None, :])


def attend_back(queries, keys_all, values_all, places, log_sums, grads, tables):
    rows = queries.shape[0]
    length = places.shape[0]
    steps = length // ROW_BLOCK
    row = pl.BlockSpec((ROW_BLOCK, HD), lambda m, i: (m * steps + i, 0))
    every = pl.BlockSpec((length, HD), lambda m, i: (m, 0))
    out = jax.ShapeDtypeStruct((rows, 3 * HD), BF16)
    return pl.pallas_call(
        attend_back_kernel,
        grid=(rows // length, steps),
        in_specs=[
            row,
            every,
            every,
            pl.BlockSpec((ROW_BLOCK, 1), lambda m, i: (i, 0)),
            pl.BlockSpec((1, length), lambda m, i: (0, 0)),
            pl.BlockSpec((ROW_BLOCK, 1), lambda m, i: (m * steps + i, 0)),
            row,
            whole(tables[0].shape),
            whole(tables[1].shape),
        ],
        out_specs=pl.BlockSpec((length, 3 * HD), lambda m, i: (m, 0)),
        out_shape=out,
        scratch_shapes=[pltpu.VMEM((length, HD), F32), pltpu.VMEM((length, HD), F32)],
        cost_estimate=cost(10 * rows * length * HD, queries, keys_all, values_all, grads, out),
        name="attend_back",
    )(queries, keys_all, values_all, places[:, None], places[None, :], log_sums, grads, *tables)


def local(
    inputs,
    cotangent,
    qkv_weight,
    qkv_bias,
    out_weight,
    fc_in_weight,
    fc_in_bias,
    fc_out_weight,
    norm1_gain,
    norm1_bias,
    norm2_gain,
    norm2_bias,
    out_bias,
    fc_out_bias,
):
    s, r, c = (lax.axis_index("section"), lax.axis_index("row"), lax.axis_index("col"))
    rows_axis, cols_axis = (lax.axis_size("row"), lax.axis_size("col"))
    low = s == 0
    qkv_w, out_w, fc_in_w, fc_out_w = (
        qkv_weight[0], out_weight[0], fc_in_weight[0], fc_out_weight[0],
    )
    deep, heads_here = qkv_w.shape[0], qkv_w.shape[1]
    per = heads_here // 2 * 3 * HD
    inner_here = fc_in_w.shape[1]
    model = inputs.shape[2]

    def both_layers(own_first, own_second):
        return (jnp.where(low, own_first, own_second), jnp.where(low, own_second, own_first))

    def trade(value, axis):
        size = value.shape[axis] // 2
        kept = take(value, axis, s, size)
        return both_layers(kept, swap(take(value, axis, 1 - s, size), "section", 1))

    def gathered(shard, axis):
        return lax.all_gather(shard, "row", axis=axis, tiled=True)

    held = jnp.stack(
        [
            norm1_gain[0].astype(F32),
            norm1_bias[0].astype(F32),
            norm2_gain[0].astype(F32),
            norm2_bias[0].astype(F32),
            out_bias[0].astype(F32) + fc_out_bias[0].astype(F32),
        ]
    )
    held = sum_over(place(held, 1, c, deep), "col")
    gain_one, shift_one, gain_two, shift_two, end_bias = (held[i] for i in range(5))

    out_pair = trade(out_w, 0)
    fc_out_pair = trade(fc_out_w, 0)
    qkv_flat = qkv_w.reshape(deep, -1)
    qkv_pair = trade((qkv_flat.astype(F32) * gain_one[:, None]).astype(BF16), 1)
    fc_in_pair = trade((fc_in_w.astype(F32) * gain_two[:, None]).astype(BF16), 1)

    own_qkv = mm(shift_one.astype(BF16)[None], qkv_flat)[0]
    own_fc = mm(shift_two.astype(BF16)[None], fc_in_w)[0]
    own_qkv = own_qkv + place(qkv_bias[0].astype(F32), 1, r, 3 * HD).reshape(-1)
    own_fc = own_fc + place(fc_in_bias[0].astype(F32), 0, r, inner_here)
    biases = sum_over(
        jnp.concatenate([own_qkv, own_fc, place(end_bias, 0, r, model)]), "row"
    )
    biases = both_layers(biases, swap(biases, "section", 1))
    qkv_e, fc_e, end_e = ([], [], [])
    for member in biases:
        qkv_e.append(take(member[: 2 * per], 0, s, per)[None])
        fc_e.append(take(member[2 * per : 2 * per + inner_here], 0, s, inner_here // 2)[None])
        end_e.append(member[2 * per + inner_here :])

    block_rows = inputs.shape[1]
    masks = jnp.array([0, 2, 1, 3], jnp.int32)
    places = ((c ^ masks)[:, None] * block_rows + jnp.arange(block_rows)[None]).reshape(-1)
    half_rot = ROT // 2
    inverse = 10000.0 ** (-jnp.arange(0, ROT, 2).astype(F32) / ROT)
    angles = places.astype(F32)[:, None] * inverse[None]
    ones = jnp.ones((places.shape[0], LANES - ROT), F32)
    cosines, sines = (jnp.cos(angles), jnp.sin(angles))
    tables = (
        jnp.concatenate([cosines, cosines, ones], axis=1),
        jnp.concatenate([-sines, sines, 0.0 * ones], axis=1),
    )

    hidden = lax.dynamic_index_in_dim(inputs, s, 0, keepdims=False)
    seed = lax.dynamic_index_in_dim(cotangent, s, 0, keepdims=False)

    hidden_list, kept_list, ends = ([], [], [])
    for layer in range(2):
        hidden_list.append(hidden)
        scaled, unused = norm_rows(hidden.astype(F32))
        x, unused = gather_rows(scaled.astype(BF16))
        w_out = gathered(out_pair[layer], 1)
        w_fc_out = gathered(fc_out_pair[layer], 1)
        w_qkv = gathered(qkv_pair[layer], 0)
        w_fc_in = gathered(fc_in_pair[layer], 0)
        queries, keys_all, values_all = project(x, w_qkv, qkv_e[layer], tables)
        attended, log_sums = attend(queries, keys_all, values_all, places)
        activated, slopes = inner_layer(x, w_fc_in, fc_e[layer])
        partial = two_products(
            two_kernel, attended, w_out, activated, w_fc_out, model, "outer"
        )
        summed = scatter_rows(partial)
        hidden = (hidden.astype(F32) + summed + end_e[layer]).astype(BF16)
        ends.append(hidden)
        kept_list.append(
            (x, queries, keys_all, values_all, attended, log_sums, activated, slopes,
             w_qkv, w_out, w_fc_in, w_fc_out)
        )

    def reduced(value, axis):
        return lax.psum_scatter(value, "row", scatter_dimension=axis, tiled=True)

    grads = seed
    grads_out, matrix_list, small_list = ([None, None], [None, None], [None, None])
    for layer in (1, 0):
        (x, queries, keys_all, values_all, attended, log_sums, activated, slopes,
         w_qkv, w_out, w_fc_in, w_fc_out) = kept_list[layer]
        dy, across = gather_rows(grads)
        if layer == 0:
            grads_out[1] = jnp.where(low, grads, across), jnp.where(low, across, grads)
        dy_sum = jnp.sum(grads.astype(F32), axis=0)
        out_part = reduced(contract_rows(attended, dy).astype(BF16), 1)
        fc_out_part = reduced(contract_rows(activated, dy).astype(BF16), 1)
        grad_attended = contract_cols(dy, w_out).astype(BF16)
        grad_inner = (contract_cols(dy, w_fc_out) * slopes.astype(F32)).astype(BF16)
        grad_projected = attend_back(
            queries, keys_all, values_all, places, log_sums, grad_attended, tables
        )
        fc_in_part = reduced(contract_rows(x, grad_inner).astype(BF16), 0)
        qkv_part = reduced(contract_rows(x, grad_projected).astype(BF16), 0)
        partial = two_products(
            two_turned_kernel, grad_projected, w_qkv, grad_inner, w_fc_in, model, "inward"
        )
        combined = scatter_rows(partial)
        scaled, inverse_std = norm_rows(hidden_list[layer].astype(F32))
        grad_norm = inverse_std * (
            combined
            - jnp.mean(combined, axis=-1, keepdims=True)
            - scaled * jnp.mean(combined * scaled, axis=-1, keepdims=True)
        )
        grads = (grads.astype(F32) + grad_norm).astype(BF16)
        small = jnp.concatenate(
            [
                jnp.sum(grad_projected.astype(F32), axis=0),
                jnp.sum(grad_inner.astype(F32), axis=0),
                sum_over(sum_over(dy_sum, "section"), "col"),
            ]
        )
        matrix_list[layer] = (qkv_part, out_part, fc_in_part, fc_out_part)
        small_list[layer] = sum_over(small, "row")

    def to_owner(first, second):
        upper = lax.ppermute(first, "section", [(1, 0)])
        lower = lax.ppermute(second, "section", [(0, 1)])
        return (jnp.where(low, first, lower), jnp.where(low, upper, second))

    smalls = to_owner(*small_list)
    qkv_b_grad = jnp.concatenate([member[:per] for member in smalls])
    fc_in_b_grad = jnp.concatenate([member[per : per + inner_here // 2] for member in smalls])
    end_grad = jnp.where(low, small_list[0], small_list[1])[per + inner_here // 2 :]
    qkv_g, out_g, fc_in_g, fc_out_g = (
        to_owner(*members) for members in zip(*matrix_list)
    )
    qkv_g = jnp.concatenate(qkv_g, axis=1).astype(F32)
    fc_in_g = jnp.concatenate(fc_in_g, axis=1).astype(F32)
    qkv_w_grad = gain_one[:, None] * qkv_g + shift_one[:, None] * qkv_b_grad[None]
    fc_in_w_grad = gain_two[:, None] * fc_in_g + shift_two[:, None] * fc_in_b_grad[None]
    qkv_full, fc_full = (qkv_flat.astype(F32), fc_in_w.astype(F32))
    norms = jnp.stack(
        [
            jnp.sum(qkv_full * qkv_g, axis=1),
            jnp.sum(qkv_full * qkv_b_grad[None], axis=1),
            jnp.sum(fc_full * fc_in_g, axis=1),
            jnp.sum(fc_full * fc_in_b_grad[None], axis=1),
        ]
    )
    norms = take(sum_over(norms, "col"), 1, c, deep // cols_axis)
    end_grad = take(end_grad, 0, r * cols_axis + c, deep // cols_axis)
    last = lax.ppermute(ends[1], "section", [(0, 1)])
    middle = swap(ends[0], "section", 1)
    layer_outputs = jnp.stack([jnp.where(low, ends[0], last), jnp.where(low, middle, ends[1])])
    first = lax.ppermute(grads, "section", [(1, 0)])
    input_gradients = jnp.stack(
        [jnp.where(low, grads, grads_out[1][0]), jnp.where(low, first, grads_out[1][1])]
    )
    return (
        layer_outputs[None],
        input_gradients[None],
        qkv_w_grad.reshape(qkv_w.shape)[None],
        take(qkv_b_grad.reshape(heads_here, -1), 1, r, 3 * HD // rows_axis)[None],
        jnp.concatenate(out_g, axis=0).astype(F32)[None],
        fc_in_w_grad[None],
        take(fc_in_b_grad, 0, r, inner_here // rows_axis)[None],
        jnp.concatenate(fc_out_g, axis=0).astype(F32)[None],
        norms[0][None],
        norms[1][None],
        norms[2][None],
        norms[3][None],
        end_grad[None],
        end_grad[None],
    )


def solution(mesh):
    sizes = mesh.shape
    paired = sizes["section"] == 2 and sizes["col"] == 4
    rows_even = sizes["row"] & (sizes["row"] - 1) == 0
    body = local if paired and rows_even else relay_local
    return jax.shard_map(
        body,
        mesh=mesh,
        in_specs=(
            P(None, ("row", "col"), None),
            P(None, ("row", "col"), None),
            P("section", "row", "col", None),
            P("section", "col", "row"),
            P("section", "col", "row"),
            P("section", "row", "col"),
            P("section", ("col", "row")),
            P("section", "col", "row"),
            P("section", ("row", "col")),
            P("section", ("row", "col")),
            P("section", ("row", "col")),
            P("section", ("row", "col")),
            P("section", ("row", "col")),
            P("section", ("row", "col")),
        ),
        out_specs=(
            P("section", None, ("row", "col"), None),
            P("section", None, ("row", "col"), None),
            P("section", "row", "col", None),
            P("section", "col", "row"),
            P("section", "col", "row"),
            P("section", "row", "col"),
            P("section", ("col", "row")),
            P("section", "col", "row"),
            P("section", ("row", "col")),
            P("section", ("row", "col")),
            P("section", ("row", "col")),
            P("section", ("row", "col")),
            P("section", ("row", "col")),
            P("section", ("row", "col")),
        ),
        check_vma=False,
    )
```

```python
import math

import jax
import jax.numpy as jnp
from jax import lax
from jax.experimental import pallas as pl
from jax.experimental.pallas import tpu as pltpu
from jax.sharding import PartitionSpec as P


SECTION, ROW, COL = ("section", "row", "col")
HD = 256
ROT = 64
SEQ_LEN = 1024


def from_behind(value, axis, steps):
    count = lax.axis_size(axis)
    initial, last = (max(0, -steps), min(count, count - steps))
    return lax.ppermute(value, axis, [(source, source + steps) for source in range(initial, last)])


def rotary_tables(length):
    positions = jnp.arange(length).astype(jnp.float32)
    inverse = 10000.0 ** (-jnp.arange(0, ROT, 2).astype(jnp.float32) / ROT)
    angles = positions[:, None] * inverse[None, :]
    angles = jnp.concatenate([angles, angles], axis=-1)
    return (jnp.cos(angles)[:, None, :], jnp.sin(angles)[:, None, :])


def rotate(values, cosines, sines):
    half_rot = ROT // 2
    turned = values[..., :ROT]
    first_half = turned[..., :half_rot]
    second_half = turned[..., half_rot:]
    swapped = jnp.concatenate([-second_half, first_half], axis=-1)
    return jnp.concatenate([turned * cosines + swapped * sines, values[..., ROT:]], axis=-1)


def rotate_back(grads, cosines, sines):

    def turn_values(values):
        return rotate(values, cosines, sines)

    _, turn_pull = jax.vjp(turn_values, grads)
    return turn_pull(grads)[0]


def gelu_exact(values):
    return jax.nn.gelu(values, approximate=False)


def norm_rows(row_values):
    centred = row_values - jnp.mean(row_values, axis=-1, keepdims=True)
    inverse_std = lax.rsqrt(jnp.mean(centred * centred, axis=-1, keepdims=True) + 1e-05)
    return (centred * inverse_std, inverse_std)


def contract_rows(first_operand, second_operand):
    return lax.dot_general(
        first_operand, second_operand, (((0,), (0,)), ((), ())), preferred_element_type=jnp.float32
    )


def contract_cols(first_operand, second_operand):
    return lax.dot_general(
        first_operand, second_operand, (((1,), (1,)), ((), ())), preferred_element_type=jnp.float32
    )


def causal_block(row_start, block_rows, row_stop):
    query_pos = row_start + lax.broadcasted_iota(jnp.int32, (block_rows, row_stop), 0)
    key_pos = lax.broadcasted_iota(jnp.int32, (block_rows, row_stop), 1)
    return query_pos >= key_pos


def attention_forward(queries, keys_all, values_all):
    length = queries.shape[0]
    block_rows = min(512, length)
    score_scale = HD ** (-0.5)
    outputs_list = []
    sums_list = []
    for block_index in range(length // block_rows):
        row_start = block_index * block_rows
        row_stop = row_start + block_rows
        scores = (
            jnp.einsum(
                "qhd,khd->hqk",
                queries[row_start:row_stop],
                keys_all[:row_stop],
                preferred_element_type=jnp.float32,
            )
            * score_scale
        )
        scores = jnp.where(causal_block(row_start, block_rows, row_stop)[None], scores, -1e30)
        row_peak = jnp.max(scores, axis=-1, keepdims=True)
        exponents = jnp.exp(scores - row_peak)
        row_total = jnp.sum(exponents, axis=-1, keepdims=True)
        attention_probs = (exponents / row_total).astype(jnp.bfloat16)
        outputs_list.append(
            jnp.einsum(
                "hqk,khd->qhd",
                attention_probs,
                values_all[:row_stop],
                preferred_element_type=jnp.float32,
            )
        )
        sums_list.append((row_peak + jnp.log(row_total))[..., 0])
    attended = jnp.concatenate(outputs_list, axis=0).astype(jnp.bfloat16).reshape(length, -1)
    return (attended, jnp.concatenate(sums_list, axis=1))


def attention_backward(queries, keys_all, values_all, log_sums, grad_attended):
    length, heads_here = (queries.shape[0], queries.shape[1])
    block_rows = min(512, length)
    score_scale = HD ** (-0.5)
    grad_out = grad_attended.reshape(length, heads_here, HD)
    grad_queries_list = []
    grad_keys = jnp.zeros(queries.shape, jnp.float32)
    grad_values = jnp.zeros(queries.shape, jnp.float32)
    for block_index in range(length // block_rows):
        row_start = block_index * block_rows
        row_stop = row_start + block_rows
        scores = (
            jnp.einsum(
                "qhd,khd->hqk",
                queries[row_start:row_stop],
                keys_all[:row_stop],
                preferred_element_type=jnp.float32,
            )
            * score_scale
        )
        scores = jnp.where(causal_block(row_start, block_rows, row_stop)[None], scores, -1e30)
        attention_probs = jnp.exp(scores - log_sums[:, row_start:row_stop, None])
        low_probs = attention_probs.astype(jnp.bfloat16)
        grad_probs = jnp.einsum(
            "qhd,khd->hqk",
            grad_out[row_start:row_stop],
            values_all[:row_stop],
            preferred_element_type=jnp.float32,
        )
        centre_term = jnp.sum(attention_probs * grad_probs, axis=-1, keepdims=True)
        grad_scores = (attention_probs * (grad_probs - centre_term)).astype(jnp.bfloat16)
        grad_queries_list.append(
            jnp.einsum(
                "hqk,khd->qhd", grad_scores, keys_all[:row_stop], preferred_element_type=jnp.float32
            )
            * score_scale
        )
        grad_keys = grad_keys.at[:row_stop].add(
            jnp.einsum(
                "hqk,qhd->khd",
                grad_scores,
                queries[row_start:row_stop],
                preferred_element_type=jnp.float32,
            )
            * score_scale
        )
        grad_values = grad_values.at[:row_stop].add(
            jnp.einsum(
                "hqk,qhd->khd",
                low_probs,
                grad_out[row_start:row_stop],
                preferred_element_type=jnp.float32,
            )
        )
    return (jnp.concatenate(grad_queries_list, axis=0), grad_keys, grad_values)


def forward_turn(my_rows, weights, vectors, cosines, sines):
    qkv_w, qkv_b, out_w, fc_in_w, fc_in_b, fc_out_w = weights
    gain_one, bias_one, gain_two, bias_two, out_b, fc_out_b = vectors
    gathered = lax.all_gather(my_rows, COL, axis=0, tiled=True)
    scaled, _ = norm_rows(gathered.astype(jnp.float32))
    normed_one = (scaled * gain_one + bias_one).astype(jnp.bfloat16)
    normed_two = (scaled * gain_two + bias_two).astype(jnp.bfloat16)
    length = gathered.shape[0]
    heads_here = qkv_w.shape[1]
    projected = jnp.dot(
        normed_one, qkv_w.reshape(qkv_w.shape[0], -1), preferred_element_type=jnp.float32
    ) + qkv_b.reshape(-1).astype(jnp.float32)
    projected = projected.reshape(length, heads_here, 3, HD)
    queries = rotate(projected[:, :, 0], cosines, sines).astype(jnp.bfloat16)
    keys_all = rotate(projected[:, :, 1], cosines, sines).astype(jnp.bfloat16)
    values_all = projected[:, :, 2].astype(jnp.bfloat16)
    attended, log_sums = attention_forward(queries, keys_all, values_all)
    inner_act = jnp.dot(normed_two, fc_in_w, preferred_element_type=jnp.float32) + fc_in_b.astype(
        jnp.float32
    )
    activated = gelu_exact(inner_act).astype(jnp.bfloat16)
    summed = lax.psum_scatter(
        jnp.dot(attended, out_w, preferred_element_type=jnp.float32)
        + jnp.dot(activated, fc_out_w, preferred_element_type=jnp.float32),
        COL,
        scatter_dimension=0,
        tiled=True,
    )
    output = (my_rows.astype(jnp.float32) + summed + out_b + fc_out_b).astype(jnp.bfloat16)
    kept_values = (
        gathered,
        normed_one,
        normed_two,
        queries,
        keys_all,
        values_all,
        attended,
        log_sums,
        inner_act,
    )
    return (output, kept_values)


def backward_turn(grad_rows, kept_values, weights, vectors, cosines, sines):
    (
        gathered,
        normed_one,
        normed_two,
        queries,
        keys_all,
        values_all,
        attended,
        log_sums,
        inner_act,
    ) = kept_values
    qkv_w, qkv_b, out_w, fc_in_w, _, fc_out_w = weights
    gain_one, _, gain_two, _, _, _ = vectors
    grad_full = lax.all_gather(grad_rows, COL, axis=0, tiled=True)
    length = grad_full.shape[0]
    rows_here = grad_rows.shape[0]
    own_start = lax.axis_index(COL) * rows_here
    activated = gelu_exact(inner_act).astype(jnp.bfloat16)
    out_w_grad = contract_rows(attended, grad_full)
    fc_out_w_grad = contract_rows(activated, grad_full)
    grad_attended = contract_cols(grad_full, out_w).astype(jnp.bfloat16)
    grad_activated = contract_cols(grad_full, fc_out_w)
    _, gelu_pull = jax.vjp(gelu_exact, inner_act)
    grad_inner = gelu_pull(grad_activated)[0].astype(jnp.bfloat16)
    grad_queries, grad_keys, grad_values = attention_backward(
        queries, keys_all, values_all, log_sums, grad_attended
    )
    grad_q_pre = rotate_back(grad_queries, cosines, sines)
    grad_k_pre = rotate_back(grad_keys, cosines, sines)
    grad_projected = (
        jnp.stack([grad_q_pre, grad_k_pre, grad_values], axis=2)
        .astype(jnp.bfloat16)
        .reshape(length, -1)
    )
    qkv_flat = qkv_w.reshape(qkv_w.shape[0], -1)
    qkv_w_grad = contract_rows(normed_one, grad_projected).reshape(qkv_w.shape)
    qkv_b_grad = jnp.sum(grad_projected.astype(jnp.float32), axis=0).reshape(qkv_b.shape)
    fc_in_w_grad = contract_rows(normed_two, grad_inner)
    fc_in_b_grad = jnp.sum(grad_inner.astype(jnp.float32), axis=0)
    width = qkv_w.shape[0]
    scaled_full, inverse_full = norm_rows(gathered.astype(jnp.float32))
    scaled = lax.dynamic_slice_in_dim(scaled_full, own_start, rows_here, 0)
    inverse_std = lax.dynamic_slice_in_dim(inverse_full, own_start, rows_here, 0)
    dy_sum = jnp.sum(grad_rows.astype(jnp.float32), axis=0)
    both_grads = lax.psum_scatter(
        jnp.concatenate(
            [contract_cols(grad_projected, qkv_flat), contract_cols(grad_inner, fc_in_w)], axis=1
        ),
        COL,
        scatter_dimension=0,
        tiled=True,
    )
    grad_one = both_grads[:, :width]
    grad_two = both_grads[:, width:]
    combined = gain_one * grad_one + gain_two * grad_two
    vector_grads = (
        jnp.sum(grad_one * scaled, axis=0),
        jnp.sum(grad_one, axis=0),
        jnp.sum(grad_two * scaled, axis=0),
        jnp.sum(grad_two, axis=0),
        dy_sum,
    )
    grad_norm = inverse_std * (
        combined
        - jnp.mean(combined, axis=-1, keepdims=True)
        - scaled * jnp.mean(combined * scaled, axis=-1, keepdims=True)
    )
    grad_input = (grad_rows.astype(jnp.float32) + grad_norm).astype(jnp.bfloat16)
    matrix_grads = (qkv_w_grad, qkv_b_grad, out_w_grad, fc_in_w_grad, fc_in_b_grad, fc_out_w_grad)
    return (grad_input, matrix_grads, vector_grads)


def add_tuples(running, addend):
    if running is None:
        return addend
    return tuple((first_part + second_part for first_part, second_part in zip(running, addend)))


def relay_local(
    inputs,
    cotangent,
    qkv_weight,
    qkv_bias,
    out_weight,
    fc_in_weight,
    fc_in_bias,
    fc_out_weight,
    norm1_gain,
    norm1_bias,
    norm2_gain,
    norm2_bias,
    out_bias,
    fc_out_bias,
):
    sections = lax.axis_size(SECTION)
    section_index = lax.axis_index(SECTION)
    micro_count = inputs.shape[0]
    tick_count = micro_count + sections - 1
    is_first = section_index == 0
    is_last = section_index == sections - 1
    cosines, sines = rotary_tables(SEQ_LEN)
    vectors = (
        lax.all_gather(norm1_gain[0], (ROW, COL), axis=0, tiled=True),
        lax.all_gather(norm1_bias[0], (ROW, COL), axis=0, tiled=True),
        lax.all_gather(norm2_gain[0], (ROW, COL), axis=0, tiled=True),
        lax.all_gather(norm2_bias[0], (ROW, COL), axis=0, tiled=True),
        lax.all_gather(out_bias[0], (ROW, COL), axis=0, tiled=True),
        lax.all_gather(fc_out_bias[0], (ROW, COL), axis=0, tiled=True),
    )
    vectors = tuple((member.astype(jnp.float32) for member in vectors))
    received = jnp.zeros_like(inputs[0])
    outputs_list = []
    kept_list = []
    for tick_index in range(tick_count):
        weights = (
            lax.all_gather(qkv_weight[0], ROW, axis=0, tiled=True),
            lax.all_gather(qkv_bias[0], ROW, axis=1, tiled=True),
            lax.all_gather(out_weight[0], ROW, axis=1, tiled=True),
            lax.all_gather(fc_in_weight[0], ROW, axis=0, tiled=True),
            lax.all_gather(fc_in_bias[0], ROW, axis=0, tiled=True),
            lax.all_gather(fc_out_weight[0], ROW, axis=1, tiled=True),
        )
        first_rows = inputs[min(tick_index, micro_count - 1)]
        my_rows = jnp.where(is_first, first_rows, received)
        output, kept_values = forward_turn(my_rows, weights, vectors, cosines, sines)
        outputs_list.append(output)
        kept_list.append(kept_values)
        if tick_index + 1 < tick_count:
            received = from_behind(output, SECTION, 1)
    layer_outputs = lax.dynamic_slice_in_dim(jnp.stack(outputs_list), section_index, micro_count, 0)
    stacked_kept = tuple((jnp.stack(members) for members in zip(*kept_list)))
    received_grad = jnp.zeros_like(inputs[0])
    grads_list = []
    matrix_total = None
    vector_total = None
    for tick_index in range(tick_count):
        weights = (
            lax.all_gather(qkv_weight[0], ROW, axis=0, tiled=True),
            lax.all_gather(qkv_bias[0], ROW, axis=1, tiled=True),
            lax.all_gather(out_weight[0], ROW, axis=1, tiled=True),
            lax.all_gather(fc_in_weight[0], ROW, axis=0, tiled=True),
            lax.all_gather(fc_in_bias[0], ROW, axis=0, tiled=True),
            lax.all_gather(fc_out_weight[0], ROW, axis=1, tiled=True),
        )
        if tick_index < micro_count:
            seed_grad = cotangent[tick_index]
        else:
            seed_grad = jnp.zeros_like(cotangent[0])
        grad_rows = jnp.where(is_last, seed_grad, received_grad)
        forward_index = jnp.clip(tick_index - sections + 1 + 2 * section_index, 0, tick_count - 1)
        kept_values = tuple(
            (
                lax.dynamic_index_in_dim(member, forward_index, 0, keepdims=False)
                for member in stacked_kept
            )
        )
        grad_input, matrix_grads, vector_grads = backward_turn(
            grad_rows, kept_values, weights, vectors, cosines, sines
        )
        grads_list.append(grad_input)
        if tick_index + 1 < tick_count:
            received_grad = from_behind(grad_input, SECTION, -1)
        matrix_part = (
            lax.psum_scatter(matrix_grads[0], ROW, scatter_dimension=0, tiled=True),
            lax.psum_scatter(matrix_grads[1], ROW, scatter_dimension=1, tiled=True),
            lax.psum_scatter(matrix_grads[2], ROW, scatter_dimension=1, tiled=True),
            lax.psum_scatter(matrix_grads[3], ROW, scatter_dimension=0, tiled=True),
            lax.psum_scatter(matrix_grads[4], ROW, scatter_dimension=0, tiled=True),
            lax.psum_scatter(matrix_grads[5], ROW, scatter_dimension=1, tiled=True),
        )
        vector_part = (
            lax.psum_scatter(vector_grads[0], (ROW, COL), scatter_dimension=0, tiled=True),
            lax.psum_scatter(vector_grads[1], (ROW, COL), scatter_dimension=0, tiled=True),
            lax.psum_scatter(vector_grads[2], (ROW, COL), scatter_dimension=0, tiled=True),
            lax.psum_scatter(vector_grads[3], (ROW, COL), scatter_dimension=0, tiled=True),
            lax.psum_scatter(vector_grads[4], (ROW, COL), scatter_dimension=0, tiled=True),
        )
        matrix_total = add_tuples(matrix_total, tuple(matrix_part))
        vector_total = add_tuples(vector_total, tuple(vector_part))
    input_gradients = lax.dynamic_slice_in_dim(
        jnp.stack(grads_list), sections - 1 - section_index, micro_count, 0
    )
    return (
        layer_outputs[None],
        input_gradients[None],
        matrix_total[0][None],
        matrix_total[1][None],
        matrix_total[2][None],
        matrix_total[3][None],
        matrix_total[4][None],
        matrix_total[5][None],
        vector_total[0][None],
        vector_total[1][None],
        vector_total[2][None],
        vector_total[3][None],
        vector_total[4][None],
        vector_total[4][None],
    )


F32 = jnp.float32
BF16 = jnp.bfloat16
LANES = 128


def swap(value, axis, bit):
    count = lax.axis_size(axis)
    return lax.ppermute(value, axis, [(source, source ^ bit) for source in range(count)])


def sum_over(value, axis):
    bit = 1
    while bit < lax.axis_size(axis):
        value = value + swap(value, axis, bit)
        bit *= 2
    return value


def place(part, axis, index, length):
    shape = list(part.shape)
    shape[axis] = length
    start = index * part.shape[axis]
    return lax.dynamic_update_slice_in_dim(jnp.zeros(shape, part.dtype), part, start, axis)


def take(value, axis, index, size):
    return lax.dynamic_slice_in_dim(value, index * size, size, axis)


def after(value, *others):
    return lax.optimization_barrier((value, *others))[0]


def gather_rows(block):
    half = block.shape[0] // 2
    across = swap(block, SECTION, 1)
    beside = swap(block, COL, 2)
    corner = jnp.concatenate(
        [swap(beside[:half], SECTION, 1), swap(across[half:], COL, 2)], axis=0
    )
    near = jnp.concatenate([block, beside], axis=0)
    far = jnp.concatenate([across, corner], axis=0)
    return jnp.concatenate([near, swap(near, COL, 1), far, swap(far, COL, 1)], axis=0), across


def pair_sum(keep_ref, came_ref, start, size):
    rows = pl.ds(start, size)
    return keep_ref[rows, :].astype(F32) + came_ref[rows, :].astype(F32)


def first_sum_kernel(keep_ref, came_ref, across_ref, beside_ref):
    block = keep_ref.shape[0] // 4
    half = block // 2
    for ref, starts in (
        (across_ref, (2 * block, 3 * block)),
        (beside_ref, (block + half, 3 * block + half)),
    ):
        for place, start in enumerate(starts):
            ref[place * half : (place + 1) * half, :] = pair_sum(
                keep_ref, came_ref, start, half
            ).astype(BF16)


def second_sum_kernel(keep_ref, came_ref, across_ref, beside_ref, top_ref, low_ref, kept_ref):
    block = keep_ref.shape[0] // 4
    half = block // 2
    kept_ref[:half, :] = pair_sum(keep_ref, came_ref, 0, half) + across_ref[:half, :].astype(F32)
    kept_ref[half:, :] = (
        pair_sum(keep_ref, came_ref, half, half) + beside_ref[:half, :].astype(F32)
    )
    top = pair_sum(keep_ref, came_ref, block, half) + across_ref[half:, :].astype(F32)
    top_ref[...] = top.astype(BF16)
    low = pair_sum(keep_ref, came_ref, 2 * block + half, half) + beside_ref[half:, :].astype(F32)
    low_ref[...] = low.astype(BF16)


def column_call(kernel, width, ins, outs):
    tile = 512

    def spec(shape):
        lead = shape[:-1]
        return pl.BlockSpec(lead + (tile,), lambda i: (0,) * len(lead) + (i,))

    return pl.pallas_call(
        kernel,
        grid=(width // tile,),
        in_specs=[spec(member.shape) for member in ins],
        out_specs=[spec(member.shape) for member in outs],
        out_shape=outs,
        cost_estimate=cost(0, *ins, *outs),
    )(*ins)


def scatter_rows(product):
    sent = product(1)
    came = swap(sent, COL, 1)
    keep = product(0)
    rows, width = keep.shape
    block = rows // 4
    half = block // 2
    whole_block = jax.ShapeDtypeStruct((block, width), BF16)
    half_block = jax.ShapeDtypeStruct((half, width), BF16)
    across, beside = column_call(first_sum_kernel, width, [keep, came], [whole_block, whole_block])
    across = swap(across, SECTION, 1)
    beside = swap(beside, COL, 2)
    top, low, keep = column_call(
        second_sum_kernel,
        width,
        [keep, came, across, beside],
        [half_block, half_block, jax.ShapeDtypeStruct((block, width), F32)],
    )
    arrived = jnp.concatenate([swap(top, COL, 2), swap(low, SECTION, 1)], axis=0)
    return keep + arrived.astype(F32)


def turn(values, cosines, sines):
    lead = values[:, :LANES]
    lane = lax.broadcasted_iota(jnp.int32, lead.shape, 1)
    ahead = pltpu.roll(lead, LANES - ROT // 2, 1)
    behind = pltpu.roll(lead, ROT // 2, 1)
    lead = lead * cosines + jnp.where(lane < ROT // 2, ahead, behind) * sines
    return jnp.concatenate([lead, values[:, LANES:]], axis=1)


def mm(first_operand, second_operand):
    return jnp.dot(first_operand, second_operand, preferred_element_type=F32)


def project_kernel(x_ref, wq_ref, wk_ref, wv_ref, e_ref, cos_ref, sin_ref, q_ref, k_ref, v_ref):
    x, cosines, sines = (x_ref[...], cos_ref[...], sin_ref[...])
    queries = mm(x, wq_ref[...]) + e_ref[:, :HD]
    q_ref[...] = (turn(queries, cosines, sines) * HD ** (-0.5)).astype(BF16)
    keys_here = mm(x, wk_ref[...]) + e_ref[:, HD : 2 * HD]
    k_ref[...] = turn(keys_here, cosines, sines).astype(BF16)
    v_ref[...] = (mm(x, wv_ref[...]) + e_ref[:, 2 * HD :]).astype(BF16)


def inner_kernel(x_ref, w_ref, e_ref, held_ref, act_ref, slope_ref):
    inner = mm(x_ref[...], w_ref[...]) + e_ref[...]
    below = 0.5 + 0.5 * lax.erf(inner * 0.7071067811865476)
    act_ref[...] = (inner * below).astype(BF16)
    density = jnp.exp(-0.5 * inner * inner) * 0.3989422804014327
    slope_ref[...] = (below + inner * density).astype(BF16)


def outer_kernel(act_ref, w_ref, wo_ref, out_ref):
    inner = w_ref.shape[0]
    total = mm(act_ref[:, :inner], w_ref[...]) + mm(act_ref[:, inner:], wo_ref[...])
    out_ref[...] = total.astype(BF16)


def outer_back_kernel(dy_ref, w_ref, wo_ref, slope_ref, dz_ref, do_ref, sum_ref):
    dy = dy_ref[...]
    dz = (contract_cols(dy, w_ref[...]) * slope_ref[...].astype(F32)).astype(BF16)
    dz_ref[...] = dz
    do_ref[...] = contract_cols(dy, wo_ref[...]).astype(BF16)

    @pl.when(pl.program_id(0) == 0)
    def _():
        sum_ref[...] = jnp.zeros_like(sum_ref)

    sum_ref[...] += jnp.sum(dz.astype(F32), axis=0, keepdims=True)


def inward_kernel(dz_ref, wf_ref, wq_ref, wk_ref, wv_ref, out_ref):
    start = wf_ref.shape[1]
    total = contract_cols(dz_ref[:, :start], wf_ref[...])
    for w_ref in (wq_ref, wk_ref, wv_ref):
        total += contract_cols(dz_ref[:, start : start + HD], w_ref[...])
        start += HD
    out_ref[...] = total.astype(BF16)


def attend_kernel(q_ref, k_ref, v_ref, row_ref, col_ref, out_ref, log_ref):
    scores = contract_cols(q_ref[...], k_ref[...])
    scores = jnp.where(row_ref[...] >= col_ref[...], scores, -1e30)
    peak = jnp.max(scores, axis=1, keepdims=True)
    exponents = jnp.exp(scores - peak)
    total = jnp.sum(exponents, axis=1, keepdims=True)
    out_ref[...] = mm((exponents / total).astype(BF16), v_ref[...]).astype(BF16)
    log_ref[...] = peak + jnp.log(total)


def attend_back_kernel(
    q_ref, k_ref, v_ref, row_ref, col_ref, log_ref, do_ref, cos_ref, sin_ref, held_ref,
    all_ref, sum_ref, out_ref, dk_ref, dv_ref, sem,
):
    step = pl.program_id(1)
    block = q_ref.shape[0]

    @pl.when(step == 0)
    def _():
        dk_ref[...] = jnp.zeros_like(dk_ref)
        dv_ref[...] = jnp.zeros_like(dv_ref)

    @pl.when((step == 0) & (pl.program_id(0) == 0))
    def _():
        sum_ref[...] = jnp.zeros_like(sum_ref)

    def column_sum(values):
        return jnp.sum(values.astype(F32), axis=0, keepdims=True)

    queries, keys_all, grads = (q_ref[...], k_ref[...], do_ref[...])
    scores = contract_cols(queries, keys_all)
    scores = jnp.where(row_ref[...] >= col_ref[...], scores, -1e30)
    probs = jnp.exp(scores - log_ref[...])
    grad_probs = contract_cols(grads, v_ref[...])
    centre = jnp.sum(probs * grad_probs, axis=1, keepdims=True)
    grad_scores = (probs * (grad_probs - centre)).astype(BF16)
    rows = pl.ds(pl.multiple_of(step * block, block), block)
    cosines, sines = cos_ref[rows, :], sin_ref[rows, :]
    grad_queries = mm(grad_scores, keys_all) * HD ** (-0.5)
    grad_queries = turn(grad_queries, cosines, -sines).astype(BF16)
    out_ref[rows, :HD] = grad_queries
    sum_ref[:, :HD] += column_sum(grad_queries)
    dk_ref[...] += contract_rows(grad_scores, queries)
    dv_ref[...] += contract_rows(probs.astype(BF16), grads)

    @pl.when(step == pl.num_programs(1) - 1)
    def _():
        grad_keys = turn(dk_ref[...], cos_ref[...], -sin_ref[...]).astype(BF16)
        grad_values = dv_ref[...].astype(BF16)
        out_ref[:, HD : 2 * HD] = grad_keys
        out_ref[:, 2 * HD :] = grad_values
        sum_ref[:, HD : 2 * HD] += column_sum(grad_keys)
        sum_ref[:, 2 * HD :] += column_sum(grad_values)
        length, width = out_ref.shape
        micro = pl.ds(pl.multiple_of(pl.program_id(0) * length, length), length)
        copy = pltpu.make_async_copy(
            out_ref, all_ref.at[micro, pl.ds(all_ref.shape[1] - width, width)], sem
        )
        copy.start()
        copy.wait()


ROW_BLOCK = 256


def by_rows(width, block=ROW_BLOCK):
    return pl.BlockSpec((block, width), lambda i: (i, 0))


def whole(shape):
    return pl.BlockSpec(shape, lambda *unused: (0,) * len(shape))


def panel(width, place):
    return lambda deep: pl.BlockSpec((deep, width), lambda *unused: (0, place))


def cost(flops, *arrays):
    return pl.CostEstimate(
        flops=flops,
        transcendentals=0,
        bytes_accessed=sum(math.prod(array.shape) * array.dtype.itemsize for array in arrays),
    )


def heads_panels(array, inner):
    return [panel(HD, inner // HD + part)(array.shape[0]) for part in range(3)]


def project(x, w, inner, e, tables):
    rows, width = x.shape
    per_micro = tables[0].shape[0] // ROW_BLOCK
    table = pl.BlockSpec((ROW_BLOCK, LANES), lambda i: (i % per_micro, 0))
    out = jax.ShapeDtypeStruct((rows, HD), BF16)
    return pl.pallas_call(
        project_kernel,
        grid=(rows // ROW_BLOCK,),
        in_specs=[by_rows(width), *heads_panels(w, inner), whole(e.shape), table, table],
        out_specs=[by_rows(HD)] * 3,
        out_shape=[out] * 3,
        cost_estimate=cost(6 * rows * width * HD, x, out, out, out),
        name="project",
    )(x, w, w, w, e, *tables)


def inner_layer(x, w, e, held):
    rows, width = x.shape
    inner = e.shape[1]
    slope = jax.ShapeDtypeStruct((rows, inner), BF16)
    return pl.pallas_call(
        inner_kernel,
        grid=(rows // ROW_BLOCK,),
        in_specs=[
            by_rows(width),
            panel(inner, 0)(width),
            whole(e.shape),
            pl.BlockSpec(memory_space=pl.ANY),
        ],
        out_specs=[by_rows(inner)] * 2,
        out_shape=[jax.ShapeDtypeStruct(held.shape, BF16), slope],
        input_output_aliases={3: 0},
        cost_estimate=cost(2 * rows * width * inner, x, slope, slope),
        name="inner",
    )(x, w, e, held)


def split_rows(width, other):
    return pl.BlockSpec((ROW_BLOCK, width), lambda i: (i // 2 * 4 + 2 * other + i % 2, 0))


def outer_panels(pair, inner):
    (w, first), (wo, second) = pair
    return [
        pl.BlockSpec((inner, w.shape[1]), lambda *unused: (first // inner, 0)),
        pl.BlockSpec((HD, wo.shape[1]), lambda *unused: (second // HD, 0)),
    ]


def outer(act, pair, other):
    rows, width = (act.shape[0] // 2, pair[0][0].shape[1])
    out = jax.ShapeDtypeStruct((rows, width), BF16)
    return pl.pallas_call(
        outer_kernel,
        grid=(rows // ROW_BLOCK,),
        in_specs=[split_rows(act.shape[1], other), *outer_panels(pair, act.shape[1] - HD)],
        out_specs=by_rows(width),
        out_shape=out,
        cost_estimate=cost(2 * rows * width * act.shape[1], act, out),
        name="outer",
    )(act, pair[0][0], pair[1][0])


def inward(dz, w_in, w_qkv, offset, other):
    rows, width = (dz.shape[0] // 2, w_in.shape[0])
    out = jax.ShapeDtypeStruct((rows, width), BF16)
    return pl.pallas_call(
        inward_kernel,
        grid=(rows // ROW_BLOCK,),
        in_specs=[
            split_rows(dz.shape[1], other),
            panel(dz.shape[1] - 3 * HD, 0)(width),
            *heads_panels(w_qkv, offset),
        ],
        out_specs=by_rows(width),
        out_shape=out,
        cost_estimate=cost(2 * rows * width * dz.shape[1], dz, out),
        name="inward",
    )(dz, w_in, w_qkv, w_qkv, w_qkv)


def outer_back(dy, pair, slopes):
    rows, width = dy.shape
    inner = slopes.shape[1]
    dz = jax.ShapeDtypeStruct((rows, inner + 3 * HD), BF16)
    return pl.pallas_call(
        outer_back_kernel,
        grid=(rows // ROW_BLOCK,),
        in_specs=[by_rows(width), *outer_panels(pair, inner), by_rows(inner)],
        out_specs=[by_rows(inner), by_rows(HD), whole((1, inner))],
        out_shape=[
            dz,
            jax.ShapeDtypeStruct((rows, HD), BF16),
            jax.ShapeDtypeStruct((1, inner), F32),
        ],
        cost_estimate=cost(2 * rows * width * (inner + HD), dy, slopes, slopes),
        name="outer_back",
    )(dy, pair[0][0], pair[1][0], slopes)


def attend(queries, keys_all, values_all, places, inner):
    rows = queries.shape[0]
    length = places.shape[0]
    steps = length // ROW_BLOCK
    row = pl.BlockSpec((ROW_BLOCK, HD), lambda m, i: (m * steps + i, 0))
    every = pl.BlockSpec((length, HD), lambda m, i: (m, 0))
    return pl.pallas_call(
        attend_kernel,
        grid=(rows // length, steps),
        in_specs=[
            row,
            every,
            every,
            pl.BlockSpec((ROW_BLOCK, 1), lambda m, i: (i, 0)),
            pl.BlockSpec((1, length), lambda m, i: (0, 0)),
        ],
        out_specs=[
            pl.BlockSpec((ROW_BLOCK, HD), lambda m, i: (m * steps + i, inner // HD)),
            pl.BlockSpec((ROW_BLOCK, 1), lambda m, i: (m * steps + i, 0)),
        ],
        out_shape=[
            jax.ShapeDtypeStruct((rows, inner + HD), BF16),
            jax.ShapeDtypeStruct((rows, 1), F32),
        ],
        cost_estimate=cost(4 * rows * length * HD, queries, keys_all, values_all, queries),
        name="attend",
    )(queries, keys_all, values_all, places[:, None], places[None, :])


def attend_back(queries, keys_all, values_all, places, log_sums, grads, tables, held):
    rows = queries.shape[0]
    length = places.shape[0]
    steps = length // ROW_BLOCK
    row = pl.BlockSpec((ROW_BLOCK, HD), lambda m, i: (m * steps + i, 0))
    every = pl.BlockSpec((length, HD), lambda m, i: (m, 0))
    anywhere = pl.BlockSpec(memory_space=pl.ANY)
    return pl.pallas_call(
        attend_back_kernel,
        grid=(rows // length, steps),
        in_specs=[
            row,
            every,
            every,
            pl.BlockSpec((ROW_BLOCK, 1), lambda m, i: (i, 0)),
            pl.BlockSpec((1, length), lambda m, i: (0, 0)),
            pl.BlockSpec((ROW_BLOCK, 1), lambda m, i: (m * steps + i, 0)),
            row,
            whole(tables[0].shape),
            whole(tables[1].shape),
            anywhere,
        ],
        out_specs=[anywhere, whole((1, 3 * HD))],
        out_shape=[
            jax.ShapeDtypeStruct(held.shape, BF16),
            jax.ShapeDtypeStruct((1, 3 * HD), F32),
        ],
        scratch_shapes=[
            pltpu.VMEM((length, 3 * HD), BF16),
            pltpu.VMEM((length, HD), F32),
            pltpu.VMEM((length, HD), F32),
            pltpu.SemaphoreType.DMA,
        ],
        input_output_aliases={9: 0},
        cost_estimate=cost(10 * rows * length * HD, queries, keys_all, values_all, grads),
        name="attend_back",
    )(
        queries, keys_all, values_all, places[:, None], places[None, :], log_sums, grads, *tables,
        held,
    )


def local(
    inputs,
    cotangent,
    qkv_weight,
    qkv_bias,
    out_weight,
    fc_in_weight,
    fc_in_bias,
    fc_out_weight,
    norm1_gain,
    norm1_bias,
    norm2_gain,
    norm2_bias,
    out_bias,
    fc_out_bias,
):
    s, r, c = (lax.axis_index(SECTION), lax.axis_index(ROW), lax.axis_index(COL))
    rows_axis, cols_axis = (lax.axis_size(ROW), lax.axis_size(COL))
    low = s == 0
    qkv_w, out_w, fc_in_w, fc_out_w = (
        qkv_weight[0], out_weight[0], fc_in_weight[0], fc_out_weight[0],
    )
    deep, heads_here = qkv_w.shape[0], qkv_w.shape[1]
    per = 3 * HD
    inner = fc_in_w.shape[1] // 2
    model = inputs.shape[2]

    def both_layers(own_first, own_second):
        return (jnp.where(low, own_first, own_second), jnp.where(low, own_second, own_first))

    def trade(value, axis, *others):
        size = value.shape[axis] // 2
        kept = take(value, axis, s, size)
        came = swap(after(take(value, axis, 1 - s, size), *others), SECTION, 1)
        return kept, came

    def gathered(shard, axis):
        return lax.all_gather(shard, ROW, axis=axis, tiled=True)

    held = jnp.stack(
        [
            norm1_gain[0].astype(F32),
            norm1_bias[0].astype(F32),
            norm2_gain[0].astype(F32),
            norm2_bias[0].astype(F32),
            out_bias[0].astype(F32) + fc_out_bias[0].astype(F32),
        ]
    )
    held_both = jnp.stack([held, swap(held, SECTION, 1)])
    out_half = trade(out_w, 0, held_both)
    qkv_half = trade(qkv_w, 1, out_half[1])
    qkv_half = tuple(member.reshape(deep, per) for member in qkv_half)
    fc_in_half = trade(fc_in_w, 1, qkv_half[1])
    fc_out_half = trade(fc_out_w, 0, fc_in_half[1])
    held_both = sum_over(place(held_both, 2, c, deep), COL)
    held = held_both[0]
    gain_one, shift_one, gain_two, shift_two, end_bias = (held[i] for i in range(5))
    gains = both_layers(held, held_both[1])

    def scaled_pair(half, row):
        return tuple(
            (part.astype(F32) * gain[row][:, None]).astype(BF16)
            for part, gain in zip(both_layers(*half), gains)
        )

    out_pair = both_layers(*out_half)
    qkv_pair = scaled_pair(qkv_half, 0)
    fc_in_pair = scaled_pair(fc_in_half, 2)
    fc_out_pair = both_layers(*fc_out_half)
    w_out0 = gathered(out_pair[0], 1)
    w_qkv0 = gathered(qkv_pair[0], 0)
    w_fc_in0 = gathered(fc_in_pair[0], 0)
    w_fc_out0 = gathered(fc_out_pair[0], 1)
    w_ins1 = gathered(jnp.concatenate([fc_in_pair[1], qkv_pair[1]], axis=1), 0)
    w_outs1 = gathered(jnp.concatenate([fc_out_pair[1], out_pair[1]], axis=0), 1)
    w_ins = ((w_fc_in0, w_qkv0, 0), (w_ins1, w_ins1, inner))
    w_outs = (((w_fc_out0, 0), (w_out0, 0)), ((w_outs1, 0), (w_outs1, inner)))
    qkv_flat = qkv_w.reshape(deep, -1)

    own_qkv = mm(shift_one.astype(BF16)[None], qkv_flat)[0]
    own_fc = mm(shift_two.astype(BF16)[None], fc_in_w)[0]
    own_qkv = own_qkv + place(qkv_bias[0].astype(F32), 1, r, per).reshape(-1)
    own_fc = own_fc + place(fc_in_bias[0].astype(F32), 0, r, 2 * inner)
    biases = sum_over(
        jnp.concatenate([own_qkv, own_fc, place(end_bias, 0, r, model)]), ROW
    )
    biases = both_layers(biases, swap(biases, SECTION, 1))
    qkv_e, fc_e, end_e = ([], [], [])
    for member in biases:
        qkv_e.append(take(member[: 2 * per], 0, s, per)[None])
        fc_e.append(take(member[2 * per : 2 * per + 2 * inner], 0, s, inner)[None])
        end_e.append(member[2 * per + 2 * inner :])

    block_rows = inputs.shape[1]
    masks = jnp.array([0, 2, 1, 3], jnp.int32)
    places = ((c ^ masks)[:, None] * block_rows + jnp.arange(block_rows)[None]).reshape(-1)
    inverse = 10000.0 ** (-jnp.arange(0, ROT, 2).astype(F32) / ROT)
    angles = places.astype(F32)[:, None] * inverse[None]
    ones = jnp.ones((places.shape[0], LANES - ROT), F32)
    cosines, sines = (jnp.cos(angles), jnp.sin(angles))
    tables = (
        jnp.concatenate([cosines, cosines, ones], axis=1),
        jnp.concatenate([-sines, sines, 0.0 * ones], axis=1),
    )

    hidden = lax.dynamic_index_in_dim(inputs, s, 0, keepdims=False)
    seed = lax.dynamic_index_in_dim(cotangent, s, 0, keepdims=False)
    hidden = after(hidden, fc_out_half[1])

    hidden_list, kept_list, ends = ([], [], [])
    seed_rows = None
    for layer in range(2):
        hidden_list.append(hidden)
        scaled, unused = norm_rows(hidden.astype(F32))
        x, unused = gather_rows(scaled.astype(BF16))
        if layer == 0:
            seed_rows, unused = gather_rows(after(seed, x))
            x = after(x, seed_rows)
        w_fc_in, w_qkv, offset = w_ins[layer]
        queries, keys_all, values_all = project(x, w_qkv, offset, qkv_e[layer], tables)
        attended, log_sums = attend(queries, keys_all, values_all, places, inner)
        act, slopes = inner_layer(x, w_fc_in, fc_e[layer], attended)
        kept = (x, queries, keys_all, values_all, log_sums, slopes, act)
        if layer == 1:
            outs_grad1 = contract_rows(act, seed_rows).astype(BF16)
            seed_rows = after(seed_rows, outs_grad1)
        kept_list.append(kept)
        if layer == 0:
            summed = scatter_rows(lambda other: outer(act, w_outs[0], other))
            hidden = (hidden.astype(F32) + summed + end_e[layer]).astype(BF16)
            ends.append(hidden)
            middle = swap(hidden, SECTION, 1)

    def reduced(value, axis):
        return lax.psum_scatter(value, ROW, scatter_dimension=axis, tiled=True)

    outs_part1 = reduced(outs_grad1, 1)
    grads = seed
    ins_list, small_list = ([None, None], [None, None])
    for layer in (1, 0):
        x, queries, keys_all, values_all, log_sums, slopes, act = kept_list[layer]
        w_fc_in, w_qkv, offset = w_ins[layer]
        if layer == 1:
            dy = seed_rows
        else:
            dy, across = gather_rows(grads)
            middle_grads = (jnp.where(low, grads, across), jnp.where(low, across, grads))
        dy_sum = jnp.sum(grads.astype(F32), axis=0)
        dz, grad_attended, inner_sum = outer_back(dy, w_outs[layer], slopes)
        dz, heads_sum = attend_back(
            queries, keys_all, values_all, places, log_sums, grad_attended, tables, dz
        )
        combined = scatter_rows(lambda other: inward(dz, w_fc_in, w_qkv, offset, other))
        ins_grad = contract_rows(x, dz).astype(BF16)
        ins_list[layer] = reduced(ins_grad, 0)
        scaled, inverse_std = norm_rows(hidden_list[layer].astype(F32))
        grad_norm = inverse_std * (
            combined
            - jnp.mean(combined, axis=-1, keepdims=True)
            - scaled * jnp.mean(combined * scaled, axis=-1, keepdims=True)
        )
        grads = (grads.astype(F32) + grad_norm).astype(BF16)
        small_list[layer] = (heads_sum[0], inner_sum[0], dy_sum)
        if layer == 0:
            fc_out_part0 = reduced(contract_rows(act[:, :inner], dy).astype(BF16), 1)
            out_part0 = reduced(contract_rows(act[:, inner:], dy).astype(BF16), 1)
    act = after(kept_list[1][-1], small_list[0][0])
    summed = scatter_rows(lambda other: outer(act, w_outs[1], other))
    ends.append((hidden_list[1].astype(F32) + summed + end_e[1]).astype(BF16))

    def to_owner(first, second, upper, lower):
        return (jnp.where(low, first, lower), jnp.where(low, upper, second))

    def to_first(value):
        return lax.ppermute(value, SECTION, [(1, 0)])

    def to_second(value):
        return lax.ppermute(value, SECTION, [(0, 1)])

    ends_sum = jnp.concatenate([member[2] for member in small_list])
    ends_sum = sum_over(sum_over(ends_sum, SECTION), COL)
    small = sum_over(
        jnp.concatenate([*small_list[0][:2], *small_list[1][:2], ends_sum]), ROW
    )
    sums = small[: 2 * (per + inner)]
    smalls = to_owner(
        *jnp.split(sums, 2), *jnp.split(swap(sums, SECTION, 1), 2)
    )
    end_grad = jnp.where(low, *jnp.split(small[2 * (per + inner) :], 2))
    qkv_b_grad = jnp.concatenate([member[:per] for member in smalls])
    fc_in_b_grad = jnp.concatenate([member[per:] for member in smalls])
    outs_lower = to_second(outs_part1)
    ins_lower = to_second(ins_list[1])
    ins_upper = to_first(ins_list[0])
    ins_g = to_owner(*ins_list, ins_upper, ins_lower)
    qkv_g = jnp.concatenate([member[:, inner:] for member in ins_g], axis=1).astype(F32)
    fc_in_g = jnp.concatenate([member[:, :inner] for member in ins_g], axis=1).astype(F32)
    qkv_w_grad = gain_one[:, None] * qkv_g + shift_one[:, None] * qkv_b_grad[None]
    fc_in_w_grad = gain_two[:, None] * fc_in_g + shift_two[:, None] * fc_in_b_grad[None]
    qkv_full, fc_full = (qkv_flat.astype(F32), fc_in_w.astype(F32))
    norms = jnp.stack(
        [
            jnp.sum(qkv_full * qkv_g, axis=1),
            jnp.sum(qkv_full * qkv_b_grad[None], axis=1),
            jnp.sum(fc_full * fc_in_g, axis=1),
            jnp.sum(fc_full * fc_in_b_grad[None], axis=1),
        ]
    )
    norms = take(sum_over(norms, COL), 1, c, deep // cols_axis)
    end_grad = take(end_grad, 0, r * cols_axis + c, deep // cols_axis)
    fc_out_upper = to_first(after(fc_out_part0, ins_upper))
    fc_out_w_grad = jnp.concatenate(
        [
            jnp.where(low, fc_out_part0, outs_lower[:inner]),
            jnp.where(low, fc_out_upper, outs_part1[:inner]),
        ],
        axis=0,
    ).astype(F32)[None]
    qkv_w_grad = qkv_w_grad.reshape(qkv_w.shape)[None]
    fc_in_w_grad = fc_in_w_grad[None]
    out_part0, fc_out_w_grad, norms = lax.optimization_barrier(
        (out_part0, fc_out_w_grad, norms)
    )
    out_upper = to_first(out_part0)
    out_w_grad = jnp.concatenate(
        [
            jnp.where(low, out_part0, outs_lower[inner:]),
            jnp.where(low, out_upper, outs_part1[inner:]),
        ],
        axis=0,
    ).astype(F32)
    last = to_second(ends[1])
    layer_outputs = jnp.stack([jnp.where(low, ends[0], last), jnp.where(low, middle, ends[1])])
    first = to_first(grads)
    input_gradients = jnp.stack(
        [jnp.where(low, grads, middle_grads[0]), jnp.where(low, first, middle_grads[1])]
    )
    return (
        layer_outputs[None],
        input_gradients[None],
        qkv_w_grad,
        take(qkv_b_grad.reshape(heads_here, -1), 1, r, per // rows_axis)[None],
        out_w_grad[None],
        fc_in_w_grad,
        take(fc_in_b_grad, 0, r, 2 * inner // rows_axis)[None],
        fc_out_w_grad,
        norms[0][None],
        norms[1][None],
        norms[2][None],
        norms[3][None],
        end_grad[None],
        end_grad[None],
    )


def all_of_it(*arrays):
    return local(*arrays)


def solution(mesh):
    sizes = mesh.shape
    paired = sizes[SECTION] == 2 and sizes[COL] == 4
    rows_even = sizes[ROW] & (sizes[ROW] - 1) == 0
    body = all_of_it if paired and rows_even else relay_local
    step = jax.shard_map(
        body,
        mesh=mesh,
        in_specs=(
            P(None, (ROW, COL), None),
            P(None, (ROW, COL), None),
            P(SECTION, ROW, COL, None),
            P(SECTION, COL, ROW),
            P(SECTION, COL, ROW),
            P(SECTION, ROW, COL),
            P(SECTION, (COL, ROW)),
            P(SECTION, COL, ROW),
            P(SECTION, (ROW, COL)),
            P(SECTION, (ROW, COL)),
            P(SECTION, (ROW, COL)),
            P(SECTION, (ROW, COL)),
            P(SECTION, (ROW, COL)),
            P(SECTION, (ROW, COL)),
        ),
        out_specs=(
            P(SECTION, None, (ROW, COL), None),
            P(SECTION, None, (ROW, COL), None),
            P(SECTION, ROW, COL, None),
            P(SECTION, COL, ROW),
            P(SECTION, COL, ROW),
            P(SECTION, ROW, COL),
            P(SECTION, (COL, ROW)),
            P(SECTION, COL, ROW),
            P(SECTION, (ROW, COL)),
            P(SECTION, (ROW, COL)),
            P(SECTION, (ROW, COL)),
            P(SECTION, (ROW, COL)),
            P(SECTION, (ROW, COL)),
            P(SECTION, (ROW, COL)),
        ),
        check_vma=False,
    )
    if body is relay_local:
        return step
    return step
```

```python
import math

import jax
import jax.numpy as jnp
from jax import lax
from jax.experimental import pallas as pl
from jax.experimental.pallas import tpu as pltpu
from jax.sharding import PartitionSpec as P


SECTION, ROW, COL = ("section", "row", "col")
HD = 256
ROT = 64
SEQ_LEN = 1024


def from_behind(value, axis, steps):
    count = lax.axis_size(axis)
    initial, last = (max(0, -steps), min(count, count - steps))
    return lax.ppermute(value, axis, [(source, source + steps) for source in range(initial, last)])


def rotary_tables(length):
    positions = jnp.arange(length).astype(jnp.float32)
    inverse = 10000.0 ** (-jnp.arange(0, ROT, 2).astype(jnp.float32) / ROT)
    angles = positions[:, None] * inverse[None, :]
    angles = jnp.concatenate([angles, angles], axis=-1)
    return (jnp.cos(angles)[:, None, :], jnp.sin(angles)[:, None, :])


def rotate(values, cosines, sines):
    half_rot = ROT // 2
    turned = values[..., :ROT]
    first_half = turned[..., :half_rot]
    second_half = turned[..., half_rot:]
    swapped = jnp.concatenate([-second_half, first_half], axis=-1)
    return jnp.concatenate([turned * cosines + swapped * sines, values[..., ROT:]], axis=-1)


def rotate_back(grads, cosines, sines):

    def turn_values(values):
        return rotate(values, cosines, sines)

    _, turn_pull = jax.vjp(turn_values, grads)
    return turn_pull(grads)[0]


def gelu_exact(values):
    return jax.nn.gelu(values, approximate=False)


def norm_rows(row_values):
    centred = row_values - jnp.mean(row_values, axis=-1, keepdims=True)
    inverse_std = lax.rsqrt(jnp.mean(centred * centred, axis=-1, keepdims=True) + 1e-05)
    return (centred * inverse_std, inverse_std)


def contract_rows(first_operand, second_operand):
    return lax.dot_general(
        first_operand, second_operand, (((0,), (0,)), ((), ())), preferred_element_type=jnp.float32
    )


def contract_cols(first_operand, second_operand):
    return lax.dot_general(
        first_operand, second_operand, (((1,), (1,)), ((), ())), preferred_element_type=jnp.float32
    )


def causal_block(row_start, block_rows, row_stop):
    query_pos = row_start + lax.broadcasted_iota(jnp.int32, (block_rows, row_stop), 0)
    key_pos = lax.broadcasted_iota(jnp.int32, (block_rows, row_stop), 1)
    return query_pos >= key_pos


def attention_forward(queries, keys_all, values_all):
    length = queries.shape[0]
    block_rows = min(512, length)
    score_scale = HD ** (-0.5)
    outputs_list = []
    sums_list = []
    for block_index in range(length // block_rows):
        row_start = block_index * block_rows
        row_stop = row_start + block_rows
        scores = (
            jnp.einsum(
                "qhd,khd->hqk",
                queries[row_start:row_stop],
                keys_all[:row_stop],
                preferred_element_type=jnp.float32,
            )
            * score_scale
        )
        scores = jnp.where(causal_block(row_start, block_rows, row_stop)[None], scores, -1e30)
        row_peak = jnp.max(scores, axis=-1, keepdims=True)
        exponents = jnp.exp(scores - row_peak)
        row_total = jnp.sum(exponents, axis=-1, keepdims=True)
        attention_probs = (exponents / row_total).astype(jnp.bfloat16)
        outputs_list.append(
            jnp.einsum(
                "hqk,khd->qhd",
                attention_probs,
                values_all[:row_stop],
                preferred_element_type=jnp.float32,
            )
        )
        sums_list.append((row_peak + jnp.log(row_total))[..., 0])
    attended = jnp.concatenate(outputs_list, axis=0).astype(jnp.bfloat16).reshape(length, -1)
    return (attended, jnp.concatenate(sums_list, axis=1))


def attention_backward(queries, keys_all, values_all, log_sums, grad_attended):
    length, heads_here = (queries.shape[0], queries.shape[1])
    block_rows = min(512, length)
    score_scale = HD ** (-0.5)
    grad_out = grad_attended.reshape(length, heads_here, HD)
    grad_queries_list = []
    grad_keys = jnp.zeros(queries.shape, jnp.float32)
    grad_values = jnp.zeros(queries.shape, jnp.float32)
    for block_index in range(length // block_rows):
        row_start = block_index * block_rows
        row_stop = row_start + block_rows
        scores = (
            jnp.einsum(
                "qhd,khd->hqk",
                queries[row_start:row_stop],
                keys_all[:row_stop],
                preferred_element_type=jnp.float32,
            )
            * score_scale
        )
        scores = jnp.where(causal_block(row_start, block_rows, row_stop)[None], scores, -1e30)
        attention_probs = jnp.exp(scores - log_sums[:, row_start:row_stop, None])
        low_probs = attention_probs.astype(jnp.bfloat16)
        grad_probs = jnp.einsum(
            "qhd,khd->hqk",
            grad_out[row_start:row_stop],
            values_all[:row_stop],
            preferred_element_type=jnp.float32,
        )
        centre_term = jnp.sum(attention_probs * grad_probs, axis=-1, keepdims=True)
        grad_scores = (attention_probs * (grad_probs - centre_term)).astype(jnp.bfloat16)
        grad_queries_list.append(
            jnp.einsum(
                "hqk,khd->qhd", grad_scores, keys_all[:row_stop], preferred_element_type=jnp.float32
            )
            * score_scale
        )
        grad_keys = grad_keys.at[:row_stop].add(
            jnp.einsum(
                "hqk,qhd->khd",
                grad_scores,
                queries[row_start:row_stop],
                preferred_element_type=jnp.float32,
            )
            * score_scale
        )
        grad_values = grad_values.at[:row_stop].add(
            jnp.einsum(
                "hqk,qhd->khd",
                low_probs,
                grad_out[row_start:row_stop],
                preferred_element_type=jnp.float32,
            )
        )
    return (jnp.concatenate(grad_queries_list, axis=0), grad_keys, grad_values)


def forward_turn(my_rows, weights, vectors, cosines, sines):
    qkv_w, qkv_b, out_w, fc_in_w, fc_in_b, fc_out_w = weights
    gain_one, bias_one, gain_two, bias_two, out_b, fc_out_b = vectors
    gathered = lax.all_gather(my_rows, COL, axis=0, tiled=True)
    scaled, _ = norm_rows(gathered.astype(jnp.float32))
    normed_one = (scaled * gain_one + bias_one).astype(jnp.bfloat16)
    normed_two = (scaled * gain_two + bias_two).astype(jnp.bfloat16)
    length = gathered.shape[0]
    heads_here = qkv_w.shape[1]
    projected = jnp.dot(
        normed_one, qkv_w.reshape(qkv_w.shape[0], -1), preferred_element_type=jnp.float32
    ) + qkv_b.reshape(-1).astype(jnp.float32)
    projected = projected.reshape(length, heads_here, 3, HD)
    queries = rotate(projected[:, :, 0], cosines, sines).astype(jnp.bfloat16)
    keys_all = rotate(projected[:, :, 1], cosines, sines).astype(jnp.bfloat16)
    values_all = projected[:, :, 2].astype(jnp.bfloat16)
    attended, log_sums = attention_forward(queries, keys_all, values_all)
    inner_act = jnp.dot(normed_two, fc_in_w, preferred_element_type=jnp.float32) + fc_in_b.astype(
        jnp.float32
    )
    activated = gelu_exact(inner_act).astype(jnp.bfloat16)
    summed = lax.psum_scatter(
        jnp.dot(attended, out_w, preferred_element_type=jnp.float32)
        + jnp.dot(activated, fc_out_w, preferred_element_type=jnp.float32),
        COL,
        scatter_dimension=0,
        tiled=True,
    )
    output = (my_rows.astype(jnp.float32) + summed + out_b + fc_out_b).astype(jnp.bfloat16)
    kept_values = (
        gathered,
        normed_one,
        normed_two,
        queries,
        keys_all,
        values_all,
        attended,
        log_sums,
        inner_act,
    )
    return (output, kept_values)


def backward_turn(grad_rows, kept_values, weights, vectors, cosines, sines):
    (
        gathered,
        normed_one,
        normed_two,
        queries,
        keys_all,
        values_all,
        attended,
        log_sums,
        inner_act,
    ) = kept_values
    qkv_w, qkv_b, out_w, fc_in_w, _, fc_out_w = weights
    gain_one, _, gain_two, _, _, _ = vectors
    grad_full = lax.all_gather(grad_rows, COL, axis=0, tiled=True)
    length = grad_full.shape[0]
    rows_here = grad_rows.shape[0]
    own_start = lax.axis_index(COL) * rows_here
    activated = gelu_exact(inner_act).astype(jnp.bfloat16)
    out_w_grad = contract_rows(attended, grad_full)
    fc_out_w_grad = contract_rows(activated, grad_full)
    grad_attended = contract_cols(grad_full, out_w).astype(jnp.bfloat16)
    grad_activated = contract_cols(grad_full, fc_out_w)
    _, gelu_pull = jax.vjp(gelu_exact, inner_act)
    grad_inner = gelu_pull(grad_activated)[0].astype(jnp.bfloat16)
    grad_queries, grad_keys, grad_values = attention_backward(
        queries, keys_all, values_all, log_sums, grad_attended
    )
    grad_q_pre = rotate_back(grad_queries, cosines, sines)
    grad_k_pre = rotate_back(grad_keys, cosines, sines)
    grad_projected = (
        jnp.stack([grad_q_pre, grad_k_pre, grad_values], axis=2)
        .astype(jnp.bfloat16)
        .reshape(length, -1)
    )
    qkv_flat = qkv_w.reshape(qkv_w.shape[0], -1)
    qkv_w_grad = contract_rows(normed_one, grad_projected).reshape(qkv_w.shape)
    qkv_b_grad = jnp.sum(grad_projected.astype(jnp.float32), axis=0).reshape(qkv_b.shape)
    fc_in_w_grad = contract_rows(normed_two, grad_inner)
    fc_in_b_grad = jnp.sum(grad_inner.astype(jnp.float32), axis=0)
    width = qkv_w.shape[0]
    scaled_full, inverse_full = norm_rows(gathered.astype(jnp.float32))
    scaled = lax.dynamic_slice_in_dim(scaled_full, own_start, rows_here, 0)
    inverse_std = lax.dynamic_slice_in_dim(inverse_full, own_start, rows_here, 0)
    dy_sum = jnp.sum(grad_rows.astype(jnp.float32), axis=0)
    both_grads = lax.psum_scatter(
        jnp.concatenate(
            [contract_cols(grad_projected, qkv_flat), contract_cols(grad_inner, fc_in_w)], axis=1
        ),
        COL,
        scatter_dimension=0,
        tiled=True,
    )
    grad_one = both_grads[:, :width]
    grad_two = both_grads[:, width:]
    combined = gain_one * grad_one + gain_two * grad_two
    vector_grads = (
        jnp.sum(grad_one * scaled, axis=0),
        jnp.sum(grad_one, axis=0),
        jnp.sum(grad_two * scaled, axis=0),
        jnp.sum(grad_two, axis=0),
        dy_sum,
    )
    grad_norm = inverse_std * (
        combined
        - jnp.mean(combined, axis=-1, keepdims=True)
        - scaled * jnp.mean(combined * scaled, axis=-1, keepdims=True)
    )
    grad_input = (grad_rows.astype(jnp.float32) + grad_norm).astype(jnp.bfloat16)
    matrix_grads = (qkv_w_grad, qkv_b_grad, out_w_grad, fc_in_w_grad, fc_in_b_grad, fc_out_w_grad)
    return (grad_input, matrix_grads, vector_grads)


def add_tuples(running, addend):
    if running is None:
        return addend
    return tuple((first_part + second_part for first_part, second_part in zip(running, addend)))


def relay_local(
    inputs,
    cotangent,
    qkv_weight,
    qkv_bias,
    out_weight,
    fc_in_weight,
    fc_in_bias,
    fc_out_weight,
    norm1_gain,
    norm1_bias,
    norm2_gain,
    norm2_bias,
    out_bias,
    fc_out_bias,
):
    sections = lax.axis_size(SECTION)
    section_index = lax.axis_index(SECTION)
    micro_count = inputs.shape[0]
    tick_count = micro_count + sections - 1
    is_first = section_index == 0
    is_last = section_index == sections - 1
    cosines, sines = rotary_tables(SEQ_LEN)
    vectors = (
        lax.all_gather(norm1_gain[0], (ROW, COL), axis=0, tiled=True),
        lax.all_gather(norm1_bias[0], (ROW, COL), axis=0, tiled=True),
        lax.all_gather(norm2_gain[0], (ROW, COL), axis=0, tiled=True),
        lax.all_gather(norm2_bias[0], (ROW, COL), axis=0, tiled=True),
        lax.all_gather(out_bias[0], (ROW, COL), axis=0, tiled=True),
        lax.all_gather(fc_out_bias[0], (ROW, COL), axis=0, tiled=True),
    )
    vectors = tuple((member.astype(jnp.float32) for member in vectors))
    received = jnp.zeros_like(inputs[0])
    outputs_list = []
    kept_list = []
    for tick_index in range(tick_count):
        weights = (
            lax.all_gather(qkv_weight[0], ROW, axis=0, tiled=True),
            lax.all_gather(qkv_bias[0], ROW, axis=1, tiled=True),
            lax.all_gather(out_weight[0], ROW, axis=1, tiled=True),
            lax.all_gather(fc_in_weight[0], ROW, axis=0, tiled=True),
            lax.all_gather(fc_in_bias[0], ROW, axis=0, tiled=True),
            lax.all_gather(fc_out_weight[0], ROW, axis=1, tiled=True),
        )
        first_rows = inputs[min(tick_index, micro_count - 1)]
        my_rows = jnp.where(is_first, first_rows, received)
        output, kept_values = forward_turn(my_rows, weights, vectors, cosines, sines)
        outputs_list.append(output)
        kept_list.append(kept_values)
        if tick_index + 1 < tick_count:
            received = from_behind(output, SECTION, 1)
    layer_outputs = lax.dynamic_slice_in_dim(jnp.stack(outputs_list), section_index, micro_count, 0)
    stacked_kept = tuple((jnp.stack(members) for members in zip(*kept_list)))
    received_grad = jnp.zeros_like(inputs[0])
    grads_list = []
    matrix_total = None
    vector_total = None
    for tick_index in range(tick_count):
        weights = (
            lax.all_gather(qkv_weight[0], ROW, axis=0, tiled=True),
            lax.all_gather(qkv_bias[0], ROW, axis=1, tiled=True),
            lax.all_gather(out_weight[0], ROW, axis=1, tiled=True),
            lax.all_gather(fc_in_weight[0], ROW, axis=0, tiled=True),
            lax.all_gather(fc_in_bias[0], ROW, axis=0, tiled=True),
            lax.all_gather(fc_out_weight[0], ROW, axis=1, tiled=True),
        )
        if tick_index < micro_count:
            seed_grad = cotangent[tick_index]
        else:
            seed_grad = jnp.zeros_like(cotangent[0])
        grad_rows = jnp.where(is_last, seed_grad, received_grad)
        forward_index = jnp.clip(tick_index - sections + 1 + 2 * section_index, 0, tick_count - 1)
        kept_values = tuple(
            (
                lax.dynamic_index_in_dim(member, forward_index, 0, keepdims=False)
                for member in stacked_kept
            )
        )
        grad_input, matrix_grads, vector_grads = backward_turn(
            grad_rows, kept_values, weights, vectors, cosines, sines
        )
        grads_list.append(grad_input)
        if tick_index + 1 < tick_count:
            received_grad = from_behind(grad_input, SECTION, -1)
        matrix_part = (
            lax.psum_scatter(matrix_grads[0], ROW, scatter_dimension=0, tiled=True),
            lax.psum_scatter(matrix_grads[1], ROW, scatter_dimension=1, tiled=True),
            lax.psum_scatter(matrix_grads[2], ROW, scatter_dimension=1, tiled=True),
            lax.psum_scatter(matrix_grads[3], ROW, scatter_dimension=0, tiled=True),
            lax.psum_scatter(matrix_grads[4], ROW, scatter_dimension=0, tiled=True),
            lax.psum_scatter(matrix_grads[5], ROW, scatter_dimension=1, tiled=True),
        )
        vector_part = (
            lax.psum_scatter(vector_grads[0], (ROW, COL), scatter_dimension=0, tiled=True),
            lax.psum_scatter(vector_grads[1], (ROW, COL), scatter_dimension=0, tiled=True),
            lax.psum_scatter(vector_grads[2], (ROW, COL), scatter_dimension=0, tiled=True),
            lax.psum_scatter(vector_grads[3], (ROW, COL), scatter_dimension=0, tiled=True),
            lax.psum_scatter(vector_grads[4], (ROW, COL), scatter_dimension=0, tiled=True),
        )
        matrix_total = add_tuples(matrix_total, tuple(matrix_part))
        vector_total = add_tuples(vector_total, tuple(vector_part))
    input_gradients = lax.dynamic_slice_in_dim(
        jnp.stack(grads_list), sections - 1 - section_index, micro_count, 0
    )
    return (
        layer_outputs[None],
        input_gradients[None],
        matrix_total[0][None],
        matrix_total[1][None],
        matrix_total[2][None],
        matrix_total[3][None],
        matrix_total[4][None],
        matrix_total[5][None],
        vector_total[0][None],
        vector_total[1][None],
        vector_total[2][None],
        vector_total[3][None],
        vector_total[4][None],
        vector_total[4][None],
    )


F32 = jnp.float32
BF16 = jnp.bfloat16
LANES = 128


def swap(value, axis, bit):
    count = lax.axis_size(axis)
    return lax.ppermute(value, axis, [(source, source ^ bit) for source in range(count)])


def sum_over(value, axis):
    bit = 1
    while bit < lax.axis_size(axis):
        value = value + swap(value, axis, bit)
        bit *= 2
    return value


def place(part, axis, index, length):
    shape = list(part.shape)
    shape[axis] = length
    start = index * part.shape[axis]
    return lax.dynamic_update_slice_in_dim(jnp.zeros(shape, part.dtype), part, start, axis)


def take(value, axis, index, size):
    return lax.dynamic_slice_in_dim(value, index * size, size, axis)


def after(value, *others):
    return lax.optimization_barrier((value, *others))[0]


def gather_rows(block):
    half = block.shape[0] // 2
    across = swap(block, SECTION, 1)
    beside = swap(block, COL, 2)
    corner = jnp.concatenate([swap(beside[:half], SECTION, 1), swap(across[half:], COL, 2)], axis=0)
    near = jnp.concatenate([block, beside], axis=0)
    far = jnp.concatenate([across, corner], axis=0)
    near_other, far_other = (swap(near, COL, 1), swap(far, COL, 1))
    return jnp.concatenate([near, near_other, far, far_other], axis=0), across


def pair_sum(keep_ref, came_ref, start, size):
    rows = pl.ds(start, size)
    return keep_ref[rows, :].astype(F32) + came_ref[rows, :].astype(F32)


def first_sum_kernel(keep_ref, came_ref, across_ref, beside_ref):
    block = keep_ref.shape[0] // 4
    half = block // 2
    for ref, starts in (
        (across_ref, (2 * block, 3 * block)),
        (beside_ref, (block + half, 3 * block + half)),
    ):
        for place, start in enumerate(starts):
            ref[place * half : (place + 1) * half, :] = pair_sum(
                keep_ref, came_ref, start, half
            ).astype(BF16)


def second_sum_kernel(keep_ref, came_ref, across_ref, beside_ref, top_ref, low_ref, kept_ref):
    block = keep_ref.shape[0] // 4
    half = block // 2
    kept_ref[:half, :] = pair_sum(keep_ref, came_ref, 0, half) + across_ref[:half, :].astype(F32)
    kept_ref[half:, :] = (
        pair_sum(keep_ref, came_ref, half, half) + beside_ref[:half, :].astype(F32)
    )
    top = pair_sum(keep_ref, came_ref, block, half) + across_ref[half:, :].astype(F32)
    top_ref[...] = top.astype(BF16)
    low = pair_sum(keep_ref, came_ref, 2 * block + half, half) + beside_ref[half:, :].astype(F32)
    low_ref[...] = low.astype(BF16)


def column_call(kernel, width, ins, outs):
    tile = 512

    def spec(shape):
        lead = shape[:-1]
        return pl.BlockSpec(lead + (tile,), lambda i: (0,) * len(lead) + (i,))

    return pl.pallas_call(
        kernel,
        grid=(width // tile,),
        in_specs=[spec(member.shape) for member in ins],
        out_specs=[spec(member.shape) for member in outs],
        out_shape=outs,
        cost_estimate=cost(0, *ins, *outs),
    )(*ins)


def scatter_rows(product):
    sent = product(1)
    came = swap(sent, COL, 1)
    keep = product(0)
    rows, width = keep.shape
    block = rows // 4
    half = block // 2
    whole_block = jax.ShapeDtypeStruct((block, width), BF16)
    half_block = jax.ShapeDtypeStruct((half, width), BF16)
    across, beside = column_call(first_sum_kernel, width, [keep, came], [whole_block, whole_block])
    across = swap(across, SECTION, 1)
    beside = swap(beside, COL, 2)
    top, low, keep = column_call(
        second_sum_kernel,
        width,
        [keep, came, across, beside],
        [half_block, half_block, jax.ShapeDtypeStruct((block, width), F32)],
    )
    arrived = jnp.concatenate([swap(top, COL, 2), swap(low, SECTION, 1)], axis=0)
    return keep + arrived.astype(F32)


def turn(values, cosines, sines):
    lead = values[:, :LANES]
    lane = lax.broadcasted_iota(jnp.int32, lead.shape, 1)
    ahead = pltpu.roll(lead, LANES - ROT // 2, 1)
    behind = pltpu.roll(lead, ROT // 2, 1)
    lead = lead * cosines + jnp.where(lane < ROT // 2, ahead, behind) * sines
    return jnp.concatenate([lead, values[:, LANES:]], axis=1)


def mm(first_operand, second_operand):
    return jnp.dot(first_operand, second_operand, preferred_element_type=F32)


def project_kernel(x_ref, wq_ref, wk_ref, wv_ref, e_ref, cos_ref, sin_ref, q_ref, k_ref, v_ref):
    x, cosines, sines = (x_ref[...], cos_ref[...], sin_ref[...])
    queries = mm(x, wq_ref[...]) + e_ref[:, :HD]
    q_ref[...] = (turn(queries, cosines, sines) * HD ** (-0.5)).astype(BF16)
    keys_here = mm(x, wk_ref[...]) + e_ref[:, HD : 2 * HD]
    k_ref[...] = turn(keys_here, cosines, sines).astype(BF16)
    v_ref[...] = (mm(x, wv_ref[...]) + e_ref[:, 2 * HD :]).astype(BF16)


def inner_kernel(x_ref, w_ref, e_ref, held_ref, act_ref, slope_ref):
    inner = mm(x_ref[...], w_ref[...]) + e_ref[...]
    below = 0.5 + 0.5 * lax.erf(inner * 0.7071067811865476)
    act_ref[...] = (inner * below).astype(BF16)
    density = jnp.exp(-0.5 * inner * inner) * 0.3989422804014327
    slope_ref[...] = (below + inner * density).astype(BF16)


def outer_kernel(act_ref, w_ref, wo_ref, out_ref):
    inner = w_ref.shape[0]
    total = mm(act_ref[:, :inner], w_ref[...]) + mm(act_ref[:, inner:], wo_ref[...])
    out_ref[...] = total.astype(BF16)


def outer_back_kernel(dy_ref, w_ref, wo_ref, slope_ref, dz_ref, do_ref, sum_ref, dy_sum_ref):
    dy = dy_ref[...]
    dz = (contract_cols(dy, w_ref[...]) * slope_ref[...].astype(F32)).astype(BF16)
    dz_ref[...] = dz
    do_ref[...] = contract_cols(dy, wo_ref[...]).astype(BF16)

    @pl.when(pl.program_id(0) == 0)
    def _():
        sum_ref[...] = jnp.zeros_like(sum_ref)
        dy_sum_ref[...] = jnp.zeros_like(dy_sum_ref)

    sum_ref[...] += jnp.sum(dz.astype(F32), axis=0, keepdims=True)
    dy_sum_ref[...] += jnp.sum(dy.astype(F32), axis=0, keepdims=True)


def inward_kernel(dz_ref, wf_ref, wq_ref, wk_ref, wv_ref, out_ref):
    start = wf_ref.shape[1]
    total = contract_cols(dz_ref[:, :start], wf_ref[...])
    for w_ref in (wq_ref, wk_ref, wv_ref):
        total += contract_cols(dz_ref[:, start : start + HD], w_ref[...])
        start += HD
    out_ref[...] = total.astype(BF16)


def attend_kernel(q_ref, k_ref, v_ref, row_ref, col_ref, out_ref, log_ref):
    scores = contract_cols(q_ref[...], k_ref[...])
    scores = jnp.where(row_ref[...] >= col_ref[...], scores, -1e30)
    peak = jnp.max(scores, axis=1, keepdims=True)
    exponents = jnp.exp(scores - peak)
    total = jnp.sum(exponents, axis=1, keepdims=True)
    out_ref[...] = mm((exponents / total).astype(BF16), v_ref[...]).astype(BF16)
    log_ref[...] = peak + jnp.log(total)


def attend_back_kernel(
    q_ref, k_ref, v_ref, row_ref, col_ref, log_ref, do_ref, cos_ref, sin_ref, held_ref,
    all_ref, sum_ref, out_ref, dk_ref, dv_ref, sem,
):
    step = pl.program_id(1)
    block = q_ref.shape[0]

    @pl.when(step == 0)
    def _():
        dk_ref[...] = jnp.zeros_like(dk_ref)
        dv_ref[...] = jnp.zeros_like(dv_ref)

    @pl.when((step == 0) & (pl.program_id(0) == 0))
    def _():
        sum_ref[...] = jnp.zeros_like(sum_ref)

    def column_sum(values):
        return jnp.sum(values.astype(F32), axis=0, keepdims=True)

    queries, keys_all, grads = (q_ref[...], k_ref[...], do_ref[...])
    scores = contract_cols(queries, keys_all)
    scores = jnp.where(row_ref[...] >= col_ref[...], scores, -1e30)
    probs = jnp.exp(scores - log_ref[...])
    grad_probs = contract_cols(grads, v_ref[...])
    centre = jnp.sum(probs * grad_probs, axis=1, keepdims=True)
    grad_scores = (probs * (grad_probs - centre)).astype(BF16)
    rows = pl.ds(pl.multiple_of(step * block, block), block)
    cosines, sines = cos_ref[rows, :], sin_ref[rows, :]
    grad_queries = mm(grad_scores, keys_all) * HD ** (-0.5)
    grad_queries = turn(grad_queries, cosines, -sines).astype(BF16)
    out_ref[rows, :HD] = grad_queries
    sum_ref[:, :HD] += column_sum(grad_queries)
    dk_ref[...] += contract_rows(grad_scores, queries)
    dv_ref[...] += contract_rows(probs.astype(BF16), grads)

    @pl.when(step == pl.num_programs(1) - 1)
    def _():
        grad_keys = turn(dk_ref[...], cos_ref[...], -sin_ref[...]).astype(BF16)
        grad_values = dv_ref[...].astype(BF16)
        out_ref[:, HD : 2 * HD] = grad_keys
        out_ref[:, 2 * HD :] = grad_values
        sum_ref[:, HD : 2 * HD] += column_sum(grad_keys)
        sum_ref[:, 2 * HD :] += column_sum(grad_values)
        length, width = out_ref.shape
        micro = pl.ds(pl.multiple_of(pl.program_id(0) * length, length), length)
        copy = pltpu.make_async_copy(
            out_ref, all_ref.at[micro, pl.ds(all_ref.shape[1] - width, width)], sem
        )
        copy.start()
        copy.wait()


ROW_BLOCK = 256


def by_rows(width, block=ROW_BLOCK):
    return pl.BlockSpec((block, width), lambda i: (i, 0))


def whole(shape):
    return pl.BlockSpec(shape, lambda *unused: (0,) * len(shape))


def panel(width, place):
    return lambda deep: pl.BlockSpec((deep, width), lambda *unused: (0, place))


def cost(flops, *arrays):
    return pl.CostEstimate(
        flops=flops,
        transcendentals=0,
        bytes_accessed=sum(math.prod(array.shape) * array.dtype.itemsize for array in arrays),
    )


def heads_panels(array, inner):
    return [panel(HD, inner // HD + part)(array.shape[0]) for part in range(3)]


def project(x, w, inner, e, tables):
    rows, width = x.shape
    per_micro = tables[0].shape[0] // ROW_BLOCK
    table = pl.BlockSpec((ROW_BLOCK, LANES), lambda i: (i % per_micro, 0))
    out = jax.ShapeDtypeStruct((rows, HD), BF16)
    return pl.pallas_call(
        project_kernel,
        grid=(rows // ROW_BLOCK,),
        in_specs=[by_rows(width), *heads_panels(w, inner), whole(e.shape), table, table],
        out_specs=[by_rows(HD)] * 3,
        out_shape=[out] * 3,
        cost_estimate=cost(6 * rows * width * HD, x, out, out, out),
        name="project",
    )(x, w, w, w, e, *tables)


def inner_layer(x, w, e, held):
    rows, width = x.shape
    inner = e.shape[1]
    slope = jax.ShapeDtypeStruct((rows, inner), BF16)
    return pl.pallas_call(
        inner_kernel,
        grid=(rows // ROW_BLOCK,),
        in_specs=[
            by_rows(width),
            panel(inner, 0)(width),
            whole(e.shape),
            pl.BlockSpec(memory_space=pl.ANY),
        ],
        out_specs=[by_rows(inner)] * 2,
        out_shape=[jax.ShapeDtypeStruct(held.shape, BF16), slope],
        input_output_aliases={3: 0},
        cost_estimate=cost(2 * rows * width * inner, x, slope, slope),
        name="inner",
    )(x, w, e, held)


def split_rows(width, other):
    return pl.BlockSpec((ROW_BLOCK, width), lambda i: (i // 2 * 4 + 2 * other + i % 2, 0))


def outer_panels(pair, inner):
    (w, first), (wo, second) = pair
    return [
        pl.BlockSpec((inner, w.shape[1]), lambda *unused: (first // inner, 0)),
        pl.BlockSpec((HD, wo.shape[1]), lambda *unused: (second // HD, 0)),
    ]


def outer(act, pair, other):
    rows, width = (act.shape[0] // 2, pair[0][0].shape[1])
    out = jax.ShapeDtypeStruct((rows, width), BF16)
    return pl.pallas_call(
        outer_kernel,
        grid=(rows // ROW_BLOCK,),
        in_specs=[split_rows(act.shape[1], other), *outer_panels(pair, act.shape[1] - HD)],
        out_specs=by_rows(width),
        out_shape=out,
        cost_estimate=cost(2 * rows * width * act.shape[1], act, out),
        name="outer",
    )(act, pair[0][0], pair[1][0])


def inward(dz, w_in, w_qkv, offset, other):
    rows, width = (dz.shape[0] // 2, w_in.shape[0])
    out = jax.ShapeDtypeStruct((rows, width), BF16)
    return pl.pallas_call(
        inward_kernel,
        grid=(rows // ROW_BLOCK,),
        in_specs=[
            split_rows(dz.shape[1], other),
            panel(dz.shape[1] - 3 * HD, 0)(width),
            *heads_panels(w_qkv, offset),
        ],
        out_specs=by_rows(width),
        out_shape=out,
        cost_estimate=cost(2 * rows * width * dz.shape[1], dz, out),
        name="inward",
    )(dz, w_in, w_qkv, w_qkv, w_qkv)


def outer_back(dy, pair, slopes):
    rows, width = dy.shape
    inner = slopes.shape[1]
    dz = jax.ShapeDtypeStruct((rows, inner + 3 * HD), BF16)
    return pl.pallas_call(
        outer_back_kernel,
        grid=(rows // ROW_BLOCK,),
        in_specs=[by_rows(width), *outer_panels(pair, inner), by_rows(inner)],
        out_specs=[by_rows(inner), by_rows(HD), whole((1, inner)), whole((1, width))],
        out_shape=[
            dz,
            jax.ShapeDtypeStruct((rows, HD), BF16),
            jax.ShapeDtypeStruct((1, inner), F32),
            jax.ShapeDtypeStruct((1, width), F32),
        ],
        cost_estimate=cost(2 * rows * width * (inner + HD), dy, slopes, slopes),
        name="outer_back",
    )(dy, pair[0][0], pair[1][0], slopes)


def attend(queries, keys_all, values_all, places, inner):
    rows = queries.shape[0]
    length = places.shape[0]
    steps = length // ROW_BLOCK
    row = pl.BlockSpec((ROW_BLOCK, HD), lambda m, i: (m * steps + i, 0))
    every = pl.BlockSpec((length, HD), lambda m, i: (m, 0))
    return pl.pallas_call(
        attend_kernel,
        grid=(rows // length, steps),
        in_specs=[
            row,
            every,
            every,
            pl.BlockSpec((ROW_BLOCK, 1), lambda m, i: (i, 0)),
            pl.BlockSpec((1, length), lambda m, i: (0, 0)),
        ],
        out_specs=[
            pl.BlockSpec((ROW_BLOCK, HD), lambda m, i: (m * steps + i, inner // HD)),
            pl.BlockSpec((ROW_BLOCK, 1), lambda m, i: (m * steps + i, 0)),
        ],
        out_shape=[
            jax.ShapeDtypeStruct((rows, inner + HD), BF16),
            jax.ShapeDtypeStruct((rows, 1), F32),
        ],
        cost_estimate=cost(4 * rows * length * HD, queries, keys_all, values_all, queries),
        name="attend",
    )(queries, keys_all, values_all, places[:, None], places[None, :])


def attend_back(queries, keys_all, values_all, places, log_sums, grads, tables, held):
    rows = queries.shape[0]
    length = places.shape[0]
    steps = length // ROW_BLOCK
    row = pl.BlockSpec((ROW_BLOCK, HD), lambda m, i: (m * steps + i, 0))
    every = pl.BlockSpec((length, HD), lambda m, i: (m, 0))
    anywhere = pl.BlockSpec(memory_space=pl.ANY)
    return pl.pallas_call(
        attend_back_kernel,
        grid=(rows // length, steps),
        in_specs=[
            row,
            every,
            every,
            pl.BlockSpec((ROW_BLOCK, 1), lambda m, i: (i, 0)),
            pl.BlockSpec((1, length), lambda m, i: (0, 0)),
            pl.BlockSpec((ROW_BLOCK, 1), lambda m, i: (m * steps + i, 0)),
            row,
            whole(tables[0].shape),
            whole(tables[1].shape),
            anywhere,
        ],
        out_specs=[anywhere, whole((1, 3 * HD))],
        out_shape=[
            jax.ShapeDtypeStruct(held.shape, BF16),
            jax.ShapeDtypeStruct((1, 3 * HD), F32),
        ],
        scratch_shapes=[
            pltpu.VMEM((length, 3 * HD), BF16),
            pltpu.VMEM((length, HD), F32),
            pltpu.VMEM((length, HD), F32),
            pltpu.SemaphoreType.DMA,
        ],
        input_output_aliases={9: 0},
        cost_estimate=cost(10 * rows * length * HD, queries, keys_all, values_all, grads),
        name="attend_back",
    )(
        queries, keys_all, values_all, places[:, None], places[None, :], log_sums, grads, *tables,
        held,
    )


def local(
    inputs,
    cotangent,
    qkv_weight,
    qkv_bias,
    out_weight,
    fc_in_weight,
    fc_in_bias,
    fc_out_weight,
    norm1_gain,
    norm1_bias,
    norm2_gain,
    norm2_bias,
    out_bias,
    fc_out_bias,
):
    s, r, c = (lax.axis_index(SECTION), lax.axis_index(ROW), lax.axis_index(COL))
    rows_axis, cols_axis = (lax.axis_size(ROW), lax.axis_size(COL))
    low = s == 0
    qkv_w, out_w, fc_in_w, fc_out_w = (
        qkv_weight[0], out_weight[0], fc_in_weight[0], fc_out_weight[0],
    )
    deep, heads_here = qkv_w.shape[0], qkv_w.shape[1]
    per = 3 * HD
    inner = fc_in_w.shape[1] // 2
    model = inputs.shape[2]

    def both_layers(own_first, own_second):
        return (jnp.where(low, own_first, own_second), jnp.where(low, own_second, own_first))

    def trade(value, axis, *others):
        size = value.shape[axis] // 2
        kept = take(value, axis, s, size)
        came = swap(after(take(value, axis, 1 - s, size), *others), SECTION, 1)
        return kept, came

    def gathered(shard, axis):
        return lax.all_gather(shard, ROW, axis=axis, tiled=True)

    held = jnp.stack(
        [
            norm1_gain[0].astype(F32),
            norm1_bias[0].astype(F32),
            norm2_gain[0].astype(F32),
            norm2_bias[0].astype(F32),
            out_bias[0].astype(F32) + fc_out_bias[0].astype(F32),
        ]
    )
    held_both = jnp.stack([held, swap(held, SECTION, 1)])
    qkv_flat = qkv_w.reshape(deep, -1)
    qkv_half = trade(qkv_flat, 1, held_both)
    fc_in_half = trade(fc_in_w, 1, qkv_half[1])
    outs_kept = jnp.concatenate([take(fc_out_w, 0, s, inner), take(out_w, 0, s, HD)], axis=0)
    outs_sent = jnp.concatenate([take(fc_out_w, 0, 1 - s, inner), take(out_w, 0, 1 - s, HD)], axis=0)
    outs_came = swap(after(outs_sent, fc_in_half[1]), SECTION, 1)
    held_both = sum_over(place(held_both, 2, c, deep), COL)
    held = held_both[0]
    gain_one, shift_one, gain_two, shift_two, end_bias = (held[i] for i in range(5))
    gains = both_layers(held, held_both[1])

    def scaled_pair(half, row):
        return tuple(
            (part.astype(F32) * gain[row][:, None]).astype(BF16)
            for part, gain in zip(both_layers(*half), gains)
        )

    qkv_pair = scaled_pair(qkv_half, 0)
    fc_in_pair = scaled_pair(fc_in_half, 2)
    outs_pair = both_layers(outs_kept, outs_came)
    w_qkv0 = gathered(qkv_pair[0], 0)
    w_fc_in0 = gathered(fc_in_pair[0], 0)
    w_outs0 = gathered(outs_pair[0], 1)
    w_ins1 = gathered(jnp.concatenate([fc_in_pair[1], qkv_pair[1]], axis=1), 0)
    w_outs1 = gathered(outs_pair[1], 1)
    w_ins = ((w_fc_in0, w_qkv0, 0), (w_ins1, w_ins1, inner))
    w_outs = tuple(((member, 0), (member, inner)) for member in (w_outs0, w_outs1))

    own_qkv = mm(shift_one.astype(BF16)[None], qkv_flat)[0]
    own_fc = mm(shift_two.astype(BF16)[None], fc_in_w)[0]
    own_qkv = own_qkv + place(qkv_bias[0].astype(F32), 1, r, per).reshape(-1)
    own_fc = own_fc + place(fc_in_bias[0].astype(F32), 0, r, 2 * inner)
    biases = sum_over(
        jnp.concatenate([own_qkv, own_fc, place(end_bias, 0, r, model)]), ROW
    )
    biases = both_layers(biases, swap(biases, SECTION, 1))
    qkv_e, fc_e, end_e = ([], [], [])
    for member in biases:
        qkv_e.append(take(member[: 2 * per], 0, s, per)[None])
        fc_e.append(take(member[2 * per : 2 * per + 2 * inner], 0, s, inner)[None])
        end_e.append(member[2 * per + 2 * inner :])

    block_rows = inputs.shape[1]
    masks = jnp.array([0, 2, 1, 3], jnp.int32)
    places = ((c ^ masks)[:, None] * block_rows + jnp.arange(block_rows)[None]).reshape(-1)
    inverse = 10000.0 ** (-jnp.arange(0, ROT, 2).astype(F32) / ROT)
    angles = places.astype(F32)[:, None] * inverse[None]
    ones = jnp.ones((places.shape[0], LANES - ROT), F32)
    cosines, sines = (jnp.cos(angles), jnp.sin(angles))
    tables = (
        jnp.concatenate([cosines, cosines, ones], axis=1),
        jnp.concatenate([-sines, sines, 0.0 * ones], axis=1),
    )

    hidden = lax.dynamic_index_in_dim(inputs, s, 0, keepdims=False)
    seed = lax.dynamic_index_in_dim(cotangent, s, 0, keepdims=False)
    hidden = after(hidden, outs_came)

    hidden_list, kept_list, ends = ([], [], [])
    seed_rows = None
    for layer in range(2):
        hidden_list.append(hidden)
        scaled, unused = norm_rows(hidden.astype(F32))
        x, unused = gather_rows(scaled.astype(BF16))
        if layer == 0:
            seed_rows, unused = gather_rows(after(seed, x))
            x = after(x, seed_rows)
        w_fc_in, w_qkv, offset = w_ins[layer]
        queries, keys_all, values_all = project(x, w_qkv, offset, qkv_e[layer], tables)
        attended, log_sums = attend(queries, keys_all, values_all, places, inner)
        act, slopes = inner_layer(x, w_fc_in, fc_e[layer], attended)
        kept = (x, queries, keys_all, values_all, log_sums, slopes, act)
        if layer == 1:
            outs_grad1 = contract_rows(act, seed_rows).astype(BF16)
            seed_rows = after(seed_rows, outs_grad1)
        kept_list.append(kept)
        if layer == 0:
            summed = scatter_rows(lambda other: outer(act, w_outs[0], other))
            hidden = (hidden.astype(F32) + summed + end_e[layer]).astype(BF16)
            ends.append(hidden)
            middle = swap(hidden, SECTION, 1)

    def reduced(value, axis):
        return lax.psum_scatter(value, ROW, scatter_dimension=axis, tiled=True)

    outs_part1 = reduced(outs_grad1, 1)
    grads = seed
    ins_list, small_list = ([None, None], [None, None])
    for layer in (1, 0):
        x, queries, keys_all, values_all, log_sums, slopes, act = kept_list[layer]
        w_fc_in, w_qkv, offset = w_ins[layer]
        if layer == 1:
            dy = seed_rows
        else:
            dy, across = gather_rows(grads)
            middle_grads = (jnp.where(low, grads, across), jnp.where(low, across, grads))
        dz, grad_attended, inner_sum, dy_sum = outer_back(dy, w_outs[layer], slopes)
        dz, heads_sum = attend_back(
            queries, keys_all, values_all, places, log_sums, grad_attended, tables, dz
        )
        combined = scatter_rows(lambda other: inward(dz, w_fc_in, w_qkv, offset, other))
        ins_grad = contract_rows(x, dz).astype(BF16)
        ins_list[layer] = reduced(ins_grad, 0)
        scaled, inverse_std = norm_rows(hidden_list[layer].astype(F32))
        grad_norm = inverse_std * (
            combined
            - jnp.mean(combined, axis=-1, keepdims=True)
            - scaled * jnp.mean(combined * scaled, axis=-1, keepdims=True)
        )
        grads = (grads.astype(F32) + grad_norm).astype(BF16)
        small_list[layer] = (heads_sum[0], inner_sum[0], dy_sum[0])
        if layer == 0:
            fc_out_part0 = reduced(contract_rows(act[:, :inner], dy).astype(BF16), 1)
            out_part0 = reduced(contract_rows(act[:, inner:], dy).astype(BF16), 1)
    act = kept_list[1][-1]
    summed = scatter_rows(lambda other: outer(act, w_outs[1], other))
    summed = after(summed, small_list[0][0])
    ends.append((hidden_list[1].astype(F32) + summed + end_e[1]).astype(BF16))

    def to_owner(first, second, upper, lower):
        return (jnp.where(low, first, lower), jnp.where(low, upper, second))

    def to_first(value):
        return lax.ppermute(value, SECTION, [(1, 0)])

    def to_second(value):
        return lax.ppermute(value, SECTION, [(0, 1)])

    small = sum_over(
        jnp.concatenate(
            [*small_list[0][:2], *small_list[1][:2], small_list[0][2], small_list[1][2]]
        ),
        ROW,
    )
    sums = small[: 2 * (per + inner)]
    smalls = to_owner(*jnp.split(sums, 2), *jnp.split(swap(sums, SECTION, 1), 2))
    end_grad = jnp.where(low, *jnp.split(small[2 * (per + inner) :], 2))
    qkv_b_grad = jnp.concatenate([member[:per] for member in smalls])
    fc_in_b_grad = jnp.concatenate([member[per:] for member in smalls])
    outs_lower = to_second(outs_part1)
    ins_lower = to_second(ins_list[1])
    ins_upper = to_first(ins_list[0])
    ins_g = to_owner(*ins_list, ins_upper, ins_lower)
    qkv_g = jnp.concatenate([member[:, inner:] for member in ins_g], axis=1).astype(F32)
    fc_in_g = jnp.concatenate([member[:, :inner] for member in ins_g], axis=1).astype(F32)
    qkv_w_grad = gain_one[:, None] * qkv_g + shift_one[:, None] * qkv_b_grad[None]
    fc_in_w_grad = gain_two[:, None] * fc_in_g + shift_two[:, None] * fc_in_b_grad[None]
    qkv_full, fc_full = (qkv_flat.astype(F32), fc_in_w.astype(F32))
    norms = jnp.stack(
        [
            jnp.sum(qkv_full * qkv_g, axis=1),
            jnp.sum(qkv_full * qkv_b_grad[None], axis=1),
            jnp.sum(fc_full * fc_in_g, axis=1),
            jnp.sum(fc_full * fc_in_b_grad[None], axis=1),
        ]
    )
    norms = take(sum_over(norms, COL), 1, c, deep // cols_axis)
    end_grad = take(end_grad, 0, r * cols_axis + c, deep // cols_axis)
    fc_out_upper = to_first(after(fc_out_part0, ins_upper))
    fc_out_w_grad = jnp.concatenate(
        [
            jnp.where(low, fc_out_part0, outs_lower[:inner]),
            jnp.where(low, fc_out_upper, outs_part1[:inner]),
        ],
        axis=0,
    ).astype(F32)[None]
    qkv_w_grad = qkv_w_grad.reshape(qkv_w.shape)[None]
    fc_in_w_grad = fc_in_w_grad[None]
    out_part0, fc_out_w_grad, norms = lax.optimization_barrier(
        (out_part0, fc_out_w_grad, norms)
    )
    out_upper = to_first(out_part0)
    out_w_grad = jnp.concatenate(
        [
            jnp.where(low, out_part0, outs_lower[inner:]),
            jnp.where(low, out_upper, outs_part1[inner:]),
        ],
        axis=0,
    ).astype(F32)
    last = to_second(ends[1])
    layer_outputs = jnp.stack([jnp.where(low, ends[0], last), jnp.where(low, middle, ends[1])])
    first = to_first(grads)
    input_gradients = jnp.stack(
        [jnp.where(low, grads, middle_grads[0]), jnp.where(low, first, middle_grads[1])]
    )
    return (
        layer_outputs[None],
        input_gradients[None],
        qkv_w_grad,
        take(qkv_b_grad.reshape(heads_here, -1), 1, r, per // rows_axis)[None],
        out_w_grad[None],
        fc_in_w_grad,
        take(fc_in_b_grad, 0, r, 2 * inner // rows_axis)[None],
        fc_out_w_grad,
        norms[0][None],
        norms[1][None],
        norms[2][None],
        norms[3][None],
        end_grad[None],
        end_grad[None],
    )


def all_of_it(*arrays):
    return local(*arrays)


def solution(mesh):
    sizes = mesh.shape
    paired = sizes[SECTION] == 2 and sizes[COL] == 4
    rows_even = sizes[ROW] & (sizes[ROW] - 1) == 0
    body = all_of_it if paired and rows_even else relay_local
    step = jax.shard_map(
        body,
        mesh=mesh,
        in_specs=(
            P(None, (ROW, COL), None),
            P(None, (ROW, COL), None),
            P(SECTION, ROW, COL, None),
            P(SECTION, COL, ROW),
            P(SECTION, COL, ROW),
            P(SECTION, ROW, COL),
            P(SECTION, (COL, ROW)),
            P(SECTION, COL, ROW),
            P(SECTION, (ROW, COL)),
            P(SECTION, (ROW, COL)),
            P(SECTION, (ROW, COL)),
            P(SECTION, (ROW, COL)),
            P(SECTION, (ROW, COL)),
            P(SECTION, (ROW, COL)),
        ),
        out_specs=(
            P(SECTION, None, (ROW, COL), None),
            P(SECTION, None, (ROW, COL), None),
            P(SECTION, ROW, COL, None),
            P(SECTION, COL, ROW),
            P(SECTION, COL, ROW),
            P(SECTION, ROW, COL),
            P(SECTION, (COL, ROW)),
            P(SECTION, COL, ROW),
            P(SECTION, (ROW, COL)),
            P(SECTION, (ROW, COL)),
            P(SECTION, (ROW, COL)),
            P(SECTION, (ROW, COL)),
            P(SECTION, (ROW, COL)),
            P(SECTION, (ROW, COL)),
        ),
        check_vma=False,
    )
    if body is relay_local:
        return step
    return step
```

```python
import math

import jax
import jax.numpy as jnp
from jax import lax
from jax.experimental import pallas as pl
from jax.experimental.pallas import tpu as pltpu
from jax.sharding import PartitionSpec as P


SECTION, ROW, COL = ("section", "row", "col")
HD = 256
ROT = 64
SEQ_LEN = 1024


def from_behind(value, axis, steps):
    count = lax.axis_size(axis)
    initial, last = (max(0, -steps), min(count, count - steps))
    return lax.ppermute(value, axis, [(source, source + steps) for source in range(initial, last)])


def rotary_tables(length):
    positions = jnp.arange(length).astype(jnp.float32)
    inverse = 10000.0 ** (-jnp.arange(0, ROT, 2).astype(jnp.float32) / ROT)
    angles = positions[:, None] * inverse[None, :]
    angles = jnp.concatenate([angles, angles], axis=-1)
    return (jnp.cos(angles)[:, None, :], jnp.sin(angles)[:, None, :])


def rotate(values, cosines, sines):
    half_rot = ROT // 2
    turned = values[..., :ROT]
    first_half = turned[..., :half_rot]
    second_half = turned[..., half_rot:]
    swapped = jnp.concatenate([-second_half, first_half], axis=-1)
    return jnp.concatenate([turned * cosines + swapped * sines, values[..., ROT:]], axis=-1)


def rotate_back(grads, cosines, sines):

    def turn_values(values):
        return rotate(values, cosines, sines)

    _, turn_pull = jax.vjp(turn_values, grads)
    return turn_pull(grads)[0]


def gelu_exact(values):
    return jax.nn.gelu(values, approximate=False)


def norm_rows(row_values):
    centred = row_values - jnp.mean(row_values, axis=-1, keepdims=True)
    inverse_std = lax.rsqrt(jnp.mean(centred * centred, axis=-1, keepdims=True) + 1e-05)
    return (centred * inverse_std, inverse_std)


def contract_rows(first_operand, second_operand):
    return lax.dot_general(
        first_operand, second_operand, (((0,), (0,)), ((), ())), preferred_element_type=jnp.float32
    )


def contract_cols(first_operand, second_operand):
    return lax.dot_general(
        first_operand, second_operand, (((1,), (1,)), ((), ())), preferred_element_type=jnp.float32
    )


def causal_block(row_start, block_rows, row_stop):
    query_pos = row_start + lax.broadcasted_iota(jnp.int32, (block_rows, row_stop), 0)
    key_pos = lax.broadcasted_iota(jnp.int32, (block_rows, row_stop), 1)
    return query_pos >= key_pos


def attention_forward(queries, keys_all, values_all):
    length = queries.shape[0]
    block_rows = min(512, length)
    score_scale = HD ** (-0.5)
    outputs_list = []
    sums_list = []
    for block_index in range(length // block_rows):
        row_start = block_index * block_rows
        row_stop = row_start + block_rows
        scores = (
            jnp.einsum(
                "qhd,khd->hqk",
                queries[row_start:row_stop],
                keys_all[:row_stop],
                preferred_element_type=jnp.float32,
            )
            * score_scale
        )
        scores = jnp.where(causal_block(row_start, block_rows, row_stop)[None], scores, -1e30)
        row_peak = jnp.max(scores, axis=-1, keepdims=True)
        exponents = jnp.exp(scores - row_peak)
        row_total = jnp.sum(exponents, axis=-1, keepdims=True)
        attention_probs = (exponents / row_total).astype(jnp.bfloat16)
        outputs_list.append(
            jnp.einsum(
                "hqk,khd->qhd",
                attention_probs,
                values_all[:row_stop],
                preferred_element_type=jnp.float32,
            )
        )
        sums_list.append((row_peak + jnp.log(row_total))[..., 0])
    attended = jnp.concatenate(outputs_list, axis=0).astype(jnp.bfloat16).reshape(length, -1)
    return (attended, jnp.concatenate(sums_list, axis=1))


def attention_backward(queries, keys_all, values_all, log_sums, grad_attended):
    length, heads_here = (queries.shape[0], queries.shape[1])
    block_rows = min(512, length)
    score_scale = HD ** (-0.5)
    grad_out = grad_attended.reshape(length, heads_here, HD)
    grad_queries_list = []
    grad_keys = jnp.zeros(queries.shape, jnp.float32)
    grad_values = jnp.zeros(queries.shape, jnp.float32)
    for block_index in range(length // block_rows):
        row_start = block_index * block_rows
        row_stop = row_start + block_rows
        scores = (
            jnp.einsum(
                "qhd,khd->hqk",
                queries[row_start:row_stop],
                keys_all[:row_stop],
                preferred_element_type=jnp.float32,
            )
            * score_scale
        )
        scores = jnp.where(causal_block(row_start, block_rows, row_stop)[None], scores, -1e30)
        attention_probs = jnp.exp(scores - log_sums[:, row_start:row_stop, None])
        low_probs = attention_probs.astype(jnp.bfloat16)
        grad_probs = jnp.einsum(
            "qhd,khd->hqk",
            grad_out[row_start:row_stop],
            values_all[:row_stop],
            preferred_element_type=jnp.float32,
        )
        centre_term = jnp.sum(attention_probs * grad_probs, axis=-1, keepdims=True)
        grad_scores = (attention_probs * (grad_probs - centre_term)).astype(jnp.bfloat16)
        grad_queries_list.append(
            jnp.einsum(
                "hqk,khd->qhd", grad_scores, keys_all[:row_stop], preferred_element_type=jnp.float32
            )
            * score_scale
        )
        grad_keys = grad_keys.at[:row_stop].add(
            jnp.einsum(
                "hqk,qhd->khd",
                grad_scores,
                queries[row_start:row_stop],
                preferred_element_type=jnp.float32,
            )
            * score_scale
        )
        grad_values = grad_values.at[:row_stop].add(
            jnp.einsum(
                "hqk,qhd->khd",
                low_probs,
                grad_out[row_start:row_stop],
                preferred_element_type=jnp.float32,
            )
        )
    return (jnp.concatenate(grad_queries_list, axis=0), grad_keys, grad_values)


def forward_turn(my_rows, weights, vectors, cosines, sines):
    qkv_w, qkv_b, out_w, fc_in_w, fc_in_b, fc_out_w = weights
    gain_one, bias_one, gain_two, bias_two, out_b, fc_out_b = vectors
    gathered = lax.all_gather(my_rows, COL, axis=0, tiled=True)
    scaled, _ = norm_rows(gathered.astype(jnp.float32))
    normed_one = (scaled * gain_one + bias_one).astype(jnp.bfloat16)
    normed_two = (scaled * gain_two + bias_two).astype(jnp.bfloat16)
    length = gathered.shape[0]
    heads_here = qkv_w.shape[1]
    projected = jnp.dot(
        normed_one, qkv_w.reshape(qkv_w.shape[0], -1), preferred_element_type=jnp.float32
    ) + qkv_b.reshape(-1).astype(jnp.float32)
    projected = projected.reshape(length, heads_here, 3, HD)
    queries = rotate(projected[:, :, 0], cosines, sines).astype(jnp.bfloat16)
    keys_all = rotate(projected[:, :, 1], cosines, sines).astype(jnp.bfloat16)
    values_all = projected[:, :, 2].astype(jnp.bfloat16)
    attended, log_sums = attention_forward(queries, keys_all, values_all)
    inner_act = jnp.dot(normed_two, fc_in_w, preferred_element_type=jnp.float32) + fc_in_b.astype(
        jnp.float32
    )
    activated = gelu_exact(inner_act).astype(jnp.bfloat16)
    summed = lax.psum_scatter(
        jnp.dot(attended, out_w, preferred_element_type=jnp.float32)
        + jnp.dot(activated, fc_out_w, preferred_element_type=jnp.float32),
        COL,
        scatter_dimension=0,
        tiled=True,
    )
    output = (my_rows.astype(jnp.float32) + summed + out_b + fc_out_b).astype(jnp.bfloat16)
    kept_values = (
        gathered,
        normed_one,
        normed_two,
        queries,
        keys_all,
        values_all,
        attended,
        log_sums,
        inner_act,
    )
    return (output, kept_values)


def backward_turn(grad_rows, kept_values, weights, vectors, cosines, sines):
    (
        gathered,
        normed_one,
        normed_two,
        queries,
        keys_all,
        values_all,
        attended,
        log_sums,
        inner_act,
    ) = kept_values
    qkv_w, qkv_b, out_w, fc_in_w, _, fc_out_w = weights
    gain_one, _, gain_two, _, _, _ = vectors
    grad_full = lax.all_gather(grad_rows, COL, axis=0, tiled=True)
    length = grad_full.shape[0]
    rows_here = grad_rows.shape[0]
    own_start = lax.axis_index(COL) * rows_here
    activated = gelu_exact(inner_act).astype(jnp.bfloat16)
    out_w_grad = contract_rows(attended, grad_full)
    fc_out_w_grad = contract_rows(activated, grad_full)
    grad_attended = contract_cols(grad_full, out_w).astype(jnp.bfloat16)
    grad_activated = contract_cols(grad_full, fc_out_w)
    _, gelu_pull = jax.vjp(gelu_exact, inner_act)
    grad_inner = gelu_pull(grad_activated)[0].astype(jnp.bfloat16)
    grad_queries, grad_keys, grad_values = attention_backward(
        queries, keys_all, values_all, log_sums, grad_attended
    )
    grad_q_pre = rotate_back(grad_queries, cosines, sines)
    grad_k_pre = rotate_back(grad_keys, cosines, sines)
    grad_projected = (
        jnp.stack([grad_q_pre, grad_k_pre, grad_values], axis=2)
        .astype(jnp.bfloat16)
        .reshape(length, -1)
    )
    qkv_flat = qkv_w.reshape(qkv_w.shape[0], -1)
    qkv_w_grad = contract_rows(normed_one, grad_projected).reshape(qkv_w.shape)
    qkv_b_grad = jnp.sum(grad_projected.astype(jnp.float32), axis=0).reshape(qkv_b.shape)
    fc_in_w_grad = contract_rows(normed_two, grad_inner)
    fc_in_b_grad = jnp.sum(grad_inner.astype(jnp.float32), axis=0)
    width = qkv_w.shape[0]
    scaled_full, inverse_full = norm_rows(gathered.astype(jnp.float32))
    scaled = lax.dynamic_slice_in_dim(scaled_full, own_start, rows_here, 0)
    inverse_std = lax.dynamic_slice_in_dim(inverse_full, own_start, rows_here, 0)
    dy_sum = jnp.sum(grad_rows.astype(jnp.float32), axis=0)
    both_grads = lax.psum_scatter(
        jnp.concatenate(
            [contract_cols(grad_projected, qkv_flat), contract_cols(grad_inner, fc_in_w)], axis=1
        ),
        COL,
        scatter_dimension=0,
        tiled=True,
    )
    grad_one = both_grads[:, :width]
    grad_two = both_grads[:, width:]
    combined = gain_one * grad_one + gain_two * grad_two
    vector_grads = (
        jnp.sum(grad_one * scaled, axis=0),
        jnp.sum(grad_one, axis=0),
        jnp.sum(grad_two * scaled, axis=0),
        jnp.sum(grad_two, axis=0),
        dy_sum,
    )
    grad_norm = inverse_std * (
        combined
        - jnp.mean(combined, axis=-1, keepdims=True)
        - scaled * jnp.mean(combined * scaled, axis=-1, keepdims=True)
    )
    grad_input = (grad_rows.astype(jnp.float32) + grad_norm).astype(jnp.bfloat16)
    matrix_grads = (qkv_w_grad, qkv_b_grad, out_w_grad, fc_in_w_grad, fc_in_b_grad, fc_out_w_grad)
    return (grad_input, matrix_grads, vector_grads)


def add_tuples(running, addend):
    if running is None:
        return addend
    return tuple((first_part + second_part for first_part, second_part in zip(running, addend)))


def relay_local(
    inputs,
    cotangent,
    qkv_weight,
    qkv_bias,
    out_weight,
    fc_in_weight,
    fc_in_bias,
    fc_out_weight,
    norm1_gain,
    norm1_bias,
    norm2_gain,
    norm2_bias,
    out_bias,
    fc_out_bias,
):
    sections = lax.axis_size(SECTION)
    section_index = lax.axis_index(SECTION)
    micro_count = inputs.shape[0]
    tick_count = micro_count + sections - 1
    is_first = section_index == 0
    is_last = section_index == sections - 1
    cosines, sines = rotary_tables(SEQ_LEN)
    vectors = (
        lax.all_gather(norm1_gain[0], (ROW, COL), axis=0, tiled=True),
        lax.all_gather(norm1_bias[0], (ROW, COL), axis=0, tiled=True),
        lax.all_gather(norm2_gain[0], (ROW, COL), axis=0, tiled=True),
        lax.all_gather(norm2_bias[0], (ROW, COL), axis=0, tiled=True),
        lax.all_gather(out_bias[0], (ROW, COL), axis=0, tiled=True),
        lax.all_gather(fc_out_bias[0], (ROW, COL), axis=0, tiled=True),
    )
    vectors = tuple((member.astype(jnp.float32) for member in vectors))
    received = jnp.zeros_like(inputs[0])
    outputs_list = []
    kept_list = []
    for tick_index in range(tick_count):
        weights = (
            lax.all_gather(qkv_weight[0], ROW, axis=0, tiled=True),
            lax.all_gather(qkv_bias[0], ROW, axis=1, tiled=True),
            lax.all_gather(out_weight[0], ROW, axis=1, tiled=True),
            lax.all_gather(fc_in_weight[0], ROW, axis=0, tiled=True),
            lax.all_gather(fc_in_bias[0], ROW, axis=0, tiled=True),
            lax.all_gather(fc_out_weight[0], ROW, axis=1, tiled=True),
        )
        first_rows = inputs[min(tick_index, micro_count - 1)]
        my_rows = jnp.where(is_first, first_rows, received)
        output, kept_values = forward_turn(my_rows, weights, vectors, cosines, sines)
        outputs_list.append(output)
        kept_list.append(kept_values)
        if tick_index + 1 < tick_count:
            received = from_behind(output, SECTION, 1)
    layer_outputs = lax.dynamic_slice_in_dim(jnp.stack(outputs_list), section_index, micro_count, 0)
    stacked_kept = tuple((jnp.stack(members) for members in zip(*kept_list)))
    received_grad = jnp.zeros_like(inputs[0])
    grads_list = []
    matrix_total = None
    vector_total = None
    for tick_index in range(tick_count):
        weights = (
            lax.all_gather(qkv_weight[0], ROW, axis=0, tiled=True),
            lax.all_gather(qkv_bias[0], ROW, axis=1, tiled=True),
            lax.all_gather(out_weight[0], ROW, axis=1, tiled=True),
            lax.all_gather(fc_in_weight[0], ROW, axis=0, tiled=True),
            lax.all_gather(fc_in_bias[0], ROW, axis=0, tiled=True),
            lax.all_gather(fc_out_weight[0], ROW, axis=1, tiled=True),
        )
        if tick_index < micro_count:
            seed_grad = cotangent[tick_index]
        else:
            seed_grad = jnp.zeros_like(cotangent[0])
        grad_rows = jnp.where(is_last, seed_grad, received_grad)
        forward_index = jnp.clip(tick_index - sections + 1 + 2 * section_index, 0, tick_count - 1)
        kept_values = tuple(
            (
                lax.dynamic_index_in_dim(member, forward_index, 0, keepdims=False)
                for member in stacked_kept
            )
        )
        grad_input, matrix_grads, vector_grads = backward_turn(
            grad_rows, kept_values, weights, vectors, cosines, sines
        )
        grads_list.append(grad_input)
        if tick_index + 1 < tick_count:
            received_grad = from_behind(grad_input, SECTION, -1)
        matrix_part = (
            lax.psum_scatter(matrix_grads[0], ROW, scatter_dimension=0, tiled=True),
            lax.psum_scatter(matrix_grads[1], ROW, scatter_dimension=1, tiled=True),
            lax.psum_scatter(matrix_grads[2], ROW, scatter_dimension=1, tiled=True),
            lax.psum_scatter(matrix_grads[3], ROW, scatter_dimension=0, tiled=True),
            lax.psum_scatter(matrix_grads[4], ROW, scatter_dimension=0, tiled=True),
            lax.psum_scatter(matrix_grads[5], ROW, scatter_dimension=1, tiled=True),
        )
        vector_part = (
            lax.psum_scatter(vector_grads[0], (ROW, COL), scatter_dimension=0, tiled=True),
            lax.psum_scatter(vector_grads[1], (ROW, COL), scatter_dimension=0, tiled=True),
            lax.psum_scatter(vector_grads[2], (ROW, COL), scatter_dimension=0, tiled=True),
            lax.psum_scatter(vector_grads[3], (ROW, COL), scatter_dimension=0, tiled=True),
            lax.psum_scatter(vector_grads[4], (ROW, COL), scatter_dimension=0, tiled=True),
        )
        matrix_total = add_tuples(matrix_total, tuple(matrix_part))
        vector_total = add_tuples(vector_total, tuple(vector_part))
    input_gradients = lax.dynamic_slice_in_dim(
        jnp.stack(grads_list), sections - 1 - section_index, micro_count, 0
    )
    return (
        layer_outputs[None],
        input_gradients[None],
        matrix_total[0][None],
        matrix_total[1][None],
        matrix_total[2][None],
        matrix_total[3][None],
        matrix_total[4][None],
        matrix_total[5][None],
        vector_total[0][None],
        vector_total[1][None],
        vector_total[2][None],
        vector_total[3][None],
        vector_total[4][None],
        vector_total[4][None],
    )


F32 = jnp.float32
BF16 = jnp.bfloat16
LANES = 128


def swap(value, axis, bit):
    count = lax.axis_size(axis)
    return lax.ppermute(value, axis, [(source, source ^ bit) for source in range(count)])


def sum_over(value, axis):
    bit = 1
    while bit < lax.axis_size(axis):
        value = value + swap(value, axis, bit)
        bit *= 2
    return value


def place(part, axis, index, length):
    shape = list(part.shape)
    shape[axis] = length
    start = index * part.shape[axis]
    return lax.dynamic_update_slice_in_dim(jnp.zeros(shape, part.dtype), part, start, axis)


def take(value, axis, index, size):
    return lax.dynamic_slice_in_dim(value, index * size, size, axis)


def after(value, *others):
    return lax.optimization_barrier((value, *others))[0]


def gather_rows(block):
    half = block.shape[0] // 2
    across = swap(block, SECTION, 1)
    beside = swap(block, COL, 2)
    across, beside = lax.optimization_barrier((across, beside))
    corner = jnp.concatenate([swap(beside[:half], SECTION, 1), swap(across[half:], COL, 2)], axis=0)
    near = jnp.concatenate([block, beside], axis=0)
    far = jnp.concatenate([across, corner], axis=0)
    near_other, far_other = (swap(near, COL, 1), swap(far, COL, 1))
    return jnp.concatenate([near, near_other, far, far_other], axis=0), across


def gather_pieces(shard):
    def send(value, pairs):
        return lax.ppermute(value, ROW, pairs)

    opposite = swap(shard, ROW, 2)
    behind = send(shard, [(0, 1), (1, 2), (2, 3)])
    ahead = send(shard, [(3, 2), (2, 1), (1, 0)])
    last = send(opposite, [(2, 3), (1, 0)])
    return shard, ahead, opposite, behind, last


def in_turn(pieces, row):
    shard, ahead, opposite, behind, last = pieces
    return (shard, jnp.where(row == 3, last, ahead), opposite, jnp.where(row == 0, last, behind))


def pair_sum(keep_ref, came_ref, start, size):
    rows = pl.ds(start, size)
    return keep_ref[rows, :].astype(F32) + came_ref[rows, :].astype(F32)


def first_sum_kernel(keep_ref, came_ref, across_ref, beside_ref):
    block = keep_ref.shape[0] // 4
    half = block // 2
    for ref, starts in (
        (across_ref, (2 * block, 3 * block)),
        (beside_ref, (block + half, 3 * block + half)),
    ):
        for place, start in enumerate(starts):
            ref[place * half : (place + 1) * half, :] = pair_sum(
                keep_ref, came_ref, start, half
            ).astype(BF16)


def second_sum_kernel(keep_ref, came_ref, across_ref, beside_ref, top_ref, low_ref, kept_ref):
    block = keep_ref.shape[0] // 4
    half = block // 2
    kept_ref[:half, :] = pair_sum(keep_ref, came_ref, 0, half) + across_ref[:half, :].astype(F32)
    kept_ref[half:, :] = (
        pair_sum(keep_ref, came_ref, half, half) + beside_ref[:half, :].astype(F32)
    )
    top = pair_sum(keep_ref, came_ref, block, half) + across_ref[half:, :].astype(F32)
    top_ref[...] = top.astype(BF16)
    low = pair_sum(keep_ref, came_ref, 2 * block + half, half) + beside_ref[half:, :].astype(F32)
    low_ref[...] = low.astype(BF16)


def column_call(kernel, width, ins, outs):
    tile = 512

    def spec(shape):
        lead = shape[:-1]
        return pl.BlockSpec(lead + (tile,), lambda i: (0,) * len(lead) + (i,))

    return pl.pallas_call(
        kernel,
        grid=(width // tile,),
        in_specs=[spec(member.shape) for member in ins],
        out_specs=[spec(member.shape) for member in outs],
        out_shape=outs,
        cost_estimate=cost(0, *ins, *outs),
    )(*ins)


def scatter_rows(product):
    sent = product(1)
    came = swap(sent, COL, 1)
    keep = product(0)
    rows, width = keep.shape
    block = rows // 4
    half = block // 2
    whole_block = jax.ShapeDtypeStruct((block, width), BF16)
    half_block = jax.ShapeDtypeStruct((half, width), BF16)
    across, beside = column_call(first_sum_kernel, width, [keep, came], [whole_block, whole_block])
    across = swap(across, SECTION, 1)
    beside = swap(beside, COL, 2)
    top, low, keep = column_call(
        second_sum_kernel,
        width,
        [keep, came, across, beside],
        [half_block, half_block, jax.ShapeDtypeStruct((block, width), F32)],
    )
    arrived = jnp.concatenate([swap(top, COL, 2), swap(low, SECTION, 1)], axis=0)
    return keep + arrived.astype(F32)


def turn(values, cosines, sines):
    lead = values[:, :LANES]
    lane = lax.broadcasted_iota(jnp.int32, lead.shape, 1)
    ahead = pltpu.roll(lead, LANES - ROT // 2, 1)
    behind = pltpu.roll(lead, ROT // 2, 1)
    lead = lead * cosines + jnp.where(lane < ROT // 2, ahead, behind) * sines
    return jnp.concatenate([lead, values[:, LANES:]], axis=1)


def mm(first_operand, second_operand):
    return jnp.dot(first_operand, second_operand, preferred_element_type=F32)


def project_kernel(x_ref, wq_ref, wk_ref, wv_ref, e_ref, cos_ref, sin_ref, q_ref, k_ref, v_ref):
    x, cosines, sines = (x_ref[...], cos_ref[...], sin_ref[...])
    queries = mm(x, wq_ref[...]) + e_ref[:, :HD]
    q_ref[...] = (turn(queries, cosines, sines) * HD ** (-0.5)).astype(BF16)
    keys_here = mm(x, wk_ref[...]) + e_ref[:, HD : 2 * HD]
    k_ref[...] = turn(keys_here, cosines, sines).astype(BF16)
    v_ref[...] = (mm(x, wv_ref[...]) + e_ref[:, 2 * HD :]).astype(BF16)


def inner_kernel(x_ref, w_ref, e_ref, held_ref, act_ref, slope_ref):
    inner = mm(x_ref[...], w_ref[...]) + e_ref[...]
    below = 0.5 + 0.5 * lax.erf(inner * 0.7071067811865476)
    act_ref[...] = (inner * below).astype(BF16)
    density = jnp.exp(-0.5 * inner * inner) * 0.3989422804014327
    slope_ref[...] = (below + inner * density).astype(BF16)


def piece_columns(row_ref, w_refs):
    width = w_refs[0].shape[1]
    for step, w_ref in enumerate(w_refs):
        place = lax.rem(row_ref[0] + step, len(w_refs))
        yield w_ref, pl.ds(pl.multiple_of(place * width, width), width)


def outer_kernel(row_ref, act_ref, w0_ref, w1_ref, w2_ref, w3_ref, out_ref):
    act = act_ref[...]
    for w_ref, columns in piece_columns(row_ref, (w0_ref, w1_ref, w2_ref, w3_ref)):
        out_ref[:, columns] = mm(act, w_ref[...]).astype(BF16)


def outer_back_kernel(
    row_ref, dy_ref, w0_ref, w1_ref, w2_ref, w3_ref, slope_ref, dz_ref, do_ref, sum_ref, dy_sum_ref
):
    inner = slope_ref.shape[1]
    total = None
    for w_ref, columns in piece_columns(row_ref, (w0_ref, w1_ref, w2_ref, w3_ref)):
        part = contract_cols(dy_ref[:, columns], w_ref[...])
        total = part if total is None else total + part
    dy = dy_ref[...]
    dz = (total[:, :inner] * slope_ref[...].astype(F32)).astype(BF16)
    dz_ref[...] = dz
    do_ref[...] = total[:, inner:].astype(BF16)

    @pl.when(pl.program_id(0) == 0)
    def _():
        sum_ref[...] = jnp.zeros_like(sum_ref)
        dy_sum_ref[...] = jnp.zeros_like(dy_sum_ref)

    sum_ref[...] += jnp.sum(dz.astype(F32), axis=0, keepdims=True)
    dy_sum_ref[...] += jnp.sum(dy.astype(F32), axis=0, keepdims=True)


def inward_kernel(dz_ref, wf_ref, wq_ref, wk_ref, wv_ref, out_ref):
    start = wf_ref.shape[1]
    total = contract_cols(dz_ref[:, :start], wf_ref[...])
    for w_ref in (wq_ref, wk_ref, wv_ref):
        total += contract_cols(dz_ref[:, start : start + HD], w_ref[...])
        start += HD
    out_ref[...] = total.astype(BF16)


def attend_kernel(q_ref, k_ref, v_ref, row_ref, col_ref, out_ref, log_ref):
    scores = contract_cols(q_ref[...], k_ref[...])
    scores = jnp.where(row_ref[...] >= col_ref[...], scores, -1e30)
    peak = jnp.max(scores, axis=1, keepdims=True)
    exponents = jnp.exp(scores - peak)
    total = jnp.sum(exponents, axis=1, keepdims=True)
    out_ref[...] = mm((exponents / total).astype(BF16), v_ref[...]).astype(BF16)
    log_ref[...] = peak + jnp.log(total)


def attend_back_kernel(
    q_ref, k_ref, v_ref, row_ref, col_ref, log_ref, do_ref, cos_ref, sin_ref, held_ref,
    all_ref, sum_ref, out_ref, dk_ref, dv_ref, sem,
):
    step = pl.program_id(1)
    block = q_ref.shape[0]

    @pl.when(step == 0)
    def _():
        dk_ref[...] = jnp.zeros_like(dk_ref)
        dv_ref[...] = jnp.zeros_like(dv_ref)

    @pl.when((step == 0) & (pl.program_id(0) == 0))
    def _():
        sum_ref[...] = jnp.zeros_like(sum_ref)

    def column_sum(values):
        return jnp.sum(values.astype(F32), axis=0, keepdims=True)

    queries, keys_all, grads = (q_ref[...], k_ref[...], do_ref[...])
    scores = contract_cols(queries, keys_all)
    scores = jnp.where(row_ref[...] >= col_ref[...], scores, -1e30)
    probs = jnp.exp(scores - log_ref[...])
    grad_probs = contract_cols(grads, v_ref[...])
    centre = jnp.sum(probs * grad_probs, axis=1, keepdims=True)
    grad_scores = (probs * (grad_probs - centre)).astype(BF16)
    rows = pl.ds(pl.multiple_of(step * block, block), block)
    cosines, sines = cos_ref[rows, :], sin_ref[rows, :]
    grad_queries = mm(grad_scores, keys_all) * HD ** (-0.5)
    grad_queries = turn(grad_queries, cosines, -sines).astype(BF16)
    out_ref[rows, :HD] = grad_queries
    sum_ref[:, :HD] += column_sum(grad_queries)
    dk_ref[...] += contract_rows(grad_scores, queries)
    dv_ref[...] += contract_rows(probs.astype(BF16), grads)

    @pl.when(step == pl.num_programs(1) - 1)
    def _():
        grad_keys = turn(dk_ref[...], cos_ref[...], -sin_ref[...]).astype(BF16)
        grad_values = dv_ref[...].astype(BF16)
        out_ref[:, HD : 2 * HD] = grad_keys
        out_ref[:, 2 * HD :] = grad_values
        sum_ref[:, HD : 2 * HD] += column_sum(grad_keys)
        sum_ref[:, 2 * HD :] += column_sum(grad_values)
        length, width = out_ref.shape
        micro = pl.ds(pl.multiple_of(pl.program_id(0) * length, length), length)
        copy = pltpu.make_async_copy(
            out_ref, all_ref.at[micro, pl.ds(all_ref.shape[1] - width, width)], sem
        )
        copy.start()
        copy.wait()


ROW_BLOCK = 256


def by_rows(width, block=ROW_BLOCK):
    return pl.BlockSpec((block, width), lambda i: (i, 0))


def whole(shape):
    return pl.BlockSpec(shape, lambda *unused: (0,) * len(shape))


def panel(width, place):
    return lambda deep: pl.BlockSpec((deep, width), lambda *unused: (0, place))


def cost(flops, *arrays):
    return pl.CostEstimate(
        flops=flops,
        transcendentals=0,
        bytes_accessed=sum(math.prod(array.shape) * array.dtype.itemsize for array in arrays),
    )


def heads_panels(array, inner):
    return [panel(HD, inner // HD + part)(array.shape[0]) for part in range(3)]


def project(x, w, inner, e, tables):
    rows, width = x.shape
    per_micro = tables[0].shape[0] // ROW_BLOCK
    table = pl.BlockSpec((ROW_BLOCK, LANES), lambda i: (i % per_micro, 0))
    out = jax.ShapeDtypeStruct((rows, HD), BF16)
    return pl.pallas_call(
        project_kernel,
        grid=(rows // ROW_BLOCK,),
        in_specs=[by_rows(width), *heads_panels(w, inner), whole(e.shape), table, table],
        out_specs=[by_rows(HD)] * 3,
        out_shape=[out] * 3,
        cost_estimate=cost(6 * rows * width * HD, x, out, out, out),
        name="project",
    )(x, w, w, w, e, *tables)


def inner_layer(x, w, e, held):
    rows, width = x.shape
    inner = e.shape[1]
    slope = jax.ShapeDtypeStruct((rows, inner), BF16)
    return pl.pallas_call(
        inner_kernel,
        grid=(rows // ROW_BLOCK,),
        in_specs=[
            by_rows(width),
            panel(inner, 0)(width),
            whole(e.shape),
            pl.BlockSpec(memory_space=pl.ANY),
        ],
        out_specs=[by_rows(inner)] * 2,
        out_shape=[jax.ShapeDtypeStruct(held.shape, BF16), slope],
        input_output_aliases={3: 0},
        cost_estimate=cost(2 * rows * width * inner, x, slope, slope),
        name="inner",
    )(x, w, e, held)


def split_rows(width, other):
    return pl.BlockSpec((ROW_BLOCK, width), lambda i: (i // 2 * 4 + 2 * other + i % 2, 0))


def outer(act, pieces, row, other):
    rows, width = (act.shape[0] // 2, len(pieces) * pieces[0].shape[1])
    out = jax.ShapeDtypeStruct((rows, width), BF16)
    return pl.pallas_call(
        outer_kernel,
        grid=(rows // ROW_BLOCK,),
        in_specs=[
            pl.BlockSpec(memory_space=pltpu.SMEM),
            split_rows(act.shape[1], other),
            *(whole(piece.shape) for piece in pieces),
        ],
        out_specs=by_rows(width),
        out_shape=out,
        cost_estimate=cost(2 * rows * width * act.shape[1], act, out),
        name="outer",
    )(row, act, *pieces)


def inward(dz, w_in, w_qkv, offset, other):
    rows, width = (dz.shape[0] // 2, w_in.shape[0])
    out = jax.ShapeDtypeStruct((rows, width), BF16)
    return pl.pallas_call(
        inward_kernel,
        grid=(rows // ROW_BLOCK,),
        in_specs=[
            split_rows(dz.shape[1], other),
            panel(dz.shape[1] - 3 * HD, 0)(width),
            *heads_panels(w_qkv, offset),
        ],
        out_specs=by_rows(width),
        out_shape=out,
        cost_estimate=cost(2 * rows * width * dz.shape[1], dz, out),
        name="inward",
    )(dz, w_in, w_qkv, w_qkv, w_qkv)


def outer_back(dy, pieces, row, slopes):
    rows, width = dy.shape
    inner = slopes.shape[1]
    dz = jax.ShapeDtypeStruct((rows, inner + 3 * HD), BF16)
    return pl.pallas_call(
        outer_back_kernel,
        grid=(rows // ROW_BLOCK,),
        in_specs=[
            pl.BlockSpec(memory_space=pltpu.SMEM),
            by_rows(width),
            *(whole(piece.shape) for piece in pieces),
            by_rows(inner),
        ],
        out_specs=[by_rows(inner), by_rows(HD), whole((1, inner)), whole((1, width))],
        out_shape=[
            dz,
            jax.ShapeDtypeStruct((rows, HD), BF16),
            jax.ShapeDtypeStruct((1, inner), F32),
            jax.ShapeDtypeStruct((1, width), F32),
        ],
        cost_estimate=cost(2 * rows * width * (inner + HD), dy, slopes, slopes),
        name="outer_back",
    )(row, dy, *pieces, slopes)


def attend(queries, keys_all, values_all, places, inner):
    rows = queries.shape[0]
    length = places.shape[0]
    steps = length // ROW_BLOCK
    row = pl.BlockSpec((ROW_BLOCK, HD), lambda m, i: (m * steps + i, 0))
    every = pl.BlockSpec((length, HD), lambda m, i: (m, 0))
    return pl.pallas_call(
        attend_kernel,
        grid=(rows // length, steps),
        in_specs=[
            row,
            every,
            every,
            pl.BlockSpec((ROW_BLOCK, 1), lambda m, i: (i, 0)),
            pl.BlockSpec((1, length), lambda m, i: (0, 0)),
        ],
        out_specs=[
            pl.BlockSpec((ROW_BLOCK, HD), lambda m, i: (m * steps + i, inner // HD)),
            pl.BlockSpec((ROW_BLOCK, 1), lambda m, i: (m * steps + i, 0)),
        ],
        out_shape=[
            jax.ShapeDtypeStruct((rows, inner + HD), BF16),
            jax.ShapeDtypeStruct((rows, 1), F32),
        ],
        cost_estimate=cost(4 * rows * length * HD, queries, keys_all, values_all, queries),
        name="attend",
    )(queries, keys_all, values_all, places[:, None], places[None, :])


def attend_back(queries, keys_all, values_all, places, log_sums, grads, tables, held):
    rows = queries.shape[0]
    length = places.shape[0]
    steps = length // ROW_BLOCK
    row = pl.BlockSpec((ROW_BLOCK, HD), lambda m, i: (m * steps + i, 0))
    every = pl.BlockSpec((length, HD), lambda m, i: (m, 0))
    anywhere = pl.BlockSpec(memory_space=pl.ANY)
    return pl.pallas_call(
        attend_back_kernel,
        grid=(rows // length, steps),
        in_specs=[
            row,
            every,
            every,
            pl.BlockSpec((ROW_BLOCK, 1), lambda m, i: (i, 0)),
            pl.BlockSpec((1, length), lambda m, i: (0, 0)),
            pl.BlockSpec((ROW_BLOCK, 1), lambda m, i: (m * steps + i, 0)),
            row,
            whole(tables[0].shape),
            whole(tables[1].shape),
            anywhere,
        ],
        out_specs=[anywhere, whole((1, 3 * HD))],
        out_shape=[
            jax.ShapeDtypeStruct(held.shape, BF16),
            jax.ShapeDtypeStruct((1, 3 * HD), F32),
        ],
        scratch_shapes=[
            pltpu.VMEM((length, 3 * HD), BF16),
            pltpu.VMEM((length, HD), F32),
            pltpu.VMEM((length, HD), F32),
            pltpu.SemaphoreType.DMA,
        ],
        input_output_aliases={9: 0},
        cost_estimate=cost(10 * rows * length * HD, queries, keys_all, values_all, grads),
        name="attend_back",
    )(
        queries, keys_all, values_all, places[:, None], places[None, :], log_sums, grads, *tables,
        held,
    )


def local(
    inputs,
    cotangent,
    qkv_weight,
    qkv_bias,
    out_weight,
    fc_in_weight,
    fc_in_bias,
    fc_out_weight,
    norm1_gain,
    norm1_bias,
    norm2_gain,
    norm2_bias,
    out_bias,
    fc_out_bias,
):
    s, r, c = (lax.axis_index(SECTION), lax.axis_index(ROW), lax.axis_index(COL))
    rows_axis, cols_axis = (lax.axis_size(ROW), lax.axis_size(COL))
    low = s == 0
    qkv_w, out_w, fc_in_w, fc_out_w = (
        qkv_weight[0], out_weight[0], fc_in_weight[0], fc_out_weight[0],
    )
    deep, heads_here = qkv_w.shape[0], qkv_w.shape[1]
    per = 3 * HD
    inner = fc_in_w.shape[1] // 2
    model = inputs.shape[2]

    def both_layers(own_first, own_second):
        return (jnp.where(low, own_first, own_second), jnp.where(low, own_second, own_first))

    def trade(value, axis, *others):
        size = value.shape[axis] // 2
        kept = take(value, axis, s, size)
        came = swap(after(take(value, axis, 1 - s, size), *others), SECTION, 1)
        return kept, came

    def gathered(shard, axis):
        return lax.all_gather(shard, ROW, axis=axis, tiled=True)

    held = jnp.stack(
        [
            norm1_gain[0].astype(F32),
            norm1_bias[0].astype(F32),
            norm2_gain[0].astype(F32),
            norm2_bias[0].astype(F32),
            out_bias[0].astype(F32) + fc_out_bias[0].astype(F32),
        ]
    )
    held_both = jnp.stack([held, swap(held, SECTION, 1)])
    qkv_flat = qkv_w.reshape(deep, -1)
    qkv_half = trade(qkv_flat, 1, held_both)
    fc_in_half = trade(fc_in_w, 1, qkv_half[1])
    outs_kept = jnp.concatenate([take(fc_out_w, 0, s, inner), take(out_w, 0, s, HD)], axis=0)
    outs_sent = jnp.concatenate([take(fc_out_w, 0, 1 - s, inner), take(out_w, 0, 1 - s, HD)], axis=0)
    outs_came = swap(after(outs_sent, fc_in_half[1]), SECTION, 1)
    held_both = sum_over(place(held_both, 2, c, deep), COL)
    held = held_both[0]
    gain_one, shift_one, gain_two, shift_two, end_bias = (held[i] for i in range(5))
    gains = both_layers(held, held_both[1])

    def scaled_pair(half, row):
        return tuple(
            (part.astype(F32) * gain[row][:, None]).astype(BF16)
            for part, gain in zip(both_layers(*half), gains)
        )

    qkv_pair = scaled_pair(qkv_half, 0)
    fc_in_pair = scaled_pair(fc_in_half, 2)
    outs_pair = both_layers(outs_kept, outs_came)
    w_qkv0 = gathered(qkv_pair[0], 0)
    w_fc_in0 = gathered(fc_in_pair[0], 0)
    w_ins1 = gathered(jnp.concatenate([fc_in_pair[1], qkv_pair[1]], axis=1), 0)
    w_ins = ((w_fc_in0, w_qkv0, 0), (w_ins1, w_ins1, inner))
    w_outs = [gather_pieces(outs_pair[layer]) for layer in range(2)]
    row = r.astype(jnp.int32)[None]

    own_qkv = mm(shift_one.astype(BF16)[None], qkv_flat)[0]
    own_fc = mm(shift_two.astype(BF16)[None], fc_in_w)[0]
    own_qkv = own_qkv + place(qkv_bias[0].astype(F32), 1, r, per).reshape(-1)
    own_fc = own_fc + place(fc_in_bias[0].astype(F32), 0, r, 2 * inner)
    biases = sum_over(
        jnp.concatenate([own_qkv, own_fc, place(end_bias, 0, r, model)]), ROW
    )
    biases = both_layers(biases, swap(biases, SECTION, 1))
    qkv_e, fc_e, end_e = ([], [], [])
    for member in biases:
        qkv_e.append(take(member[: 2 * per], 0, s, per)[None])
        fc_e.append(take(member[2 * per : 2 * per + 2 * inner], 0, s, inner)[None])
        end_e.append(member[2 * per + 2 * inner :])

    block_rows = inputs.shape[1]
    masks = jnp.array([0, 2, 1, 3], jnp.int32)
    places = ((c ^ masks)[:, None] * block_rows + jnp.arange(block_rows)[None]).reshape(-1)
    inverse = 10000.0 ** (-jnp.arange(0, ROT, 2).astype(F32) / ROT)
    angles = places.astype(F32)[:, None] * inverse[None]
    ones = jnp.ones((places.shape[0], LANES - ROT), F32)
    cosines, sines = (jnp.cos(angles), jnp.sin(angles))
    tables = (
        jnp.concatenate([cosines, cosines, ones], axis=1),
        jnp.concatenate([-sines, sines, 0.0 * ones], axis=1),
    )

    hidden = lax.dynamic_index_in_dim(inputs, s, 0, keepdims=False)
    seed = lax.dynamic_index_in_dim(cotangent, s, 0, keepdims=False)
    hidden = after(hidden, outs_came)

    hidden_list, kept_list, ends = ([], [], [])
    seed_rows = None
    for layer in range(2):
        hidden_list.append(hidden)
        scaled, unused = norm_rows(hidden.astype(F32))
        x, unused = gather_rows(scaled.astype(BF16))
        if layer == 0:
            seed_rows, unused = gather_rows(after(seed, x))
        w_fc_in, w_qkv, offset = w_ins[layer]
        queries, keys_all, values_all = project(x, w_qkv, offset, qkv_e[layer], tables)
        attended, log_sums = attend(queries, keys_all, values_all, places, inner)
        act, slopes = inner_layer(x, w_fc_in, fc_e[layer], attended)
        if layer == 0:
            *pieces, act, unused = lax.optimization_barrier((*w_outs[0][1:], act, seed_rows))
            w_outs[0] = in_turn((w_outs[0][0], *pieces), r)
        kept = (x, queries, keys_all, values_all, log_sums, slopes, act)
        if layer == 1:
            outs_grad1 = contract_rows(act, seed_rows).astype(BF16)
            seed_rows = after(seed_rows, outs_grad1)
            *pieces, unused = lax.optimization_barrier((*w_outs[1][1:], outs_grad1))
            w_outs[1] = in_turn((w_outs[1][0], *pieces), r)
        kept_list.append(kept)
        if layer == 0:
            summed = scatter_rows(lambda other: outer(act, w_outs[0], row, other))
            hidden = (hidden.astype(F32) + summed + end_e[layer]).astype(BF16)
            ends.append(hidden)
            middle = swap(hidden, SECTION, 1)

    def reduced(value, axis):
        return lax.psum_scatter(value, ROW, scatter_dimension=axis, tiled=True)

    outs_part1 = reduced(outs_grad1, 1)
    grads = seed
    ins_list, small_list = ([None, None], [None, None])
    for layer in (1, 0):
        x, queries, keys_all, values_all, log_sums, slopes, act = kept_list[layer]
        w_fc_in, w_qkv, offset = w_ins[layer]
        if layer == 1:
            dy = seed_rows
        else:
            dy, across = gather_rows(grads)
            middle_grads = (jnp.where(low, grads, across), jnp.where(low, across, grads))
        dz, grad_attended, inner_sum, dy_sum = outer_back(dy, w_outs[layer], row, slopes)
        dz, heads_sum = attend_back(
            queries, keys_all, values_all, places, log_sums, grad_attended, tables, dz
        )
        combined = scatter_rows(lambda other: inward(dz, w_fc_in, w_qkv, offset, other))
        ins_grad = contract_rows(x, dz).astype(BF16)
        ins_list[layer] = reduced(ins_grad, 0)
        scaled, inverse_std = norm_rows(hidden_list[layer].astype(F32))
        grad_norm = inverse_std * (
            combined
            - jnp.mean(combined, axis=-1, keepdims=True)
            - scaled * jnp.mean(combined * scaled, axis=-1, keepdims=True)
        )
        grads = (grads.astype(F32) + grad_norm).astype(BF16)
        small_list[layer] = (heads_sum[0], inner_sum[0], dy_sum[0])
        if layer == 0:
            fc_out_part0 = reduced(contract_rows(act[:, :inner], dy).astype(BF16), 1)
            out_part0 = reduced(contract_rows(act[:, inner:], dy).astype(BF16), 1)
    act = kept_list[1][-1]
    summed = scatter_rows(lambda other: outer(act, w_outs[1], row, other))
    summed = after(summed, small_list[0][0])
    ends.append((hidden_list[1].astype(F32) + summed + end_e[1]).astype(BF16))

    def to_owner(first, second, upper, lower):
        return (jnp.where(low, first, lower), jnp.where(low, upper, second))

    def to_first(value):
        return lax.ppermute(value, SECTION, [(1, 0)])

    def to_second(value):
        return lax.ppermute(value, SECTION, [(0, 1)])

    small = sum_over(
        jnp.concatenate(
            [*small_list[0][:2], *small_list[1][:2], small_list[0][2], small_list[1][2]]
        ),
        ROW,
    )
    sums = small[: 2 * (per + inner)]
    sums_other = swap(sums, SECTION, 1)
    smalls = to_owner(*jnp.split(sums, 2), *jnp.split(sums_other, 2))
    end_grad = jnp.where(low, *jnp.split(small[2 * (per + inner) :], 2))
    qkv_b_grad = jnp.concatenate([member[:per] for member in smalls])
    fc_in_b_grad = jnp.concatenate([member[per:] for member in smalls])
    outs_lower = to_second(outs_part1)
    ins_lower = to_second(ins_list[1])
    ins_upper = to_first(ins_list[0])
    ins_g = to_owner(*ins_list, ins_upper, ins_lower)
    qkv_g = jnp.concatenate([member[:, inner:] for member in ins_g], axis=1).astype(F32)
    fc_in_g = jnp.concatenate([member[:, :inner] for member in ins_g], axis=1).astype(F32)
    qkv_w_grad = gain_one[:, None] * qkv_g + shift_one[:, None] * qkv_b_grad[None]
    fc_in_w_grad = gain_two[:, None] * fc_in_g + shift_two[:, None] * fc_in_b_grad[None]
    norm_parts = []
    for layer, (w_q, w_f) in enumerate(zip(both_layers(*qkv_half), both_layers(*fc_in_half))):
        w_q, w_f = (w_q.astype(F32), w_f.astype(F32))
        heads, hidden_sum = jnp.split(sums[layer * (per + inner) :][: per + inner], [per])
        part = ins_list[layer].astype(F32)
        norm_parts.append(
            jnp.stack(
                [
                    jnp.sum(w_q * part[:, inner:], axis=1),
                    jnp.sum(w_q * heads[None], axis=1),
                    jnp.sum(w_f * part[:, :inner], axis=1),
                    jnp.sum(w_f * hidden_sum[None], axis=1),
                ]
            )
        )
    norms = jnp.where(low, *norm_parts) + swap(jnp.where(low, *norm_parts[::-1]), SECTION, 1)
    norms = take(sum_over(norms, COL), 1, c, deep // cols_axis)
    end_grad = take(end_grad, 0, r * cols_axis + c, deep // cols_axis)
    fc_out_upper = to_first(after(fc_out_part0, ins_upper))
    fc_out_w_grad = jnp.concatenate(
        [
            jnp.where(low, fc_out_part0, outs_lower[:inner]),
            jnp.where(low, fc_out_upper, outs_part1[:inner]),
        ],
        axis=0,
    ).astype(F32)[None]
    qkv_w_grad = qkv_w_grad.reshape(qkv_w.shape)[None]
    fc_in_w_grad = fc_in_w_grad[None]
    out_part0, fc_out_w_grad, norms = lax.optimization_barrier(
        (out_part0, fc_out_w_grad, norms)
    )
    out_upper = to_first(out_part0)
    out_w_grad = jnp.concatenate(
        [
            jnp.where(low, out_part0, outs_lower[inner:]),
            jnp.where(low, out_upper, outs_part1[inner:]),
        ],
        axis=0,
    ).astype(F32)
    last = to_second(ends[1])
    layer_outputs = jnp.stack([jnp.where(low, ends[0], last), jnp.where(low, middle, ends[1])])
    first = to_first(grads)
    input_gradients = jnp.stack(
        [jnp.where(low, grads, middle_grads[0]), jnp.where(low, first, middle_grads[1])]
    )
    return (
        layer_outputs[None],
        input_gradients[None],
        qkv_w_grad,
        take(qkv_b_grad.reshape(heads_here, -1), 1, r, per // rows_axis)[None],
        out_w_grad[None],
        fc_in_w_grad,
        take(fc_in_b_grad, 0, r, 2 * inner // rows_axis)[None],
        fc_out_w_grad,
        norms[0][None],
        norms[1][None],
        norms[2][None],
        norms[3][None],
        end_grad[None],
        end_grad[None],
    )


def all_of_it(*arrays):
    return local(*arrays)


def solution(mesh):
    sizes = mesh.shape
    paired = sizes[SECTION] == 2 and sizes[COL] == 4
    body = all_of_it if paired and sizes[ROW] == 4 else relay_local
    step = jax.shard_map(
        body,
        mesh=mesh,
        in_specs=(
            P(None, (ROW, COL), None),
            P(None, (ROW, COL), None),
            P(SECTION, ROW, COL, None),
            P(SECTION, COL, ROW),
            P(SECTION, COL, ROW),
            P(SECTION, ROW, COL),
            P(SECTION, (COL, ROW)),
            P(SECTION, COL, ROW),
            P(SECTION, (ROW, COL)),
            P(SECTION, (ROW, COL)),
            P(SECTION, (ROW, COL)),
            P(SECTION, (ROW, COL)),
            P(SECTION, (ROW, COL)),
            P(SECTION, (ROW, COL)),
        ),
        out_specs=(
            P(SECTION, None, (ROW, COL), None),
            P(SECTION, None, (ROW, COL), None),
            P(SECTION, ROW, COL, None),
            P(SECTION, COL, ROW),
            P(SECTION, COL, ROW),
            P(SECTION, ROW, COL),
            P(SECTION, (COL, ROW)),
            P(SECTION, COL, ROW),
            P(SECTION, (ROW, COL)),
            P(SECTION, (ROW, COL)),
            P(SECTION, (ROW, COL)),
            P(SECTION, (ROW, COL)),
            P(SECTION, (ROW, COL)),
            P(SECTION, (ROW, COL)),
        ),
        check_vma=False,
    )
    if body is relay_local:
        return step
    return step
```

```python
import math

import jax
import jax.numpy as jnp
from jax import lax
from jax.experimental import pallas as pl
from jax.experimental.pallas import tpu as pltpu
from jax.sharding import PartitionSpec as P


SECTION, ROW, COL = ("section", "row", "col")
HD = 256
ROT = 64
SEQ_LEN = 1024


def from_behind(value, axis, steps):
    count = lax.axis_size(axis)
    initial, last = (max(0, -steps), min(count, count - steps))
    return lax.ppermute(value, axis, [(source, source + steps) for source in range(initial, last)])


def rotary_tables(length):
    positions = jnp.arange(length).astype(jnp.float32)
    inverse = 10000.0 ** (-jnp.arange(0, ROT, 2).astype(jnp.float32) / ROT)
    angles = positions[:, None] * inverse[None, :]
    angles = jnp.concatenate([angles, angles], axis=-1)
    return (jnp.cos(angles)[:, None, :], jnp.sin(angles)[:, None, :])


def rotate(values, cosines, sines):
    half_rot = ROT // 2
    turned = values[..., :ROT]
    first_half = turned[..., :half_rot]
    second_half = turned[..., half_rot:]
    swapped = jnp.concatenate([-second_half, first_half], axis=-1)
    return jnp.concatenate([turned * cosines + swapped * sines, values[..., ROT:]], axis=-1)


def rotate_back(grads, cosines, sines):

    def turn_values(values):
        return rotate(values, cosines, sines)

    _, turn_pull = jax.vjp(turn_values, grads)
    return turn_pull(grads)[0]


def gelu_exact(values):
    return jax.nn.gelu(values, approximate=False)


def norm_rows(row_values):
    centred = row_values - jnp.mean(row_values, axis=-1, keepdims=True)
    inverse_std = lax.rsqrt(jnp.mean(centred * centred, axis=-1, keepdims=True) + 1e-05)
    return (centred * inverse_std, inverse_std)


def contract_rows(first_operand, second_operand):
    return lax.dot_general(
        first_operand, second_operand, (((0,), (0,)), ((), ())), preferred_element_type=jnp.float32
    )


def contract_cols(first_operand, second_operand):
    return lax.dot_general(
        first_operand, second_operand, (((1,), (1,)), ((), ())), preferred_element_type=jnp.float32
    )


def causal_block(row_start, block_rows, row_stop):
    query_pos = row_start + lax.broadcasted_iota(jnp.int32, (block_rows, row_stop), 0)
    key_pos = lax.broadcasted_iota(jnp.int32, (block_rows, row_stop), 1)
    return query_pos >= key_pos


def attention_forward(queries, keys_all, values_all):
    length = queries.shape[0]
    block_rows = min(512, length)
    score_scale = HD ** (-0.5)
    outputs_list = []
    sums_list = []
    for block_index in range(length // block_rows):
        row_start = block_index * block_rows
        row_stop = row_start + block_rows
        scores = (
            jnp.einsum(
                "qhd,khd->hqk",
                queries[row_start:row_stop],
                keys_all[:row_stop],
                preferred_element_type=jnp.float32,
            )
            * score_scale
        )
        scores = jnp.where(causal_block(row_start, block_rows, row_stop)[None], scores, -1e30)
        row_peak = jnp.max(scores, axis=-1, keepdims=True)
        exponents = jnp.exp(scores - row_peak)
        row_total = jnp.sum(exponents, axis=-1, keepdims=True)
        attention_probs = (exponents / row_total).astype(jnp.bfloat16)
        outputs_list.append(
            jnp.einsum(
                "hqk,khd->qhd",
                attention_probs,
                values_all[:row_stop],
                preferred_element_type=jnp.float32,
            )
        )
        sums_list.append((row_peak + jnp.log(row_total))[..., 0])
    attended = jnp.concatenate(outputs_list, axis=0).astype(jnp.bfloat16).reshape(length, -1)
    return (attended, jnp.concatenate(sums_list, axis=1))


def attention_backward(queries, keys_all, values_all, log_sums, grad_attended):
    length, heads_here = (queries.shape[0], queries.shape[1])
    block_rows = min(512, length)
    score_scale = HD ** (-0.5)
    grad_out = grad_attended.reshape(length, heads_here, HD)
    grad_queries_list = []
    grad_keys = jnp.zeros(queries.shape, jnp.float32)
    grad_values = jnp.zeros(queries.shape, jnp.float32)
    for block_index in range(length // block_rows):
        row_start = block_index * block_rows
        row_stop = row_start + block_rows
        scores = (
            jnp.einsum(
                "qhd,khd->hqk",
                queries[row_start:row_stop],
                keys_all[:row_stop],
                preferred_element_type=jnp.float32,
            )
            * score_scale
        )
        scores = jnp.where(causal_block(row_start, block_rows, row_stop)[None], scores, -1e30)
        attention_probs = jnp.exp(scores - log_sums[:, row_start:row_stop, None])
        low_probs = attention_probs.astype(jnp.bfloat16)
        grad_probs = jnp.einsum(
            "qhd,khd->hqk",
            grad_out[row_start:row_stop],
            values_all[:row_stop],
            preferred_element_type=jnp.float32,
        )
        centre_term = jnp.sum(attention_probs * grad_probs, axis=-1, keepdims=True)
        grad_scores = (attention_probs * (grad_probs - centre_term)).astype(jnp.bfloat16)
        grad_queries_list.append(
            jnp.einsum(
                "hqk,khd->qhd", grad_scores, keys_all[:row_stop], preferred_element_type=jnp.float32
            )
            * score_scale
        )
        grad_keys = grad_keys.at[:row_stop].add(
            jnp.einsum(
                "hqk,qhd->khd",
                grad_scores,
                queries[row_start:row_stop],
                preferred_element_type=jnp.float32,
            )
            * score_scale
        )
        grad_values = grad_values.at[:row_stop].add(
            jnp.einsum(
                "hqk,qhd->khd",
                low_probs,
                grad_out[row_start:row_stop],
                preferred_element_type=jnp.float32,
            )
        )
    return (jnp.concatenate(grad_queries_list, axis=0), grad_keys, grad_values)


def forward_turn(my_rows, weights, vectors, cosines, sines):
    qkv_w, qkv_b, out_w, fc_in_w, fc_in_b, fc_out_w = weights
    gain_one, bias_one, gain_two, bias_two, out_b, fc_out_b = vectors
    gathered = lax.all_gather(my_rows, COL, axis=0, tiled=True)
    scaled, _ = norm_rows(gathered.astype(jnp.float32))
    normed_one = (scaled * gain_one + bias_one).astype(jnp.bfloat16)
    normed_two = (scaled * gain_two + bias_two).astype(jnp.bfloat16)
    length = gathered.shape[0]
    heads_here = qkv_w.shape[1]
    projected = jnp.dot(
        normed_one, qkv_w.reshape(qkv_w.shape[0], -1), preferred_element_type=jnp.float32
    ) + qkv_b.reshape(-1).astype(jnp.float32)
    projected = projected.reshape(length, heads_here, 3, HD)
    queries = rotate(projected[:, :, 0], cosines, sines).astype(jnp.bfloat16)
    keys_all = rotate(projected[:, :, 1], cosines, sines).astype(jnp.bfloat16)
    values_all = projected[:, :, 2].astype(jnp.bfloat16)
    attended, log_sums = attention_forward(queries, keys_all, values_all)
    inner_act = jnp.dot(normed_two, fc_in_w, preferred_element_type=jnp.float32) + fc_in_b.astype(
        jnp.float32
    )
    activated = gelu_exact(inner_act).astype(jnp.bfloat16)
    summed = lax.psum_scatter(
        jnp.dot(attended, out_w, preferred_element_type=jnp.float32)
        + jnp.dot(activated, fc_out_w, preferred_element_type=jnp.float32),
        COL,
        scatter_dimension=0,
        tiled=True,
    )
    output = (my_rows.astype(jnp.float32) + summed + out_b + fc_out_b).astype(jnp.bfloat16)
    kept_values = (
        gathered,
        normed_one,
        normed_two,
        queries,
        keys_all,
        values_all,
        attended,
        log_sums,
        inner_act,
    )
    return (output, kept_values)


def backward_turn(grad_rows, kept_values, weights, vectors, cosines, sines):
    (
        gathered,
        normed_one,
        normed_two,
        queries,
        keys_all,
        values_all,
        attended,
        log_sums,
        inner_act,
    ) = kept_values
    qkv_w, qkv_b, out_w, fc_in_w, _, fc_out_w = weights
    gain_one, _, gain_two, _, _, _ = vectors
    grad_full = lax.all_gather(grad_rows, COL, axis=0, tiled=True)
    length = grad_full.shape[0]
    rows_here = grad_rows.shape[0]
    own_start = lax.axis_index(COL) * rows_here
    activated = gelu_exact(inner_act).astype(jnp.bfloat16)
    out_w_grad = contract_rows(attended, grad_full)
    fc_out_w_grad = contract_rows(activated, grad_full)
    grad_attended = contract_cols(grad_full, out_w).astype(jnp.bfloat16)
    grad_activated = contract_cols(grad_full, fc_out_w)
    _, gelu_pull = jax.vjp(gelu_exact, inner_act)
    grad_inner = gelu_pull(grad_activated)[0].astype(jnp.bfloat16)
    grad_queries, grad_keys, grad_values = attention_backward(
        queries, keys_all, values_all, log_sums, grad_attended
    )
    grad_q_pre = rotate_back(grad_queries, cosines, sines)
    grad_k_pre = rotate_back(grad_keys, cosines, sines)
    grad_projected = (
        jnp.stack([grad_q_pre, grad_k_pre, grad_values], axis=2)
        .astype(jnp.bfloat16)
        .reshape(length, -1)
    )
    qkv_flat = qkv_w.reshape(qkv_w.shape[0], -1)
    qkv_w_grad = contract_rows(normed_one, grad_projected).reshape(qkv_w.shape)
    qkv_b_grad = jnp.sum(grad_projected.astype(jnp.float32), axis=0).reshape(qkv_b.shape)
    fc_in_w_grad = contract_rows(normed_two, grad_inner)
    fc_in_b_grad = jnp.sum(grad_inner.astype(jnp.float32), axis=0)
    width = qkv_w.shape[0]
    scaled_full, inverse_full = norm_rows(gathered.astype(jnp.float32))
    scaled = lax.dynamic_slice_in_dim(scaled_full, own_start, rows_here, 0)
    inverse_std = lax.dynamic_slice_in_dim(inverse_full, own_start, rows_here, 0)
    dy_sum = jnp.sum(grad_rows.astype(jnp.float32), axis=0)
    both_grads = lax.psum_scatter(
        jnp.concatenate(
            [contract_cols(grad_projected, qkv_flat), contract_cols(grad_inner, fc_in_w)], axis=1
        ),
        COL,
        scatter_dimension=0,
        tiled=True,
    )
    grad_one = both_grads[:, :width]
    grad_two = both_grads[:, width:]
    combined = gain_one * grad_one + gain_two * grad_two
    vector_grads = (
        jnp.sum(grad_one * scaled, axis=0),
        jnp.sum(grad_one, axis=0),
        jnp.sum(grad_two * scaled, axis=0),
        jnp.sum(grad_two, axis=0),
        dy_sum,
    )
    grad_norm = inverse_std * (
        combined
        - jnp.mean(combined, axis=-1, keepdims=True)
        - scaled * jnp.mean(combined * scaled, axis=-1, keepdims=True)
    )
    grad_input = (grad_rows.astype(jnp.float32) + grad_norm).astype(jnp.bfloat16)
    matrix_grads = (qkv_w_grad, qkv_b_grad, out_w_grad, fc_in_w_grad, fc_in_b_grad, fc_out_w_grad)
    return (grad_input, matrix_grads, vector_grads)


def add_tuples(running, addend):
    if running is None:
        return addend
    return tuple((first_part + second_part for first_part, second_part in zip(running, addend)))


def relay_local(
    inputs,
    cotangent,
    qkv_weight,
    qkv_bias,
    out_weight,
    fc_in_weight,
    fc_in_bias,
    fc_out_weight,
    norm1_gain,
    norm1_bias,
    norm2_gain,
    norm2_bias,
    out_bias,
    fc_out_bias,
):
    sections = lax.axis_size(SECTION)
    section_index = lax.axis_index(SECTION)
    micro_count = inputs.shape[0]
    tick_count = micro_count + sections - 1
    is_first = section_index == 0
    is_last = section_index == sections - 1
    cosines, sines = rotary_tables(SEQ_LEN)
    vectors = (
        lax.all_gather(norm1_gain[0], (ROW, COL), axis=0, tiled=True),
        lax.all_gather(norm1_bias[0], (ROW, COL), axis=0, tiled=True),
        lax.all_gather(norm2_gain[0], (ROW, COL), axis=0, tiled=True),
        lax.all_gather(norm2_bias[0], (ROW, COL), axis=0, tiled=True),
        lax.all_gather(out_bias[0], (ROW, COL), axis=0, tiled=True),
        lax.all_gather(fc_out_bias[0], (ROW, COL), axis=0, tiled=True),
    )
    vectors = tuple((member.astype(jnp.float32) for member in vectors))
    received = jnp.zeros_like(inputs[0])
    outputs_list = []
    kept_list = []
    for tick_index in range(tick_count):
        weights = (
            lax.all_gather(qkv_weight[0], ROW, axis=0, tiled=True),
            lax.all_gather(qkv_bias[0], ROW, axis=1, tiled=True),
            lax.all_gather(out_weight[0], ROW, axis=1, tiled=True),
            lax.all_gather(fc_in_weight[0], ROW, axis=0, tiled=True),
            lax.all_gather(fc_in_bias[0], ROW, axis=0, tiled=True),
            lax.all_gather(fc_out_weight[0], ROW, axis=1, tiled=True),
        )
        first_rows = inputs[min(tick_index, micro_count - 1)]
        my_rows = jnp.where(is_first, first_rows, received)
        output, kept_values = forward_turn(my_rows, weights, vectors, cosines, sines)
        outputs_list.append(output)
        kept_list.append(kept_values)
        if tick_index + 1 < tick_count:
            received = from_behind(output, SECTION, 1)
    layer_outputs = lax.dynamic_slice_in_dim(jnp.stack(outputs_list), section_index, micro_count, 0)
    stacked_kept = tuple((jnp.stack(members) for members in zip(*kept_list)))
    received_grad = jnp.zeros_like(inputs[0])
    grads_list = []
    matrix_total = None
    vector_total = None
    for tick_index in range(tick_count):
        weights = (
            lax.all_gather(qkv_weight[0], ROW, axis=0, tiled=True),
            lax.all_gather(qkv_bias[0], ROW, axis=1, tiled=True),
            lax.all_gather(out_weight[0], ROW, axis=1, tiled=True),
            lax.all_gather(fc_in_weight[0], ROW, axis=0, tiled=True),
            lax.all_gather(fc_in_bias[0], ROW, axis=0, tiled=True),
            lax.all_gather(fc_out_weight[0], ROW, axis=1, tiled=True),
        )
        if tick_index < micro_count:
            seed_grad = cotangent[tick_index]
        else:
            seed_grad = jnp.zeros_like(cotangent[0])
        grad_rows = jnp.where(is_last, seed_grad, received_grad)
        forward_index = jnp.clip(tick_index - sections + 1 + 2 * section_index, 0, tick_count - 1)
        kept_values = tuple(
            (
                lax.dynamic_index_in_dim(member, forward_index, 0, keepdims=False)
                for member in stacked_kept
            )
        )
        grad_input, matrix_grads, vector_grads = backward_turn(
            grad_rows, kept_values, weights, vectors, cosines, sines
        )
        grads_list.append(grad_input)
        if tick_index + 1 < tick_count:
            received_grad = from_behind(grad_input, SECTION, -1)
        matrix_part = (
            lax.psum_scatter(matrix_grads[0], ROW, scatter_dimension=0, tiled=True),
            lax.psum_scatter(matrix_grads[1], ROW, scatter_dimension=1, tiled=True),
            lax.psum_scatter(matrix_grads[2], ROW, scatter_dimension=1, tiled=True),
            lax.psum_scatter(matrix_grads[3], ROW, scatter_dimension=0, tiled=True),
            lax.psum_scatter(matrix_grads[4], ROW, scatter_dimension=0, tiled=True),
            lax.psum_scatter(matrix_grads[5], ROW, scatter_dimension=1, tiled=True),
        )
        vector_part = (
            lax.psum_scatter(vector_grads[0], (ROW, COL), scatter_dimension=0, tiled=True),
            lax.psum_scatter(vector_grads[1], (ROW, COL), scatter_dimension=0, tiled=True),
            lax.psum_scatter(vector_grads[2], (ROW, COL), scatter_dimension=0, tiled=True),
            lax.psum_scatter(vector_grads[3], (ROW, COL), scatter_dimension=0, tiled=True),
            lax.psum_scatter(vector_grads[4], (ROW, COL), scatter_dimension=0, tiled=True),
        )
        matrix_total = add_tuples(matrix_total, tuple(matrix_part))
        vector_total = add_tuples(vector_total, tuple(vector_part))
    input_gradients = lax.dynamic_slice_in_dim(
        jnp.stack(grads_list), sections - 1 - section_index, micro_count, 0
    )
    return (
        layer_outputs[None],
        input_gradients[None],
        matrix_total[0][None],
        matrix_total[1][None],
        matrix_total[2][None],
        matrix_total[3][None],
        matrix_total[4][None],
        matrix_total[5][None],
        vector_total[0][None],
        vector_total[1][None],
        vector_total[2][None],
        vector_total[3][None],
        vector_total[4][None],
        vector_total[4][None],
    )


F32 = jnp.float32
BF16 = jnp.bfloat16
LANES = 128


def swap(value, axis, bit):
    count = lax.axis_size(axis)
    return lax.ppermute(value, axis, [(source, source ^ bit) for source in range(count)])


def sum_over(value, axis):
    bit = 1
    while bit < lax.axis_size(axis):
        value = value + swap(value, axis, bit)
        bit *= 2
    return value


def place(part, axis, index, length):
    shape = list(part.shape)
    shape[axis] = length
    start = index * part.shape[axis]
    return lax.dynamic_update_slice_in_dim(jnp.zeros(shape, part.dtype), part, start, axis)


def take(value, axis, index, size):
    return lax.dynamic_slice_in_dim(value, index * size, size, axis)


def after(value, *others):
    return lax.optimization_barrier((value, *others))[0]


def gather_rows(block):
    half = block.shape[0] // 2
    across = swap(block, SECTION, 1)
    beside = swap(block, COL, 2)
    across, beside = lax.optimization_barrier((across, beside))
    corner = jnp.concatenate([swap(beside[:half], SECTION, 1), swap(across[half:], COL, 2)], axis=0)
    near = jnp.concatenate([block, beside], axis=0)
    far = jnp.concatenate([across, corner], axis=0)
    near_other, far_other = (swap(near, COL, 1), swap(far, COL, 1))
    return jnp.concatenate([near, near_other, far, far_other], axis=0), across


def gather_pieces(shard):
    def send(value, pairs):
        return lax.ppermute(value, ROW, pairs)

    opposite = swap(shard, ROW, 2)
    behind = send(shard, [(0, 1), (1, 2), (2, 3)])
    ahead = send(shard, [(3, 2), (2, 1), (1, 0)])
    last = send(opposite, [(2, 3), (1, 0)])
    return shard, ahead, opposite, behind, last


def in_turn(pieces, row):
    shard, ahead, opposite, behind, last = pieces
    return (shard, jnp.where(row == 3, last, ahead), opposite, jnp.where(row == 0, last, behind))


def pair_sum(keep_ref, came_ref, start, size):
    rows = pl.ds(start, size)
    return keep_ref[rows, :].astype(F32) + came_ref[rows, :].astype(F32)


def first_sum_kernel(keep_ref, came_ref, across_ref, beside_ref):
    block = keep_ref.shape[0] // 4
    half = block // 2
    for ref, starts in (
        (across_ref, (2 * block, 3 * block)),
        (beside_ref, (block + half, 3 * block + half)),
    ):
        for place, start in enumerate(starts):
            ref[place * half : (place + 1) * half, :] = pair_sum(
                keep_ref, came_ref, start, half
            ).astype(BF16)


def second_sum_kernel(keep_ref, came_ref, across_ref, beside_ref, top_ref, low_ref, kept_ref):
    block = keep_ref.shape[0] // 4
    half = block // 2
    kept_ref[:half, :] = pair_sum(keep_ref, came_ref, 0, half) + across_ref[:half, :].astype(F32)
    kept_ref[half:, :] = (
        pair_sum(keep_ref, came_ref, half, half) + beside_ref[:half, :].astype(F32)
    )
    top = pair_sum(keep_ref, came_ref, block, half) + across_ref[half:, :].astype(F32)
    top_ref[...] = top.astype(BF16)
    low = pair_sum(keep_ref, came_ref, 2 * block + half, half) + beside_ref[half:, :].astype(F32)
    low_ref[...] = low.astype(BF16)


def column_call(kernel, width, ins, outs):
    tile = 512

    def spec(shape):
        lead = shape[:-1]
        return pl.BlockSpec(lead + (tile,), lambda i: (0,) * len(lead) + (i,))

    return pl.pallas_call(
        kernel,
        grid=(width // tile,),
        in_specs=[spec(member.shape) for member in ins],
        out_specs=[spec(member.shape) for member in outs],
        out_shape=outs,
        cost_estimate=cost(0, *ins, *outs),
    )(*ins)


def scatter_rows(product):
    sent = product(1)
    came = swap(sent, COL, 1)
    keep = product(0)
    rows, width = keep.shape
    block = rows // 4
    half = block // 2
    whole_block = jax.ShapeDtypeStruct((block, width), BF16)
    half_block = jax.ShapeDtypeStruct((half, width), BF16)
    across, beside = column_call(first_sum_kernel, width, [keep, came], [whole_block, whole_block])
    across = swap(across, SECTION, 1)
    beside = swap(beside, COL, 2)
    top, low, keep = column_call(
        second_sum_kernel,
        width,
        [keep, came, across, beside],
        [half_block, half_block, jax.ShapeDtypeStruct((block, width), F32)],
    )
    arrived = jnp.concatenate([swap(top, COL, 2), swap(low, SECTION, 1)], axis=0)
    return keep + arrived.astype(F32)


def turn(values, cosines, sines):
    lead = values[:, :LANES]
    lane = lax.broadcasted_iota(jnp.int32, lead.shape, 1)
    ahead = pltpu.roll(lead, LANES - ROT // 2, 1)
    behind = pltpu.roll(lead, ROT // 2, 1)
    lead = lead * cosines + jnp.where(lane < ROT // 2, ahead, behind) * sines
    return jnp.concatenate([lead, values[:, LANES:]], axis=1)


def mm(first_operand, second_operand):
    return jnp.dot(first_operand, second_operand, preferred_element_type=F32)


def project_kernel(x_ref, wq_ref, wk_ref, wv_ref, e_ref, cos_ref, sin_ref, q_ref, k_ref, v_ref):
    x, cosines, sines = (x_ref[...], cos_ref[...], sin_ref[...])
    queries = mm(x, wq_ref[...]) + e_ref[:, :HD]
    q_ref[...] = (turn(queries, cosines, sines) * HD ** (-0.5)).astype(BF16)
    keys_here = mm(x, wk_ref[...]) + e_ref[:, HD : 2 * HD]
    k_ref[...] = turn(keys_here, cosines, sines).astype(BF16)
    v_ref[...] = (mm(x, wv_ref[...]) + e_ref[:, 2 * HD :]).astype(BF16)


def inner_kernel(x_ref, w_ref, e_ref, held_ref, act_ref, slope_ref):
    inner = mm(x_ref[...], w_ref[...]) + e_ref[...]
    below = 0.5 + 0.5 * lax.erf(inner * 0.7071067811865476)
    act_ref[...] = (inner * below).astype(BF16)
    density = jnp.exp(-0.5 * inner * inner) * 0.3989422804014327
    slope_ref[...] = (below + inner * density).astype(BF16)


def piece_columns(row_ref, w_refs):
    width = w_refs[0].shape[1]
    for step, w_ref in enumerate(w_refs):
        place = lax.rem(row_ref[0] + step, len(w_refs))
        yield w_ref, pl.ds(pl.multiple_of(place * width, width), width)


def outer_kernel(row_ref, act_ref, w0_ref, w1_ref, w2_ref, w3_ref, out_ref):
    act = act_ref[...]
    for w_ref, columns in piece_columns(row_ref, (w0_ref, w1_ref, w2_ref, w3_ref)):
        out_ref[:, columns] = mm(act, w_ref[...]).astype(BF16)


def outer_back_kernel(
    row_ref, dy_ref, w0_ref, w1_ref, w2_ref, w3_ref, slope_ref, dz_ref, do_ref, sum_ref, dy_sum_ref
):
    inner = slope_ref.shape[1]
    total = None
    for w_ref, columns in piece_columns(row_ref, (w0_ref, w1_ref, w2_ref, w3_ref)):
        part = contract_cols(dy_ref[:, columns], w_ref[...])
        total = part if total is None else total + part
    dy = dy_ref[...]
    dz = (total[:, :inner] * slope_ref[...].astype(F32)).astype(BF16)
    dz_ref[...] = dz
    do_ref[...] = total[:, inner:].astype(BF16)

    @pl.when(pl.program_id(0) == 0)
    def _():
        sum_ref[...] = jnp.zeros_like(sum_ref)
        dy_sum_ref[...] = jnp.zeros_like(dy_sum_ref)

    sum_ref[...] += jnp.sum(dz.astype(F32), axis=0, keepdims=True)
    dy_sum_ref[...] += jnp.sum(dy.astype(F32), axis=0, keepdims=True)


def inward_kernel(dz_ref, wf_ref, wq_ref, wk_ref, wv_ref, out_ref):
    start = wf_ref.shape[1]
    total = contract_cols(dz_ref[:, :start], wf_ref[...])
    for w_ref in (wq_ref, wk_ref, wv_ref):
        total += contract_cols(dz_ref[:, start : start + HD], w_ref[...])
        start += HD
    out_ref[...] = total.astype(BF16)


def attend_kernel(q_ref, k_ref, v_ref, row_ref, col_ref, out_ref, log_ref):
    scores = contract_cols(q_ref[...], k_ref[...])
    scores = jnp.where(row_ref[...] >= col_ref[...], scores, -1e30)
    peak = jnp.max(scores, axis=1, keepdims=True)
    exponents = jnp.exp(scores - peak)
    total = jnp.sum(exponents, axis=1, keepdims=True)
    out_ref[...] = mm((exponents / total).astype(BF16), v_ref[...]).astype(BF16)
    log_ref[...] = peak + jnp.log(total)


def attend_back_kernel(
    q_ref, k_ref, v_ref, row_ref, col_ref, log_ref, do_ref, cos_ref, sin_ref, held_ref,
    all_ref, sum_ref, out_ref, dk_ref, dv_ref, sem,
):
    step = pl.program_id(1)
    block = q_ref.shape[0]

    @pl.when(step == 0)
    def _():
        dk_ref[...] = jnp.zeros_like(dk_ref)
        dv_ref[...] = jnp.zeros_like(dv_ref)

    @pl.when((step == 0) & (pl.program_id(0) == 0))
    def _():
        sum_ref[...] = jnp.zeros_like(sum_ref)

    def column_sum(values):
        return jnp.sum(values.astype(F32), axis=0, keepdims=True)

    queries, keys_all, grads = (q_ref[...], k_ref[...], do_ref[...])
    scores = contract_cols(queries, keys_all)
    scores = jnp.where(row_ref[...] >= col_ref[...], scores, -1e30)
    probs = jnp.exp(scores - log_ref[...])
    grad_probs = contract_cols(grads, v_ref[...])
    centre = jnp.sum(probs * grad_probs, axis=1, keepdims=True)
    grad_scores = (probs * (grad_probs - centre)).astype(BF16)
    rows = pl.ds(pl.multiple_of(step * block, block), block)
    cosines, sines = cos_ref[rows, :], sin_ref[rows, :]
    grad_queries = mm(grad_scores, keys_all) * HD ** (-0.5)
    grad_queries = turn(grad_queries, cosines, -sines).astype(BF16)
    out_ref[rows, :HD] = grad_queries
    sum_ref[:, :HD] += column_sum(grad_queries)
    dk_ref[...] += contract_rows(grad_scores, queries)
    dv_ref[...] += contract_rows(probs.astype(BF16), grads)

    @pl.when(step == pl.num_programs(1) - 1)
    def _():
        grad_keys = turn(dk_ref[...], cos_ref[...], -sin_ref[...]).astype(BF16)
        grad_values = dv_ref[...].astype(BF16)
        out_ref[:, HD : 2 * HD] = grad_keys
        out_ref[:, 2 * HD :] = grad_values
        sum_ref[:, HD : 2 * HD] += column_sum(grad_keys)
        sum_ref[:, 2 * HD :] += column_sum(grad_values)
        length, width = out_ref.shape
        micro = pl.ds(pl.multiple_of(pl.program_id(0) * length, length), length)
        copy = pltpu.make_async_copy(
            out_ref, all_ref.at[micro, pl.ds(all_ref.shape[1] - width, width)], sem
        )
        copy.start()
        copy.wait()


ROW_BLOCK = 256


def by_rows(width, block=ROW_BLOCK):
    return pl.BlockSpec((block, width), lambda i: (i, 0))


def whole(shape):
    return pl.BlockSpec(shape, lambda *unused: (0,) * len(shape))


def panel(width, place):
    return lambda deep: pl.BlockSpec((deep, width), lambda *unused: (0, place))


def cost(flops, *arrays):
    return pl.CostEstimate(
        flops=flops,
        transcendentals=0,
        bytes_accessed=sum(math.prod(array.shape) * array.dtype.itemsize for array in arrays),
    )


def heads_panels(array, inner):
    return [panel(HD, inner // HD + part)(array.shape[0]) for part in range(3)]


def project(x, w, inner, e, tables):
    rows, width = x.shape
    per_micro = tables[0].shape[0] // ROW_BLOCK
    table = pl.BlockSpec((ROW_BLOCK, LANES), lambda i: (i % per_micro, 0))
    out = jax.ShapeDtypeStruct((rows, HD), BF16)
    return pl.pallas_call(
        project_kernel,
        grid=(rows // ROW_BLOCK,),
        in_specs=[by_rows(width), *heads_panels(w, inner), whole(e.shape), table, table],
        out_specs=[by_rows(HD)] * 3,
        out_shape=[out] * 3,
        cost_estimate=cost(6 * rows * width * HD, x, out, out, out),
        name="project",
    )(x, w, w, w, e, *tables)


def inner_layer(x, w, e, held):
    rows, width = x.shape
    inner = e.shape[1]
    slope = jax.ShapeDtypeStruct((rows, inner), BF16)
    return pl.pallas_call(
        inner_kernel,
        grid=(rows // ROW_BLOCK,),
        in_specs=[
            by_rows(width),
            panel(inner, 0)(width),
            whole(e.shape),
            pl.BlockSpec(memory_space=pl.ANY),
        ],
        out_specs=[by_rows(inner)] * 2,
        out_shape=[jax.ShapeDtypeStruct(held.shape, BF16), slope],
        input_output_aliases={3: 0},
        cost_estimate=cost(2 * rows * width * inner, x, slope, slope),
        name="inner",
    )(x, w, e, held)


def split_rows(width, other):
    return pl.BlockSpec((ROW_BLOCK, width), lambda i: (i // 2 * 4 + 2 * other + i % 2, 0))


def outer(act, pieces, row, other):
    rows, width = (act.shape[0] // 2, len(pieces) * pieces[0].shape[1])
    out = jax.ShapeDtypeStruct((rows, width), BF16)
    return pl.pallas_call(
        outer_kernel,
        grid=(rows // ROW_BLOCK,),
        in_specs=[
            pl.BlockSpec(memory_space=pltpu.SMEM),
            split_rows(act.shape[1], other),
            *(whole(piece.shape) for piece in pieces),
        ],
        out_specs=by_rows(width),
        out_shape=out,
        cost_estimate=cost(2 * rows * width * act.shape[1], act, out),
        name="outer",
    )(row, act, *pieces)


def inward(dz, w_in, w_qkv, offset, other):
    rows, width = (dz.shape[0] // 2, w_in.shape[0])
    out = jax.ShapeDtypeStruct((rows, width), BF16)
    return pl.pallas_call(
        inward_kernel,
        grid=(rows // ROW_BLOCK,),
        in_specs=[
            split_rows(dz.shape[1], other),
            panel(dz.shape[1] - 3 * HD, 0)(width),
            *heads_panels(w_qkv, offset),
        ],
        out_specs=by_rows(width),
        out_shape=out,
        cost_estimate=cost(2 * rows * width * dz.shape[1], dz, out),
        name="inward",
    )(dz, w_in, w_qkv, w_qkv, w_qkv)


def outer_back(dy, pieces, row, slopes):
    rows, width = dy.shape
    inner = slopes.shape[1]
    dz = jax.ShapeDtypeStruct((rows, inner + 3 * HD), BF16)
    return pl.pallas_call(
        outer_back_kernel,
        grid=(rows // ROW_BLOCK,),
        in_specs=[
            pl.BlockSpec(memory_space=pltpu.SMEM),
            by_rows(width),
            *(whole(piece.shape) for piece in pieces),
            by_rows(inner),
        ],
        out_specs=[by_rows(inner), by_rows(HD), whole((1, inner)), whole((1, width))],
        out_shape=[
            dz,
            jax.ShapeDtypeStruct((rows, HD), BF16),
            jax.ShapeDtypeStruct((1, inner), F32),
            jax.ShapeDtypeStruct((1, width), F32),
        ],
        cost_estimate=cost(2 * rows * width * (inner + HD), dy, slopes, slopes),
        name="outer_back",
    )(row, dy, *pieces, slopes)


def attend(queries, keys_all, values_all, places, inner):
    rows = queries.shape[0]
    length = places.shape[0]
    steps = length // ROW_BLOCK
    row = pl.BlockSpec((ROW_BLOCK, HD), lambda m, i: (m * steps + i, 0))
    every = pl.BlockSpec((length, HD), lambda m, i: (m, 0))
    return pl.pallas_call(
        attend_kernel,
        grid=(rows // length, steps),
        in_specs=[
            row,
            every,
            every,
            pl.BlockSpec((ROW_BLOCK, 1), lambda m, i: (i, 0)),
            pl.BlockSpec((1, length), lambda m, i: (0, 0)),
        ],
        out_specs=[
            pl.BlockSpec((ROW_BLOCK, HD), lambda m, i: (m * steps + i, inner // HD)),
            pl.BlockSpec((ROW_BLOCK, 1), lambda m, i: (m * steps + i, 0)),
        ],
        out_shape=[
            jax.ShapeDtypeStruct((rows, inner + HD), BF16),
            jax.ShapeDtypeStruct((rows, 1), F32),
        ],
        cost_estimate=cost(4 * rows * length * HD, queries, keys_all, values_all, queries),
        name="attend",
    )(queries, keys_all, values_all, places[:, None], places[None, :])


def attend_back(queries, keys_all, values_all, places, log_sums, grads, tables, held):
    rows = queries.shape[0]
    length = places.shape[0]
    steps = length // ROW_BLOCK
    row = pl.BlockSpec((ROW_BLOCK, HD), lambda m, i: (m * steps + i, 0))
    every = pl.BlockSpec((length, HD), lambda m, i: (m, 0))
    anywhere = pl.BlockSpec(memory_space=pl.ANY)
    return pl.pallas_call(
        attend_back_kernel,
        grid=(rows // length, steps),
        in_specs=[
            row,
            every,
            every,
            pl.BlockSpec((ROW_BLOCK, 1), lambda m, i: (i, 0)),
            pl.BlockSpec((1, length), lambda m, i: (0, 0)),
            pl.BlockSpec((ROW_BLOCK, 1), lambda m, i: (m * steps + i, 0)),
            row,
            whole(tables[0].shape),
            whole(tables[1].shape),
            anywhere,
        ],
        out_specs=[anywhere, whole((1, 3 * HD))],
        out_shape=[
            jax.ShapeDtypeStruct(held.shape, BF16),
            jax.ShapeDtypeStruct((1, 3 * HD), F32),
        ],
        scratch_shapes=[
            pltpu.VMEM((length, 3 * HD), BF16),
            pltpu.VMEM((length, HD), F32),
            pltpu.VMEM((length, HD), F32),
            pltpu.SemaphoreType.DMA,
        ],
        input_output_aliases={9: 0},
        cost_estimate=cost(10 * rows * length * HD, queries, keys_all, values_all, grads),
        name="attend_back",
    )(
        queries, keys_all, values_all, places[:, None], places[None, :], log_sums, grads, *tables,
        held,
    )


def local(
    inputs,
    cotangent,
    qkv_weight,
    qkv_bias,
    out_weight,
    fc_in_weight,
    fc_in_bias,
    fc_out_weight,
    norm1_gain,
    norm1_bias,
    norm2_gain,
    norm2_bias,
    out_bias,
    fc_out_bias,
):
    s, r, c = (lax.axis_index(SECTION), lax.axis_index(ROW), lax.axis_index(COL))
    rows_axis, cols_axis = (lax.axis_size(ROW), lax.axis_size(COL))
    low = s == 0
    qkv_w, out_w, fc_in_w, fc_out_w = (
        qkv_weight[0], out_weight[0], fc_in_weight[0], fc_out_weight[0],
    )
    deep, heads_here = qkv_w.shape[0], qkv_w.shape[1]
    per = 3 * HD
    inner = fc_in_w.shape[1] // 2
    model = inputs.shape[2]

    def both_layers(own_first, own_second):
        return (jnp.where(low, own_first, own_second), jnp.where(low, own_second, own_first))

    def trade(value, axis, *others):
        size = value.shape[axis] // 2
        kept = take(value, axis, s, size)
        came = swap(after(take(value, axis, 1 - s, size), *others), SECTION, 1)
        return kept, came

    def gathered(shard, axis):
        return lax.all_gather(shard, ROW, axis=axis, tiled=True)

    held = jnp.stack(
        [
            norm1_gain[0].astype(F32),
            norm1_bias[0].astype(F32),
            norm2_gain[0].astype(F32),
            norm2_bias[0].astype(F32),
            out_bias[0].astype(F32) + fc_out_bias[0].astype(F32),
        ]
    )
    held_both = jnp.stack([held, swap(held, SECTION, 1)])
    qkv_flat = qkv_w.reshape(deep, -1)
    qkv_half = trade(qkv_flat, 1, held_both)
    fc_in_half = trade(fc_in_w, 1, qkv_half[1])
    outs_kept = jnp.concatenate([take(fc_out_w, 0, s, inner), take(out_w, 0, s, HD)], axis=0)
    outs_sent = jnp.concatenate([take(fc_out_w, 0, 1 - s, inner), take(out_w, 0, 1 - s, HD)], axis=0)
    outs_came = swap(after(outs_sent, fc_in_half[1]), SECTION, 1)
    held_both = sum_over(place(held_both, 2, c, deep), COL)
    held = held_both[0]
    gain_one, shift_one, gain_two, shift_two, end_bias = (held[i] for i in range(5))
    gains = both_layers(held, held_both[1])

    def scaled_pair(half, row):
        return tuple(
            (part.astype(F32) * gain[row][:, None]).astype(BF16)
            for part, gain in zip(both_layers(*half), gains)
        )

    qkv_pair = scaled_pair(qkv_half, 0)
    fc_in_pair = scaled_pair(fc_in_half, 2)
    outs_pair = both_layers(outs_kept, outs_came)
    w_qkv0 = gathered(qkv_pair[0], 0)
    w_fc_in0 = gathered(fc_in_pair[0], 0)
    w_ins1 = gathered(jnp.concatenate([fc_in_pair[1], qkv_pair[1]], axis=1), 0)
    w_ins = ((w_fc_in0, w_qkv0, 0), (w_ins1, w_ins1, inner))
    w_outs = [gather_pieces(outs_pair[layer]) for layer in range(2)]
    row = r.astype(jnp.int32)[None]

    own_qkv = mm(shift_one.astype(BF16)[None], qkv_flat)[0]
    own_fc = mm(shift_two.astype(BF16)[None], fc_in_w)[0]
    own_qkv = own_qkv + place(qkv_bias[0].astype(F32), 1, r, per).reshape(-1)
    own_fc = own_fc + place(fc_in_bias[0].astype(F32), 0, r, 2 * inner)
    biases = sum_over(
        jnp.concatenate([own_qkv, own_fc, place(end_bias, 0, r, model)]), ROW
    )
    biases = both_layers(biases, swap(biases, SECTION, 1))
    qkv_e, fc_e, end_e = ([], [], [])
    for member in biases:
        qkv_e.append(take(member[: 2 * per], 0, s, per)[None])
        fc_e.append(take(member[2 * per : 2 * per + 2 * inner], 0, s, inner)[None])
        end_e.append(member[2 * per + 2 * inner :])

    block_rows = inputs.shape[1]
    masks = jnp.array([0, 2, 1, 3], jnp.int32)
    places = ((c ^ masks)[:, None] * block_rows + jnp.arange(block_rows)[None]).reshape(-1)
    inverse = 10000.0 ** (-jnp.arange(0, ROT, 2).astype(F32) / ROT)
    angles = places.astype(F32)[:, None] * inverse[None]
    ones = jnp.ones((places.shape[0], LANES - ROT), F32)
    cosines, sines = (jnp.cos(angles), jnp.sin(angles))
    tables = (
        jnp.concatenate([cosines, cosines, ones], axis=1),
        jnp.concatenate([-sines, sines, 0.0 * ones], axis=1),
    )

    hidden = lax.dynamic_index_in_dim(inputs, s, 0, keepdims=False)
    seed = lax.dynamic_index_in_dim(cotangent, s, 0, keepdims=False)
    hidden = after(hidden, outs_came)

    hidden_list, kept_list, ends = ([], [], [])
    seed_rows = None
    for layer in range(2):
        hidden_list.append(hidden)
        scaled, unused = norm_rows(hidden.astype(F32))
        x, unused = gather_rows(scaled.astype(BF16))
        if layer == 0:
            seed_rows, unused = gather_rows(after(seed, x))
        w_fc_in, w_qkv, offset = w_ins[layer]
        queries, keys_all, values_all = project(x, w_qkv, offset, qkv_e[layer], tables)
        attended, log_sums = attend(queries, keys_all, values_all, places, inner)
        act, slopes = inner_layer(x, w_fc_in, fc_e[layer], attended)
        if layer == 0:
            *pieces, act, unused = lax.optimization_barrier((*w_outs[0][1:], act, seed_rows))
            w_outs[0] = in_turn((w_outs[0][0], *pieces), r)
        kept = (x, queries, keys_all, values_all, log_sums, slopes, act)
        if layer == 1:
            outs_grad1 = contract_rows(act, seed_rows).astype(BF16)
            seed_rows = after(seed_rows, outs_grad1)
            *pieces, unused = lax.optimization_barrier((*w_outs[1][1:], outs_grad1))
            w_outs[1] = in_turn((w_outs[1][0], *pieces), r)
        kept_list.append(kept)
        if layer == 0:
            summed = scatter_rows(lambda other: outer(act, w_outs[0], row, other))
            hidden = (hidden.astype(F32) + summed + end_e[layer]).astype(BF16)
            ends.append(hidden)
            middle = swap(hidden, SECTION, 1)

    def reduced(value, axis):
        return lax.psum_scatter(value, ROW, scatter_dimension=axis, tiled=True)

    outs_part1 = reduced(outs_grad1, 1)
    grads = seed
    ins_list, small_list = ([None, None], [None, None])
    for layer in (1, 0):
        x, queries, keys_all, values_all, log_sums, slopes, act = kept_list[layer]
        w_fc_in, w_qkv, offset = w_ins[layer]
        if layer == 1:
            dy = seed_rows
        else:
            dy, across = gather_rows(grads)
            middle_grads = (jnp.where(low, grads, across), jnp.where(low, across, grads))
        dz, grad_attended, inner_sum, dy_sum = outer_back(dy, w_outs[layer], row, slopes)
        dz, heads_sum = attend_back(
            queries, keys_all, values_all, places, log_sums, grad_attended, tables, dz
        )
        combined = scatter_rows(lambda other: inward(dz, w_fc_in, w_qkv, offset, other))
        ins_grad = contract_rows(x, dz).astype(BF16)
        ins_list[layer] = reduced(ins_grad, 0)
        scaled, inverse_std = norm_rows(hidden_list[layer].astype(F32))
        grad_norm = inverse_std * (
            combined
            - jnp.mean(combined, axis=-1, keepdims=True)
            - scaled * jnp.mean(combined * scaled, axis=-1, keepdims=True)
        )
        grads = (grads.astype(F32) + grad_norm).astype(BF16)
        small_list[layer] = (heads_sum[0], inner_sum[0], dy_sum[0])
        if layer == 0:
            fc_out_part0 = reduced(contract_rows(act[:, :inner], dy).astype(BF16), 1)
            out_part0 = reduced(contract_rows(act[:, inner:], dy).astype(BF16), 1)
    act = kept_list[1][-1]
    summed = scatter_rows(lambda other: outer(act, w_outs[1], row, other))
    summed = after(summed, small_list[0][0])
    ends.append((hidden_list[1].astype(F32) + summed + end_e[1]).astype(BF16))

    def to_owner(first, second, upper, lower):
        return (jnp.where(low, first, lower), jnp.where(low, upper, second))

    def to_first(value):
        return lax.ppermute(value, SECTION, [(1, 0)])

    def to_second(value):
        return lax.ppermute(value, SECTION, [(0, 1)])

    small = sum_over(
        jnp.concatenate(
            [*small_list[0][:2], *small_list[1][:2], small_list[0][2], small_list[1][2]]
        ),
        ROW,
    )
    sums = small[: 2 * (per + inner)]
    sums_other = swap(sums, SECTION, 1)
    smalls = to_owner(*jnp.split(sums, 2), *jnp.split(sums_other, 2))
    end_grad = jnp.where(low, *jnp.split(small[2 * (per + inner) :], 2))
    qkv_b_grad = jnp.concatenate([member[:per] for member in smalls])
    fc_in_b_grad = jnp.concatenate([member[per:] for member in smalls])
    outs_lower = to_second(outs_part1)
    ins_lower = to_second(ins_list[1])
    ins_upper = to_first(ins_list[0])
    ins_g = to_owner(*ins_list, ins_upper, ins_lower)
    qkv_g = jnp.concatenate([member[:, inner:] for member in ins_g], axis=1).astype(F32)
    fc_in_g = jnp.concatenate([member[:, :inner] for member in ins_g], axis=1).astype(F32)
    qkv_w_grad = gain_one[:, None] * qkv_g + shift_one[:, None] * qkv_b_grad[None]
    fc_in_w_grad = gain_two[:, None] * fc_in_g + shift_two[:, None] * fc_in_b_grad[None]
    norm_parts = []
    for layer, (w_q, w_f) in enumerate(zip(both_layers(*qkv_half), both_layers(*fc_in_half))):
        w_q, w_f = (w_q.astype(F32), w_f.astype(F32))
        heads, hidden_sum = jnp.split(sums[layer * (per + inner) :][: per + inner], [per])
        part = ins_list[layer].astype(F32)
        norm_parts.append(
            jnp.stack(
                [
                    jnp.sum(w_q * part[:, inner:], axis=1),
                    jnp.sum(w_q * heads[None], axis=1),
                    jnp.sum(w_f * part[:, :inner], axis=1),
                    jnp.sum(w_f * hidden_sum[None], axis=1),
                ]
            )
        )
    norms = jnp.where(low, *norm_parts) + swap(jnp.where(low, *norm_parts[::-1]), SECTION, 1)
    norms = take(sum_over(norms, COL), 1, c, deep // cols_axis)
    end_grad = take(end_grad, 0, r * cols_axis + c, deep // cols_axis)
    fc_out_part0 = after(fc_out_part0, ins_upper, norms)
    fc_out_upper = to_first(fc_out_part0)
    fc_out_w_grad = jnp.concatenate(
        [
            jnp.where(low, fc_out_part0, outs_lower[:inner]),
            jnp.where(low, fc_out_upper, outs_part1[:inner]),
        ],
        axis=0,
    ).astype(F32)[None]
    qkv_w_grad = qkv_w_grad.reshape(qkv_w.shape)[None]
    fc_in_w_grad = fc_in_w_grad[None]
    out_part0, norms = lax.optimization_barrier((out_part0, norms))
    out_upper = to_first(out_part0)
    out_w_grad = jnp.concatenate(
        [
            jnp.where(low, out_part0, outs_lower[inner:]),
            jnp.where(low, out_upper, outs_part1[inner:]),
        ],
        axis=0,
    ).astype(F32)
    last = to_second(ends[1])
    first = to_first(grads)
    last, first = (after(last, norms), after(first, norms))
    layer_outputs = jnp.stack([jnp.where(low, ends[0], last), jnp.where(low, middle, ends[1])])
    input_gradients = jnp.stack(
        [jnp.where(low, grads, middle_grads[0]), jnp.where(low, first, middle_grads[1])]
    )
    return (
        layer_outputs[None],
        input_gradients[None],
        qkv_w_grad,
        take(qkv_b_grad.reshape(heads_here, -1), 1, r, per // rows_axis)[None],
        out_w_grad[None],
        fc_in_w_grad,
        take(fc_in_b_grad, 0, r, 2 * inner // rows_axis)[None],
        fc_out_w_grad,
        norms[0][None],
        norms[1][None],
        norms[2][None],
        norms[3][None],
        end_grad[None],
        end_grad[None],
    )


def all_of_it(*arrays):
    return local(*arrays)


def solution(mesh):
    sizes = mesh.shape
    paired = sizes[SECTION] == 2 and sizes[COL] == 4
    body = all_of_it if paired and sizes[ROW] == 4 else relay_local
    step = jax.shard_map(
        body,
        mesh=mesh,
        in_specs=(
            P(None, (ROW, COL), None),
            P(None, (ROW, COL), None),
            P(SECTION, ROW, COL, None),
            P(SECTION, COL, ROW),
            P(SECTION, COL, ROW),
            P(SECTION, ROW, COL),
            P(SECTION, (COL, ROW)),
            P(SECTION, COL, ROW),
            P(SECTION, (ROW, COL)),
            P(SECTION, (ROW, COL)),
            P(SECTION, (ROW, COL)),
            P(SECTION, (ROW, COL)),
            P(SECTION, (ROW, COL)),
            P(SECTION, (ROW, COL)),
        ),
        out_specs=(
            P(SECTION, None, (ROW, COL), None),
            P(SECTION, None, (ROW, COL), None),
            P(SECTION, ROW, COL, None),
            P(SECTION, COL, ROW),
            P(SECTION, COL, ROW),
            P(SECTION, ROW, COL),
            P(SECTION, (COL, ROW)),
            P(SECTION, COL, ROW),
            P(SECTION, (ROW, COL)),
            P(SECTION, (ROW, COL)),
            P(SECTION, (ROW, COL)),
            P(SECTION, (ROW, COL)),
            P(SECTION, (ROW, COL)),
            P(SECTION, (ROW, COL)),
        ),
        check_vma=False,
    )
    if body is relay_local:
        return step
    return step
```

```python
import functools
import math

import jax
import jax.numpy as jnp
from jax import lax
from jax.experimental import pallas as pl
from jax.experimental.pallas import tpu as pltpu
from jax.sharding import PartitionSpec as P


SECTION, ROW, COL = ("section", "row", "col")
HD = 256
ROT = 64
SEQ_LEN = 1024


def from_behind(value, axis, steps):
    count = lax.axis_size(axis)
    initial, last = (max(0, -steps), min(count, count - steps))
    return lax.ppermute(value, axis, [(source, source + steps) for source in range(initial, last)])


def rotary_tables(length):
    positions = jnp.arange(length).astype(jnp.float32)
    inverse = 10000.0 ** (-jnp.arange(0, ROT, 2).astype(jnp.float32) / ROT)
    angles = positions[:, None] * inverse[None, :]
    angles = jnp.concatenate([angles, angles], axis=-1)
    return (jnp.cos(angles)[:, None, :], jnp.sin(angles)[:, None, :])


def rotate(values, cosines, sines):
    half_rot = ROT // 2
    turned = values[..., :ROT]
    first_half = turned[..., :half_rot]
    second_half = turned[..., half_rot:]
    swapped = jnp.concatenate([-second_half, first_half], axis=-1)
    return jnp.concatenate([turned * cosines + swapped * sines, values[..., ROT:]], axis=-1)


def rotate_back(grads, cosines, sines):

    def turn_values(values):
        return rotate(values, cosines, sines)

    _, turn_pull = jax.vjp(turn_values, grads)
    return turn_pull(grads)[0]


def gelu_exact(values):
    return jax.nn.gelu(values, approximate=False)


def norm_rows(row_values):
    centred = row_values - jnp.mean(row_values, axis=-1, keepdims=True)
    inverse_std = lax.rsqrt(jnp.mean(centred * centred, axis=-1, keepdims=True) + 1e-05)
    return (centred * inverse_std, inverse_std)


def contract_rows(first_operand, second_operand):
    return lax.dot_general(
        first_operand, second_operand, (((0,), (0,)), ((), ())), preferred_element_type=jnp.float32
    )


def contract_cols(first_operand, second_operand):
    return lax.dot_general(
        first_operand, second_operand, (((1,), (1,)), ((), ())), preferred_element_type=jnp.float32
    )


def causal_block(row_start, block_rows, row_stop):
    query_pos = row_start + lax.broadcasted_iota(jnp.int32, (block_rows, row_stop), 0)
    key_pos = lax.broadcasted_iota(jnp.int32, (block_rows, row_stop), 1)
    return query_pos >= key_pos


def attention_forward(queries, keys_all, values_all):
    length = queries.shape[0]
    block_rows = min(512, length)
    score_scale = HD ** (-0.5)
    outputs_list = []
    sums_list = []
    for block_index in range(length // block_rows):
        row_start = block_index * block_rows
        row_stop = row_start + block_rows
        scores = (
            jnp.einsum(
                "qhd,khd->hqk",
                queries[row_start:row_stop],
                keys_all[:row_stop],
                preferred_element_type=jnp.float32,
            )
            * score_scale
        )
        scores = jnp.where(causal_block(row_start, block_rows, row_stop)[None], scores, -1e30)
        row_peak = jnp.max(scores, axis=-1, keepdims=True)
        exponents = jnp.exp(scores - row_peak)
        row_total = jnp.sum(exponents, axis=-1, keepdims=True)
        attention_probs = (exponents / row_total).astype(jnp.bfloat16)
        outputs_list.append(
            jnp.einsum(
                "hqk,khd->qhd",
                attention_probs,
                values_all[:row_stop],
                preferred_element_type=jnp.float32,
            )
        )
        sums_list.append((row_peak + jnp.log(row_total))[..., 0])
    attended = jnp.concatenate(outputs_list, axis=0).astype(jnp.bfloat16).reshape(length, -1)
    return (attended, jnp.concatenate(sums_list, axis=1))


def attention_backward(queries, keys_all, values_all, log_sums, grad_attended):
    length, heads_here = (queries.shape[0], queries.shape[1])
    block_rows = min(512, length)
    score_scale = HD ** (-0.5)
    grad_out = grad_attended.reshape(length, heads_here, HD)
    grad_queries_list = []
    grad_keys = jnp.zeros(queries.shape, jnp.float32)
    grad_values = jnp.zeros(queries.shape, jnp.float32)
    for block_index in range(length // block_rows):
        row_start = block_index * block_rows
        row_stop = row_start + block_rows
        scores = (
            jnp.einsum(
                "qhd,khd->hqk",
                queries[row_start:row_stop],
                keys_all[:row_stop],
                preferred_element_type=jnp.float32,
            )
            * score_scale
        )
        scores = jnp.where(causal_block(row_start, block_rows, row_stop)[None], scores, -1e30)
        attention_probs = jnp.exp(scores - log_sums[:, row_start:row_stop, None])
        low_probs = attention_probs.astype(jnp.bfloat16)
        grad_probs = jnp.einsum(
            "qhd,khd->hqk",
            grad_out[row_start:row_stop],
            values_all[:row_stop],
            preferred_element_type=jnp.float32,
        )
        centre_term = jnp.sum(attention_probs * grad_probs, axis=-1, keepdims=True)
        grad_scores = (attention_probs * (grad_probs - centre_term)).astype(jnp.bfloat16)
        grad_queries_list.append(
            jnp.einsum(
                "hqk,khd->qhd", grad_scores, keys_all[:row_stop], preferred_element_type=jnp.float32
            )
            * score_scale
        )
        grad_keys = grad_keys.at[:row_stop].add(
            jnp.einsum(
                "hqk,qhd->khd",
                grad_scores,
                queries[row_start:row_stop],
                preferred_element_type=jnp.float32,
            )
            * score_scale
        )
        grad_values = grad_values.at[:row_stop].add(
            jnp.einsum(
                "hqk,qhd->khd",
                low_probs,
                grad_out[row_start:row_stop],
                preferred_element_type=jnp.float32,
            )
        )
    return (jnp.concatenate(grad_queries_list, axis=0), grad_keys, grad_values)


def forward_turn(my_rows, weights, vectors, cosines, sines):
    qkv_w, qkv_b, out_w, fc_in_w, fc_in_b, fc_out_w = weights
    gain_one, bias_one, gain_two, bias_two, out_b, fc_out_b = vectors
    gathered = lax.all_gather(my_rows, COL, axis=0, tiled=True)
    scaled, _ = norm_rows(gathered.astype(jnp.float32))
    normed_one = (scaled * gain_one + bias_one).astype(jnp.bfloat16)
    normed_two = (scaled * gain_two + bias_two).astype(jnp.bfloat16)
    length = gathered.shape[0]
    heads_here = qkv_w.shape[1]
    projected = jnp.dot(
        normed_one, qkv_w.reshape(qkv_w.shape[0], -1), preferred_element_type=jnp.float32
    ) + qkv_b.reshape(-1).astype(jnp.float32)
    projected = projected.reshape(length, heads_here, 3, HD)
    queries = rotate(projected[:, :, 0], cosines, sines).astype(jnp.bfloat16)
    keys_all = rotate(projected[:, :, 1], cosines, sines).astype(jnp.bfloat16)
    values_all = projected[:, :, 2].astype(jnp.bfloat16)
    attended, log_sums = attention_forward(queries, keys_all, values_all)
    inner_act = jnp.dot(normed_two, fc_in_w, preferred_element_type=jnp.float32) + fc_in_b.astype(
        jnp.float32
    )
    activated = gelu_exact(inner_act).astype(jnp.bfloat16)
    summed = lax.psum_scatter(
        jnp.dot(attended, out_w, preferred_element_type=jnp.float32)
        + jnp.dot(activated, fc_out_w, preferred_element_type=jnp.float32),
        COL,
        scatter_dimension=0,
        tiled=True,
    )
    output = (my_rows.astype(jnp.float32) + summed + out_b + fc_out_b).astype(jnp.bfloat16)
    kept_values = (
        gathered,
        normed_one,
        normed_two,
        queries,
        keys_all,
        values_all,
        attended,
        log_sums,
        inner_act,
    )
    return (output, kept_values)


def backward_turn(grad_rows, kept_values, weights, vectors, cosines, sines):
    (
        gathered,
        normed_one,
        normed_two,
        queries,
        keys_all,
        values_all,
        attended,
        log_sums,
        inner_act,
    ) = kept_values
    qkv_w, qkv_b, out_w, fc_in_w, _, fc_out_w = weights
    gain_one, _, gain_two, _, _, _ = vectors
    grad_full = lax.all_gather(grad_rows, COL, axis=0, tiled=True)
    length = grad_full.shape[0]
    rows_here = grad_rows.shape[0]
    own_start = lax.axis_index(COL) * rows_here
    activated = gelu_exact(inner_act).astype(jnp.bfloat16)
    out_w_grad = contract_rows(attended, grad_full)
    fc_out_w_grad = contract_rows(activated, grad_full)
    grad_attended = contract_cols(grad_full, out_w).astype(jnp.bfloat16)
    grad_activated = contract_cols(grad_full, fc_out_w)
    _, gelu_pull = jax.vjp(gelu_exact, inner_act)
    grad_inner = gelu_pull(grad_activated)[0].astype(jnp.bfloat16)
    grad_queries, grad_keys, grad_values = attention_backward(
        queries, keys_all, values_all, log_sums, grad_attended
    )
    grad_q_pre = rotate_back(grad_queries, cosines, sines)
    grad_k_pre = rotate_back(grad_keys, cosines, sines)
    grad_projected = (
        jnp.stack([grad_q_pre, grad_k_pre, grad_values], axis=2)
        .astype(jnp.bfloat16)
        .reshape(length, -1)
    )
    qkv_flat = qkv_w.reshape(qkv_w.shape[0], -1)
    qkv_w_grad = contract_rows(normed_one, grad_projected).reshape(qkv_w.shape)
    qkv_b_grad = jnp.sum(grad_projected.astype(jnp.float32), axis=0).reshape(qkv_b.shape)
    fc_in_w_grad = contract_rows(normed_two, grad_inner)
    fc_in_b_grad = jnp.sum(grad_inner.astype(jnp.float32), axis=0)
    width = qkv_w.shape[0]
    scaled_full, inverse_full = norm_rows(gathered.astype(jnp.float32))
    scaled = lax.dynamic_slice_in_dim(scaled_full, own_start, rows_here, 0)
    inverse_std = lax.dynamic_slice_in_dim(inverse_full, own_start, rows_here, 0)
    dy_sum = jnp.sum(grad_rows.astype(jnp.float32), axis=0)
    both_grads = lax.psum_scatter(
        jnp.concatenate(
            [contract_cols(grad_projected, qkv_flat), contract_cols(grad_inner, fc_in_w)], axis=1
        ),
        COL,
        scatter_dimension=0,
        tiled=True,
    )
    grad_one = both_grads[:, :width]
    grad_two = both_grads[:, width:]
    combined = gain_one * grad_one + gain_two * grad_two
    vector_grads = (
        jnp.sum(grad_one * scaled, axis=0),
        jnp.sum(grad_one, axis=0),
        jnp.sum(grad_two * scaled, axis=0),
        jnp.sum(grad_two, axis=0),
        dy_sum,
    )
    grad_norm = inverse_std * (
        combined
        - jnp.mean(combined, axis=-1, keepdims=True)
        - scaled * jnp.mean(combined * scaled, axis=-1, keepdims=True)
    )
    grad_input = (grad_rows.astype(jnp.float32) + grad_norm).astype(jnp.bfloat16)
    matrix_grads = (qkv_w_grad, qkv_b_grad, out_w_grad, fc_in_w_grad, fc_in_b_grad, fc_out_w_grad)
    return (grad_input, matrix_grads, vector_grads)


def add_tuples(running, addend):
    if running is None:
        return addend
    return tuple((first_part + second_part for first_part, second_part in zip(running, addend)))


def relay_local(
    inputs,
    cotangent,
    qkv_weight,
    qkv_bias,
    out_weight,
    fc_in_weight,
    fc_in_bias,
    fc_out_weight,
    norm1_gain,
    norm1_bias,
    norm2_gain,
    norm2_bias,
    out_bias,
    fc_out_bias,
):
    sections = lax.axis_size(SECTION)
    section_index = lax.axis_index(SECTION)
    micro_count = inputs.shape[0]
    tick_count = micro_count + sections - 1
    is_first = section_index == 0
    is_last = section_index == sections - 1
    cosines, sines = rotary_tables(SEQ_LEN)
    vectors = (
        lax.all_gather(norm1_gain[0], (ROW, COL), axis=0, tiled=True),
        lax.all_gather(norm1_bias[0], (ROW, COL), axis=0, tiled=True),
        lax.all_gather(norm2_gain[0], (ROW, COL), axis=0, tiled=True),
        lax.all_gather(norm2_bias[0], (ROW, COL), axis=0, tiled=True),
        lax.all_gather(out_bias[0], (ROW, COL), axis=0, tiled=True),
        lax.all_gather(fc_out_bias[0], (ROW, COL), axis=0, tiled=True),
    )
    vectors = tuple((member.astype(jnp.float32) for member in vectors))
    received = jnp.zeros_like(inputs[0])
    outputs_list = []
    kept_list = []
    for tick_index in range(tick_count):
        weights = (
            lax.all_gather(qkv_weight[0], ROW, axis=0, tiled=True),
            lax.all_gather(qkv_bias[0], ROW, axis=1, tiled=True),
            lax.all_gather(out_weight[0], ROW, axis=1, tiled=True),
            lax.all_gather(fc_in_weight[0], ROW, axis=0, tiled=True),
            lax.all_gather(fc_in_bias[0], ROW, axis=0, tiled=True),
            lax.all_gather(fc_out_weight[0], ROW, axis=1, tiled=True),
        )
        first_rows = inputs[min(tick_index, micro_count - 1)]
        my_rows = jnp.where(is_first, first_rows, received)
        output, kept_values = forward_turn(my_rows, weights, vectors, cosines, sines)
        outputs_list.append(output)
        kept_list.append(kept_values)
        if tick_index + 1 < tick_count:
            received = from_behind(output, SECTION, 1)
    layer_outputs = lax.dynamic_slice_in_dim(jnp.stack(outputs_list), section_index, micro_count, 0)
    stacked_kept = tuple((jnp.stack(members) for members in zip(*kept_list)))
    received_grad = jnp.zeros_like(inputs[0])
    grads_list = []
    matrix_total = None
    vector_total = None
    for tick_index in range(tick_count):
        weights = (
            lax.all_gather(qkv_weight[0], ROW, axis=0, tiled=True),
            lax.all_gather(qkv_bias[0], ROW, axis=1, tiled=True),
            lax.all_gather(out_weight[0], ROW, axis=1, tiled=True),
            lax.all_gather(fc_in_weight[0], ROW, axis=0, tiled=True),
            lax.all_gather(fc_in_bias[0], ROW, axis=0, tiled=True),
            lax.all_gather(fc_out_weight[0], ROW, axis=1, tiled=True),
        )
        if tick_index < micro_count:
            seed_grad = cotangent[tick_index]
        else:
            seed_grad = jnp.zeros_like(cotangent[0])
        grad_rows = jnp.where(is_last, seed_grad, received_grad)
        forward_index = jnp.clip(tick_index - sections + 1 + 2 * section_index, 0, tick_count - 1)
        kept_values = tuple(
            (
                lax.dynamic_index_in_dim(member, forward_index, 0, keepdims=False)
                for member in stacked_kept
            )
        )
        grad_input, matrix_grads, vector_grads = backward_turn(
            grad_rows, kept_values, weights, vectors, cosines, sines
        )
        grads_list.append(grad_input)
        if tick_index + 1 < tick_count:
            received_grad = from_behind(grad_input, SECTION, -1)
        matrix_part = (
            lax.psum_scatter(matrix_grads[0], ROW, scatter_dimension=0, tiled=True),
            lax.psum_scatter(matrix_grads[1], ROW, scatter_dimension=1, tiled=True),
            lax.psum_scatter(matrix_grads[2], ROW, scatter_dimension=1, tiled=True),
            lax.psum_scatter(matrix_grads[3], ROW, scatter_dimension=0, tiled=True),
            lax.psum_scatter(matrix_grads[4], ROW, scatter_dimension=0, tiled=True),
            lax.psum_scatter(matrix_grads[5], ROW, scatter_dimension=1, tiled=True),
        )
        vector_part = (
            lax.psum_scatter(vector_grads[0], (ROW, COL), scatter_dimension=0, tiled=True),
            lax.psum_scatter(vector_grads[1], (ROW, COL), scatter_dimension=0, tiled=True),
            lax.psum_scatter(vector_grads[2], (ROW, COL), scatter_dimension=0, tiled=True),
            lax.psum_scatter(vector_grads[3], (ROW, COL), scatter_dimension=0, tiled=True),
            lax.psum_scatter(vector_grads[4], (ROW, COL), scatter_dimension=0, tiled=True),
        )
        matrix_total = add_tuples(matrix_total, tuple(matrix_part))
        vector_total = add_tuples(vector_total, tuple(vector_part))
    input_gradients = lax.dynamic_slice_in_dim(
        jnp.stack(grads_list), sections - 1 - section_index, micro_count, 0
    )
    return (
        layer_outputs[None],
        input_gradients[None],
        matrix_total[0][None],
        matrix_total[1][None],
        matrix_total[2][None],
        matrix_total[3][None],
        matrix_total[4][None],
        matrix_total[5][None],
        vector_total[0][None],
        vector_total[1][None],
        vector_total[2][None],
        vector_total[3][None],
        vector_total[4][None],
        vector_total[4][None],
    )


F32 = jnp.float32
BF16 = jnp.bfloat16
LANES = 128


def swap(value, axis, bit):
    count = lax.axis_size(axis)
    return lax.ppermute(value, axis, [(source, source ^ bit) for source in range(count)])


def sum_over(value, axis):
    bit = 1
    while bit < lax.axis_size(axis):
        value = value + swap(value, axis, bit)
        bit *= 2
    return value


def place(part, axis, index, length):
    shape = list(part.shape)
    shape[axis] = length
    start = index * part.shape[axis]
    return lax.dynamic_update_slice_in_dim(jnp.zeros(shape, part.dtype), part, start, axis)


def take(value, axis, index, size):
    return lax.dynamic_slice_in_dim(value, index * size, size, axis)


def after(value, *others):
    return lax.optimization_barrier((value, *others))[0]


def gather_rows(block):
    half = block.shape[0] // 2
    across = swap(block, SECTION, 1)
    beside = swap(block, COL, 2)
    across, beside = lax.optimization_barrier((across, beside))
    corner = jnp.concatenate([swap(beside[:half], SECTION, 1), swap(across[half:], COL, 2)], axis=0)
    near = jnp.concatenate([block, beside], axis=0)
    far = jnp.concatenate([across, corner], axis=0)
    near_other, far_other = (swap(near, COL, 1), swap(far, COL, 1))
    return (near, near_other, far, far_other), across


def gather_pieces(shard):
    def send(value, pairs):
        return lax.ppermute(value, ROW, pairs)

    opposite = swap(shard, ROW, 2)
    behind = send(shard, [(0, 1), (1, 2), (2, 3)])
    ahead = send(shard, [(3, 2), (2, 1), (1, 0)])
    last = send(opposite, [(2, 3), (1, 0)])
    return shard, ahead, opposite, behind, last


def in_turn(pieces, row):
    shard, ahead, opposite, behind, last = pieces
    return (shard, jnp.where(row == 3, last, ahead), opposite, jnp.where(row == 0, last, behind))


def pair_sum(keep_ref, came_ref, start, size):
    rows = pl.ds(start, size)
    return keep_ref[rows, :].astype(F32) + came_ref[rows, :].astype(F32)


def first_sum_kernel(keep_ref, came_ref, across_ref, beside_ref):
    block = keep_ref.shape[0] // 4
    half = block // 2
    for ref, starts in (
        (across_ref, (2 * block, 3 * block)),
        (beside_ref, (block + half, 3 * block + half)),
    ):
        for place, start in enumerate(starts):
            ref[place * half : (place + 1) * half, :] = pair_sum(
                keep_ref, came_ref, start, half
            ).astype(BF16)


def second_sum_kernel(keep_ref, came_ref, across_ref, beside_ref, top_ref, low_ref, kept_ref):
    block = keep_ref.shape[0] // 4
    half = block // 2
    kept_ref[:half, :] = pair_sum(keep_ref, came_ref, 0, half) + across_ref[:half, :].astype(F32)
    kept_ref[half:, :] = (
        pair_sum(keep_ref, came_ref, half, half) + beside_ref[:half, :].astype(F32)
    )
    top = pair_sum(keep_ref, came_ref, block, half) + across_ref[half:, :].astype(F32)
    top_ref[...] = top.astype(BF16)
    low = pair_sum(keep_ref, came_ref, 2 * block + half, half) + beside_ref[half:, :].astype(F32)
    low_ref[...] = low.astype(BF16)


def column_call(kernel, width, ins, outs):
    tile = 512

    def spec(shape):
        lead = shape[:-1]
        return pl.BlockSpec(lead + (tile,), lambda i: (0,) * len(lead) + (i,))

    return pl.pallas_call(
        kernel,
        grid=(width // tile,),
        in_specs=[spec(member.shape) for member in ins],
        out_specs=[spec(member.shape) for member in outs],
        out_shape=outs,
        cost_estimate=cost(0, *ins, *outs),
    )(*ins)


def scatter_rows(product):
    sent = product(1)
    came = swap(sent, COL, 1)
    keep = product(0)
    rows, width = keep.shape
    block = rows // 4
    half = block // 2
    whole_block = jax.ShapeDtypeStruct((block, width), BF16)
    half_block = jax.ShapeDtypeStruct((half, width), BF16)
    across, beside = column_call(first_sum_kernel, width, [keep, came], [whole_block, whole_block])
    across = swap(across, SECTION, 1)
    beside = swap(beside, COL, 2)
    top, low, keep = column_call(
        second_sum_kernel,
        width,
        [keep, came, across, beside],
        [half_block, half_block, jax.ShapeDtypeStruct((block, width), F32)],
    )
    arrived = jnp.concatenate([swap(top, COL, 2), swap(low, SECTION, 1)], axis=0)
    return keep + arrived.astype(F32)


def turn(values, cosines, sines):
    lead = values[:, :LANES]
    lane = lax.broadcasted_iota(jnp.int32, lead.shape, 1)
    ahead = pltpu.roll(lead, LANES - ROT // 2, 1)
    behind = pltpu.roll(lead, ROT // 2, 1)
    lead = lead * cosines + jnp.where(lane < ROT // 2, ahead, behind) * sines
    return jnp.concatenate([lead, values[:, LANES:]], axis=1)


def mm(first_operand, second_operand):
    return jnp.dot(first_operand, second_operand, preferred_element_type=F32)


def project_kernel(x_ref, wq_ref, wk_ref, wv_ref, e_ref, cos_ref, sin_ref, q_ref, k_ref, v_ref):
    x, cosines, sines = (x_ref[...], cos_ref[...], sin_ref[...])
    queries = mm(x, wq_ref[...]) + e_ref[:, :HD]
    q_ref[...] = (turn(queries, cosines, sines) * HD ** (-0.5)).astype(BF16)
    keys_here = mm(x, wk_ref[...]) + e_ref[:, HD : 2 * HD]
    k_ref[...] = turn(keys_here, cosines, sines).astype(BF16)
    v_ref[...] = (mm(x, wv_ref[...]) + e_ref[:, 2 * HD :]).astype(BF16)


def inner_kernel(x_ref, w_ref, e_ref, held_ref, act_ref, slope_ref):
    inner = mm(x_ref[...], w_ref[...]) + e_ref[...]
    below = 0.5 + 0.5 * lax.erf(inner * 0.7071067811865476)
    act_ref[...] = (inner * below).astype(BF16)
    density = jnp.exp(-0.5 * inner * inner) * 0.3989422804014327
    slope_ref[...] = (below + inner * density).astype(BF16)


def piece_columns(row_ref, w_refs):
    width = w_refs[0].shape[1]
    for step, w_ref in enumerate(w_refs):
        place = lax.rem(row_ref[0] + step, len(w_refs))
        yield w_ref, pl.ds(pl.multiple_of(place * width, width), width)


def outer_kernel(row_ref, act_ref, w0_ref, w1_ref, w2_ref, w3_ref, out_ref):
    act = act_ref[...]
    for w_ref, columns in piece_columns(row_ref, (w0_ref, w1_ref, w2_ref, w3_ref)):
        out_ref[:, columns] = mm(act, w_ref[...]).astype(BF16)


def outer_back_kernel(count, row_ref, *refs):
    dys, (w0_ref, w1_ref, w2_ref, w3_ref, slope_ref) = (refs[:count], refs[count : count + 5])
    dz_ref, do_ref, sum_ref, dy_sum_ref, dy_ref = refs[-5:]
    inner = slope_ref.shape[1]
    dy = dys[0][...]
    for place, ref in enumerate(dys[1:], 1):
        start = place * (pl.num_programs(0) // count)
        dy = jnp.where(pl.program_id(0) >= start, ref[...], dy)
    dy_ref[...] = dy
    total = None
    for w_ref, columns in piece_columns(row_ref, (w0_ref, w1_ref, w2_ref, w3_ref)):
        part = contract_cols(dy_ref[:, columns], w_ref[...])
        total = part if total is None else total + part
    dz = (total[:, :inner] * slope_ref[...].astype(F32)).astype(BF16)
    dz_ref[...] = dz
    do_ref[...] = total[:, inner:].astype(BF16)

    @pl.when(pl.program_id(0) == 0)
    def _():
        sum_ref[...] = jnp.zeros_like(sum_ref)
        dy_sum_ref[...] = jnp.zeros_like(dy_sum_ref)

    sum_ref[...] += jnp.sum(dz.astype(F32), axis=0, keepdims=True)
    dy_sum_ref[...] += jnp.sum(dy.astype(F32), axis=0, keepdims=True)


def inward_kernel(dz_ref, wf_ref, wq_ref, wk_ref, wv_ref, out_ref):
    start = wf_ref.shape[1]
    total = contract_cols(dz_ref[:, :start], wf_ref[...])
    for w_ref in (wq_ref, wk_ref, wv_ref):
        total += contract_cols(dz_ref[:, start : start + HD], w_ref[...])
        start += HD
    out_ref[...] = total.astype(BF16)


def attend_kernel(q_ref, k_ref, v_ref, row_ref, col_ref, out_ref, log_ref):
    scores = contract_cols(q_ref[...], k_ref[...])
    scores = jnp.where(row_ref[...] >= col_ref[...], scores, -1e30)
    peak = jnp.max(scores, axis=1, keepdims=True)
    exponents = jnp.exp(scores - peak)
    total = jnp.sum(exponents, axis=1, keepdims=True)
    out_ref[...] = mm((exponents / total).astype(BF16), v_ref[...]).astype(BF16)
    log_ref[...] = peak + jnp.log(total)


def attend_back_kernel(
    first, q_ref, k_ref, v_ref, row_ref, col_ref, log_ref, do_ref, cos_ref, sin_ref, held_ref,
    all_ref, sum_ref, out_ref, dk_ref, dv_ref, sem,
):
    step = pl.program_id(1)
    block = q_ref.shape[0]

    @pl.when(step == 0)
    def _():
        dk_ref[...] = jnp.zeros_like(dk_ref)
        dv_ref[...] = jnp.zeros_like(dv_ref)

    @pl.when((step == 0) & (pl.program_id(0) == 0))
    def _():
        sum_ref[...] = jnp.zeros_like(sum_ref)

    def column_sum(values):
        return jnp.sum(values.astype(F32), axis=0, keepdims=True)

    queries, keys_all, grads = (q_ref[...], k_ref[...], do_ref[...])
    scores = contract_cols(queries, keys_all)
    scores = jnp.where(row_ref[...] >= col_ref[...], scores, -1e30)
    probs = jnp.exp(scores - log_ref[...])
    grad_probs = contract_cols(grads, v_ref[...])
    centre = jnp.sum(probs * grad_probs, axis=1, keepdims=True)
    grad_scores = (probs * (grad_probs - centre)).astype(BF16)
    rows = pl.ds(pl.multiple_of(step * block, block), block)
    cosines, sines = cos_ref[rows, :], sin_ref[rows, :]
    grad_queries = mm(grad_scores, keys_all) * HD ** (-0.5)
    grad_queries = turn(grad_queries, cosines, -sines).astype(BF16)
    out_ref[rows, :HD] = grad_queries
    sum_ref[:, :HD] += column_sum(grad_queries)
    dk_ref[...] += contract_rows(grad_scores, queries)
    dv_ref[...] += contract_rows(probs.astype(BF16), grads)

    @pl.when(step == pl.num_programs(1) - 1)
    def _():
        grad_keys = turn(dk_ref[...], cos_ref[...], -sin_ref[...]).astype(BF16)
        grad_values = dv_ref[...].astype(BF16)
        out_ref[:, HD : 2 * HD] = grad_keys
        out_ref[:, 2 * HD :] = grad_values
        sum_ref[:, HD : 2 * HD] += column_sum(grad_keys)
        sum_ref[:, 2 * HD :] += column_sum(grad_values)
        length, width = out_ref.shape
        micro = pl.ds(pl.multiple_of((first + pl.program_id(0)) * length, length), length)
        copy = pltpu.make_async_copy(
            out_ref, all_ref.at[micro, pl.ds(all_ref.shape[1] - width, width)], sem
        )
        copy.start()
        copy.wait()


ROW_BLOCK = 256


def by_rows(width, block=ROW_BLOCK):
    return pl.BlockSpec((block, width), lambda i: (i, 0))


def whole(shape):
    return pl.BlockSpec(shape, lambda *unused: (0,) * len(shape))


def panel(width, place):
    return lambda deep: pl.BlockSpec((deep, width), lambda *unused: (0, place))


def cost(flops, *arrays):
    return pl.CostEstimate(
        flops=flops,
        transcendentals=0,
        bytes_accessed=sum(math.prod(array.shape) * array.dtype.itemsize for array in arrays),
    )


def heads_panels(array, inner):
    return [panel(HD, inner // HD + part)(array.shape[0]) for part in range(3)]


def project(x, w, inner, e, tables):
    rows, width = x.shape
    per_micro = tables[0].shape[0] // ROW_BLOCK
    table = pl.BlockSpec((ROW_BLOCK, LANES), lambda i: (i % per_micro, 0))
    out = jax.ShapeDtypeStruct((rows, HD), BF16)
    return pl.pallas_call(
        project_kernel,
        grid=(rows // ROW_BLOCK,),
        in_specs=[by_rows(width), *heads_panels(w, inner), whole(e.shape), table, table],
        out_specs=[by_rows(HD)] * 3,
        out_shape=[out] * 3,
        cost_estimate=cost(6 * rows * width * HD, x, out, out, out),
        name="project",
    )(x, w, w, w, e, *tables)


def inner_layer(x, w, e, held):
    rows, width = x.shape
    inner = e.shape[1]
    slope = jax.ShapeDtypeStruct((rows, inner), BF16)
    return pl.pallas_call(
        inner_kernel,
        grid=(rows // ROW_BLOCK,),
        in_specs=[
            by_rows(width),
            panel(inner, 0)(width),
            whole(e.shape),
            pl.BlockSpec(memory_space=pl.ANY),
        ],
        out_specs=[by_rows(inner)] * 2,
        out_shape=[jax.ShapeDtypeStruct(held.shape, BF16), slope],
        input_output_aliases={3: 0},
        cost_estimate=cost(2 * rows * width * inner, x, slope, slope),
        name="inner",
    )(x, w, e, held)


def split_rows(width, other):
    return pl.BlockSpec((ROW_BLOCK, width), lambda i: (i // 2 * 4 + 2 * other + i % 2, 0))


def outer(act, pieces, row, other):
    rows, width = (act.shape[0] // 2, len(pieces) * pieces[0].shape[1])
    out = jax.ShapeDtypeStruct((rows, width), BF16)
    return pl.pallas_call(
        outer_kernel,
        grid=(rows // ROW_BLOCK,),
        in_specs=[
            pl.BlockSpec(memory_space=pltpu.SMEM),
            split_rows(act.shape[1], other),
            *(whole(piece.shape) for piece in pieces),
        ],
        out_specs=by_rows(width),
        out_shape=out,
        cost_estimate=cost(2 * rows * width * act.shape[1], act, out),
        name="outer",
    )(row, act, *pieces)


def inward(dz, w_in, w_qkv, offset, other):
    rows, width = (dz.shape[0] // 2, w_in.shape[0])
    out = jax.ShapeDtypeStruct((rows, width), BF16)
    return pl.pallas_call(
        inward_kernel,
        grid=(rows // ROW_BLOCK,),
        in_specs=[
            split_rows(dz.shape[1], other),
            panel(dz.shape[1] - 3 * HD, 0)(width),
            *heads_panels(w_qkv, offset),
        ],
        out_specs=by_rows(width),
        out_shape=out,
        cost_estimate=cost(2 * rows * width * dz.shape[1], dz, out),
        name="inward",
    )(dz, w_in, w_qkv, w_qkv, w_qkv)


def outer_back(dys, pieces, row, slopes, start=0, held=None):
    rows, width = (sum(dy.shape[0] for dy in dys), dys[0].shape[1])
    inner = slopes.shape[1]
    each, first = (dys[0].shape[0] // ROW_BLOCK, start // ROW_BLOCK)

    def part(place):
        return pl.BlockSpec(
            (ROW_BLOCK, width), lambda i: (jnp.clip(i - place * each, 0, each - 1), 0)
        )

    below = pl.BlockSpec((ROW_BLOCK, inner), lambda i: (first + i, 0))
    extra = () if held is None else (held,)
    return pl.pallas_call(
        functools.partial(outer_back_kernel, len(dys)),
        grid=(rows // ROW_BLOCK,),
        in_specs=[
            pl.BlockSpec(memory_space=pltpu.SMEM),
            *(part(place) for place in range(len(dys))),
            *(whole(piece.shape) for piece in pieces),
            below,
            *(pl.BlockSpec(memory_space=pl.ANY) for member in extra),
        ],
        out_specs=[below, by_rows(HD), whole((1, inner)), whole((1, width))],
        out_shape=[
            jax.ShapeDtypeStruct((slopes.shape[0], inner + 3 * HD), BF16),
            jax.ShapeDtypeStruct((rows, HD), BF16),
            jax.ShapeDtypeStruct((1, inner), F32),
            jax.ShapeDtypeStruct((1, width), F32),
        ],
        scratch_shapes=[pltpu.VMEM((ROW_BLOCK, width), BF16)],
        input_output_aliases={6 + len(dys): 0} if extra else {},
        cost_estimate=cost(2 * rows * width * (inner + HD), *dys, slopes),
        name="outer_back",
    )(row, *dys, *pieces, slopes, *extra)


def attend(queries, keys_all, values_all, places, inner):
    rows = queries.shape[0]
    length = places.shape[0]
    steps = length // ROW_BLOCK
    row = pl.BlockSpec((ROW_BLOCK, HD), lambda m, i: (m * steps + i, 0))
    every = pl.BlockSpec((length, HD), lambda m, i: (m, 0))
    return pl.pallas_call(
        attend_kernel,
        grid=(rows // length, steps),
        in_specs=[
            row,
            every,
            every,
            pl.BlockSpec((ROW_BLOCK, 1), lambda m, i: (i, 0)),
            pl.BlockSpec((1, length), lambda m, i: (0, 0)),
        ],
        out_specs=[
            pl.BlockSpec((ROW_BLOCK, HD), lambda m, i: (m * steps + i, inner // HD)),
            pl.BlockSpec((ROW_BLOCK, 1), lambda m, i: (m * steps + i, 0)),
        ],
        out_shape=[
            jax.ShapeDtypeStruct((rows, inner + HD), BF16),
            jax.ShapeDtypeStruct((rows, 1), F32),
        ],
        cost_estimate=cost(4 * rows * length * HD, queries, keys_all, values_all, queries),
        name="attend",
    )(queries, keys_all, values_all, places[:, None], places[None, :])


def attend_back(queries, keys_all, values_all, places, log_sums, grads, tables, held, first=0):
    rows = grads.shape[0]
    length = places.shape[0]
    steps = length // ROW_BLOCK
    row = pl.BlockSpec((ROW_BLOCK, HD), lambda m, i: ((first + m) * steps + i, 0))
    every = pl.BlockSpec((length, HD), lambda m, i: (first + m, 0))
    anywhere = pl.BlockSpec(memory_space=pl.ANY)
    return pl.pallas_call(
        functools.partial(attend_back_kernel, first),
        grid=(rows // length, steps),
        in_specs=[
            row,
            every,
            every,
            pl.BlockSpec((ROW_BLOCK, 1), lambda m, i: (i, 0)),
            pl.BlockSpec((1, length), lambda m, i: (0, 0)),
            pl.BlockSpec((ROW_BLOCK, 1), lambda m, i: ((first + m) * steps + i, 0)),
            pl.BlockSpec((ROW_BLOCK, HD), lambda m, i: (m * steps + i, 0)),
            whole(tables[0].shape),
            whole(tables[1].shape),
            anywhere,
        ],
        out_specs=[anywhere, whole((1, 3 * HD))],
        out_shape=[
            jax.ShapeDtypeStruct(held.shape, BF16),
            jax.ShapeDtypeStruct((1, 3 * HD), F32),
        ],
        scratch_shapes=[
            pltpu.VMEM((length, 3 * HD), BF16),
            pltpu.VMEM((length, HD), F32),
            pltpu.VMEM((length, HD), F32),
            pltpu.SemaphoreType.DMA,
        ],
        input_output_aliases={9: 0},
        cost_estimate=cost(10 * rows * length * HD, queries, keys_all, values_all, grads),
        name="attend_back",
    )(
        queries, keys_all, values_all, places[:, None], places[None, :], log_sums, grads, *tables,
        held,
    )


def local(
    inputs,
    cotangent,
    qkv_weight,
    qkv_bias,
    out_weight,
    fc_in_weight,
    fc_in_bias,
    fc_out_weight,
    norm1_gain,
    norm1_bias,
    norm2_gain,
    norm2_bias,
    out_bias,
    fc_out_bias,
):
    s, r, c = (lax.axis_index(SECTION), lax.axis_index(ROW), lax.axis_index(COL))
    rows_axis, cols_axis = (lax.axis_size(ROW), lax.axis_size(COL))
    low = s == 0
    qkv_w, out_w, fc_in_w, fc_out_w = (
        qkv_weight[0], out_weight[0], fc_in_weight[0], fc_out_weight[0],
    )
    deep, heads_here = qkv_w.shape[0], qkv_w.shape[1]
    per = 3 * HD
    inner = fc_in_w.shape[1] // 2
    model = inputs.shape[2]

    def both_layers(own_first, own_second):
        return (jnp.where(low, own_first, own_second), jnp.where(low, own_second, own_first))

    def trade(value, axis, *others):
        size = value.shape[axis] // 2
        kept = take(value, axis, s, size)
        came = swap(after(take(value, axis, 1 - s, size), *others), SECTION, 1)
        return kept, came

    def gathered(shard, axis):
        return lax.all_gather(shard, ROW, axis=axis, tiled=True)

    held = jnp.stack(
        [
            norm1_gain[0].astype(F32),
            norm1_bias[0].astype(F32),
            norm2_gain[0].astype(F32),
            norm2_bias[0].astype(F32),
            out_bias[0].astype(F32) + fc_out_bias[0].astype(F32),
        ]
    )
    held_both = jnp.stack([held, swap(held, SECTION, 1)])
    qkv_flat = qkv_w.reshape(deep, -1)
    qkv_half = trade(qkv_flat, 1, held_both)
    fc_in_half = trade(fc_in_w, 1, qkv_half[1])
    outs_kept = jnp.concatenate([take(fc_out_w, 0, s, inner), take(out_w, 0, s, HD)], axis=0)
    outs_sent = jnp.concatenate([take(fc_out_w, 0, 1 - s, inner), take(out_w, 0, 1 - s, HD)], axis=0)
    outs_came = swap(after(outs_sent, fc_in_half[1]), SECTION, 1)
    held_both = sum_over(place(held_both, 2, c, deep), COL)
    held = held_both[0]
    gain_one, shift_one, gain_two, shift_two, end_bias = (held[i] for i in range(5))
    gains = both_layers(held, held_both[1])

    def scaled_pair(half, row):
        return tuple(
            (part.astype(F32) * gain[row][:, None]).astype(BF16)
            for part, gain in zip(both_layers(*half), gains)
        )

    qkv_pair = scaled_pair(qkv_half, 0)
    fc_in_pair = scaled_pair(fc_in_half, 2)
    outs_pair = both_layers(outs_kept, outs_came)
    w_qkv0 = gathered(qkv_pair[0], 0)
    w_fc_in0 = gathered(fc_in_pair[0], 0)
    w_ins1 = gathered(jnp.concatenate([fc_in_pair[1], qkv_pair[1]], axis=1), 0)
    w_ins = ((w_fc_in0, w_qkv0, 0), (w_ins1, w_ins1, inner))
    w_outs = [gather_pieces(outs_pair[layer]) for layer in range(2)]
    row = r.astype(jnp.int32)[None]

    own_qkv = mm(shift_one.astype(BF16)[None], qkv_flat)[0]
    own_fc = mm(shift_two.astype(BF16)[None], fc_in_w)[0]
    own_qkv = own_qkv + place(qkv_bias[0].astype(F32), 1, r, per).reshape(-1)
    own_fc = own_fc + place(fc_in_bias[0].astype(F32), 0, r, 2 * inner)
    biases = sum_over(
        jnp.concatenate([own_qkv, own_fc, place(end_bias, 0, r, model)]), ROW
    )
    biases = both_layers(biases, swap(biases, SECTION, 1))
    qkv_e, fc_e, end_e = ([], [], [])
    for member in biases:
        qkv_e.append(take(member[: 2 * per], 0, s, per)[None])
        fc_e.append(take(member[2 * per : 2 * per + 2 * inner], 0, s, inner)[None])
        end_e.append(member[2 * per + 2 * inner :])

    block_rows = inputs.shape[1]
    masks = jnp.array([0, 2, 1, 3], jnp.int32)
    places = ((c ^ masks)[:, None] * block_rows + jnp.arange(block_rows)[None]).reshape(-1)
    inverse = 10000.0 ** (-jnp.arange(0, ROT, 2).astype(F32) / ROT)
    angles = places.astype(F32)[:, None] * inverse[None]
    ones = jnp.ones((places.shape[0], LANES - ROT), F32)
    cosines, sines = (jnp.cos(angles), jnp.sin(angles))
    tables = (
        jnp.concatenate([cosines, cosines, ones], axis=1),
        jnp.concatenate([-sines, sines, 0.0 * ones], axis=1),
    )

    hidden = lax.dynamic_index_in_dim(inputs, s, 0, keepdims=False)
    seed = lax.dynamic_index_in_dim(cotangent, s, 0, keepdims=False)
    hidden = after(hidden, outs_came)

    hidden_list, kept_list, ends = ([], [], [])
    seed_rows = None
    for layer in range(2):
        hidden_list.append(hidden)
        scaled, unused = norm_rows(hidden.astype(F32))
        x, unused = gather_rows(scaled.astype(BF16))
        x = jnp.concatenate(x, axis=0)
        if layer == 0:
            seed_rows, unused = gather_rows(after(seed, x))
            seed_rows = jnp.concatenate(seed_rows, axis=0)
        w_fc_in, w_qkv, offset = w_ins[layer]
        queries, keys_all, values_all = project(x, w_qkv, offset, qkv_e[layer], tables)
        attended, log_sums = attend(queries, keys_all, values_all, places, inner)
        act, slopes = inner_layer(x, w_fc_in, fc_e[layer], attended)
        if layer == 0:
            *pieces, act, unused = lax.optimization_barrier((*w_outs[0][1:], act, seed_rows))
            w_outs[0] = in_turn((w_outs[0][0], *pieces), r)
        kept = (x, queries, keys_all, values_all, log_sums, slopes, act)
        if layer == 1:
            outs_grad1 = contract_rows(act, seed_rows).astype(BF16)
            seed_rows = after(seed_rows, outs_grad1)
            *pieces, unused = lax.optimization_barrier((*w_outs[1][1:], outs_grad1))
            w_outs[1] = in_turn((w_outs[1][0], *pieces), r)
        kept_list.append(kept)
        if layer == 0:
            summed = scatter_rows(lambda other: outer(act, w_outs[0], row, other))
            hidden = (hidden.astype(F32) + summed + end_e[layer]).astype(BF16)
            ends.append(hidden)
            middle = swap(hidden, SECTION, 1)

    def reduced(value, axis):
        return lax.psum_scatter(value, ROW, scatter_dimension=axis, tiled=True)

    outs_part1 = reduced(outs_grad1, 1)
    grads = seed
    ins_list, small_list = ([None, None], [None, None])
    for layer in (1, 0):
        x, queries, keys_all, values_all, log_sums, slopes, act = kept_list[layer]
        w_fc_in, w_qkv, offset = w_ins[layer]
        if layer == 1:
            dy = seed_rows
        else:
            dys, across = gather_rows(grads)
            dy = jnp.concatenate(lax.optimization_barrier(dys), axis=0)
            middle_grads = (jnp.where(low, grads, across), jnp.where(low, across, grads))
        halves = ((dy,),) if layer == 1 else (dys[:2], dys[2:])
        dz, start, column_sums = (None, 0, [])
        for half in halves:
            dz, grad_attended, inner_sum, dy_sum = outer_back(
                half, w_outs[layer], row, slopes, start, dz
            )
            dz, heads_sum = attend_back(
                queries, keys_all, values_all, places, log_sums, grad_attended, tables, dz,
                start // places.shape[0],
            )
            start += grad_attended.shape[0]
            column_sums.append((heads_sum[0], inner_sum[0], dy_sum[0]))
        combined = scatter_rows(lambda other: inward(dz, w_fc_in, w_qkv, offset, other))
        ins_grad = contract_rows(x, dz).astype(BF16)
        ins_list[layer] = reduced(ins_grad, 0)
        scaled, inverse_std = norm_rows(hidden_list[layer].astype(F32))
        grad_norm = inverse_std * (
            combined
            - jnp.mean(combined, axis=-1, keepdims=True)
            - scaled * jnp.mean(combined * scaled, axis=-1, keepdims=True)
        )
        grads = (grads.astype(F32) + grad_norm).astype(BF16)
        small_list[layer] = tuple(sum(members) for members in zip(*column_sums))
        if layer == 0:
            fc_out_part0 = reduced(contract_rows(act[:, :inner], dy).astype(BF16), 1)
            out_part0 = reduced(contract_rows(act[:, inner:], dy).astype(BF16), 1)
    act = kept_list[1][-1]
    summed = scatter_rows(lambda other: outer(act, w_outs[1], row, other))
    summed = after(summed, small_list[0][0])
    ends.append((hidden_list[1].astype(F32) + summed + end_e[1]).astype(BF16))

    def to_owner(first, second, upper, lower):
        return (jnp.where(low, first, lower), jnp.where(low, upper, second))

    def to_first(value):
        return lax.ppermute(value, SECTION, [(1, 0)])

    def to_second(value):
        return lax.ppermute(value, SECTION, [(0, 1)])

    small = sum_over(
        jnp.concatenate(
            [*small_list[0][:2], *small_list[1][:2], small_list[0][2], small_list[1][2]]
        ),
        ROW,
    )
    sums = small[: 2 * (per + inner)]
    sums_other = swap(sums, SECTION, 1)
    smalls = to_owner(*jnp.split(sums, 2), *jnp.split(sums_other, 2))
    end_grad = jnp.where(low, *jnp.split(small[2 * (per + inner) :], 2))
    qkv_b_grad = jnp.concatenate([member[:per] for member in smalls])
    fc_in_b_grad = jnp.concatenate([member[per:] for member in smalls])
    outs_lower = to_second(outs_part1)
    ins_lower = to_second(ins_list[1])
    ins_upper = to_first(ins_list[0])
    ins_g = to_owner(*ins_list, ins_upper, ins_lower)
    qkv_g = jnp.concatenate([member[:, inner:] for member in ins_g], axis=1).astype(F32)
    fc_in_g = jnp.concatenate([member[:, :inner] for member in ins_g], axis=1).astype(F32)
    qkv_w_grad = gain_one[:, None] * qkv_g + shift_one[:, None] * qkv_b_grad[None]
    fc_in_w_grad = gain_two[:, None] * fc_in_g + shift_two[:, None] * fc_in_b_grad[None]
    norm_parts = []
    for layer, (w_q, w_f) in enumerate(zip(both_layers(*qkv_half), both_layers(*fc_in_half))):
        w_q, w_f = (w_q.astype(F32), w_f.astype(F32))
        heads, hidden_sum = jnp.split(sums[layer * (per + inner) :][: per + inner], [per])
        part = ins_list[layer].astype(F32)
        norm_parts.append(
            jnp.stack(
                [
                    jnp.sum(w_q * part[:, inner:], axis=1),
                    jnp.sum(w_q * heads[None], axis=1),
                    jnp.sum(w_f * part[:, :inner], axis=1),
                    jnp.sum(w_f * hidden_sum[None], axis=1),
                ]
            )
        )
    norms = jnp.where(low, *norm_parts) + swap(jnp.where(low, *norm_parts[::-1]), SECTION, 1)
    norms = take(sum_over(norms, COL), 1, c, deep // cols_axis)
    end_grad = take(end_grad, 0, r * cols_axis + c, deep // cols_axis)
    fc_out_part0 = after(fc_out_part0, ins_upper, norms)
    fc_out_upper = to_first(fc_out_part0)
    fc_out_w_grad = jnp.concatenate(
        [
            jnp.where(low, fc_out_part0, outs_lower[:inner]),
            jnp.where(low, fc_out_upper, outs_part1[:inner]),
        ],
        axis=0,
    ).astype(F32)[None]
    qkv_w_grad = qkv_w_grad.reshape(qkv_w.shape)[None]
    fc_in_w_grad = fc_in_w_grad[None]
    out_part0, norms, unused = lax.optimization_barrier((out_part0, norms, fc_out_upper))
    out_upper = to_first(out_part0)
    out_w_grad = jnp.concatenate(
        [
            jnp.where(low, out_part0, outs_lower[inner:]),
            jnp.where(low, out_upper, outs_part1[inner:]),
        ],
        axis=0,
    ).astype(F32)
    last = to_second(ends[1])
    first = to_first(grads)
    last, first = (after(last, norms), after(first, norms))
    layer_outputs = jnp.stack([jnp.where(low, ends[0], last), jnp.where(low, middle, ends[1])])
    input_gradients = jnp.stack(
        [jnp.where(low, grads, middle_grads[0]), jnp.where(low, first, middle_grads[1])]
    )
    return (
        layer_outputs[None],
        input_gradients[None],
        qkv_w_grad,
        take(qkv_b_grad.reshape(heads_here, -1), 1, r, per // rows_axis)[None],
        out_w_grad[None],
        fc_in_w_grad,
        take(fc_in_b_grad, 0, r, 2 * inner // rows_axis)[None],
        fc_out_w_grad,
        norms[0][None],
        norms[1][None],
        norms[2][None],
        norms[3][None],
        end_grad[None],
        end_grad[None],
    )


def all_of_it(*arrays):
    return local(*arrays)


def solution(mesh):
    sizes = mesh.shape
    paired = sizes[SECTION] == 2 and sizes[COL] == 4
    body = all_of_it if paired and sizes[ROW] == 4 else relay_local
    step = jax.shard_map(
        body,
        mesh=mesh,
        in_specs=(
            P(None, (ROW, COL), None),
            P(None, (ROW, COL), None),
            P(SECTION, ROW, COL, None),
            P(SECTION, COL, ROW),
            P(SECTION, COL, ROW),
            P(SECTION, ROW, COL),
            P(SECTION, (COL, ROW)),
            P(SECTION, COL, ROW),
            P(SECTION, (ROW, COL)),
            P(SECTION, (ROW, COL)),
            P(SECTION, (ROW, COL)),
            P(SECTION, (ROW, COL)),
            P(SECTION, (ROW, COL)),
            P(SECTION, (ROW, COL)),
        ),
        out_specs=(
            P(SECTION, None, (ROW, COL), None),
            P(SECTION, None, (ROW, COL), None),
            P(SECTION, ROW, COL, None),
            P(SECTION, COL, ROW),
            P(SECTION, COL, ROW),
            P(SECTION, ROW, COL),
            P(SECTION, (COL, ROW)),
            P(SECTION, COL, ROW),
            P(SECTION, (ROW, COL)),
            P(SECTION, (ROW, COL)),
            P(SECTION, (ROW, COL)),
            P(SECTION, (ROW, COL)),
            P(SECTION, (ROW, COL)),
            P(SECTION, (ROW, COL)),
        ),
        check_vma=False,
    )
    if body is relay_local:
        return step
    return step
```

```python
import functools
import math

import jax
import jax.numpy as jnp
from jax import lax
from jax.experimental import pallas as pl
from jax.experimental.pallas import tpu as pltpu
from jax.sharding import PartitionSpec as P


SECTION, ROW, COL = ("section", "row", "col")
HD = 256
ROT = 64
SEQ_LEN = 1024


def from_behind(value, axis, steps):
    count = lax.axis_size(axis)
    initial, last = (max(0, -steps), min(count, count - steps))
    return lax.ppermute(value, axis, [(source, source + steps) for source in range(initial, last)])


def rotary_tables(length):
    positions = jnp.arange(length).astype(jnp.float32)
    inverse = 10000.0 ** (-jnp.arange(0, ROT, 2).astype(jnp.float32) / ROT)
    angles = positions[:, None] * inverse[None, :]
    angles = jnp.concatenate([angles, angles], axis=-1)
    return (jnp.cos(angles)[:, None, :], jnp.sin(angles)[:, None, :])


def rotate(values, cosines, sines):
    half_rot = ROT // 2
    turned = values[..., :ROT]
    first_half = turned[..., :half_rot]
    second_half = turned[..., half_rot:]
    swapped = jnp.concatenate([-second_half, first_half], axis=-1)
    return jnp.concatenate([turned * cosines + swapped * sines, values[..., ROT:]], axis=-1)


def rotate_back(grads, cosines, sines):

    def turn_values(values):
        return rotate(values, cosines, sines)

    _, turn_pull = jax.vjp(turn_values, grads)
    return turn_pull(grads)[0]


def gelu_exact(values):
    return jax.nn.gelu(values, approximate=False)


def norm_rows(row_values):
    centred = row_values - jnp.mean(row_values, axis=-1, keepdims=True)
    inverse_std = lax.rsqrt(jnp.mean(centred * centred, axis=-1, keepdims=True) + 1e-05)
    return (centred * inverse_std, inverse_std)


def contract_rows(first_operand, second_operand):
    return lax.dot_general(
        first_operand, second_operand, (((0,), (0,)), ((), ())), preferred_element_type=jnp.float32
    )


def contract_cols(first_operand, second_operand):
    return lax.dot_general(
        first_operand, second_operand, (((1,), (1,)), ((), ())), preferred_element_type=jnp.float32
    )


def causal_block(row_start, block_rows, row_stop):
    query_pos = row_start + lax.broadcasted_iota(jnp.int32, (block_rows, row_stop), 0)
    key_pos = lax.broadcasted_iota(jnp.int32, (block_rows, row_stop), 1)
    return query_pos >= key_pos


def attention_forward(queries, keys_all, values_all):
    length = queries.shape[0]
    block_rows = min(512, length)
    score_scale = HD ** (-0.5)
    outputs_list = []
    sums_list = []
    for block_index in range(length // block_rows):
        row_start = block_index * block_rows
        row_stop = row_start + block_rows
        scores = (
            jnp.einsum(
                "qhd,khd->hqk",
                queries[row_start:row_stop],
                keys_all[:row_stop],
                preferred_element_type=jnp.float32,
            )
            * score_scale
        )
        scores = jnp.where(causal_block(row_start, block_rows, row_stop)[None], scores, -1e30)
        row_peak = jnp.max(scores, axis=-1, keepdims=True)
        exponents = jnp.exp(scores - row_peak)
        row_total = jnp.sum(exponents, axis=-1, keepdims=True)
        attention_probs = (exponents / row_total).astype(jnp.bfloat16)
        outputs_list.append(
            jnp.einsum(
                "hqk,khd->qhd",
                attention_probs,
                values_all[:row_stop],
                preferred_element_type=jnp.float32,
            )
        )
        sums_list.append((row_peak + jnp.log(row_total))[..., 0])
    attended = jnp.concatenate(outputs_list, axis=0).astype(jnp.bfloat16).reshape(length, -1)
    return (attended, jnp.concatenate(sums_list, axis=1))


def attention_backward(queries, keys_all, values_all, log_sums, grad_attended):
    length, heads_here = (queries.shape[0], queries.shape[1])
    block_rows = min(512, length)
    score_scale = HD ** (-0.5)
    grad_out = grad_attended.reshape(length, heads_here, HD)
    grad_queries_list = []
    grad_keys = jnp.zeros(queries.shape, jnp.float32)
    grad_values = jnp.zeros(queries.shape, jnp.float32)
    for block_index in range(length // block_rows):
        row_start = block_index * block_rows
        row_stop = row_start + block_rows
        scores = (
            jnp.einsum(
                "qhd,khd->hqk",
                queries[row_start:row_stop],
                keys_all[:row_stop],
                preferred_element_type=jnp.float32,
            )
            * score_scale
        )
        scores = jnp.where(causal_block(row_start, block_rows, row_stop)[None], scores, -1e30)
        attention_probs = jnp.exp(scores - log_sums[:, row_start:row_stop, None])
        low_probs = attention_probs.astype(jnp.bfloat16)
        grad_probs = jnp.einsum(
            "qhd,khd->hqk",
            grad_out[row_start:row_stop],
            values_all[:row_stop],
            preferred_element_type=jnp.float32,
        )
        centre_term = jnp.sum(attention_probs * grad_probs, axis=-1, keepdims=True)
        grad_scores = (attention_probs * (grad_probs - centre_term)).astype(jnp.bfloat16)
        grad_queries_list.append(
            jnp.einsum(
                "hqk,khd->qhd", grad_scores, keys_all[:row_stop], preferred_element_type=jnp.float32
            )
            * score_scale
        )
        grad_keys = grad_keys.at[:row_stop].add(
            jnp.einsum(
                "hqk,qhd->khd",
                grad_scores,
                queries[row_start:row_stop],
                preferred_element_type=jnp.float32,
            )
            * score_scale
        )
        grad_values = grad_values.at[:row_stop].add(
            jnp.einsum(
                "hqk,qhd->khd",
                low_probs,
                grad_out[row_start:row_stop],
                preferred_element_type=jnp.float32,
            )
        )
    return (jnp.concatenate(grad_queries_list, axis=0), grad_keys, grad_values)


def forward_turn(my_rows, weights, vectors, cosines, sines):
    qkv_w, qkv_b, out_w, fc_in_w, fc_in_b, fc_out_w = weights
    gain_one, bias_one, gain_two, bias_two, out_b, fc_out_b = vectors
    gathered = lax.all_gather(my_rows, COL, axis=0, tiled=True)
    scaled, _ = norm_rows(gathered.astype(jnp.float32))
    normed_one = (scaled * gain_one + bias_one).astype(jnp.bfloat16)
    normed_two = (scaled * gain_two + bias_two).astype(jnp.bfloat16)
    length = gathered.shape[0]
    heads_here = qkv_w.shape[1]
    projected = jnp.dot(
        normed_one, qkv_w.reshape(qkv_w.shape[0], -1), preferred_element_type=jnp.float32
    ) + qkv_b.reshape(-1).astype(jnp.float32)
    projected = projected.reshape(length, heads_here, 3, HD)
    queries = rotate(projected[:, :, 0], cosines, sines).astype(jnp.bfloat16)
    keys_all = rotate(projected[:, :, 1], cosines, sines).astype(jnp.bfloat16)
    values_all = projected[:, :, 2].astype(jnp.bfloat16)
    attended, log_sums = attention_forward(queries, keys_all, values_all)
    inner_act = jnp.dot(normed_two, fc_in_w, preferred_element_type=jnp.float32) + fc_in_b.astype(
        jnp.float32
    )
    activated = gelu_exact(inner_act).astype(jnp.bfloat16)
    summed = lax.psum_scatter(
        jnp.dot(attended, out_w, preferred_element_type=jnp.float32)
        + jnp.dot(activated, fc_out_w, preferred_element_type=jnp.float32),
        COL,
        scatter_dimension=0,
        tiled=True,
    )
    output = (my_rows.astype(jnp.float32) + summed + out_b + fc_out_b).astype(jnp.bfloat16)
    kept_values = (
        gathered,
        normed_one,
        normed_two,
        queries,
        keys_all,
        values_all,
        attended,
        log_sums,
        inner_act,
    )
    return (output, kept_values)


def backward_turn(grad_rows, kept_values, weights, vectors, cosines, sines):
    (
        gathered,
        normed_one,
        normed_two,
        queries,
        keys_all,
        values_all,
        attended,
        log_sums,
        inner_act,
    ) = kept_values
    qkv_w, qkv_b, out_w, fc_in_w, _, fc_out_w = weights
    gain_one, _, gain_two, _, _, _ = vectors
    grad_full = lax.all_gather(grad_rows, COL, axis=0, tiled=True)
    length = grad_full.shape[0]
    rows_here = grad_rows.shape[0]
    own_start = lax.axis_index(COL) * rows_here
    activated = gelu_exact(inner_act).astype(jnp.bfloat16)
    out_w_grad = contract_rows(attended, grad_full)
    fc_out_w_grad = contract_rows(activated, grad_full)
    grad_attended = contract_cols(grad_full, out_w).astype(jnp.bfloat16)
    grad_activated = contract_cols(grad_full, fc_out_w)
    _, gelu_pull = jax.vjp(gelu_exact, inner_act)
    grad_inner = gelu_pull(grad_activated)[0].astype(jnp.bfloat16)
    grad_queries, grad_keys, grad_values = attention_backward(
        queries, keys_all, values_all, log_sums, grad_attended
    )
    grad_q_pre = rotate_back(grad_queries, cosines, sines)
    grad_k_pre = rotate_back(grad_keys, cosines, sines)
    grad_projected = (
        jnp.stack([grad_q_pre, grad_k_pre, grad_values], axis=2)
        .astype(jnp.bfloat16)
        .reshape(length, -1)
    )
    qkv_flat = qkv_w.reshape(qkv_w.shape[0], -1)
    qkv_w_grad = contract_rows(normed_one, grad_projected).reshape(qkv_w.shape)
    qkv_b_grad = jnp.sum(grad_projected.astype(jnp.float32), axis=0).reshape(qkv_b.shape)
    fc_in_w_grad = contract_rows(normed_two, grad_inner)
    fc_in_b_grad = jnp.sum(grad_inner.astype(jnp.float32), axis=0)
    width = qkv_w.shape[0]
    scaled_full, inverse_full = norm_rows(gathered.astype(jnp.float32))
    scaled = lax.dynamic_slice_in_dim(scaled_full, own_start, rows_here, 0)
    inverse_std = lax.dynamic_slice_in_dim(inverse_full, own_start, rows_here, 0)
    dy_sum = jnp.sum(grad_rows.astype(jnp.float32), axis=0)
    both_grads = lax.psum_scatter(
        jnp.concatenate(
            [contract_cols(grad_projected, qkv_flat), contract_cols(grad_inner, fc_in_w)], axis=1
        ),
        COL,
        scatter_dimension=0,
        tiled=True,
    )
    grad_one = both_grads[:, :width]
    grad_two = both_grads[:, width:]
    combined = gain_one * grad_one + gain_two * grad_two
    vector_grads = (
        jnp.sum(grad_one * scaled, axis=0),
        jnp.sum(grad_one, axis=0),
        jnp.sum(grad_two * scaled, axis=0),
        jnp.sum(grad_two, axis=0),
        dy_sum,
    )
    grad_norm = inverse_std * (
        combined
        - jnp.mean(combined, axis=-1, keepdims=True)
        - scaled * jnp.mean(combined * scaled, axis=-1, keepdims=True)
    )
    grad_input = (grad_rows.astype(jnp.float32) + grad_norm).astype(jnp.bfloat16)
    matrix_grads = (qkv_w_grad, qkv_b_grad, out_w_grad, fc_in_w_grad, fc_in_b_grad, fc_out_w_grad)
    return (grad_input, matrix_grads, vector_grads)


def add_tuples(running, addend):
    if running is None:
        return addend
    return tuple((first_part + second_part for first_part, second_part in zip(running, addend)))


def relay_local(
    inputs,
    cotangent,
    qkv_weight,
    qkv_bias,
    out_weight,
    fc_in_weight,
    fc_in_bias,
    fc_out_weight,
    norm1_gain,
    norm1_bias,
    norm2_gain,
    norm2_bias,
    out_bias,
    fc_out_bias,
):
    sections = lax.axis_size(SECTION)
    section_index = lax.axis_index(SECTION)
    micro_count = inputs.shape[0]
    tick_count = micro_count + sections - 1
    is_first = section_index == 0
    is_last = section_index == sections - 1
    cosines, sines = rotary_tables(SEQ_LEN)
    vectors = (
        lax.all_gather(norm1_gain[0], (ROW, COL), axis=0, tiled=True),
        lax.all_gather(norm1_bias[0], (ROW, COL), axis=0, tiled=True),
        lax.all_gather(norm2_gain[0], (ROW, COL), axis=0, tiled=True),
        lax.all_gather(norm2_bias[0], (ROW, COL), axis=0, tiled=True),
        lax.all_gather(out_bias[0], (ROW, COL), axis=0, tiled=True),
        lax.all_gather(fc_out_bias[0], (ROW, COL), axis=0, tiled=True),
    )
    vectors = tuple((member.astype(jnp.float32) for member in vectors))
    received = jnp.zeros_like(inputs[0])
    outputs_list = []
    kept_list = []
    for tick_index in range(tick_count):
        weights = (
            lax.all_gather(qkv_weight[0], ROW, axis=0, tiled=True),
            lax.all_gather(qkv_bias[0], ROW, axis=1, tiled=True),
            lax.all_gather(out_weight[0], ROW, axis=1, tiled=True),
            lax.all_gather(fc_in_weight[0], ROW, axis=0, tiled=True),
            lax.all_gather(fc_in_bias[0], ROW, axis=0, tiled=True),
            lax.all_gather(fc_out_weight[0], ROW, axis=1, tiled=True),
        )
        first_rows = inputs[min(tick_index, micro_count - 1)]
        my_rows = jnp.where(is_first, first_rows, received)
        output, kept_values = forward_turn(my_rows, weights, vectors, cosines, sines)
        outputs_list.append(output)
        kept_list.append(kept_values)
        if tick_index + 1 < tick_count:
            received = from_behind(output, SECTION, 1)
    layer_outputs = lax.dynamic_slice_in_dim(jnp.stack(outputs_list), section_index, micro_count, 0)
    stacked_kept = tuple((jnp.stack(members) for members in zip(*kept_list)))
    received_grad = jnp.zeros_like(inputs[0])
    grads_list = []
    matrix_total = None
    vector_total = None
    for tick_index in range(tick_count):
        weights = (
            lax.all_gather(qkv_weight[0], ROW, axis=0, tiled=True),
            lax.all_gather(qkv_bias[0], ROW, axis=1, tiled=True),
            lax.all_gather(out_weight[0], ROW, axis=1, tiled=True),
            lax.all_gather(fc_in_weight[0], ROW, axis=0, tiled=True),
            lax.all_gather(fc_in_bias[0], ROW, axis=0, tiled=True),
            lax.all_gather(fc_out_weight[0], ROW, axis=1, tiled=True),
        )
        if tick_index < micro_count:
            seed_grad = cotangent[tick_index]
        else:
            seed_grad = jnp.zeros_like(cotangent[0])
        grad_rows = jnp.where(is_last, seed_grad, received_grad)
        forward_index = jnp.clip(tick_index - sections + 1 + 2 * section_index, 0, tick_count - 1)
        kept_values = tuple(
            (
                lax.dynamic_index_in_dim(member, forward_index, 0, keepdims=False)
                for member in stacked_kept
            )
        )
        grad_input, matrix_grads, vector_grads = backward_turn(
            grad_rows, kept_values, weights, vectors, cosines, sines
        )
        grads_list.append(grad_input)
        if tick_index + 1 < tick_count:
            received_grad = from_behind(grad_input, SECTION, -1)
        matrix_part = (
            lax.psum_scatter(matrix_grads[0], ROW, scatter_dimension=0, tiled=True),
            lax.psum_scatter(matrix_grads[1], ROW, scatter_dimension=1, tiled=True),
            lax.psum_scatter(matrix_grads[2], ROW, scatter_dimension=1, tiled=True),
            lax.psum_scatter(matrix_grads[3], ROW, scatter_dimension=0, tiled=True),
            lax.psum_scatter(matrix_grads[4], ROW, scatter_dimension=0, tiled=True),
            lax.psum_scatter(matrix_grads[5], ROW, scatter_dimension=1, tiled=True),
        )
        vector_part = (
            lax.psum_scatter(vector_grads[0], (ROW, COL), scatter_dimension=0, tiled=True),
            lax.psum_scatter(vector_grads[1], (ROW, COL), scatter_dimension=0, tiled=True),
            lax.psum_scatter(vector_grads[2], (ROW, COL), scatter_dimension=0, tiled=True),
            lax.psum_scatter(vector_grads[3], (ROW, COL), scatter_dimension=0, tiled=True),
            lax.psum_scatter(vector_grads[4], (ROW, COL), scatter_dimension=0, tiled=True),
        )
        matrix_total = add_tuples(matrix_total, tuple(matrix_part))
        vector_total = add_tuples(vector_total, tuple(vector_part))
    input_gradients = lax.dynamic_slice_in_dim(
        jnp.stack(grads_list), sections - 1 - section_index, micro_count, 0
    )
    return (
        layer_outputs[None],
        input_gradients[None],
        matrix_total[0][None],
        matrix_total[1][None],
        matrix_total[2][None],
        matrix_total[3][None],
        matrix_total[4][None],
        matrix_total[5][None],
        vector_total[0][None],
        vector_total[1][None],
        vector_total[2][None],
        vector_total[3][None],
        vector_total[4][None],
        vector_total[4][None],
    )


F32 = jnp.float32
BF16 = jnp.bfloat16
LANES = 128


def swap(value, axis, bit):
    count = lax.axis_size(axis)
    return lax.ppermute(value, axis, [(source, source ^ bit) for source in range(count)])


def sum_over(value, axis):
    bit = 1
    while bit < lax.axis_size(axis):
        value = value + swap(value, axis, bit)
        bit *= 2
    return value


def place(part, axis, index, length):
    shape = list(part.shape)
    shape[axis] = length
    start = index * part.shape[axis]
    return lax.dynamic_update_slice_in_dim(jnp.zeros(shape, part.dtype), part, start, axis)


def take(value, axis, index, size):
    return lax.dynamic_slice_in_dim(value, index * size, size, axis)


def after(value, *others):
    return lax.optimization_barrier((value, *others))[0]


def gather_rows(block):
    half = block.shape[0] // 2
    across = swap(block, SECTION, 1)
    beside = swap(block, COL, 2)
    across, beside = lax.optimization_barrier((across, beside))
    corner = jnp.concatenate([swap(beside[:half], SECTION, 1), swap(across[half:], COL, 2)], axis=0)
    near = jnp.concatenate([block, beside], axis=0)
    far = jnp.concatenate([across, corner], axis=0)
    near_other, far_other = (swap(near, COL, 1), swap(far, COL, 1))
    return (near, near_other, far, far_other), across


def gather_pieces(shard):
    def send(value, pairs):
        return lax.ppermute(value, ROW, pairs)

    opposite = swap(shard, ROW, 2)
    behind = send(shard, [(0, 1), (1, 2), (2, 3)])
    ahead = send(shard, [(3, 2), (2, 1), (1, 0)])
    last = send(opposite, [(2, 3), (1, 0)])
    return shard, ahead, opposite, behind, last


def in_turn(pieces, row):
    shard, ahead, opposite, behind, last = pieces
    return (shard, jnp.where(row == 3, last, ahead), opposite, jnp.where(row == 0, last, behind))


def pair_sum(keep_ref, came_ref, start, size):
    rows = pl.ds(start, size)
    return keep_ref[rows, :].astype(F32) + came_ref[rows, :].astype(F32)


def first_sum_kernel(keep_ref, came_ref, across_ref, beside_ref):
    block = keep_ref.shape[0] // 4
    half = block // 2
    for ref, starts in (
        (across_ref, (2 * block, 3 * block)),
        (beside_ref, (block + half, 3 * block + half)),
    ):
        for place, start in enumerate(starts):
            ref[place * half : (place + 1) * half, :] = pair_sum(
                keep_ref, came_ref, start, half
            ).astype(BF16)


def second_sum_kernel(keep_ref, came_ref, across_ref, beside_ref, top_ref, low_ref, kept_ref):
    block = keep_ref.shape[0] // 4
    half = block // 2
    kept_ref[:half, :] = pair_sum(keep_ref, came_ref, 0, half) + across_ref[:half, :].astype(F32)
    kept_ref[half:, :] = (
        pair_sum(keep_ref, came_ref, half, half) + beside_ref[:half, :].astype(F32)
    )
    top = pair_sum(keep_ref, came_ref, block, half) + across_ref[half:, :].astype(F32)
    top_ref[...] = top.astype(BF16)
    low = pair_sum(keep_ref, came_ref, 2 * block + half, half) + beside_ref[half:, :].astype(F32)
    low_ref[...] = low.astype(BF16)


def column_call(kernel, width, ins, outs):
    tile = 512

    def spec(shape):
        lead = shape[:-1]
        return pl.BlockSpec(lead + (tile,), lambda i: (0,) * len(lead) + (i,))

    return pl.pallas_call(
        kernel,
        grid=(width // tile,),
        in_specs=[spec(member.shape) for member in ins],
        out_specs=[spec(member.shape) for member in outs],
        out_shape=outs,
        cost_estimate=cost(0, *ins, *outs),
    )(*ins)


def scatter_rows(product):
    sent = product(1)
    came = swap(sent, COL, 1)
    keep = product(0)
    rows, width = keep.shape
    block = rows // 4
    half = block // 2
    whole_block = jax.ShapeDtypeStruct((block, width), BF16)
    half_block = jax.ShapeDtypeStruct((half, width), BF16)
    across, beside = column_call(first_sum_kernel, width, [keep, came], [whole_block, whole_block])
    across = swap(across, SECTION, 1)
    beside = swap(beside, COL, 2)
    top, low, keep = column_call(
        second_sum_kernel,
        width,
        [keep, came, across, beside],
        [half_block, half_block, jax.ShapeDtypeStruct((block, width), F32)],
    )
    arrived = jnp.concatenate([swap(top, COL, 2), swap(low, SECTION, 1)], axis=0)
    return keep + arrived.astype(F32)


def turn(values, cosines, sines):
    lead = values[:, :LANES]
    lane = lax.broadcasted_iota(jnp.int32, lead.shape, 1)
    ahead = pltpu.roll(lead, LANES - ROT // 2, 1)
    behind = pltpu.roll(lead, ROT // 2, 1)
    lead = lead * cosines + jnp.where(lane < ROT // 2, ahead, behind) * sines
    return jnp.concatenate([lead, values[:, LANES:]], axis=1)


def mm(first_operand, second_operand):
    return jnp.dot(first_operand, second_operand, preferred_element_type=F32)


def project_kernel(x_ref, wq_ref, wk_ref, wv_ref, e_ref, cos_ref, sin_ref, q_ref, k_ref, v_ref):
    x, cosines, sines = (x_ref[...], cos_ref[...], sin_ref[...])
    queries = mm(x, wq_ref[...]) + e_ref[:, :HD]
    q_ref[...] = (turn(queries, cosines, sines) * HD ** (-0.5)).astype(BF16)
    keys_here = mm(x, wk_ref[...]) + e_ref[:, HD : 2 * HD]
    k_ref[...] = turn(keys_here, cosines, sines).astype(BF16)
    v_ref[...] = (mm(x, wv_ref[...]) + e_ref[:, 2 * HD :]).astype(BF16)


def inner_kernel(x_ref, w_ref, e_ref, held_ref, act_ref, slope_ref):
    inner = mm(x_ref[...], w_ref[...]) + e_ref[...]
    below = 0.5 + 0.5 * lax.erf(inner * 0.7071067811865476)
    act_ref[...] = (inner * below).astype(BF16)
    density = jnp.exp(-0.5 * inner * inner) * 0.3989422804014327
    slope_ref[...] = (below + inner * density).astype(BF16)


def piece_columns(row_ref, w_refs):
    width = w_refs[0].shape[1]
    for step, w_ref in enumerate(w_refs):
        place = lax.rem(row_ref[0] + step, len(w_refs))
        yield w_ref, pl.ds(pl.multiple_of(place * width, width), width)


def outer_kernel(row_ref, act_ref, w0_ref, w1_ref, w2_ref, w3_ref, out_ref):
    act = act_ref[...]
    for w_ref, columns in piece_columns(row_ref, (w0_ref, w1_ref, w2_ref, w3_ref)):
        out_ref[:, columns] = mm(act, w_ref[...]).astype(BF16)


def outer_back_kernel(count, row_ref, *refs):
    dys, (w0_ref, w1_ref, w2_ref, w3_ref, slope_ref) = (refs[:count], refs[count : count + 5])
    dz_ref, do_ref, sum_ref, dy_sum_ref, dy_ref = refs[-5:]
    inner = slope_ref.shape[1]
    dy = dys[0][...]
    for place, ref in enumerate(dys[1:], 1):
        start = place * (pl.num_programs(0) // count)
        dy = jnp.where(pl.program_id(0) >= start, ref[...], dy)
    dy_ref[...] = dy
    total = None
    for w_ref, columns in piece_columns(row_ref, (w0_ref, w1_ref, w2_ref, w3_ref)):
        part = contract_cols(dy_ref[:, columns], w_ref[...])
        total = part if total is None else total + part
    dz = (total[:, :inner] * slope_ref[...].astype(F32)).astype(BF16)
    dz_ref[...] = dz
    do_ref[...] = total[:, inner:].astype(BF16)

    @pl.when(pl.program_id(0) == 0)
    def _():
        sum_ref[...] = jnp.zeros_like(sum_ref)
        dy_sum_ref[...] = jnp.zeros_like(dy_sum_ref)

    sum_ref[...] += jnp.sum(dz.astype(F32), axis=0, keepdims=True)
    dy_sum_ref[...] += jnp.sum(dy.astype(F32), axis=0, keepdims=True)


def inward_kernel(dz_ref, wf_ref, wq_ref, wk_ref, wv_ref, out_ref):
    start = wf_ref.shape[1]
    total = contract_cols(dz_ref[:, :start], wf_ref[...])
    for w_ref in (wq_ref, wk_ref, wv_ref):
        total += contract_cols(dz_ref[:, start : start + HD], w_ref[...])
        start += HD
    out_ref[...] = total.astype(BF16)


def attend_kernel(q_ref, k_ref, v_ref, row_ref, col_ref, out_ref, log_ref):
    scores = contract_cols(q_ref[...], k_ref[...])
    scores = jnp.where(row_ref[...] >= col_ref[...], scores, -1e30)
    peak = jnp.max(scores, axis=1, keepdims=True)
    exponents = jnp.exp(scores - peak)
    total = jnp.sum(exponents, axis=1, keepdims=True)
    out_ref[...] = mm((exponents / total).astype(BF16), v_ref[...]).astype(BF16)
    log_ref[...] = peak + jnp.log(total)


def attend_back_kernel(
    first, q_ref, k_ref, v_ref, row_ref, col_ref, log_ref, do_ref, cos_ref, sin_ref, held_ref,
    all_ref, sum_ref, out_ref, dk_ref, dv_ref, sem,
):
    step = pl.program_id(1)
    block = q_ref.shape[0]

    @pl.when(step == 0)
    def _():
        dk_ref[...] = jnp.zeros_like(dk_ref)
        dv_ref[...] = jnp.zeros_like(dv_ref)

    @pl.when((step == 0) & (pl.program_id(0) == 0))
    def _():
        sum_ref[...] = jnp.zeros_like(sum_ref)

    def column_sum(values):
        return jnp.sum(values.astype(F32), axis=0, keepdims=True)

    queries, keys_all, grads = (q_ref[...], k_ref[...], do_ref[...])
    scores = contract_cols(queries, keys_all)
    scores = jnp.where(row_ref[...] >= col_ref[...], scores, -1e30)
    probs = jnp.exp(scores - log_ref[...])
    grad_probs = contract_cols(grads, v_ref[...])
    centre = jnp.sum(probs * grad_probs, axis=1, keepdims=True)
    grad_scores = (probs * (grad_probs - centre)).astype(BF16)
    rows = pl.ds(pl.multiple_of(step * block, block), block)
    cosines, sines = cos_ref[rows, :], sin_ref[rows, :]
    grad_queries = mm(grad_scores, keys_all) * HD ** (-0.5)
    grad_queries = turn(grad_queries, cosines, -sines).astype(BF16)
    out_ref[rows, :HD] = grad_queries
    sum_ref[:, :HD] += column_sum(grad_queries)
    dk_ref[...] += contract_rows(grad_scores, queries)
    dv_ref[...] += contract_rows(probs.astype(BF16), grads)

    @pl.when(step == pl.num_programs(1) - 1)
    def _():
        grad_keys = turn(dk_ref[...], cos_ref[...], -sin_ref[...]).astype(BF16)
        grad_values = dv_ref[...].astype(BF16)
        out_ref[:, HD : 2 * HD] = grad_keys
        out_ref[:, 2 * HD :] = grad_values
        sum_ref[:, HD : 2 * HD] += column_sum(grad_keys)
        sum_ref[:, 2 * HD :] += column_sum(grad_values)
        length, width = out_ref.shape
        micro = pl.ds(pl.multiple_of((first + pl.program_id(0)) * length, length), length)
        copy = pltpu.make_async_copy(
            out_ref, all_ref.at[micro, pl.ds(all_ref.shape[1] - width, width)], sem
        )
        copy.start()
        copy.wait()


ROW_BLOCK = 256


def by_rows(width, block=ROW_BLOCK):
    return pl.BlockSpec((block, width), lambda i: (i, 0))


def whole(shape):
    return pl.BlockSpec(shape, lambda *unused: (0,) * len(shape))


def panel(width, place):
    return lambda deep: pl.BlockSpec((deep, width), lambda *unused: (0, place))


def cost(flops, *arrays):
    return pl.CostEstimate(
        flops=flops,
        transcendentals=0,
        bytes_accessed=sum(math.prod(array.shape) * array.dtype.itemsize for array in arrays),
    )


def heads_panels(array, inner):
    return [panel(HD, inner // HD + part)(array.shape[0]) for part in range(3)]


def project(x, w, inner, e, tables):
    rows, width = x.shape
    per_micro = tables[0].shape[0] // ROW_BLOCK
    table = pl.BlockSpec((ROW_BLOCK, LANES), lambda i: (i % per_micro, 0))
    out = jax.ShapeDtypeStruct((rows, HD), BF16)
    return pl.pallas_call(
        project_kernel,
        grid=(rows // ROW_BLOCK,),
        in_specs=[by_rows(width), *heads_panels(w, inner), whole(e.shape), table, table],
        out_specs=[by_rows(HD)] * 3,
        out_shape=[out] * 3,
        cost_estimate=cost(6 * rows * width * HD, x, out, out, out),
        name="project",
    )(x, w, w, w, e, *tables)


def inner_layer(x, w, e, held):
    rows, width = x.shape
    inner = e.shape[1]
    slope = jax.ShapeDtypeStruct((rows, inner), BF16)
    return pl.pallas_call(
        inner_kernel,
        grid=(rows // ROW_BLOCK,),
        in_specs=[
            by_rows(width),
            panel(inner, 0)(width),
            whole(e.shape),
            pl.BlockSpec(memory_space=pl.ANY),
        ],
        out_specs=[by_rows(inner)] * 2,
        out_shape=[jax.ShapeDtypeStruct(held.shape, BF16), slope],
        input_output_aliases={3: 0},
        cost_estimate=cost(2 * rows * width * inner, x, slope, slope),
        name="inner",
    )(x, w, e, held)


def split_rows(width, other):
    return pl.BlockSpec((ROW_BLOCK, width), lambda i: (i // 2 * 4 + 2 * other + i % 2, 0))


def outer(act, pieces, row, other):
    rows, width = (act.shape[0] // 2, len(pieces) * pieces[0].shape[1])
    out = jax.ShapeDtypeStruct((rows, width), BF16)
    return pl.pallas_call(
        outer_kernel,
        grid=(rows // ROW_BLOCK,),
        in_specs=[
            pl.BlockSpec(memory_space=pltpu.SMEM),
            split_rows(act.shape[1], other),
            *(whole(piece.shape) for piece in pieces),
        ],
        out_specs=by_rows(width),
        out_shape=out,
        cost_estimate=cost(2 * rows * width * act.shape[1], act, out),
        name="outer",
    )(row, act, *pieces)


def inward(dz, w_in, w_qkv, offset, other):
    rows, width = (dz.shape[0] // 2, w_in.shape[0])
    out = jax.ShapeDtypeStruct((rows, width), BF16)
    return pl.pallas_call(
        inward_kernel,
        grid=(rows // ROW_BLOCK,),
        in_specs=[
            split_rows(dz.shape[1], other),
            panel(dz.shape[1] - 3 * HD, 0)(width),
            *heads_panels(w_qkv, offset),
        ],
        out_specs=by_rows(width),
        out_shape=out,
        cost_estimate=cost(2 * rows * width * dz.shape[1], dz, out),
        name="inward",
    )(dz, w_in, w_qkv, w_qkv, w_qkv)


def outer_back(dys, pieces, row, slopes, start=0, held=None):
    rows, width = (sum(dy.shape[0] for dy in dys), dys[0].shape[1])
    inner = slopes.shape[1]
    each, first = (dys[0].shape[0] // ROW_BLOCK, start // ROW_BLOCK)

    def part(place):
        return pl.BlockSpec(
            (ROW_BLOCK, width), lambda i: (jnp.clip(i - place * each, 0, each - 1), 0)
        )

    below = pl.BlockSpec((ROW_BLOCK, inner), lambda i: (first + i, 0))
    extra = () if held is None else (held,)
    return pl.pallas_call(
        functools.partial(outer_back_kernel, len(dys)),
        grid=(rows // ROW_BLOCK,),
        in_specs=[
            pl.BlockSpec(memory_space=pltpu.SMEM),
            *(part(place) for place in range(len(dys))),
            *(whole(piece.shape) for piece in pieces),
            below,
            *(pl.BlockSpec(memory_space=pl.ANY) for member in extra),
        ],
        out_specs=[below, by_rows(HD), whole((1, inner)), whole((1, width))],
        out_shape=[
            jax.ShapeDtypeStruct((slopes.shape[0], inner + 3 * HD), BF16),
            jax.ShapeDtypeStruct((rows, HD), BF16),
            jax.ShapeDtypeStruct((1, inner), F32),
            jax.ShapeDtypeStruct((1, width), F32),
        ],
        scratch_shapes=[pltpu.VMEM((ROW_BLOCK, width), BF16)],
        input_output_aliases={6 + len(dys): 0} if extra else {},
        cost_estimate=cost(2 * rows * width * (inner + HD), *dys, slopes),
        name="outer_back",
    )(row, *dys, *pieces, slopes, *extra)


def attend(queries, keys_all, values_all, places, inner):
    rows = queries.shape[0]
    length = places.shape[0]
    steps = length // ROW_BLOCK
    row = pl.BlockSpec((ROW_BLOCK, HD), lambda m, i: (m * steps + i, 0))
    every = pl.BlockSpec((length, HD), lambda m, i: (m, 0))
    return pl.pallas_call(
        attend_kernel,
        grid=(rows // length, steps),
        in_specs=[
            row,
            every,
            every,
            pl.BlockSpec((ROW_BLOCK, 1), lambda m, i: (i, 0)),
            pl.BlockSpec((1, length), lambda m, i: (0, 0)),
        ],
        out_specs=[
            pl.BlockSpec((ROW_BLOCK, HD), lambda m, i: (m * steps + i, inner // HD)),
            pl.BlockSpec((ROW_BLOCK, 1), lambda m, i: (m * steps + i, 0)),
        ],
        out_shape=[
            jax.ShapeDtypeStruct((rows, inner + HD), BF16),
            jax.ShapeDtypeStruct((rows, 1), F32),
        ],
        cost_estimate=cost(4 * rows * length * HD, queries, keys_all, values_all, queries),
        name="attend",
    )(queries, keys_all, values_all, places[:, None], places[None, :])


def attend_back(queries, keys_all, values_all, places, log_sums, grads, tables, held, first=0):
    rows = grads.shape[0]
    length = places.shape[0]
    steps = length // ROW_BLOCK
    row = pl.BlockSpec((ROW_BLOCK, HD), lambda m, i: ((first + m) * steps + i, 0))
    every = pl.BlockSpec((length, HD), lambda m, i: (first + m, 0))
    anywhere = pl.BlockSpec(memory_space=pl.ANY)
    return pl.pallas_call(
        functools.partial(attend_back_kernel, first),
        grid=(rows // length, steps),
        in_specs=[
            row,
            every,
            every,
            pl.BlockSpec((ROW_BLOCK, 1), lambda m, i: (i, 0)),
            pl.BlockSpec((1, length), lambda m, i: (0, 0)),
            pl.BlockSpec((ROW_BLOCK, 1), lambda m, i: ((first + m) * steps + i, 0)),
            pl.BlockSpec((ROW_BLOCK, HD), lambda m, i: (m * steps + i, 0)),
            whole(tables[0].shape),
            whole(tables[1].shape),
            anywhere,
        ],
        out_specs=[anywhere, whole((1, 3 * HD))],
        out_shape=[
            jax.ShapeDtypeStruct(held.shape, BF16),
            jax.ShapeDtypeStruct((1, 3 * HD), F32),
        ],
        scratch_shapes=[
            pltpu.VMEM((length, 3 * HD), BF16),
            pltpu.VMEM((length, HD), F32),
            pltpu.VMEM((length, HD), F32),
            pltpu.SemaphoreType.DMA,
        ],
        input_output_aliases={9: 0},
        cost_estimate=cost(10 * rows * length * HD, queries, keys_all, values_all, grads),
        name="attend_back",
    )(
        queries, keys_all, values_all, places[:, None], places[None, :], log_sums, grads, *tables,
        held,
    )


def local(
    inputs,
    cotangent,
    qkv_weight,
    qkv_bias,
    out_weight,
    fc_in_weight,
    fc_in_bias,
    fc_out_weight,
    norm1_gain,
    norm1_bias,
    norm2_gain,
    norm2_bias,
    out_bias,
    fc_out_bias,
):
    s, r, c = (lax.axis_index(SECTION), lax.axis_index(ROW), lax.axis_index(COL))
    rows_axis, cols_axis = (lax.axis_size(ROW), lax.axis_size(COL))
    low = s == 0
    qkv_w, out_w, fc_in_w, fc_out_w = (
        qkv_weight[0], out_weight[0], fc_in_weight[0], fc_out_weight[0],
    )
    deep, heads_here = qkv_w.shape[0], qkv_w.shape[1]
    per = 3 * HD
    inner = fc_in_w.shape[1] // 2
    model = inputs.shape[2]

    def both_layers(own_first, own_second):
        return (jnp.where(low, own_first, own_second), jnp.where(low, own_second, own_first))

    def trade(value, axis, *others):
        size = value.shape[axis] // 2
        kept = take(value, axis, s, size)
        came = swap(after(take(value, axis, 1 - s, size), *others), SECTION, 1)
        return kept, came

    def gathered(shard, axis):
        return lax.all_gather(shard, ROW, axis=axis, tiled=True)

    held = jnp.stack(
        [
            norm1_gain[0].astype(F32),
            norm1_bias[0].astype(F32),
            norm2_gain[0].astype(F32),
            norm2_bias[0].astype(F32),
            out_bias[0].astype(F32) + fc_out_bias[0].astype(F32),
        ]
    )
    held_both = jnp.stack([held, swap(held, SECTION, 1)])
    qkv_flat = qkv_w.reshape(deep, -1)
    qkv_half = trade(qkv_flat, 1, held_both)
    fc_in_half = trade(fc_in_w, 1, qkv_half[1])
    outs_kept = jnp.concatenate([take(fc_out_w, 0, s, inner), take(out_w, 0, s, HD)], axis=0)
    outs_sent = jnp.concatenate([take(fc_out_w, 0, 1 - s, inner), take(out_w, 0, 1 - s, HD)], axis=0)
    outs_came = swap(after(outs_sent, fc_in_half[1]), SECTION, 1)
    held_both = sum_over(place(held_both, 2, c, deep), COL)
    held = held_both[0]
    gain_one, shift_one, gain_two, shift_two, end_bias = (held[i] for i in range(5))
    gains = both_layers(held, held_both[1])

    def scaled_pair(half, row):
        return tuple(
            (part.astype(F32) * gain[row][:, None]).astype(BF16)
            for part, gain in zip(both_layers(*half), gains)
        )

    qkv_pair = scaled_pair(qkv_half, 0)
    fc_in_pair = scaled_pair(fc_in_half, 2)
    outs_pair = both_layers(outs_kept, outs_came)
    w_qkv0 = gathered(qkv_pair[0], 0)
    w_fc_in0 = gathered(fc_in_pair[0], 0)
    w_qkv1 = gathered(qkv_pair[1], 0)
    w_fc_in1 = gathered(fc_in_pair[1], 0)
    w_ins = ((w_fc_in0, w_qkv0), (w_fc_in1, w_qkv1))
    w_outs = [gather_pieces(outs_pair[layer]) for layer in range(2)]
    row = r.astype(jnp.int32)[None]

    own_qkv = mm(shift_one.astype(BF16)[None], qkv_flat)[0]
    own_fc = mm(shift_two.astype(BF16)[None], fc_in_w)[0]
    own_qkv = own_qkv + place(qkv_bias[0].astype(F32), 1, r, per).reshape(-1)
    own_fc = own_fc + place(fc_in_bias[0].astype(F32), 0, r, 2 * inner)
    biases = sum_over(
        jnp.concatenate([own_qkv, own_fc, place(end_bias, 0, r, model)]), ROW
    )
    biases = both_layers(biases, swap(biases, SECTION, 1))
    qkv_e, fc_e, end_e = ([], [], [])
    for member in biases:
        qkv_e.append(take(member[: 2 * per], 0, s, per)[None])
        fc_e.append(take(member[2 * per : 2 * per + 2 * inner], 0, s, inner)[None])
        end_e.append(member[2 * per + 2 * inner :])

    block_rows = inputs.shape[1]
    masks = jnp.array([0, 2, 1, 3], jnp.int32)
    places = ((c ^ masks)[:, None] * block_rows + jnp.arange(block_rows)[None]).reshape(-1)
    inverse = 10000.0 ** (-jnp.arange(0, ROT, 2).astype(F32) / ROT)
    angles = places.astype(F32)[:, None] * inverse[None]
    ones = jnp.ones((places.shape[0], LANES - ROT), F32)
    cosines, sines = (jnp.cos(angles), jnp.sin(angles))
    tables = (
        jnp.concatenate([cosines, cosines, ones], axis=1),
        jnp.concatenate([-sines, sines, 0.0 * ones], axis=1),
    )

    hidden = lax.dynamic_index_in_dim(inputs, s, 0, keepdims=False)
    seed = lax.dynamic_index_in_dim(cotangent, s, 0, keepdims=False)
    hidden = after(hidden, outs_came)

    hidden_list, kept_list, ends = ([], [], [])
    seed_rows = None
    for layer in range(2):
        hidden_list.append(hidden)
        scaled, unused = norm_rows(hidden.astype(F32))
        x, unused = gather_rows(scaled.astype(BF16))
        x = jnp.concatenate(x, axis=0)
        if layer == 0:
            seed_rows, unused = gather_rows(after(seed, x))
            seed_rows = jnp.concatenate(seed_rows, axis=0)
        w_fc_in, w_qkv = w_ins[layer]
        queries, keys_all, values_all = project(x, w_qkv, 0, qkv_e[layer], tables)
        attended, log_sums = attend(queries, keys_all, values_all, places, inner)
        act, slopes = inner_layer(x, w_fc_in, fc_e[layer], attended)
        if layer == 0:
            *pieces, act, unused = lax.optimization_barrier((*w_outs[0][1:], act, seed_rows))
            w_outs[0] = in_turn((w_outs[0][0], *pieces), r)
        kept = (x, queries, keys_all, values_all, log_sums, slopes, act)
        if layer == 1:
            outs_grad1 = contract_rows(act, seed_rows).astype(BF16)
            seed_rows = after(seed_rows, outs_grad1)
            *pieces, unused = lax.optimization_barrier((*w_outs[1][1:], outs_grad1))
            w_outs[1] = in_turn((w_outs[1][0], *pieces), r)
        kept_list.append(kept)
        if layer == 0:
            summed = scatter_rows(lambda other: outer(act, w_outs[0], row, other))
            hidden = (hidden.astype(F32) + summed + end_e[layer]).astype(BF16)
            ends.append(hidden)
            middle = swap(hidden, SECTION, 1)

    def reduced(value, axis):
        return lax.psum_scatter(value, ROW, scatter_dimension=axis, tiled=True)

    outs_part1 = reduced(outs_grad1, 1)
    grads = seed
    ins_list, small_list = ([None, None], [None, None])
    for layer in (1, 0):
        x, queries, keys_all, values_all, log_sums, slopes, act = kept_list[layer]
        w_fc_in, w_qkv = w_ins[layer]
        if layer == 1:
            dy = seed_rows
        else:
            dys, across = gather_rows(grads)
            dy = jnp.concatenate(lax.optimization_barrier(dys), axis=0)
            middle_grads = (jnp.where(low, grads, across), jnp.where(low, across, grads))
        halves = ((dy,),) if layer == 1 else (dys[:2], dys[2:])
        dz, start, column_sums = (None, 0, [])
        for half in halves:
            dz, grad_attended, inner_sum, dy_sum = outer_back(
                half, w_outs[layer], row, slopes, start, dz
            )
            dz, heads_sum = attend_back(
                queries, keys_all, values_all, places, log_sums, grad_attended, tables, dz,
                start // places.shape[0],
            )
            start += grad_attended.shape[0]
            column_sums.append((heads_sum[0], inner_sum[0], dy_sum[0]))
        combined = scatter_rows(lambda other: inward(dz, w_fc_in, w_qkv, 0, other))
        ins_grad = contract_rows(x, dz).astype(BF16)
        ins_list[layer] = reduced(ins_grad, 0)
        scaled, inverse_std = norm_rows(hidden_list[layer].astype(F32))
        grad_norm = inverse_std * (
            combined
            - jnp.mean(combined, axis=-1, keepdims=True)
            - scaled * jnp.mean(combined * scaled, axis=-1, keepdims=True)
        )
        grads = (grads.astype(F32) + grad_norm).astype(BF16)
        small_list[layer] = tuple(sum(members) for members in zip(*column_sums))
        if layer == 0:
            fc_out_part0 = reduced(contract_rows(act[:, :inner], dy).astype(BF16), 1)
            out_part0 = reduced(contract_rows(act[:, inner:], dy).astype(BF16), 1)
    act = kept_list[1][-1]
    summed = scatter_rows(lambda other: outer(act, w_outs[1], row, other))
    summed = after(summed, small_list[0][0])
    ends.append((hidden_list[1].astype(F32) + summed + end_e[1]).astype(BF16))

    def to_owner(first, second, upper, lower):
        return (jnp.where(low, first, lower), jnp.where(low, upper, second))

    def to_first(value):
        return lax.ppermute(value, SECTION, [(1, 0)])

    def to_second(value):
        return lax.ppermute(value, SECTION, [(0, 1)])

    small = sum_over(
        jnp.concatenate(
            [*small_list[0][:2], *small_list[1][:2], small_list[0][2], small_list[1][2]]
        ),
        ROW,
    )
    sums = small[: 2 * (per + inner)]
    sums_other = swap(sums, SECTION, 1)
    smalls = to_owner(*jnp.split(sums, 2), *jnp.split(sums_other, 2))
    end_grad = jnp.where(low, *jnp.split(small[2 * (per + inner) :], 2))
    qkv_b_grad = jnp.concatenate([member[:per] for member in smalls])
    fc_in_b_grad = jnp.concatenate([member[per:] for member in smalls])
    outs_lower = to_second(outs_part1)
    ins_lower = to_second(ins_list[1])
    ins_upper = to_first(ins_list[0])
    ins_g = to_owner(*ins_list, ins_upper, ins_lower)
    qkv_g = jnp.concatenate([member[:, inner:] for member in ins_g], axis=1).astype(F32)
    fc_in_g = jnp.concatenate([member[:, :inner] for member in ins_g], axis=1).astype(F32)
    qkv_w_grad = gain_one[:, None] * qkv_g + shift_one[:, None] * qkv_b_grad[None]
    fc_in_w_grad = gain_two[:, None] * fc_in_g + shift_two[:, None] * fc_in_b_grad[None]
    norm_parts = []
    for layer, (w_q, w_f) in enumerate(zip(both_layers(*qkv_half), both_layers(*fc_in_half))):
        w_q, w_f = (w_q.astype(F32), w_f.astype(F32))
        heads, hidden_sum = jnp.split(sums[layer * (per + inner) :][: per + inner], [per])
        part = ins_list[layer].astype(F32)
        norm_parts.append(
            jnp.stack(
                [
                    jnp.sum(w_q * part[:, inner:], axis=1),
                    jnp.sum(w_q * heads[None], axis=1),
                    jnp.sum(w_f * part[:, :inner], axis=1),
                    jnp.sum(w_f * hidden_sum[None], axis=1),
                ]
            )
        )
    norms = jnp.where(low, *norm_parts) + swap(jnp.where(low, *norm_parts[::-1]), SECTION, 1)
    norms = take(sum_over(norms, COL), 1, c, deep // cols_axis)
    end_grad = take(end_grad, 0, r * cols_axis + c, deep // cols_axis)
    fc_out_part0 = after(fc_out_part0, ins_upper, norms)
    fc_out_upper = to_first(fc_out_part0)
    fc_out_w_grad = jnp.concatenate(
        [
            jnp.where(low, fc_out_part0, outs_lower[:inner]),
            jnp.where(low, fc_out_upper, outs_part1[:inner]),
        ],
        axis=0,
    ).astype(F32)[None]
    qkv_w_grad = qkv_w_grad.reshape(qkv_w.shape)[None]
    fc_in_w_grad = fc_in_w_grad[None]
    out_part0, fc_out_w_grad, norms = lax.optimization_barrier(
        (out_part0, fc_out_w_grad, norms)
    )
    out_upper = to_first(out_part0)
    out_w_grad = jnp.concatenate(
        [
            jnp.where(low, out_part0, outs_lower[inner:]),
            jnp.where(low, out_upper, outs_part1[inner:]),
        ],
        axis=0,
    ).astype(F32)
    last = to_second(ends[1])
    first = to_first(grads)
    last, first = (after(last, norms), after(first, norms))
    layer_outputs = jnp.stack([jnp.where(low, ends[0], last), jnp.where(low, middle, ends[1])])
    input_gradients = jnp.stack(
        [jnp.where(low, grads, middle_grads[0]), jnp.where(low, first, middle_grads[1])]
    )
    return (
        layer_outputs[None],
        input_gradients[None],
        qkv_w_grad,
        take(qkv_b_grad.reshape(heads_here, -1), 1, r, per // rows_axis)[None],
        out_w_grad[None],
        fc_in_w_grad,
        take(fc_in_b_grad, 0, r, 2 * inner // rows_axis)[None],
        fc_out_w_grad,
        norms[0][None],
        norms[1][None],
        norms[2][None],
        norms[3][None],
        end_grad[None],
        end_grad[None],
    )


def all_of_it(*arrays):
    return local(*arrays)


def solution(mesh):
    sizes = mesh.shape
    paired = sizes[SECTION] == 2 and sizes[COL] == 4
    body = all_of_it if paired and sizes[ROW] == 4 else relay_local
    step = jax.shard_map(
        body,
        mesh=mesh,
        in_specs=(
            P(None, (ROW, COL), None),
            P(None, (ROW, COL), None),
            P(SECTION, ROW, COL, None),
            P(SECTION, COL, ROW),
            P(SECTION, COL, ROW),
            P(SECTION, ROW, COL),
            P(SECTION, (COL, ROW)),
            P(SECTION, COL, ROW),
            P(SECTION, (ROW, COL)),
            P(SECTION, (ROW, COL)),
            P(SECTION, (ROW, COL)),
            P(SECTION, (ROW, COL)),
            P(SECTION, (ROW, COL)),
            P(SECTION, (ROW, COL)),
        ),
        out_specs=(
            P(SECTION, None, (ROW, COL), None),
            P(SECTION, None, (ROW, COL), None),
            P(SECTION, ROW, COL, None),
            P(SECTION, COL, ROW),
            P(SECTION, COL, ROW),
            P(SECTION, ROW, COL),
            P(SECTION, (COL, ROW)),
            P(SECTION, COL, ROW),
            P(SECTION, (ROW, COL)),
            P(SECTION, (ROW, COL)),
            P(SECTION, (ROW, COL)),
            P(SECTION, (ROW, COL)),
            P(SECTION, (ROW, COL)),
            P(SECTION, (ROW, COL)),
        ),
        check_vma=False,
    )
    if body is relay_local:
        return step
    return step
```

```python
import functools
import math

import jax
import jax.numpy as jnp
from jax import lax
from jax.experimental import pallas as pl
from jax.experimental.pallas import tpu as pltpu
from jax.sharding import PartitionSpec as P


SECTION, ROW, COL = ("section", "row", "col")
HD = 256
ROT = 64
SEQ_LEN = 1024


def from_behind(value, axis, steps):
    count = lax.axis_size(axis)
    initial, last = (max(0, -steps), min(count, count - steps))
    return lax.ppermute(value, axis, [(source, source + steps) for source in range(initial, last)])


def rotary_tables(length):
    positions = jnp.arange(length).astype(jnp.float32)
    inverse = 10000.0 ** (-jnp.arange(0, ROT, 2).astype(jnp.float32) / ROT)
    angles = positions[:, None] * inverse[None, :]
    angles = jnp.concatenate([angles, angles], axis=-1)
    return (jnp.cos(angles)[:, None, :], jnp.sin(angles)[:, None, :])


def rotate(values, cosines, sines):
    half_rot = ROT // 2
    turned = values[..., :ROT]
    first_half = turned[..., :half_rot]
    second_half = turned[..., half_rot:]
    swapped = jnp.concatenate([-second_half, first_half], axis=-1)
    return jnp.concatenate([turned * cosines + swapped * sines, values[..., ROT:]], axis=-1)


def rotate_back(grads, cosines, sines):

    def turn_values(values):
        return rotate(values, cosines, sines)

    _, turn_pull = jax.vjp(turn_values, grads)
    return turn_pull(grads)[0]


def gelu_exact(values):
    return jax.nn.gelu(values, approximate=False)


def norm_rows(row_values):
    centred = row_values - jnp.mean(row_values, axis=-1, keepdims=True)
    inverse_std = lax.rsqrt(jnp.mean(centred * centred, axis=-1, keepdims=True) + 1e-05)
    return (centred * inverse_std, inverse_std)


def contract_rows(first_operand, second_operand):
    return lax.dot_general(
        first_operand, second_operand, (((0,), (0,)), ((), ())), preferred_element_type=jnp.float32
    )


def contract_cols(first_operand, second_operand):
    return lax.dot_general(
        first_operand, second_operand, (((1,), (1,)), ((), ())), preferred_element_type=jnp.float32
    )


def causal_block(row_start, block_rows, row_stop):
    query_pos = row_start + lax.broadcasted_iota(jnp.int32, (block_rows, row_stop), 0)
    key_pos = lax.broadcasted_iota(jnp.int32, (block_rows, row_stop), 1)
    return query_pos >= key_pos


def attention_forward(queries, keys_all, values_all):
    length = queries.shape[0]
    block_rows = min(512, length)
    score_scale = HD ** (-0.5)
    outputs_list = []
    sums_list = []
    for block_index in range(length // block_rows):
        row_start = block_index * block_rows
        row_stop = row_start + block_rows
        scores = (
            jnp.einsum(
                "qhd,khd->hqk",
                queries[row_start:row_stop],
                keys_all[:row_stop],
                preferred_element_type=jnp.float32,
            )
            * score_scale
        )
        scores = jnp.where(causal_block(row_start, block_rows, row_stop)[None], scores, -1e30)
        row_peak = jnp.max(scores, axis=-1, keepdims=True)
        exponents = jnp.exp(scores - row_peak)
        row_total = jnp.sum(exponents, axis=-1, keepdims=True)
        attention_probs = (exponents / row_total).astype(jnp.bfloat16)
        outputs_list.append(
            jnp.einsum(
                "hqk,khd->qhd",
                attention_probs,
                values_all[:row_stop],
                preferred_element_type=jnp.float32,
            )
        )
        sums_list.append((row_peak + jnp.log(row_total))[..., 0])
    attended = jnp.concatenate(outputs_list, axis=0).astype(jnp.bfloat16).reshape(length, -1)
    return (attended, jnp.concatenate(sums_list, axis=1))


def attention_backward(queries, keys_all, values_all, log_sums, grad_attended):
    length, heads_here = (queries.shape[0], queries.shape[1])
    block_rows = min(512, length)
    score_scale = HD ** (-0.5)
    grad_out = grad_attended.reshape(length, heads_here, HD)
    grad_queries_list = []
    grad_keys = jnp.zeros(queries.shape, jnp.float32)
    grad_values = jnp.zeros(queries.shape, jnp.float32)
    for block_index in range(length // block_rows):
        row_start = block_index * block_rows
        row_stop = row_start + block_rows
        scores = (
            jnp.einsum(
                "qhd,khd->hqk",
                queries[row_start:row_stop],
                keys_all[:row_stop],
                preferred_element_type=jnp.float32,
            )
            * score_scale
        )
        scores = jnp.where(causal_block(row_start, block_rows, row_stop)[None], scores, -1e30)
        attention_probs = jnp.exp(scores - log_sums[:, row_start:row_stop, None])
        low_probs = attention_probs.astype(jnp.bfloat16)
        grad_probs = jnp.einsum(
            "qhd,khd->hqk",
            grad_out[row_start:row_stop],
            values_all[:row_stop],
            preferred_element_type=jnp.float32,
        )
        centre_term = jnp.sum(attention_probs * grad_probs, axis=-1, keepdims=True)
        grad_scores = (attention_probs * (grad_probs - centre_term)).astype(jnp.bfloat16)
        grad_queries_list.append(
            jnp.einsum(
                "hqk,khd->qhd", grad_scores, keys_all[:row_stop], preferred_element_type=jnp.float32
            )
            * score_scale
        )
        grad_keys = grad_keys.at[:row_stop].add(
            jnp.einsum(
                "hqk,qhd->khd",
                grad_scores,
                queries[row_start:row_stop],
                preferred_element_type=jnp.float32,
            )
            * score_scale
        )
        grad_values = grad_values.at[:row_stop].add(
            jnp.einsum(
                "hqk,qhd->khd",
                low_probs,
                grad_out[row_start:row_stop],
                preferred_element_type=jnp.float32,
            )
        )
    return (jnp.concatenate(grad_queries_list, axis=0), grad_keys, grad_values)


def forward_turn(my_rows, weights, vectors, cosines, sines):
    qkv_w, qkv_b, out_w, fc_in_w, fc_in_b, fc_out_w = weights
    gain_one, bias_one, gain_two, bias_two, out_b, fc_out_b = vectors
    gathered = lax.all_gather(my_rows, COL, axis=0, tiled=True)
    scaled, _ = norm_rows(gathered.astype(jnp.float32))
    normed_one = (scaled * gain_one + bias_one).astype(jnp.bfloat16)
    normed_two = (scaled * gain_two + bias_two).astype(jnp.bfloat16)
    length = gathered.shape[0]
    heads_here = qkv_w.shape[1]
    projected = jnp.dot(
        normed_one, qkv_w.reshape(qkv_w.shape[0], -1), preferred_element_type=jnp.float32
    ) + qkv_b.reshape(-1).astype(jnp.float32)
    projected = projected.reshape(length, heads_here, 3, HD)
    queries = rotate(projected[:, :, 0], cosines, sines).astype(jnp.bfloat16)
    keys_all = rotate(projected[:, :, 1], cosines, sines).astype(jnp.bfloat16)
    values_all = projected[:, :, 2].astype(jnp.bfloat16)
    attended, log_sums = attention_forward(queries, keys_all, values_all)
    inner_act = jnp.dot(normed_two, fc_in_w, preferred_element_type=jnp.float32) + fc_in_b.astype(
        jnp.float32
    )
    activated = gelu_exact(inner_act).astype(jnp.bfloat16)
    summed = lax.psum_scatter(
        jnp.dot(attended, out_w, preferred_element_type=jnp.float32)
        + jnp.dot(activated, fc_out_w, preferred_element_type=jnp.float32),
        COL,
        scatter_dimension=0,
        tiled=True,
    )
    output = (my_rows.astype(jnp.float32) + summed + out_b + fc_out_b).astype(jnp.bfloat16)
    kept_values = (
        gathered,
        normed_one,
        normed_two,
        queries,
        keys_all,
        values_all,
        attended,
        log_sums,
        inner_act,
    )
    return (output, kept_values)


def backward_turn(grad_rows, kept_values, weights, vectors, cosines, sines):
    (
        gathered,
        normed_one,
        normed_two,
        queries,
        keys_all,
        values_all,
        attended,
        log_sums,
        inner_act,
    ) = kept_values
    qkv_w, qkv_b, out_w, fc_in_w, _, fc_out_w = weights
    gain_one, _, gain_two, _, _, _ = vectors
    grad_full = lax.all_gather(grad_rows, COL, axis=0, tiled=True)
    length = grad_full.shape[0]
    rows_here = grad_rows.shape[0]
    own_start = lax.axis_index(COL) * rows_here
    activated = gelu_exact(inner_act).astype(jnp.bfloat16)
    out_w_grad = contract_rows(attended, grad_full)
    fc_out_w_grad = contract_rows(activated, grad_full)
    grad_attended = contract_cols(grad_full, out_w).astype(jnp.bfloat16)
    grad_activated = contract_cols(grad_full, fc_out_w)
    _, gelu_pull = jax.vjp(gelu_exact, inner_act)
    grad_inner = gelu_pull(grad_activated)[0].astype(jnp.bfloat16)
    grad_queries, grad_keys, grad_values = attention_backward(
        queries, keys_all, values_all, log_sums, grad_attended
    )
    grad_q_pre = rotate_back(grad_queries, cosines, sines)
    grad_k_pre = rotate_back(grad_keys, cosines, sines)
    grad_projected = (
        jnp.stack([grad_q_pre, grad_k_pre, grad_values], axis=2)
        .astype(jnp.bfloat16)
        .reshape(length, -1)
    )
    qkv_flat = qkv_w.reshape(qkv_w.shape[0], -1)
    qkv_w_grad = contract_rows(normed_one, grad_projected).reshape(qkv_w.shape)
    qkv_b_grad = jnp.sum(grad_projected.astype(jnp.float32), axis=0).reshape(qkv_b.shape)
    fc_in_w_grad = contract_rows(normed_two, grad_inner)
    fc_in_b_grad = jnp.sum(grad_inner.astype(jnp.float32), axis=0)
    width = qkv_w.shape[0]
    scaled_full, inverse_full = norm_rows(gathered.astype(jnp.float32))
    scaled = lax.dynamic_slice_in_dim(scaled_full, own_start, rows_here, 0)
    inverse_std = lax.dynamic_slice_in_dim(inverse_full, own_start, rows_here, 0)
    dy_sum = jnp.sum(grad_rows.astype(jnp.float32), axis=0)
    both_grads = lax.psum_scatter(
        jnp.concatenate(
            [contract_cols(grad_projected, qkv_flat), contract_cols(grad_inner, fc_in_w)], axis=1
        ),
        COL,
        scatter_dimension=0,
        tiled=True,
    )
    grad_one = both_grads[:, :width]
    grad_two = both_grads[:, width:]
    combined = gain_one * grad_one + gain_two * grad_two
    vector_grads = (
        jnp.sum(grad_one * scaled, axis=0),
        jnp.sum(grad_one, axis=0),
        jnp.sum(grad_two * scaled, axis=0),
        jnp.sum(grad_two, axis=0),
        dy_sum,
    )
    grad_norm = inverse_std * (
        combined
        - jnp.mean(combined, axis=-1, keepdims=True)
        - scaled * jnp.mean(combined * scaled, axis=-1, keepdims=True)
    )
    grad_input = (grad_rows.astype(jnp.float32) + grad_norm).astype(jnp.bfloat16)
    matrix_grads = (qkv_w_grad, qkv_b_grad, out_w_grad, fc_in_w_grad, fc_in_b_grad, fc_out_w_grad)
    return (grad_input, matrix_grads, vector_grads)


def add_tuples(running, addend):
    if running is None:
        return addend
    return tuple((first_part + second_part for first_part, second_part in zip(running, addend)))


def relay_local(
    inputs,
    cotangent,
    qkv_weight,
    qkv_bias,
    out_weight,
    fc_in_weight,
    fc_in_bias,
    fc_out_weight,
    norm1_gain,
    norm1_bias,
    norm2_gain,
    norm2_bias,
    out_bias,
    fc_out_bias,
):
    sections = lax.axis_size(SECTION)
    section_index = lax.axis_index(SECTION)
    micro_count = inputs.shape[0]
    tick_count = micro_count + sections - 1
    is_first = section_index == 0
    is_last = section_index == sections - 1
    cosines, sines = rotary_tables(SEQ_LEN)
    vectors = (
        lax.all_gather(norm1_gain[0], (ROW, COL), axis=0, tiled=True),
        lax.all_gather(norm1_bias[0], (ROW, COL), axis=0, tiled=True),
        lax.all_gather(norm2_gain[0], (ROW, COL), axis=0, tiled=True),
        lax.all_gather(norm2_bias[0], (ROW, COL), axis=0, tiled=True),
        lax.all_gather(out_bias[0], (ROW, COL), axis=0, tiled=True),
        lax.all_gather(fc_out_bias[0], (ROW, COL), axis=0, tiled=True),
    )
    vectors = tuple((member.astype(jnp.float32) for member in vectors))
    received = jnp.zeros_like(inputs[0])
    outputs_list = []
    kept_list = []
    for tick_index in range(tick_count):
        weights = (
            lax.all_gather(qkv_weight[0], ROW, axis=0, tiled=True),
            lax.all_gather(qkv_bias[0], ROW, axis=1, tiled=True),
            lax.all_gather(out_weight[0], ROW, axis=1, tiled=True),
            lax.all_gather(fc_in_weight[0], ROW, axis=0, tiled=True),
            lax.all_gather(fc_in_bias[0], ROW, axis=0, tiled=True),
            lax.all_gather(fc_out_weight[0], ROW, axis=1, tiled=True),
        )
        first_rows = inputs[min(tick_index, micro_count - 1)]
        my_rows = jnp.where(is_first, first_rows, received)
        output, kept_values = forward_turn(my_rows, weights, vectors, cosines, sines)
        outputs_list.append(output)
        kept_list.append(kept_values)
        if tick_index + 1 < tick_count:
            received = from_behind(output, SECTION, 1)
    layer_outputs = lax.dynamic_slice_in_dim(jnp.stack(outputs_list), section_index, micro_count, 0)
    stacked_kept = tuple((jnp.stack(members) for members in zip(*kept_list)))
    received_grad = jnp.zeros_like(inputs[0])
    grads_list = []
    matrix_total = None
    vector_total = None
    for tick_index in range(tick_count):
        weights = (
            lax.all_gather(qkv_weight[0], ROW, axis=0, tiled=True),
            lax.all_gather(qkv_bias[0], ROW, axis=1, tiled=True),
            lax.all_gather(out_weight[0], ROW, axis=1, tiled=True),
            lax.all_gather(fc_in_weight[0], ROW, axis=0, tiled=True),
            lax.all_gather(fc_in_bias[0], ROW, axis=0, tiled=True),
            lax.all_gather(fc_out_weight[0], ROW, axis=1, tiled=True),
        )
        if tick_index < micro_count:
            seed_grad = cotangent[tick_index]
        else:
            seed_grad = jnp.zeros_like(cotangent[0])
        grad_rows = jnp.where(is_last, seed_grad, received_grad)
        forward_index = jnp.clip(tick_index - sections + 1 + 2 * section_index, 0, tick_count - 1)
        kept_values = tuple(
            (
                lax.dynamic_index_in_dim(member, forward_index, 0, keepdims=False)
                for member in stacked_kept
            )
        )
        grad_input, matrix_grads, vector_grads = backward_turn(
            grad_rows, kept_values, weights, vectors, cosines, sines
        )
        grads_list.append(grad_input)
        if tick_index + 1 < tick_count:
            received_grad = from_behind(grad_input, SECTION, -1)
        matrix_part = (
            lax.psum_scatter(matrix_grads[0], ROW, scatter_dimension=0, tiled=True),
            lax.psum_scatter(matrix_grads[1], ROW, scatter_dimension=1, tiled=True),
            lax.psum_scatter(matrix_grads[2], ROW, scatter_dimension=1, tiled=True),
            lax.psum_scatter(matrix_grads[3], ROW, scatter_dimension=0, tiled=True),
            lax.psum_scatter(matrix_grads[4], ROW, scatter_dimension=0, tiled=True),
            lax.psum_scatter(matrix_grads[5], ROW, scatter_dimension=1, tiled=True),
        )
        vector_part = (
            lax.psum_scatter(vector_grads[0], (ROW, COL), scatter_dimension=0, tiled=True),
            lax.psum_scatter(vector_grads[1], (ROW, COL), scatter_dimension=0, tiled=True),
            lax.psum_scatter(vector_grads[2], (ROW, COL), scatter_dimension=0, tiled=True),
            lax.psum_scatter(vector_grads[3], (ROW, COL), scatter_dimension=0, tiled=True),
            lax.psum_scatter(vector_grads[4], (ROW, COL), scatter_dimension=0, tiled=True),
        )
        matrix_total = add_tuples(matrix_total, tuple(matrix_part))
        vector_total = add_tuples(vector_total, tuple(vector_part))
    input_gradients = lax.dynamic_slice_in_dim(
        jnp.stack(grads_list), sections - 1 - section_index, micro_count, 0
    )
    return (
        layer_outputs[None],
        input_gradients[None],
        matrix_total[0][None],
        matrix_total[1][None],
        matrix_total[2][None],
        matrix_total[3][None],
        matrix_total[4][None],
        matrix_total[5][None],
        vector_total[0][None],
        vector_total[1][None],
        vector_total[2][None],
        vector_total[3][None],
        vector_total[4][None],
        vector_total[4][None],
    )


F32 = jnp.float32
BF16 = jnp.bfloat16
LANES = 128


def swap(value, axis, bit):
    count = lax.axis_size(axis)
    return lax.ppermute(value, axis, [(source, source ^ bit) for source in range(count)])


def sum_over(value, axis):
    bit = 1
    while bit < lax.axis_size(axis):
        value = value + swap(value, axis, bit)
        bit *= 2
    return value


def place(part, axis, index, length):
    shape = list(part.shape)
    shape[axis] = length
    start = index * part.shape[axis]
    return lax.dynamic_update_slice_in_dim(jnp.zeros(shape, part.dtype), part, start, axis)


def take(value, axis, index, size):
    return lax.dynamic_slice_in_dim(value, index * size, size, axis)


def after(value, *others):
    return lax.optimization_barrier((value, *others))[0]


def gather_rows(block):
    half = block.shape[0] // 2
    across = swap(block, SECTION, 1)
    beside = swap(block, COL, 2)
    across, beside = lax.optimization_barrier((across, beside))
    corner = jnp.concatenate([swap(beside[:half], SECTION, 1), swap(across[half:], COL, 2)], axis=0)
    near = jnp.concatenate([block, beside], axis=0)
    far = jnp.concatenate([across, corner], axis=0)
    near_other, far_other = (swap(near, COL, 1), swap(far, COL, 1))
    return (near, near_other, far, far_other), across


def gather_pieces(shard):
    def send(value, pairs):
        return lax.ppermute(value, ROW, pairs)

    opposite = swap(shard, ROW, 2)
    behind = send(shard, [(0, 1), (1, 2), (2, 3)])
    ahead = send(shard, [(3, 2), (2, 1), (1, 0)])
    last = send(opposite, [(2, 3), (1, 0)])
    return shard, ahead, opposite, behind, last


def in_turn(pieces, row):
    shard, ahead, opposite, behind, last = pieces
    return (shard, jnp.where(row == 3, last, ahead), opposite, jnp.where(row == 0, last, behind))


def pair_sum(keep_ref, came_ref, start, size):
    rows = pl.ds(start, size)
    return keep_ref[rows, :].astype(F32) + came_ref[rows, :].astype(F32)


def first_sum_kernel(keep_ref, came_ref, across_ref, beside_ref):
    block = keep_ref.shape[0] // 4
    half = block // 2
    for ref, starts in (
        (across_ref, (2 * block, 3 * block)),
        (beside_ref, (block + half, 3 * block + half)),
    ):
        for place, start in enumerate(starts):
            ref[place * half : (place + 1) * half, :] = pair_sum(
                keep_ref, came_ref, start, half
            ).astype(BF16)


def second_sum_kernel(keep_ref, came_ref, across_ref, beside_ref, top_ref, low_ref, kept_ref):
    block = keep_ref.shape[0] // 4
    half = block // 2
    kept_ref[:half, :] = pair_sum(keep_ref, came_ref, 0, half) + across_ref[:half, :].astype(F32)
    kept_ref[half:, :] = (
        pair_sum(keep_ref, came_ref, half, half) + beside_ref[:half, :].astype(F32)
    )
    top = pair_sum(keep_ref, came_ref, block, half) + across_ref[half:, :].astype(F32)
    top_ref[...] = top.astype(BF16)
    low = pair_sum(keep_ref, came_ref, 2 * block + half, half) + beside_ref[half:, :].astype(F32)
    low_ref[...] = low.astype(BF16)


def column_call(kernel, width, ins, outs):
    tile = 512

    def spec(shape):
        lead = shape[:-1]
        return pl.BlockSpec(lead + (tile,), lambda i: (0,) * len(lead) + (i,))

    return pl.pallas_call(
        kernel,
        grid=(width // tile,),
        in_specs=[spec(member.shape) for member in ins],
        out_specs=[spec(member.shape) for member in outs],
        out_shape=outs,
        cost_estimate=cost(0, *ins, *outs),
    )(*ins)


def scatter_rows(product):
    sent = product(1)
    came = swap(sent, COL, 1)
    keep = product(0)
    rows, width = keep.shape
    block = rows // 4
    half = block // 2
    whole_block = jax.ShapeDtypeStruct((block, width), BF16)
    half_block = jax.ShapeDtypeStruct((half, width), BF16)
    across, beside = column_call(first_sum_kernel, width, [keep, came], [whole_block, whole_block])
    across = swap(across, SECTION, 1)
    beside = swap(beside, COL, 2)
    top, low, keep = column_call(
        second_sum_kernel,
        width,
        [keep, came, across, beside],
        [half_block, half_block, jax.ShapeDtypeStruct((block, width), F32)],
    )
    arrived = jnp.concatenate([swap(top, COL, 2), swap(low, SECTION, 1)], axis=0)
    return keep + arrived.astype(F32)


def turn(values, cosines, sines):
    lead = values[:, :LANES]
    lane = lax.broadcasted_iota(jnp.int32, lead.shape, 1)
    ahead = pltpu.roll(lead, LANES - ROT // 2, 1)
    behind = pltpu.roll(lead, ROT // 2, 1)
    lead = lead * cosines + jnp.where(lane < ROT // 2, ahead, behind) * sines
    return jnp.concatenate([lead, values[:, LANES:]], axis=1)


def mm(first_operand, second_operand):
    return jnp.dot(first_operand, second_operand, preferred_element_type=F32)


def project_kernel(x_ref, wq_ref, wk_ref, wv_ref, e_ref, cos_ref, sin_ref, q_ref, k_ref, v_ref):
    x, cosines, sines = (x_ref[...], cos_ref[...], sin_ref[...])
    queries = mm(x, wq_ref[...]) + e_ref[:, :HD]
    q_ref[...] = (turn(queries, cosines, sines) * HD ** (-0.5)).astype(BF16)
    keys_here = mm(x, wk_ref[...]) + e_ref[:, HD : 2 * HD]
    k_ref[...] = turn(keys_here, cosines, sines).astype(BF16)
    v_ref[...] = (mm(x, wv_ref[...]) + e_ref[:, 2 * HD :]).astype(BF16)


def inner_kernel(x_ref, w_ref, e_ref, held_ref, act_ref, slope_ref):
    inner = mm(x_ref[...], w_ref[...]) + e_ref[...]
    below = 0.5 + 0.5 * lax.erf(inner * 0.7071067811865476)
    act_ref[...] = (inner * below).astype(BF16)
    density = jnp.exp(-0.5 * inner * inner) * 0.3989422804014327
    slope_ref[...] = (below + inner * density).astype(BF16)


def piece_columns(row_ref, w_refs):
    width = w_refs[0].shape[1]
    for step, w_ref in enumerate(w_refs):
        place = lax.rem(row_ref[0] + step, len(w_refs))
        yield w_ref, pl.ds(pl.multiple_of(place * width, width), width)


def outer_kernel(row_ref, act_ref, w0_ref, w1_ref, w2_ref, w3_ref, out_ref):
    act = act_ref[...]
    for w_ref, columns in piece_columns(row_ref, (w0_ref, w1_ref, w2_ref, w3_ref)):
        out_ref[:, columns] = mm(act, w_ref[...]).astype(BF16)


def outer_back_kernel(count, row_ref, *refs):
    dys, (w0_ref, w1_ref, w2_ref, w3_ref, slope_ref) = (refs[:count], refs[count : count + 5])
    dz_ref, do_ref, sum_ref, dy_sum_ref, dy_ref = refs[-5:]
    inner = slope_ref.shape[1]
    dy = dys[0][...]
    for place, ref in enumerate(dys[1:], 1):
        start = place * (pl.num_programs(0) // count)
        dy = jnp.where(pl.program_id(0) >= start, ref[...], dy)
    dy_ref[...] = dy
    total = None
    for w_ref, columns in piece_columns(row_ref, (w0_ref, w1_ref, w2_ref, w3_ref)):
        part = contract_cols(dy_ref[:, columns], w_ref[...])
        total = part if total is None else total + part
    dz = (total[:, :inner] * slope_ref[...].astype(F32)).astype(BF16)
    dz_ref[...] = dz
    do_ref[...] = total[:, inner:].astype(BF16)

    @pl.when(pl.program_id(0) == 0)
    def _():
        sum_ref[...] = jnp.zeros_like(sum_ref)
        dy_sum_ref[...] = jnp.zeros_like(dy_sum_ref)

    sum_ref[...] += jnp.sum(dz.astype(F32), axis=0, keepdims=True)
    dy_sum_ref[...] += jnp.sum(dy.astype(F32), axis=0, keepdims=True)


def inward_kernel(dz_ref, wf_ref, wq_ref, wk_ref, wv_ref, out_ref):
    start = wf_ref.shape[1]
    total = contract_cols(dz_ref[:, :start], wf_ref[...])
    for w_ref in (wq_ref, wk_ref, wv_ref):
        total += contract_cols(dz_ref[:, start : start + HD], w_ref[...])
        start += HD
    out_ref[...] = total.astype(BF16)


def attend_kernel(q_ref, k_ref, v_ref, row_ref, col_ref, out_ref, log_ref):
    scores = contract_cols(q_ref[...], k_ref[...])
    scores = jnp.where(row_ref[...] >= col_ref[...], scores, -1e30)
    peak = jnp.max(scores, axis=1, keepdims=True)
    exponents = jnp.exp(scores - peak)
    total = jnp.sum(exponents, axis=1, keepdims=True)
    out_ref[...] = mm((exponents / total).astype(BF16), v_ref[...]).astype(BF16)
    log_ref[...] = peak + jnp.log(total)


def attend_back_kernel(
    first, q_ref, k_ref, v_ref, row_ref, col_ref, log_ref, do_ref, cos_ref, sin_ref, held_ref,
    all_ref, sum_ref, out_ref, dk_ref, dv_ref, sem,
):
    step = pl.program_id(1)
    block = q_ref.shape[0]

    @pl.when(step == 0)
    def _():
        dk_ref[...] = jnp.zeros_like(dk_ref)
        dv_ref[...] = jnp.zeros_like(dv_ref)

    @pl.when((step == 0) & (pl.program_id(0) == 0))
    def _():
        sum_ref[...] = jnp.zeros_like(sum_ref)

    def column_sum(values):
        return jnp.sum(values.astype(F32), axis=0, keepdims=True)

    queries, keys_all, grads = (q_ref[...], k_ref[...], do_ref[...])
    scores = contract_cols(queries, keys_all)
    scores = jnp.where(row_ref[...] >= col_ref[...], scores, -1e30)
    probs = jnp.exp(scores - log_ref[...])
    grad_probs = contract_cols(grads, v_ref[...])
    centre = jnp.sum(probs * grad_probs, axis=1, keepdims=True)
    grad_scores = (probs * (grad_probs - centre)).astype(BF16)
    rows = pl.ds(pl.multiple_of(step * block, block), block)
    cosines, sines = cos_ref[rows, :], sin_ref[rows, :]
    grad_queries = mm(grad_scores, keys_all) * HD ** (-0.5)
    grad_queries = turn(grad_queries, cosines, -sines).astype(BF16)
    out_ref[rows, :HD] = grad_queries
    sum_ref[:, :HD] += column_sum(grad_queries)
    dk_ref[...] += contract_rows(grad_scores, queries)
    dv_ref[...] += contract_rows(probs.astype(BF16), grads)

    @pl.when(step == pl.num_programs(1) - 1)
    def _():
        grad_keys = turn(dk_ref[...], cos_ref[...], -sin_ref[...]).astype(BF16)
        grad_values = dv_ref[...].astype(BF16)
        out_ref[:, HD : 2 * HD] = grad_keys
        out_ref[:, 2 * HD :] = grad_values
        sum_ref[:, HD : 2 * HD] += column_sum(grad_keys)
        sum_ref[:, 2 * HD :] += column_sum(grad_values)
        length, width = out_ref.shape
        micro = pl.ds(pl.multiple_of((first + pl.program_id(0)) * length, length), length)
        copy = pltpu.make_async_copy(
            out_ref, all_ref.at[micro, pl.ds(all_ref.shape[1] - width, width)], sem
        )
        copy.start()
        copy.wait()


ROW_BLOCK = 256


def by_rows(width, block=ROW_BLOCK):
    return pl.BlockSpec((block, width), lambda i: (i, 0))


def whole(shape):
    return pl.BlockSpec(shape, lambda *unused: (0,) * len(shape))


def panel(width, place):
    return lambda deep: pl.BlockSpec((deep, width), lambda *unused: (0, place))


def cost(flops, *arrays):
    return pl.CostEstimate(
        flops=flops,
        transcendentals=0,
        bytes_accessed=sum(math.prod(array.shape) * array.dtype.itemsize for array in arrays),
    )


def heads_panels(array, inner):
    return [panel(HD, inner // HD + part)(array.shape[0]) for part in range(3)]


def project(x, w, inner, e, tables):
    rows, width = x.shape
    per_micro = tables[0].shape[0] // ROW_BLOCK
    table = pl.BlockSpec((ROW_BLOCK, LANES), lambda i: (i % per_micro, 0))
    out = jax.ShapeDtypeStruct((rows, HD), BF16)
    return pl.pallas_call(
        project_kernel,
        grid=(rows // ROW_BLOCK,),
        in_specs=[by_rows(width), *heads_panels(w, inner), whole(e.shape), table, table],
        out_specs=[by_rows(HD)] * 3,
        out_shape=[out] * 3,
        cost_estimate=cost(6 * rows * width * HD, x, out, out, out),
        name="project",
    )(x, w, w, w, e, *tables)


def inner_layer(x, w, e, held):
    rows, width = x.shape
    inner = e.shape[1]
    slope = jax.ShapeDtypeStruct((rows, inner), BF16)
    return pl.pallas_call(
        inner_kernel,
        grid=(rows // ROW_BLOCK,),
        in_specs=[
            by_rows(width),
            panel(inner, 0)(width),
            whole(e.shape),
            pl.BlockSpec(memory_space=pl.ANY),
        ],
        out_specs=[by_rows(inner)] * 2,
        out_shape=[jax.ShapeDtypeStruct(held.shape, BF16), slope],
        input_output_aliases={3: 0},
        cost_estimate=cost(2 * rows * width * inner, x, slope, slope),
        name="inner",
    )(x, w, e, held)


def split_rows(width, other):
    return pl.BlockSpec((ROW_BLOCK, width), lambda i: (i // 2 * 4 + 2 * other + i % 2, 0))


def outer(act, pieces, row, other):
    rows, width = (act.shape[0] // 2, len(pieces) * pieces[0].shape[1])
    out = jax.ShapeDtypeStruct((rows, width), BF16)
    return pl.pallas_call(
        outer_kernel,
        grid=(rows // ROW_BLOCK,),
        in_specs=[
            pl.BlockSpec(memory_space=pltpu.SMEM),
            split_rows(act.shape[1], other),
            *(whole(piece.shape) for piece in pieces),
        ],
        out_specs=by_rows(width),
        out_shape=out,
        cost_estimate=cost(2 * rows * width * act.shape[1], act, out),
        name="outer",
    )(row, act, *pieces)


def inward(dz, w_in, w_qkv, offset, other):
    rows, width = (dz.shape[0] // 2, w_in.shape[0])
    out = jax.ShapeDtypeStruct((rows, width), BF16)
    return pl.pallas_call(
        inward_kernel,
        grid=(rows // ROW_BLOCK,),
        in_specs=[
            split_rows(dz.shape[1], other),
            panel(dz.shape[1] - 3 * HD, 0)(width),
            *heads_panels(w_qkv, offset),
        ],
        out_specs=by_rows(width),
        out_shape=out,
        cost_estimate=cost(2 * rows * width * dz.shape[1], dz, out),
        name="inward",
    )(dz, w_in, w_qkv, w_qkv, w_qkv)


def outer_back(dys, pieces, row, slopes, start=0, held=None):
    rows, width = (sum(dy.shape[0] for dy in dys), dys[0].shape[1])
    inner = slopes.shape[1]
    each, first = (dys[0].shape[0] // ROW_BLOCK, start // ROW_BLOCK)

    def part(place):
        return pl.BlockSpec(
            (ROW_BLOCK, width), lambda i: (jnp.clip(i - place * each, 0, each - 1), 0)
        )

    below = pl.BlockSpec((ROW_BLOCK, inner), lambda i: (first + i, 0))
    extra = () if held is None else (held,)
    return pl.pallas_call(
        functools.partial(outer_back_kernel, len(dys)),
        grid=(rows // ROW_BLOCK,),
        in_specs=[
            pl.BlockSpec(memory_space=pltpu.SMEM),
            *(part(place) for place in range(len(dys))),
            *(whole(piece.shape) for piece in pieces),
            below,
            *(pl.BlockSpec(memory_space=pl.ANY) for member in extra),
        ],
        out_specs=[below, by_rows(HD), whole((1, inner)), whole((1, width))],
        out_shape=[
            jax.ShapeDtypeStruct((slopes.shape[0], inner + 3 * HD), BF16),
            jax.ShapeDtypeStruct((rows, HD), BF16),
            jax.ShapeDtypeStruct((1, inner), F32),
            jax.ShapeDtypeStruct((1, width), F32),
        ],
        scratch_shapes=[pltpu.VMEM((ROW_BLOCK, width), BF16)],
        input_output_aliases={6 + len(dys): 0} if extra else {},
        cost_estimate=cost(2 * rows * width * (inner + HD), *dys, slopes),
        name="outer_back",
    )(row, *dys, *pieces, slopes, *extra)


def attend(queries, keys_all, values_all, places, inner):
    rows = queries.shape[0]
    length = places.shape[0]
    steps = length // ROW_BLOCK
    row = pl.BlockSpec((ROW_BLOCK, HD), lambda m, i: (m * steps + i, 0))
    every = pl.BlockSpec((length, HD), lambda m, i: (m, 0))
    return pl.pallas_call(
        attend_kernel,
        grid=(rows // length, steps),
        in_specs=[
            row,
            every,
            every,
            pl.BlockSpec((ROW_BLOCK, 1), lambda m, i: (i, 0)),
            pl.BlockSpec((1, length), lambda m, i: (0, 0)),
        ],
        out_specs=[
            pl.BlockSpec((ROW_BLOCK, HD), lambda m, i: (m * steps + i, inner // HD)),
            pl.BlockSpec((ROW_BLOCK, 1), lambda m, i: (m * steps + i, 0)),
        ],
        out_shape=[
            jax.ShapeDtypeStruct((rows, inner + HD), BF16),
            jax.ShapeDtypeStruct((rows, 1), F32),
        ],
        cost_estimate=cost(4 * rows * length * HD, queries, keys_all, values_all, queries),
        name="attend",
    )(queries, keys_all, values_all, places[:, None], places[None, :])


def attend_back(queries, keys_all, values_all, places, log_sums, grads, tables, held, first=0):
    rows = grads.shape[0]
    length = places.shape[0]
    steps = length // ROW_BLOCK
    row = pl.BlockSpec((ROW_BLOCK, HD), lambda m, i: ((first + m) * steps + i, 0))
    every = pl.BlockSpec((length, HD), lambda m, i: (first + m, 0))
    anywhere = pl.BlockSpec(memory_space=pl.ANY)
    return pl.pallas_call(
        functools.partial(attend_back_kernel, first),
        grid=(rows // length, steps),
        in_specs=[
            row,
            every,
            every,
            pl.BlockSpec((ROW_BLOCK, 1), lambda m, i: (i, 0)),
            pl.BlockSpec((1, length), lambda m, i: (0, 0)),
            pl.BlockSpec((ROW_BLOCK, 1), lambda m, i: ((first + m) * steps + i, 0)),
            pl.BlockSpec((ROW_BLOCK, HD), lambda m, i: (m * steps + i, 0)),
            whole(tables[0].shape),
            whole(tables[1].shape),
            anywhere,
        ],
        out_specs=[anywhere, whole((1, 3 * HD))],
        out_shape=[
            jax.ShapeDtypeStruct(held.shape, BF16),
            jax.ShapeDtypeStruct((1, 3 * HD), F32),
        ],
        scratch_shapes=[
            pltpu.VMEM((length, 3 * HD), BF16),
            pltpu.VMEM((length, HD), F32),
            pltpu.VMEM((length, HD), F32),
            pltpu.SemaphoreType.DMA,
        ],
        input_output_aliases={9: 0},
        cost_estimate=cost(10 * rows * length * HD, queries, keys_all, values_all, grads),
        name="attend_back",
    )(
        queries, keys_all, values_all, places[:, None], places[None, :], log_sums, grads, *tables,
        held,
    )


def local(
    inputs,
    cotangent,
    qkv_weight,
    qkv_bias,
    out_weight,
    fc_in_weight,
    fc_in_bias,
    fc_out_weight,
    norm1_gain,
    norm1_bias,
    norm2_gain,
    norm2_bias,
    out_bias,
    fc_out_bias,
):
    s, r, c = (lax.axis_index(SECTION), lax.axis_index(ROW), lax.axis_index(COL))
    rows_axis, cols_axis = (lax.axis_size(ROW), lax.axis_size(COL))
    low = s == 0
    qkv_w, out_w, fc_in_w, fc_out_w = (
        qkv_weight[0], out_weight[0], fc_in_weight[0], fc_out_weight[0],
    )
    deep, heads_here = qkv_w.shape[0], qkv_w.shape[1]
    per = 3 * HD
    inner = fc_in_w.shape[1] // 2
    model = inputs.shape[2]

    def both_layers(own_first, own_second):
        return (jnp.where(low, own_first, own_second), jnp.where(low, own_second, own_first))

    def trade(value, axis, *others):
        size = value.shape[axis] // 2
        kept = take(value, axis, s, size)
        came = swap(after(take(value, axis, 1 - s, size), *others), SECTION, 1)
        return kept, came

    def gathered(shard, axis):
        return lax.all_gather(shard, ROW, axis=axis, tiled=True)

    held = jnp.stack(
        [
            norm1_gain[0].astype(F32),
            norm1_bias[0].astype(F32),
            norm2_gain[0].astype(F32),
            norm2_bias[0].astype(F32),
            out_bias[0].astype(F32) + fc_out_bias[0].astype(F32),
        ]
    )
    held_both = jnp.stack([held, swap(held, SECTION, 1)])
    qkv_flat = qkv_w.reshape(deep, -1)
    qkv_half = trade(qkv_flat, 1, held_both)
    fc_in_half = trade(fc_in_w, 1, qkv_half[1])
    outs_kept = jnp.concatenate([take(fc_out_w, 0, s, inner), take(out_w, 0, s, HD)], axis=0)
    outs_sent = jnp.concatenate([take(fc_out_w, 0, 1 - s, inner), take(out_w, 0, 1 - s, HD)], axis=0)
    outs_came = swap(after(outs_sent, fc_in_half[1]), SECTION, 1)
    held_both = sum_over(place(held_both, 2, c, deep), COL)
    held = held_both[0]
    gain_one, shift_one, gain_two, shift_two, end_bias = (held[i] for i in range(5))
    gains = both_layers(held, held_both[1])

    def scaled_pair(half, row):
        return tuple(
            (part.astype(F32) * gain[row][:, None]).astype(BF16)
            for part, gain in zip(both_layers(*half), gains)
        )

    qkv_pair = scaled_pair(qkv_half, 0)
    fc_in_pair = scaled_pair(fc_in_half, 2)
    outs_pair = both_layers(outs_kept, outs_came)
    w_qkv0 = gathered(qkv_pair[0], 0)
    w_fc_in0 = gathered(fc_in_pair[0], 0)
    w_ins1 = gathered(jnp.concatenate([fc_in_pair[1], qkv_pair[1]], axis=1), 0)
    w_ins = ((w_fc_in0, w_qkv0, 0), (w_ins1, w_ins1, inner))
    w_outs = [gather_pieces(outs_pair[layer]) for layer in range(2)]
    row = r.astype(jnp.int32)[None]

    own_qkv = mm(shift_one.astype(BF16)[None], qkv_flat)[0]
    own_fc = mm(shift_two.astype(BF16)[None], fc_in_w)[0]
    own_qkv = own_qkv + place(qkv_bias[0].astype(F32), 1, r, per).reshape(-1)
    own_fc = own_fc + place(fc_in_bias[0].astype(F32), 0, r, 2 * inner)
    biases = sum_over(
        jnp.concatenate([own_qkv, own_fc, place(end_bias, 0, r, model)]), ROW
    )
    biases = both_layers(biases, swap(biases, SECTION, 1))
    qkv_e, fc_e, end_e = ([], [], [])
    for member in biases:
        qkv_e.append(take(member[: 2 * per], 0, s, per)[None])
        fc_e.append(take(member[2 * per : 2 * per + 2 * inner], 0, s, inner)[None])
        end_e.append(member[2 * per + 2 * inner :])

    block_rows = inputs.shape[1]
    masks = jnp.array([0, 2, 1, 3], jnp.int32)
    places = ((c ^ masks)[:, None] * block_rows + jnp.arange(block_rows)[None]).reshape(-1)
    inverse = 10000.0 ** (-jnp.arange(0, ROT, 2).astype(F32) / ROT)
    angles = places.astype(F32)[:, None] * inverse[None]
    ones = jnp.ones((places.shape[0], LANES - ROT), F32)
    cosines, sines = (jnp.cos(angles), jnp.sin(angles))
    tables = (
        jnp.concatenate([cosines, cosines, ones], axis=1),
        jnp.concatenate([-sines, sines, 0.0 * ones], axis=1),
    )

    hidden = lax.dynamic_index_in_dim(inputs, s, 0, keepdims=False)
    seed = lax.dynamic_index_in_dim(cotangent, s, 0, keepdims=False)
    hidden = after(hidden, outs_came)

    hidden_list, kept_list, ends = ([], [], [])
    seed_rows = None
    for layer in range(2):
        hidden_list.append(hidden)
        scaled, unused = norm_rows(hidden.astype(F32))
        x, unused = gather_rows(scaled.astype(BF16))
        x = jnp.concatenate(x, axis=0)
        if layer == 0:
            seed_rows, unused = gather_rows(after(seed, x))
            seed_rows = jnp.concatenate(seed_rows, axis=0)
        w_fc_in, w_qkv, offset = w_ins[layer]
        queries, keys_all, values_all = project(x, w_qkv, offset, qkv_e[layer], tables)
        attended, log_sums = attend(queries, keys_all, values_all, places, inner)
        if layer == 1:
            out_grad1 = contract_rows(attended[:, inner:], seed_rows).astype(BF16)
            attended = after(attended, out_grad1)
        act, slopes = inner_layer(x, w_fc_in, fc_e[layer], attended)
        if layer == 0:
            *pieces, act, unused = lax.optimization_barrier((*w_outs[0][1:], act, seed_rows))
            w_outs[0] = in_turn((w_outs[0][0], *pieces), r)
        kept = (x, queries, keys_all, values_all, log_sums, slopes, act)
        if layer == 1:
            outs_grad1 = contract_rows(act[:, :inner], seed_rows).astype(BF16)
            seed_rows = after(seed_rows, outs_grad1)
            *pieces, unused = lax.optimization_barrier((*w_outs[1][1:], outs_grad1))
            w_outs[1] = in_turn((w_outs[1][0], *pieces), r)
        kept_list.append(kept)
        if layer == 0:
            summed = scatter_rows(lambda other: outer(act, w_outs[0], row, other))
            hidden = (hidden.astype(F32) + summed + end_e[layer]).astype(BF16)
            ends.append(hidden)
            middle = swap(hidden, SECTION, 1)

    def reduced(value, axis):
        return lax.psum_scatter(value, ROW, scatter_dimension=axis, tiled=True)

    out_part1 = reduced(out_grad1, 1)
    outs_part1 = jnp.concatenate([reduced(outs_grad1, 1), out_part1], axis=0)
    grads = seed
    ins_list, small_list = ([None, None], [None, None])
    for layer in (1, 0):
        x, queries, keys_all, values_all, log_sums, slopes, act = kept_list[layer]
        w_fc_in, w_qkv, offset = w_ins[layer]
        if layer == 1:
            dy = seed_rows
        else:
            dys, across = gather_rows(grads)
            dy = jnp.concatenate(lax.optimization_barrier(dys), axis=0)
            middle_grads = (jnp.where(low, grads, across), jnp.where(low, across, grads))
        halves = ((dy,),) if layer == 1 else (dys[:2], dys[2:])
        dz, start, column_sums = (None, 0, [])
        for half in halves:
            dz, grad_attended, inner_sum, dy_sum = outer_back(
                half, w_outs[layer], row, slopes, start, dz
            )
            dz, heads_sum = attend_back(
                queries, keys_all, values_all, places, log_sums, grad_attended, tables, dz,
                start // places.shape[0],
            )
            start += grad_attended.shape[0]
            column_sums.append((heads_sum[0], inner_sum[0], dy_sum[0]))
        combined = scatter_rows(lambda other: inward(dz, w_fc_in, w_qkv, offset, other))
        ins_grad = contract_rows(x, dz).astype(BF16)
        ins_list[layer] = reduced(ins_grad, 0)
        scaled, inverse_std = norm_rows(hidden_list[layer].astype(F32))
        grad_norm = inverse_std * (
            combined
            - jnp.mean(combined, axis=-1, keepdims=True)
            - scaled * jnp.mean(combined * scaled, axis=-1, keepdims=True)
        )
        grads = (grads.astype(F32) + grad_norm).astype(BF16)
        small_list[layer] = tuple(sum(members) for members in zip(*column_sums))
        if layer == 0:
            fc_out_part0 = reduced(contract_rows(act[:, :inner], dy).astype(BF16), 1)
            out_part0 = reduced(contract_rows(act[:, inner:], dy).astype(BF16), 1)
    act = kept_list[1][-1]
    summed = scatter_rows(lambda other: outer(act, w_outs[1], row, other))
    summed = after(summed, small_list[0][0])
    ends.append((hidden_list[1].astype(F32) + summed + end_e[1]).astype(BF16))

    def to_owner(first, second, upper, lower):
        return (jnp.where(low, first, lower), jnp.where(low, upper, second))

    def to_first(value):
        return lax.ppermute(value, SECTION, [(1, 0)])

    def to_second(value):
        return lax.ppermute(value, SECTION, [(0, 1)])

    small = sum_over(
        jnp.concatenate(
            [*small_list[0][:2], *small_list[1][:2], small_list[0][2], small_list[1][2]]
        ),
        ROW,
    )
    sums = small[: 2 * (per + inner)]
    sums_other = swap(sums, SECTION, 1)
    smalls = to_owner(*jnp.split(sums, 2), *jnp.split(sums_other, 2))
    end_grad = jnp.where(low, *jnp.split(small[2 * (per + inner) :], 2))
    qkv_b_grad = jnp.concatenate([member[:per] for member in smalls])
    fc_in_b_grad = jnp.concatenate([member[per:] for member in smalls])
    outs_lower = to_second(outs_part1)
    ins_lower = to_second(ins_list[1])
    ins_upper = to_first(ins_list[0])
    ins_g = to_owner(*ins_list, ins_upper, ins_lower)
    qkv_g = jnp.concatenate([member[:, inner:] for member in ins_g], axis=1).astype(F32)
    fc_in_g = jnp.concatenate([member[:, :inner] for member in ins_g], axis=1).astype(F32)
    qkv_w_grad = gain_one[:, None] * qkv_g + shift_one[:, None] * qkv_b_grad[None]
    fc_in_w_grad = gain_two[:, None] * fc_in_g + shift_two[:, None] * fc_in_b_grad[None]
    norm_parts = []
    for layer, (w_q, w_f) in enumerate(zip(both_layers(*qkv_half), both_layers(*fc_in_half))):
        w_q, w_f = (w_q.astype(F32), w_f.astype(F32))
        heads, hidden_sum = jnp.split(sums[layer * (per + inner) :][: per + inner], [per])
        part = ins_list[layer].astype(F32)
        norm_parts.append(
            jnp.stack(
                [
                    jnp.sum(w_q * part[:, inner:], axis=1),
                    jnp.sum(w_q * heads[None], axis=1),
                    jnp.sum(w_f * part[:, :inner], axis=1),
                    jnp.sum(w_f * hidden_sum[None], axis=1),
                ]
            )
        )
    norms = jnp.where(low, *norm_parts) + swap(jnp.where(low, *norm_parts[::-1]), SECTION, 1)
    norms = take(sum_over(norms, COL), 1, c, deep // cols_axis)
    end_grad = take(end_grad, 0, r * cols_axis + c, deep // cols_axis)
    fc_out_part0 = after(fc_out_part0, ins_upper, norms)
    fc_out_upper = to_first(fc_out_part0)
    fc_out_w_grad = jnp.concatenate(
        [
            jnp.where(low, fc_out_part0, outs_lower[:inner]),
            jnp.where(low, fc_out_upper, outs_part1[:inner]),
        ],
        axis=0,
    ).astype(F32)[None]
    qkv_w_grad = qkv_w_grad.reshape(qkv_w.shape)[None]
    fc_in_w_grad = fc_in_w_grad[None]
    out_part0, fc_out_w_grad, norms = lax.optimization_barrier(
        (out_part0, fc_out_w_grad, norms)
    )
    out_upper = to_first(out_part0)
    out_w_grad = jnp.concatenate(
        [
            jnp.where(low, out_part0, outs_lower[inner:]),
            jnp.where(low, out_upper, outs_part1[inner:]),
        ],
        axis=0,
    ).astype(F32)
    last = to_second(ends[1])
    first = to_first(grads)
    last, first = (after(last, norms), after(first, norms))
    layer_outputs = jnp.stack([jnp.where(low, ends[0], last), jnp.where(low, middle, ends[1])])
    input_gradients = jnp.stack(
        [jnp.where(low, grads, middle_grads[0]), jnp.where(low, first, middle_grads[1])]
    )
    return (
        layer_outputs[None],
        input_gradients[None],
        qkv_w_grad,
        take(qkv_b_grad.reshape(heads_here, -1), 1, r, per // rows_axis)[None],
        out_w_grad[None],
        fc_in_w_grad,
        take(fc_in_b_grad, 0, r, 2 * inner // rows_axis)[None],
        fc_out_w_grad,
        norms[0][None],
        norms[1][None],
        norms[2][None],
        norms[3][None],
        end_grad[None],
        end_grad[None],
    )


def all_of_it(*arrays):
    return local(*arrays)


def solution(mesh):
    sizes = mesh.shape
    paired = sizes[SECTION] == 2 and sizes[COL] == 4
    body = all_of_it if paired and sizes[ROW] == 4 else relay_local
    step = jax.shard_map(
        body,
        mesh=mesh,
        in_specs=(
            P(None, (ROW, COL), None),
            P(None, (ROW, COL), None),
            P(SECTION, ROW, COL, None),
            P(SECTION, COL, ROW),
            P(SECTION, COL, ROW),
            P(SECTION, ROW, COL),
            P(SECTION, (COL, ROW)),
            P(SECTION, COL, ROW),
            P(SECTION, (ROW, COL)),
            P(SECTION, (ROW, COL)),
            P(SECTION, (ROW, COL)),
            P(SECTION, (ROW, COL)),
            P(SECTION, (ROW, COL)),
            P(SECTION, (ROW, COL)),
        ),
        out_specs=(
            P(SECTION, None, (ROW, COL), None),
            P(SECTION, None, (ROW, COL), None),
            P(SECTION, ROW, COL, None),
            P(SECTION, COL, ROW),
            P(SECTION, COL, ROW),
            P(SECTION, ROW, COL),
            P(SECTION, (COL, ROW)),
            P(SECTION, COL, ROW),
            P(SECTION, (ROW, COL)),
            P(SECTION, (ROW, COL)),
            P(SECTION, (ROW, COL)),
            P(SECTION, (ROW, COL)),
            P(SECTION, (ROW, COL)),
            P(SECTION, (ROW, COL)),
        ),
        check_vma=False,
    )
    if body is relay_local:
        return step
    return step
```
